32 devices in a mesh: dp: 4 (over y, x), fsdp: 8 (over z, core).
Axes of the slice: x: 2, y: 2, z: 4, core: 2. Of those that a mesh axis runs over, the one named last changes fastest.
Arguments:
- tokens: bfloat16 [32768, 1024], P(('dp', 'fsdp')), may hold values from -6 to 6
- cotangent: bfloat16 [32768, 1024], P(('dp', 'fsdp')), may hold values from -15 to 15
- clip_frames: int32 [32, 4], P(('dp', 'fsdp')), may hold values from 0 to 4, as said below
- levels: int32 [128], P(('dp', 'fsdp')), may hold values from 0 to 999
- pad_mask: int32 [32768], P(('dp', 'fsdp')), may hold values from 0 to 1, as said below
- w_mod: bfloat16 [1024, 6144], P(('dp', 'fsdp')), may hold values from -0.1875 to 0.1875
- b_mod: bfloat16 [6144], P(('dp', 'fsdp')), may hold values from -3 to 3
- w_qkv: bfloat16 [1024, 3072], P(('dp', 'fsdp')), may hold values from -0.1875 to 0.1875
- b_qkv: bfloat16 [3072], P(('dp', 'fsdp')), may hold values from -3 to 3
- w_out: bfloat16 [1024, 1024], P(('dp', 'fsdp')), may hold values from -3 to 3
- b_out: bfloat16 [1024], P(('dp', 'fsdp')), may hold values from -3 to 3
- w_up: bfloat16 [1024, 4096], P(('dp', 'fsdp')), may hold values from -0.1875 to 0.1875
- b_up: bfloat16 [4096], P(('dp', 'fsdp')), may hold values from -3 to 3
- w_down: bfloat16 [4096, 1024], P(('dp', 'fsdp')), may hold values from -0.09375 to 0.09375
- b_down: bfloat16 [1024], P(('dp', 'fsdp')), may hold values from -3 to 3
- noise_table: bfloat16 [1024, 1000], P(('dp', 'fsdp')), may hold values from -6 to 6
Outputs:
- block_out: bfloat16 [32768, 1024], P(('dp', 'fsdp'))
- token_grad: bfloat16 [32768, 1024], P(('dp', 'fsdp'))
- wmod_grad: float32 [1024, 6144], P(('dp', 'fsdp'))
- bmod_grad: float32 [6144], P(('dp', 'fsdp'))
- wqkv_grad: float32 [1024, 3072], P(('dp', 'fsdp'))
- bqkv_grad: float32 [3072], P(('dp', 'fsdp'))
- wout_grad: float32 [1024, 1024], P(('dp', 'fsdp'))
- bout_grad: float32 [1024], P(('dp', 'fsdp'))
- wup_grad: float32 [1024, 4096], P(('dp', 'fsdp'))
- bup_grad: float32 [4096], P(('dp', 'fsdp'))
- wdown_grad: float32 [4096, 1024], P(('dp', 'fsdp'))
- bdown_grad: float32 [1024], P(('dp', 'fsdp'))
- table_grad: float32 [1024, 1000], P(('dp', 'fsdp'))
The draws below stay inside these ranges and needn't reach their ends.
Inputs may be any that keep to these rules, and one draw needn't show every extreme that they name: `clip_frames`: each row sums to 4, its nonzero entries come first; in every draw some device's row is one clip of 4 frames. `pad_mask`: the first of the 256 tokens of every frame is live.
All inputs are finite; a program needn't handle non-finite values.
Results may differ from the reference program's by a relative error of at most 0.013.
The reference program's roundings to bfloat16 on the way count: a program that leaves them out, or rounds other values in their place, can miss the bound.
Values may be sent and summed in bfloat16 or wider, within the bound.
A program may use at most 256 MiB of HBM per device.

```python
import jax
import jax.numpy as jnp
from jax import lax

D = 1024
H = 16
HD = 64
FF = 4096
NLEV = 1000
PATCH = 256
FR_DEV = 4
TOK_DEV = 1024
NDEV = 32
TOKENS = 32768
FRAMES = 128


def draw_clip_frames(key, part):
    flags = jax.random.randint(key, (NDEV, FR_DEV), 0, 2)
    first = (jnp.arange(FR_DEV) == 0)[None, :]
    flags = jnp.where(first, 1, flags)
    chosen = jax.random.randint(jax.random.fold_in(key, 7), (), 0, NDEV)
    rows = jnp.arange(NDEV)[:, None]
    flags = jnp.where(rows == chosen, first.astype(jnp.int32), flags)
    which = (jnp.cumsum(flags, axis=1) - 1).astype(jnp.int32)
    slots = jnp.arange(FR_DEV)
    return jnp.sum((which[:, :, None] == slots[None, None, :]).astype(jnp.int32), axis=1).astype(jnp.int32)


def draw_pad_mask(key, part):
    live = jax.random.randint(key, (TOKENS,), 0, 8) > 0
    first = jnp.arange(TOKENS) % PATCH == 0
    return jnp.where(first | live, 1, 0).astype(jnp.int32)


def draw_cotangent(key, part):
    device_row = (jnp.arange(TOKENS) // TOK_DEV).astype(jnp.float32)
    rise = jnp.exp(jnp.log(3.0) * device_row / max(NDEV - 1, 1))
    base = jax.random.normal(key, (TOKENS, D))
    base = jnp.clip(base, -5.0, 5.0)
    return (base * rise[:, None]).astype(jnp.bfloat16)


def plant(array, own_key, low, largest):
    index_at = [jax.random.randint(jax.random.fold_in(own_key, axis), (), 0, length) for axis, length in enumerate(array.shape)]
    widest = array.shape.index(max(array.shape))
    beside = index_at[:widest] + [(index_at[widest] + 1) % array.shape[widest]] + index_at[widest + 1:]
    return array.at[tuple(index_at)].set(low).at[tuple(beside)].set(largest)


def level_of(key, shape, pieces, least, high):
    factor_of = 1.0
    for axis_at, shards_of in pieces:
        heights = jax.random.uniform(jax.random.fold_in(jax.random.fold_in(key, 6), axis_at), (shards_of,), jnp.float32, least / len(pieces), high / len(pieces))
        factor_of = factor_of * jnp.repeat(jnp.exp(heights), shape[axis_at] // shards_of).reshape((-1,) + (1,) * (len(shape) - 1 - axis_at))
    return factor_of


def scatter_about(key, extent, deviation, limit, pieces=(), kind=jnp.bfloat16):
    entries = jax.random.normal(key, extent, jnp.float32) * deviation
    if len(pieces) > 0:
        entries = level_of(key, extent, pieces, -0.22, 0.18) * entries
    return jnp.clip(entries, min=-limit, max=limit).astype(kind)


def setup_inputs(seed: int = 0) -> dict:
    seeds = jax.random.split(jax.random.key(seed), 17)
    return {
        "tokens": scatter_about(seeds[0], (TOKENS, D), 1.0, 6.0, ((0, 32),)),
        "cotangent": draw_cotangent(jax.random.fold_in(seeds[16], 71), 0),
        "clip_frames": draw_clip_frames(jax.random.fold_in(seeds[16], 71), 0),
        "levels": plant(jax.random.randint(seeds[3], (FRAMES,), 0, NLEV), jax.random.fold_in(seeds[3], 1), 0, NLEV - 1).astype(jnp.int32),
        "pad_mask": draw_pad_mask(jax.random.fold_in(seeds[16], 71), 0),
        "w_mod": scatter_about(seeds[5], (D, 6 * D), D ** -0.5, 0.1875, ((0, 32),)),
        "b_mod": scatter_about(seeds[6], (6 * D,), 0.5, 3.0, ((0, 32),)),
        "w_qkv": scatter_about(seeds[7], (D, 3 * D), D ** -0.5, 0.1875, ((0, 32),)),
        "b_qkv": scatter_about(seeds[8], (3 * D,), 0.5, 3.0, ((0, 32),)),
        "w_out": scatter_about(seeds[9], (D, D), (max(D // 256, 4)) ** -0.5, 3.0, ((0, 32),)),
        "b_out": scatter_about(seeds[10], (D,), 0.5, 3.0, ((0, 32),)),
        "w_up": scatter_about(seeds[11], (D, FF), D ** -0.5, 0.1875, ((0, 32),)),
        "b_up": scatter_about(seeds[12], (FF,), 0.5, 3.0, ((0, 32),)),
        "w_down": scatter_about(seeds[13], (FF, D), FF ** -0.5, 0.09375, ((0, 32),)),
        "b_down": scatter_about(seeds[14], (D,), 0.5, 3.0, ((0, 32),)),
        "noise_table": scatter_about(seeds[15], (D, NLEV), 1.0, 6.0, ((0, 32),)),
    }


epsilon = 1e-06
highest = lax.Precision.HIGHEST

@jax.custom_vjp
def low(v):
    return lax.optimization_barrier(v.astype(jnp.bfloat16)).astype(jnp.float32)

@jax.custom_vjp
def low_back(v):
    return v

def low_keep(v):
    return (low(v), None)

def low_pass(kept, grad):
    return (grad,)

def back_keep(v):
    return (v, None)

def back_low(kept, grad):
    return (low(grad),)
low.defvjp(low_keep, low_pass)
low_back.defvjp(back_keep, back_low)

def matmul(left, right):
    return jnp.dot(left, right, precision=highest)

def layer_norm(values):
    centred = values - lax.optimization_barrier(jnp.mean(values, axis=-1, keepdims=True))
    return centred * lax.rsqrt(lax.optimization_barrier(jnp.mean(centred * centred, axis=-1, keepdims=True)) + epsilon)

def clip_positions(clip_row, patch_size):
    frame_count = clip_row.shape[0]
    slots = jnp.arange(frame_count, dtype=jnp.int32)
    ends = jnp.cumsum(clip_row).astype(jnp.int32)
    clip_of = lax.optimization_barrier(jnp.sum((slots[:, None] >= ends[None, :]).astype(jnp.int32), axis=1)).astype(jnp.int32)
    starts = (ends - clip_row).astype(jnp.int32)
    start_of = lax.optimization_barrier(jnp.sum(jnp.where(clip_of[:, None] == slots[None, :], starts[None, :], 0), axis=1)).astype(jnp.int32)
    frame_of = (slots - start_of).astype(jnp.int32)
    return (jnp.repeat(clip_of, patch_size), jnp.repeat(frame_of, patch_size))

def rotate(values, frame_tok, patch_tok, sign):
    half_dim = values.shape[-1] // 2
    quarter_dim = half_dim // 2
    freq = 10000.0 ** (-jnp.arange(quarter_dim, dtype=jnp.float32) / quarter_dim)
    angle = jnp.concatenate([frame_tok.astype(jnp.float32)[:, None] * freq[None, :], patch_tok.astype(jnp.float32)[:, None] * freq[None, :]], axis=1)
    cosine = jnp.cos(angle)[:, None, :]
    sine = sign * jnp.sin(angle)[:, None, :]
    first = values[..., :half_dim]
    second = values[..., half_dim:]
    return jnp.concatenate([first * cosine - second * sine, second * cosine + first * sine], axis=-1)

def block_forward(params, block_x, block_levels, clip_row, block_pad):
    w_mod, b_mod, w_qkv, b_qkv, w_out, b_out, w_up, b_up, w_down, b_down, noise_table = params
    tok_count = block_x.shape[0]
    clip_tok, frame_tok = clip_positions(clip_row, PATCH)
    patch_tok = jnp.arange(tok_count, dtype=jnp.int32) % PATCH
    embedded = jnp.take(noise_table, block_levels, axis=1).T
    cond_low = low(jax.nn.silu(embedded))
    modulation = low_back(matmul(cond_low, w_mod) + b_mod)
    modulation = jnp.repeat(modulation, PATCH, axis=0)
    shift_one, scale_one, gate_one, shift_two, scale_two, gate_two = jnp.split(modulation, 6, axis=1)
    act_one = low(layer_norm(block_x) * (1.0 + scale_one) + shift_one)
    projected = low_back(matmul(act_one, w_qkv) + b_qkv)
    query_raw, key_raw, value_raw = jnp.split(projected, 3, axis=1)
    head_shape = (tok_count, H, HD)
    query = low(rotate(query_raw.reshape(head_shape), frame_tok, patch_tok, 1.0))
    keys_rot = low(rotate(key_raw.reshape(head_shape), frame_tok, patch_tok, 1.0))
    values_low = low(value_raw.reshape(head_shape))
    scores = low_back(jnp.einsum('qhd,khd->hqk', query, keys_rot, precision=highest) * 0.125)
    allowed = (clip_tok[:, None] == clip_tok[None, :]) & (frame_tok[None, :] <= frame_tok[:, None]) & (block_pad[None, :] == 1)
    scores = jnp.where(allowed[None], scores, -1e+30)
    softmax_w = low(jax.nn.softmax(scores, axis=-1))
    attended = jnp.einsum('hqk,khd->qhd', softmax_w, values_low, precision=highest).reshape(tok_count, H * HD)
    attended = low(low_back(attended))
    attn_out = low_back(matmul(attended, w_out) + b_out)
    middle = block_x + gate_one * attn_out
    act_two = low(layer_norm(middle) * (1.0 + scale_two) + shift_two)
    hidden_up = low_back(matmul(act_two, w_up) + b_up)
    activated = low(jax.nn.gelu(hidden_up, approximate=False))
    branch = low_back(matmul(activated, w_down) + b_down)
    return middle + gate_two * branch

def reference(tokens, cotangent, clip_frames, levels, pad_mask, w_mod, b_mod, w_qkv, b_qkv, w_out, b_out, w_up, b_up, w_down, b_down, noise_table):
    params = tuple((tensor.astype(jnp.float32) for tensor in (w_mod, b_mod, w_qkv, b_qkv, w_out, b_out, w_up, b_up, w_down, b_down, noise_table)))
    blocks_x = tokens.astype(jnp.float32).reshape(NDEV, TOK_DEV, D)
    block_levels = levels.reshape(NDEV, FR_DEV)
    block_pad = pad_mask.reshape(NDEV, TOK_DEV)
    checked = jax.checkpoint(block_forward)

    def forward(weights, inputs):
        return lax.map(lambda block_items: checked(weights, block_items[0], block_items[1], block_items[2], block_items[3]), (inputs, block_levels, clip_frames, block_pad))
    outputs, pullback = jax.vjp(forward, params, blocks_x)
    grads, grad_x = pullback(cotangent.astype(jnp.float32).reshape(NDEV, TOK_DEV, D))
    return (outputs.reshape(TOKENS, D).astype(jnp.bfloat16), grad_x.reshape(TOKENS, D).astype(jnp.bfloat16), grads[0], grads[1], grads[2], grads[3], grads[4], grads[5], grads[6], grads[7], grads[8], grads[9], grads[10])
```

```python
import jax
import jax.numpy as jnp
from jax import lax
from jax.experimental import pallas as pl
from jax.experimental.pallas import tpu as pltpu
from jax.sharding import PartitionSpec as P

bf16 = jnp.bfloat16
f32 = jnp.float32
AXES = ("dp", "fsdp")
HD = 64
LANE = 128
EPS = 1e-06
NN = (((1,), (0,)), ((), ()))
NT = (((1,), (1,)), ((), ()))
TN = (((0,), (0,)), ((), ()))


def dot(left, right, dims):
    return lax.dot_general(left, right, dims, preferred_element_type=f32)


def lanes(shape):
    return lax.broadcasted_iota(jnp.int32, shape, 1)


def normalize(values):
    centred = values - jnp.mean(values, axis=1, keepdims=True)
    inverse = lax.rsqrt(jnp.mean(centred * centred, axis=1, keepdims=True) + EPS)
    return centred * inverse, inverse


def normalize_back(grad, normed, inverse):
    return inverse * (
        grad
        - jnp.mean(grad, axis=1, keepdims=True)
        - normed * jnp.mean(grad * normed, axis=1, keepdims=True)
    )


def col_sum(values):
    return jnp.sum(values.astype(f32), axis=0, keepdims=True)


def partner(values):
    return jnp.where(
        lanes(values.shape) % HD < HD // 2,
        pltpu.roll(values, LANE - HD // 2, 1),
        pltpu.roll(values, HD // 2, 1),
    )


def carry_lanes(values):
    sub = lanes(values.shape) % HD
    high = values.astype(bf16).astype(f32)
    rest = values - high
    mid = rest.astype(bf16).astype(f32)
    return jnp.where(
        sub == 8, high, jnp.where(sub == 9, mid, jnp.where(sub == 10, rest - mid, 0.0))
    )


def qkv_kernel(x_ref, mod_ref, w_ref, b_ref, cos_ref, sin_ref, act_ref, q_ref, k_ref, v_ref):
    normed, _ = normalize(x_ref[...].astype(f32))
    act = (normed * (1.0 + mod_ref[0, 1:2, :]) + mod_ref[0, 0:1, :]).astype(bf16)
    act_ref[...] = act
    width = x_ref.shape[1]
    cosine, sine = cos_ref[...], sin_ref[...]
    step = 2 * LANE
    for col in range(0, 3 * width, step):
        raw = dot(act, w_ref[:, col : col + step], NN) + b_ref[:, col : col + step].astype(f32)
        for sub in range(0, step, LANE):
            part = raw[:, sub : sub + LANE]
            at = (col + sub) % width
            if col < width:
                part = (part * cosine + partner(part) * sine).astype(bf16)
                q_ref[:, at : at + LANE] = (part.astype(f32) * 0.125).astype(bf16)
            elif col < 2 * width:
                k_ref[:, at : at + LANE] = (part * cosine + partner(part) * sine).astype(bf16)
            else:
                v_ref[:, at : at + LANE] = part.astype(bf16)


def attention_forward(q_ref, k_ref, v_ref, see_ref, hot_ref, out_ref, aug_ref, *, frames):
    rows_all = q_ref.shape[0]
    size = rows_all // frames
    low = lanes((rows_all, LANE)) < HD
    low_b = lanes((size, LANE)) < HD
    k, v, see = k_ref[...], v_ref[...], see_ref[...]
    one = jnp.ones_like(v)
    keys = (jnp.where(low, k, see), jnp.where(low, see, k))
    vals = (jnp.where(low, v, one), jnp.where(low, one, v))
    for i in range(frames):
        rows = slice(i * size, (i + 1) * size)
        width = (i + 1) * size
        q, hot = q_ref[rows, :], hot_ref[rows, :]
        query = (jnp.where(low_b, q, hot), jnp.where(low_b, hot, q))
        tops, outs = [], []
        for h in range(2):
            scores = dot(query[h], keys[h][:width], NT)
            top = jnp.max(scores, axis=1, keepdims=True)
            expo = jnp.exp(scores - top).astype(bf16)
            outs.append(dot(expo, vals[h][:width], NN))
            tops.append(top)
        num = jnp.where(low_b, outs[0], outs[1])
        den = jnp.where(low_b, outs[1], outs[0])
        out_ref[rows, :] = (num / pltpu.roll(den, HD, 1)).astype(bf16)
        lse = jnp.where(low_b, tops[1], tops[0]) + jnp.log(den)
        aug_ref[rows, :] = (carry_lanes(-lse) + hot.astype(f32)).astype(bf16)


def project_kernel(att_ref, x_ref, mod_ref, w_ref, b_ref, middle_ref, attn_ref, act_ref):
    attn = dot(att_ref[...], w_ref[...], NN) + b_ref[...].astype(f32)
    attn_ref[...] = attn.astype(bf16)
    middle = x_ref[...].astype(f32) + mod_ref[0, 2:3, :] * attn
    middle_ref[...] = middle
    normed, _ = normalize(middle)
    act_ref[...] = (normed * (1.0 + mod_ref[0, 4:5, :]) + mod_ref[0, 3:4, :]).astype(bf16)


def up_kernel(act_ref, w_ref, b_ref, out_ref, slope_ref):
    hidden = dot(act_ref[...], w_ref[...], NN) + b_ref[...].astype(f32)
    share = 0.5 * (1.0 + lax.erf(hidden * 0.7071067811865476))
    out_ref[...] = (hidden * share).astype(bf16)
    slope = share + hidden * jnp.exp(-0.5 * hidden * hidden) * 0.3989422804014327
    slope_ref[...] = slope.astype(bf16)


def down_kernel(
    act_ref, w_ref, b_ref, mid_ref, cot_ref, mod_ref, out_ref, dbr_ref, gate_ref, sum_ref, acc_ref
):
    step, last = pl.program_id(0), pl.num_programs(0) - 1
    part = dot(act_ref[...], w_ref[...], NN)

    @pl.when(step == 0)
    def _():
        acc_ref[...] = part

    @pl.when(step > 0)
    def _():
        acc_ref[...] += part

    @pl.when(step == last)
    def _():
        frames = mod_ref.shape[0]
        size = acc_ref.shape[0] // frames
        total = jnp.zeros((1, acc_ref.shape[1]), f32)
        for i in range(frames):
            rows = slice(i * size, (i + 1) * size)
            gate = mod_ref[i, 5:6, :]
            branch = acc_ref[rows, :] + b_ref[...].astype(f32)
            out_ref[rows, :] = (mid_ref[rows, :] + gate * branch).astype(bf16)
            upstream = cot_ref[rows, :].astype(f32)
            d_branch = (upstream * gate).astype(bf16)
            dbr_ref[rows, :] = d_branch
            gate_ref[i : i + 1, :] = col_sum(upstream * branch)
            total += col_sum(d_branch)
        sum_ref[...] = total


def hidden_back_kernel(dbr_ref, w_ref, slope_ref, out_ref, sum_ref):
    d_hidden = (dot(dbr_ref[...], w_ref[...], NT) * slope_ref[...].astype(f32)).astype(bf16)
    out_ref[...] = d_hidden
    sum_ref[...] = col_sum(d_hidden)


def mlp_back_kernel(
    dh_ref, w_ref, mid_ref, cot_ref, attn_ref, mod_ref, dmid_ref, datt_ref, stat_ref, sum_ref, acc_ref
):
    step, last = pl.program_id(0), pl.num_programs(0) - 1
    part = dot(dh_ref[...], w_ref[...], NT)

    @pl.when(step == 0)
    def _():
        acc_ref[...] = part

    @pl.when(step > 0)
    def _():
        acc_ref[...] += part

    @pl.when(step == last)
    def _():
        frames = mod_ref.shape[0]
        size = acc_ref.shape[0] // frames
        total = jnp.zeros((1, acc_ref.shape[1]), f32)
        for i in range(frames):
            rows = slice(i * size, (i + 1) * size)
            d_act = acc_ref[rows, :]
            normed, inverse = normalize(mid_ref[rows, :])
            stat_ref[i, 1:2, :] = col_sum(d_act)
            stat_ref[i, 2:3, :] = col_sum(d_act * normed)
            d_middle = cot_ref[rows, :].astype(f32) + normalize_back(
                d_act * (1.0 + mod_ref[i, 4:5, :]), normed, inverse
            )
            dmid_ref[rows, :] = d_middle
            stat_ref[i, 0:1, :] = col_sum(d_middle * attn_ref[rows, :].astype(f32))
            d_attn = (d_middle * mod_ref[i, 2:3, :]).astype(bf16)
            datt_ref[rows, :] = d_attn
            total += col_sum(d_attn)
        sum_ref[...] = total


def attention_backward(
    q_ref, k_ref, v_ref, do_ref, o_ref, aug_ref, see_ref, cos_ref, sin_ref, out_ref, sum_ref, acc_ref, *, frames
):
    rows_all = q_ref.shape[0]
    size = rows_all // frames
    low = lanes((rows_all, LANE)) < HD
    q, aug, grad = q_ref[...], aug_ref[...], do_ref[...]
    prod = grad.astype(f32) * o_ref[...].astype(f32)
    delta_low = jnp.sum(jnp.where(low, prod, 0.0), axis=1, keepdims=True)
    delta_high = jnp.sum(jnp.where(low, 0.0, prod), axis=1, keepdims=True)
    grad_aug = carry_lanes(jnp.where(low, -delta_high, -delta_low)).astype(bf16)
    query = (jnp.where(low, q, aug), jnp.where(low, aug, q))
    upper = (jnp.where(low, grad, grad_aug), jnp.where(low, grad_aug, grad))
    low_b = lanes((size, LANE)) < HD
    sub = lanes((size, LANE)) % HD
    ones = jnp.where((sub >= 8) & (sub <= 10), 1.0, 0.0).astype(bf16)
    sum_k = sum_v = jnp.zeros((1, LANE), f32)
    for j in range(frames):
        rows = slice(j * size, (j + 1) * size)
        start = j * size
        k, v, see = k_ref[rows, :], v_ref[rows, :], see_ref[rows, :] + ones
        keys = (jnp.where(low_b, k, see), jnp.where(low_b, see, k))
        vals = (jnp.where(low_b, v, ones), jnp.where(low_b, ones, v))
        dvs, dks, dqs = [], [], []
        for h in range(2):
            probs = jnp.exp(dot(keys[h], query[h][start:], NT))
            d_scores = (probs * dot(vals[h], upper[h][start:], NT)).astype(bf16)
            dvs.append(dot(probs.astype(bf16), grad[start:], NN))
            dks.append(dot(d_scores, q[start:], NN))
            dqs.append(dot(d_scores, k, TN))
        d_value = jnp.where(low_b, dvs[0], dvs[1]).astype(bf16)
        d_key = jnp.where(low_b, dks[0], dks[1])
        d_key = (d_key * cos_ref[rows, :] - partner(d_key) * sin_ref[rows, :]).astype(bf16)
        out_ref[1, rows, :] = d_key
        out_ref[2, rows, :] = d_value
        sum_k = sum_k + col_sum(d_key)
        sum_v = sum_v + col_sum(d_value)
        d_query = jnp.where(lanes(dqs[0].shape) < HD, dqs[0], dqs[1])
        if j == 0:
            acc_ref[...] = d_query
        else:
            acc_ref[start:, :] += d_query
    d_query = acc_ref[...] * 0.125
    d_query = (d_query * cos_ref[...] - partner(d_query) * sin_ref[...]).astype(bf16)
    out_ref[0] = d_query
    sum_ref[0, 0:1, :] = col_sum(d_query)
    sum_ref[0, 1:2, :] = sum_k
    sum_ref[0, 2:3, :] = sum_v


def input_back_kernel(dp_ref, w_ref, x_ref, dmid_ref, mod_ref, out_ref, stat_ref, acc_ref):
    step, last = pl.program_id(0), pl.num_programs(0) - 1
    part = dot(dp_ref[0], w_ref[...], NT)

    @pl.when(step == 0)
    def _():
        acc_ref[...] = part

    @pl.when(step > 0)
    def _():
        acc_ref[...] += part

    @pl.when(step == last)
    def _():
        frames = mod_ref.shape[0]
        size = acc_ref.shape[0] // frames
        for i in range(frames):
            rows = slice(i * size, (i + 1) * size)
            d_act = acc_ref[rows, :]
            normed, inverse = normalize(x_ref[rows, :].astype(f32))
            stat_ref[i, 0:1, :] = col_sum(d_act)
            stat_ref[i, 1:2, :] = col_sum(d_act * normed)
            back = normalize_back(d_act * (1.0 + mod_ref[i, 1:2, :]), normed, inverse)
            out_ref[rows, :] = (dmid_ref[rows, :] + back).astype(bf16)


def weight_grad_kernel(left_ref, right_ref, out_ref):
    out_ref[...] = dot(left_ref[...], right_ref[...], TN).astype(bf16)


def qkv_grad_kernel(left_ref, right_ref, out_ref):
    out_ref[...] = dot(left_ref[...], right_ref[0], TN).astype(bf16)


def like(shape, kind):
    return jax.ShapeDtypeStruct(shape, kind)


def whole(shape):
    return pl.BlockSpec(shape, lambda i: (0,) * len(shape))


def by_rows(size, width):
    return pl.BlockSpec((size, width), lambda i: (i, 0))


def by_cols(height, size):
    return pl.BlockSpec((height, size), lambda i: (0, i))


def run(kernel, grid, ins, outs, shapes, args, scratch=(), name=None, flops=0):
    moved = sum(a.size * a.dtype.itemsize for a in args)
    return pl.pallas_call(
        kernel,
        grid=(grid,),
        in_specs=ins,
        out_specs=outs,
        out_shape=shapes,
        scratch_shapes=list(scratch),
        name=name,
        cost_estimate=pl.CostEstimate(flops=flops, bytes_accessed=2 * moved, transcendentals=0),
        compiler_params=pltpu.CompilerParams(vmem_limit_bytes=60 * 1024 * 1024),
    )(*args)


def tables(clip_row, pad, count):
    frames = clip_row.shape[0]
    size = count // frames
    slots = jnp.arange(frames, dtype=jnp.int32)
    ends = jnp.sum(jnp.where(slots[None, :] <= slots[:, None], clip_row[None, :], 0), axis=1)
    clip_of = jnp.sum((slots[:, None] >= ends[None, :]).astype(jnp.int32), axis=1)
    starts = ends - clip_row
    start_of = jnp.sum(jnp.where(clip_of[:, None] == slots[None, :], starts[None, :], 0), axis=1)
    frame_pos = slots - start_of
    frame = jnp.arange(count, dtype=jnp.int32) // size
    lane = jnp.arange(LANE, dtype=jnp.int32) % HD
    frame_hot = frame[:, None] == lane[None, :]
    own = frame[:, None] == slots[None, :]
    clip_tok = jnp.sum(jnp.where(own, clip_of[None, :], 0), axis=1)
    pos_tok = jnp.sum(jnp.where(own, frame_pos[None, :], 0), axis=1)
    lane_own = lane[:, None] == slots[None, :]
    lane_clip = jnp.sum(jnp.where(lane_own, clip_of[None, :], 0), axis=1)
    lane_pos = jnp.sum(jnp.where(lane_own, frame_pos[None, :], 0), axis=1)
    seen = (
        (clip_tok[:, None] == lane_clip[None, :])
        & (pos_tok[:, None] <= lane_pos[None, :])
        & (pad[:, None] == 1)
    )
    see = jnp.where((lane[None, :] < frames) & ~seen, -1e30, 0.0).astype(bf16)
    quarter = HD // 4
    freq = 10000.0 ** (-jnp.arange(quarter, dtype=f32) / quarter)
    patch = jnp.arange(count, dtype=jnp.int32) % size
    angle = jnp.concatenate(
        [pos_tok.astype(f32)[:, None] * freq[None, :], patch.astype(f32)[:, None] * freq[None, :]],
        axis=1,
    )
    cosine, sine = jnp.cos(angle), jnp.sin(angle)
    cosine = jnp.concatenate([cosine] * 4, axis=1)
    sine = jnp.concatenate([-sine, sine, -sine, sine], axis=1)
    return see, frame_hot.astype(bf16), cosine, sine


def per_device(
    tokens, cotangent, clip_frames, levels, pad_mask, w_mod, b_mod, w_qkv, b_qkv, w_out, b_out,
    w_up, b_up, w_down, b_down, noise_table,
):
    count, width = tokens.shape
    frames = levels.shape[0]
    size = count // frames
    hidden = w_up.shape[1]
    ndev = width // w_up.shape[0]
    me = lax.axis_index("dp") * lax.axis_size("fsdp") + lax.axis_index("fsdp")

    def gather(value):
        return lax.all_gather(value, AXES, axis=0, tiled=True)

    def scatter(value):
        return lax.psum_scatter(value, AXES, scatter_dimension=0, tiled=True)

    all_levels = gather(levels)
    hot = (all_levels[:, None] == jnp.arange(noise_table.shape[1], dtype=jnp.int32)[None, :]).astype(bf16)
    embedded = dot(hot, noise_table, NT)
    cond = jax.nn.silu(embedded).astype(bf16)
    partial = dot(cond, w_mod, NN)
    biases = [b_mod, b_qkv, b_out, b_up, b_down]
    lengths = [b.shape[0] for b in biases]
    packed = jnp.concatenate(biases)
    packed = jnp.pad(packed, (0, -packed.shape[0] % (8 * LANE))).reshape(8, -1)
    packed = gather(packed).reshape(ndev, -1)
    full_bias, at = [], 0
    for length in lengths:
        full_bias.append(packed[:, at : at + length].reshape(1, -1))
        at += length
    bias_mod, bias_qkv, bias_out, bias_up, bias_down = full_bias
    modulation = (scatter(partial) + bias_mod.astype(f32)).reshape(frames, 6, width)
    full_qkv, full_out, full_up, full_down = gather(w_qkv), gather(w_out), gather(w_up), gather(w_down)
    see, frame_hot, cosine, sine = tables(clip_frames[0], pad_mask, count)

    acts = like((count, width), bf16)
    wide = like((count, width), f32)
    tall = like((count, hidden), bf16)
    row = whole((1, width))
    mod_row = pl.BlockSpec((1, 6, width), lambda i: (i, 0, 0))
    mod_all = whole((frames, 6, width))
    rows_bf = by_rows(size, width)
    act_one, query, key, value = run(
        qkv_kernel, frames,
        [rows_bf, mod_row, whole((width, 3 * width)), whole((1, 3 * width)), by_rows(size, LANE), by_rows(size, LANE)],
        [rows_bf] * 4, [acts] * 4, (tokens, modulation, full_qkv, bias_qkv, cosine, sine), name="qkv",
    )
    pair = by_cols(count, LANE)
    table = whole((count, LANE))
    attended, aug = run(
        lambda *refs: attention_forward(*refs, frames=frames), width // LANE,
        [pair, pair, pair, table, table], [pair] * 2, [acts] * 2, (query, key, value, see, frame_hot), name="attf",
    )
    middle, attn, act_two = run(
        project_kernel, frames, [rows_bf, rows_bf, mod_row, whole((width, width)), row], [rows_bf] * 3,
        [wide, acts, acts], (attended, tokens, modulation, full_out, bias_out), name="proj",
    )
    full = whole((count, width))
    step = 512
    cols_h = by_cols(count, step)
    activated, slope = run(
        up_kernel, hidden // step, [full, by_cols(width, step), by_cols(1, step)], [cols_h] * 2, [tall] * 2,
        (act_two, full_up, bias_up), name="up",
    )
    acc = pltpu.VMEM((count, width), f32)
    block_out, d_branch, d_gate_two, bdown = run(
        down_kernel, hidden // width, [by_cols(count, width), by_rows(width, width), row, full, full, mod_all],
        [full, full, whole((frames, width)), row],
        [acts, acts, like((frames, width), f32), like((1, width), f32)],
        (activated, full_down, bias_down, middle, cotangent, modulation), [acc], name="down",
    )
    wdown = run(
        weight_grad_kernel, hidden // step, [cols_h, full], by_rows(step, width), like((hidden, width), bf16),
        (activated, d_branch), name="wdown",
    )
    wdown_grad = scatter(wdown)
    d_hidden, bup = run(
        hidden_back_kernel, hidden // step, [full, by_rows(step, width), cols_h], [cols_h, by_cols(1, step)],
        [tall, like((1, hidden), f32)], (d_branch, full_down, slope), name="dhid",
    )
    wup = run(
        weight_grad_kernel, hidden // step, [full, cols_h], by_cols(width, step), like((width, hidden), bf16),
        (act_two, d_hidden), name="wup",
    )
    wup_grad = scatter(wup)
    d_middle, d_attn, stat_two, bout = run(
        mlp_back_kernel, hidden // width,
        [by_cols(count, width), by_cols(width, width), full, full, full, mod_all],
        [full, full, whole((frames, 3, width)), row],
        [wide, acts, like((frames, 3, width), f32), like((1, width), f32)],
        (d_hidden, full_up, middle, cotangent, attn, modulation), [acc], name="dact2",
    )
    wout = run(
        weight_grad_kernel, width // step, [by_cols(count, step), full], by_rows(step, width), like((width, width), bf16),
        (attended, d_attn), name="wout",
    )
    wout_grad = scatter(wout)
    d_attended = dot(d_attn, full_out, NT).astype(bf16)
    d_projected, bqkv = run(
        lambda *refs: attention_backward(*refs, frames=frames), width // LANE, [pair] * 6 + [table] * 3,
        [pl.BlockSpec((3, count, LANE), lambda i: (0, 0, i)), pl.BlockSpec((1, 3, LANE), lambda i: (i, 0, 0))],
        [like((3, count, width), bf16), like((width // LANE, 3, LANE), f32)],
        (query, key, value, d_attended, attended, aug, see, cosine, sine), [pltpu.VMEM((count, LANE), f32)], name="attb",
    )
    stacked = pl.BlockSpec((1, count, width), lambda i: (i, 0, 0))
    wqkv = run(
        qkv_grad_kernel, 3, [full, stacked], by_cols(width, width), like((width, 3 * width), bf16),
        (act_one, d_projected), name="wqkv",
    )
    wqkv_grad = scatter(wqkv)
    token_grad, stat_one = run(
        input_back_kernel, 3, [stacked, by_cols(width, width), full, full, mod_all], [full, whole((frames, 2, width))],
        [acts, like((frames, 2, width), f32)], (d_projected, full_qkv, tokens, d_middle, modulation), [acc], name="dact1",
    )
    bqkv = jnp.transpose(bqkv, (1, 0, 2)).reshape(1, -1)
    sums = [bqkv, bout, bup, bdown]
    shares = [s.reshape(ndev, -1) for s in sums]
    packed = jnp.concatenate(shares, axis=1)
    bias_len = packed.shape[1]
    packed = jnp.pad(packed, ((0, 0), (0, -bias_len % LANE))).reshape(-1, LANE)
    bias_sum = scatter(packed).reshape(-1)[:bias_len]
    bias_grads, at = [], 0
    for share in shares:
        bias_grads.append(bias_sum[at : at + share.shape[1]])
        at += share.shape[1]
    d_modulation = jnp.concatenate(
        [stat_one[:, 0], stat_one[:, 1], stat_two[:, 0], stat_two[:, 1], stat_two[:, 2], d_gate_two], axis=1
    ).astype(bf16)
    d_mod = gather(d_modulation)
    wmod_grad = dot(cond, d_mod, TN)
    mine = b_mod.shape[0]
    bmod_grad = jnp.sum(lax.dynamic_slice(d_mod, (0, me * mine), (d_mod.shape[0], mine)).astype(f32), axis=0)
    gate = jax.nn.sigmoid(embedded)
    d_embed = dot(d_mod, w_mod, NT) * gate * (1.0 + embedded * (1.0 - gate))
    table_grad = lax.dot_general(
        d_embed, hot.astype(f32), TN, precision=lax.Precision.HIGHEST, preferred_element_type=f32
    )
    return (
        block_out, token_grad, wmod_grad, bmod_grad, wqkv_grad.astype(f32), bias_grads[0],
        wout_grad.astype(f32), bias_grads[1], wup_grad.astype(f32), bias_grads[2], wdown_grad.astype(f32),
        bias_grads[3], table_grad,
    )


def solution(mesh):
    rows, vec = P(AXES, None), P(AXES)
    return jax.shard_map(
        per_device,
        mesh=mesh,
        in_specs=(rows, rows, rows, vec, vec) + (rows, vec) * 5 + (rows,),
        out_specs=(rows, rows) + (rows, vec) * 5 + (rows,),
        check_vma=False,
    )
```

```python
import jax
import jax.numpy as jnp
from jax import lax
from jax.experimental import pallas as pl
from jax.experimental.pallas import tpu as pltpu
from jax.sharding import PartitionSpec as P

bf16 = jnp.bfloat16
f32 = jnp.float32
AXES = ("dp", "fsdp")
HD = 64
LANE = 128
EPS = 1e-06
NN = (((1,), (0,)), ((), ()))
NT = (((1,), (1,)), ((), ()))
TN = (((0,), (0,)), ((), ()))


def dot(left, right, dims):
    return lax.dot_general(left, right, dims, preferred_element_type=f32)


def lanes(shape):
    return lax.broadcasted_iota(jnp.int32, shape, 1)


def normalize(values):
    centred = values - jnp.mean(values, axis=1, keepdims=True)
    inverse = lax.rsqrt(jnp.mean(centred * centred, axis=1, keepdims=True) + EPS)
    return centred * inverse, inverse


def normalize_back(grad, normed, inverse):
    return inverse * (
        grad
        - jnp.mean(grad, axis=1, keepdims=True)
        - normed * jnp.mean(grad * normed, axis=1, keepdims=True)
    )


def col_sum(values):
    return jnp.sum(values.astype(f32), axis=0, keepdims=True)


def partner(values):
    return jnp.where(
        lanes(values.shape) % HD < HD // 2,
        pltpu.roll(values, LANE - HD // 2, 1),
        pltpu.roll(values, HD // 2, 1),
    )


def carry_lanes(values):
    sub = lanes(values.shape) % HD
    high = values.astype(bf16).astype(f32)
    rest = values - high
    mid = rest.astype(bf16).astype(f32)
    return jnp.where(
        sub == 8, high, jnp.where(sub == 9, mid, jnp.where(sub == 10, rest - mid, 0.0))
    )


def qkv_kernel(x_ref, mod_ref, w_ref, b_ref, cos_ref, sin_ref, act_ref, q_ref, k_ref, v_ref):
    normed, _ = normalize(x_ref[...].astype(f32))
    act = (normed * (1.0 + mod_ref[0, 1:2, :]) + mod_ref[0, 0:1, :]).astype(bf16)
    act_ref[...] = act
    width = x_ref.shape[1]
    cosine, sine = cos_ref[...], sin_ref[...]
    step = 2 * LANE
    for col in range(0, 3 * width, step):
        raw = dot(act, w_ref[:, col : col + step], NN) + b_ref[:, col : col + step].astype(f32)
        for sub in range(0, step, LANE):
            part = raw[:, sub : sub + LANE]
            at = (col + sub) % width
            if col < width:
                part = (part * cosine + partner(part) * sine).astype(bf16)
                q_ref[:, at : at + LANE] = (part.astype(f32) * 0.125).astype(bf16)
            elif col < 2 * width:
                k_ref[:, at : at + LANE] = (part * cosine + partner(part) * sine).astype(bf16)
            else:
                v_ref[:, at : at + LANE] = part.astype(bf16)


def attention_forward(q_ref, k_ref, v_ref, see_ref, hot_ref, out_ref, aug_ref, *, frames):
    rows_all = q_ref.shape[0]
    size = rows_all // frames
    low = lanes((rows_all, LANE)) < HD
    low_b = lanes((size, LANE)) < HD
    k, v, see = k_ref[...], v_ref[...], see_ref[...]
    one = jnp.ones_like(v)
    keys = (jnp.where(low, k, see), jnp.where(low, see, k))
    vals = (jnp.where(low, v, one), jnp.where(low, one, v))
    for i in range(frames):
        rows = slice(i * size, (i + 1) * size)
        width = (i + 1) * size
        q, hot = q_ref[rows, :], hot_ref[rows, :]
        query = (jnp.where(low_b, q, hot), jnp.where(low_b, hot, q))
        tops, outs = [], []
        for h in range(2):
            scores = dot(query[h], keys[h][:width], NT)
            top = jnp.max(scores, axis=1, keepdims=True)
            expo = jnp.exp(scores - top).astype(bf16)
            outs.append(dot(expo, vals[h][:width], NN))
            tops.append(top)
        num = jnp.where(low_b, outs[0], outs[1])
        den = jnp.where(low_b, outs[1], outs[0])
        out_ref[rows, :] = (num / pltpu.roll(den, HD, 1)).astype(bf16)
        lse = jnp.where(low_b, tops[1], tops[0]) + jnp.log(den)
        aug_ref[rows, :] = (carry_lanes(-lse) + hot.astype(f32)).astype(bf16)


def project_kernel(att_ref, x_ref, mod_ref, w_ref, b_ref, middle_ref, attn_ref, act_ref):
    attn = dot(att_ref[...], w_ref[...], NN) + b_ref[...].astype(f32)
    attn_ref[...] = attn.astype(bf16)
    middle = x_ref[...].astype(f32) + mod_ref[0, 2:3, :] * attn
    middle_ref[...] = middle
    normed, _ = normalize(middle)
    act_ref[...] = (normed * (1.0 + mod_ref[0, 4:5, :]) + mod_ref[0, 3:4, :]).astype(bf16)


def up_kernel(act_ref, w_ref, b_ref, out_ref, slope_ref):
    hidden = dot(act_ref[...], w_ref[...], NN) + b_ref[...].astype(f32)
    share = 0.5 * (1.0 + lax.erf(hidden * 0.7071067811865476))
    out_ref[...] = (hidden * share).astype(bf16)
    slope = share + hidden * jnp.exp(-0.5 * hidden * hidden) * 0.3989422804014327
    slope_ref[...] = slope.astype(bf16)


def down_kernel(
    act_ref, w_ref, b_ref, mid_ref, cot_ref, mod_ref, out_ref, dbr_ref, gate_ref, sum_ref, acc_ref
):
    step, last = pl.program_id(0), pl.num_programs(0) - 1
    part = dot(act_ref[...], w_ref[...], NN)

    @pl.when(step == 0)
    def _():
        acc_ref[...] = part

    @pl.when(step > 0)
    def _():
        acc_ref[...] += part

    @pl.when(step == last)
    def _():
        frames = mod_ref.shape[0]
        size = acc_ref.shape[0] // frames
        total = jnp.zeros((1, acc_ref.shape[1]), f32)
        for i in range(frames):
            rows = slice(i * size, (i + 1) * size)
            gate = mod_ref[i, 5:6, :]
            branch = acc_ref[rows, :] + b_ref[...].astype(f32)
            out_ref[rows, :] = (mid_ref[rows, :] + gate * branch).astype(bf16)
            upstream = cot_ref[rows, :].astype(f32)
            d_branch = (upstream * gate).astype(bf16)
            dbr_ref[rows, :] = d_branch
            gate_ref[i : i + 1, :] = col_sum(upstream * branch)
            total += col_sum(d_branch)
        sum_ref[...] = total


def hidden_back_kernel(dbr_ref, w_ref, slope_ref, out_ref, sum_ref):
    d_hidden = (dot(dbr_ref[...], w_ref[...], NT) * slope_ref[...].astype(f32)).astype(bf16)
    out_ref[...] = d_hidden
    sum_ref[...] = col_sum(d_hidden)


def mlp_back_kernel(
    dh_ref, w_ref, mid_ref, cot_ref, attn_ref, mod_ref, dmid_ref, datt_ref, stat_ref, sum_ref, acc_ref
):
    step, last = pl.program_id(0), pl.num_programs(0) - 1
    part = dot(dh_ref[...], w_ref[...], NT)

    @pl.when(step == 0)
    def _():
        acc_ref[...] = part

    @pl.when(step > 0)
    def _():
        acc_ref[...] += part

    @pl.when(step == last)
    def _():
        frames = mod_ref.shape[0]
        size = acc_ref.shape[0] // frames
        total = jnp.zeros((1, acc_ref.shape[1]), f32)
        for i in range(frames):
            rows = slice(i * size, (i + 1) * size)
            d_act = acc_ref[rows, :]
            normed, inverse = normalize(mid_ref[rows, :])
            stat_ref[i, 1:2, :] = col_sum(d_act)
            stat_ref[i, 2:3, :] = col_sum(d_act * normed)
            d_middle = cot_ref[rows, :].astype(f32) + normalize_back(
                d_act * (1.0 + mod_ref[i, 4:5, :]), normed, inverse
            )
            dmid_ref[rows, :] = d_middle
            stat_ref[i, 0:1, :] = col_sum(d_middle * attn_ref[rows, :].astype(f32))
            d_attn = (d_middle * mod_ref[i, 2:3, :]).astype(bf16)
            datt_ref[rows, :] = d_attn
            total += col_sum(d_attn)
        sum_ref[...] = total


def attention_backward(
    q_ref, k_ref, v_ref, do_ref, o_ref, aug_ref, see_ref, cos_ref, sin_ref, out_ref, sum_ref, acc_ref, *, frames
):
    rows_all = q_ref.shape[0]
    size = rows_all // frames
    low = lanes((rows_all, LANE)) < HD
    q, aug, grad = q_ref[...], aug_ref[...], do_ref[...]
    prod = grad.astype(f32) * o_ref[...].astype(f32)
    delta_low = jnp.sum(jnp.where(low, prod, 0.0), axis=1, keepdims=True)
    delta_high = jnp.sum(jnp.where(low, 0.0, prod), axis=1, keepdims=True)
    grad_aug = carry_lanes(jnp.where(low, -delta_high, -delta_low)).astype(bf16)
    query = (jnp.where(low, q, aug), jnp.where(low, aug, q))
    upper = (jnp.where(low, grad, grad_aug), jnp.where(low, grad_aug, grad))
    low_b = lanes((size, LANE)) < HD
    sub = lanes((size, LANE)) % HD
    ones = jnp.where((sub >= 8) & (sub <= 10), 1.0, 0.0).astype(bf16)
    sum_k = sum_v = jnp.zeros((1, LANE), f32)
    for j in range(frames):
        rows = slice(j * size, (j + 1) * size)
        start = j * size
        k, v, see = k_ref[rows, :], v_ref[rows, :], see_ref[rows, :] + ones
        keys = (jnp.where(low_b, k, see), jnp.where(low_b, see, k))
        vals = (jnp.where(low_b, v, ones), jnp.where(low_b, ones, v))
        dvs, dks, dqs = [], [], []
        for h in range(2):
            probs = jnp.exp(dot(keys[h], query[h][start:], NT))
            d_scores = (probs * dot(vals[h], upper[h][start:], NT)).astype(bf16)
            dvs.append(dot(probs.astype(bf16), grad[start:], NN))
            dks.append(dot(d_scores, q[start:], NN))
            dqs.append(dot(d_scores, k, TN))
        d_value = jnp.where(low_b, dvs[0], dvs[1]).astype(bf16)
        d_key = jnp.where(low_b, dks[0], dks[1])
        d_key = (d_key * cos_ref[rows, :] - partner(d_key) * sin_ref[rows, :]).astype(bf16)
        out_ref[1, rows, :] = d_key
        out_ref[2, rows, :] = d_value
        sum_k = sum_k + col_sum(d_key)
        sum_v = sum_v + col_sum(d_value)
        d_query = jnp.where(lanes(dqs[0].shape) < HD, dqs[0], dqs[1])
        if j == 0:
            acc_ref[...] = d_query
        else:
            acc_ref[start:, :] += d_query
    d_query = acc_ref[...] * 0.125
    d_query = (d_query * cos_ref[...] - partner(d_query) * sin_ref[...]).astype(bf16)
    out_ref[0] = d_query
    sum_ref[0, 0:1, :] = col_sum(d_query)
    sum_ref[0, 1:2, :] = sum_k
    sum_ref[0, 2:3, :] = sum_v


def input_back_kernel(dp_ref, w_ref, x_ref, dmid_ref, mod_ref, out_ref, stat_ref, acc_ref):
    step, last = pl.program_id(0), pl.num_programs(0) - 1
    part = dot(dp_ref[0], w_ref[...], NT)

    @pl.when(step == 0)
    def _():
        acc_ref[...] = part

    @pl.when(step > 0)
    def _():
        acc_ref[...] += part

    @pl.when(step == last)
    def _():
        frames = mod_ref.shape[0]
        size = acc_ref.shape[0] // frames
        for i in range(frames):
            rows = slice(i * size, (i + 1) * size)
            d_act = acc_ref[rows, :]
            normed, inverse = normalize(x_ref[rows, :].astype(f32))
            stat_ref[i, 0:1, :] = col_sum(d_act)
            stat_ref[i, 1:2, :] = col_sum(d_act * normed)
            back = normalize_back(d_act * (1.0 + mod_ref[i, 1:2, :]), normed, inverse)
            out_ref[rows, :] = (dmid_ref[rows, :] + back).astype(bf16)


def weight_grad_kernel(left_ref, right_ref, out_ref):
    out_ref[...] = dot(left_ref[...], right_ref[...], TN).astype(bf16)


def qkv_grad_kernel(left_ref, right_ref, out_ref):
    out_ref[...] = dot(left_ref[...], right_ref[0], TN).astype(bf16)


def like(shape, kind):
    return jax.ShapeDtypeStruct(shape, kind)


def whole(shape):
    return pl.BlockSpec(shape, lambda i: (0,) * len(shape))


def by_rows(size, width):
    return pl.BlockSpec((size, width), lambda i: (i, 0))


def by_cols(height, size):
    return pl.BlockSpec((height, size), lambda i: (0, i))


def run(kernel, grid, ins, outs, shapes, args, scratch=(), name=None, flops=0):
    moved = sum(a.size * a.dtype.itemsize for a in args)
    return pl.pallas_call(
        kernel,
        grid=(grid,),
        in_specs=ins,
        out_specs=outs,
        out_shape=shapes,
        scratch_shapes=list(scratch),
        name=name,
        cost_estimate=pl.CostEstimate(flops=flops, bytes_accessed=2 * moved, transcendentals=0),
        compiler_params=pltpu.CompilerParams(vmem_limit_bytes=60 * 1024 * 1024),
    )(*args)


MESH = pl.DeviceIdType.MESH
ANY = pl.BlockSpec(memory_space=pl.ANY)
VMEM = pl.BlockSpec(memory_space=pltpu.VMEM)


class Place:
    def __init__(self, sizes):
        self.sizes = sizes
        self.ny, self.nx, self.nz = sizes
        dp, fsdp = lax.axis_index("dp"), lax.axis_index("fsdp")
        self.dp, self.fsdp = dp, fsdp
        self.y, self.x = lax.div(dp, self.nx), lax.rem(dp, self.nx)
        self.z, self.c = lax.div(fsdp, 2), lax.rem(fsdp, 2)

    def shift(self, axis, k):
        size = dict(y=self.ny, x=self.nx, z=self.nz, c=2)[axis]
        return lax.rem(getattr(self, axis) + (k + size), size)

    def device(self, axis, k):
        at = self.shift(axis, k)
        if axis == "y":
            return (at * self.nx + self.x, self.fsdp)
        if axis == "x":
            return (self.y * self.nx + at, self.fsdp)
        if axis == "z":
            return (self.dp, at * 2 + self.c)
        return (self.dp, self.z * 2 + at)

    def peers(self):
        for axis, size in zip("yxzc", (self.ny, self.nx, self.nz, 2)):
            for k in range(1, size):
                yield axis, k

    def enter(self):
        barrier = pltpu.get_barrier_semaphore()
        peers = list(self.peers())
        for axis, k in peers:
            pl.semaphore_signal(barrier, inc=1, device_id=self.device(axis, k), device_id_type=MESH)
        pl.semaphore_wait(barrier, len(peers))


class Links:
    def __init__(self, place, send, recv):
        self.place, self.send, self.recv = place, send, recv
        self.slots, self.sent = {}, []

    def copy(self, key, src, dst, axis, k):
        slot = self.slots.setdefault(key, len(self.slots))
        return pltpu.make_async_remote_copy(
            src_ref=src, dst_ref=dst, send_sem=self.send.at[slot], recv_sem=self.recv.at[slot],
            device_id=self.place.device(axis, k), device_id_type=MESH,
        )

    def start(self, key, src, dst, axis, k):
        self.copy(key, src, dst, axis, k).start()
        self.sent.append((key, src, dst, axis, k))

    def arrived(self, key, dst, axis, k):
        self.copy(key, dst, dst, axis, k).wait_recv()

    def drain(self):
        for item in self.sent:
            self.copy(*item).wait_send()


class Gather:
    phases = 5

    @staticmethod
    def copies(sizes):
        ny, nx, nz = sizes
        return (nz - 1) + 2 * (nx - 1) + 2 * (ny - 1) + 1 + 2 * (nx - 1) + 2 * (ny - 1)

    def __init__(self, place, shard, full, send, recv, local):
        self.place, self.shard, self.full, self.local = place, shard, full, local
        self.links = Links(place, send, recv)
        half = place.nz // 2
        self.low, self.high = pl.ds(0, half), pl.ds(half, place.nz - half)

    def own(self):
        p = self.place
        return pltpu.make_async_copy(self.shard, self.full.at[p.y, p.x, p.z, p.c], self.local.at[0])

    def send(self, key, ref, axis, k):
        self.links.start(key, ref, ref, axis, k)

    def phase(self, step):
        p, full = self.place, self.full
        y, x, z, c = p.y, p.x, p.z, p.c
        if step == 0:
            self.own().start()
            for k in range(1, p.nz):
                self.links.start(("z", k), self.shard, full.at[y, x, z, c], "z", k)
        elif step == 1:
            self.own().wait()
            for k in range(1, p.nz):
                self.links.arrived(("z", k), full.at[y, x, p.shift("z", -k), c], "z", k)
            for k in range(1, p.nx):
                self.send(("x", k), full.at[y, x, self.low, c], "x", k)
            for k in range(1, p.ny):
                self.send(("y", k), full.at[y, x, self.high, c], "y", k)
            self.send("c", full.at[y, x, :, c], "c", 1)
        elif step == 2:
            for k in range(1, p.nx):
                self.links.arrived(("x", k), full.at[y, p.shift("x", -k), self.low, c], "x", k)
            for k in range(1, p.ny):
                self.links.arrived(("y", k), full.at[p.shift("y", -k), x, self.high, c], "y", k)
            for k in range(1, p.ny):
                self.send(("xy", k), full.at[y, :, self.low, c], "y", k)
            for k in range(1, p.nx):
                self.send(("yx", k), full.at[:, x, self.high, c], "x", k)
            for k in range(1, p.nx):
                self.send(("cx", k), full.at[y, p.shift("x", -k), self.low, c], "c", 1)
            for k in range(1, p.ny):
                self.send(("cy", k), full.at[p.shift("y", -k), x, self.high, c], "c", 1)
        elif step == 3:
            for k in range(1, p.ny):
                ref = full.at[p.shift("y", -k), :, self.low, c]
                self.links.arrived(("xy", k), ref, "y", k)
                self.send(("cxy", k), ref, "c", 1)
            for k in range(1, p.nx):
                ref = full.at[:, p.shift("x", -k), self.high, c]
                self.links.arrived(("yx", k), ref, "x", k)
                self.send(("cyx", k), ref, "c", 1)
        else:
            d = 1 - c
            self.links.arrived("c", full.at[y, x, :, d], "c", 1)
            for k in range(1, p.nx):
                self.links.arrived(("cx", k), full.at[y, p.shift("x", -k), self.low, d], "c", 1)
                self.links.arrived(("cyx", k), full.at[:, p.shift("x", -k), self.high, d], "c", 1)
            for k in range(1, p.ny):
                self.links.arrived(("cy", k), full.at[p.shift("y", -k), x, self.high, d], "c", 1)
                self.links.arrived(("cxy", k), full.at[p.shift("y", -k), :, self.low, d], "c", 1)
            self.links.drain()


class Reduce:
    phases = 5

    @staticmethod
    def copies(sizes):
        ny, nx, nz = sizes
        return 1 + 2 * (nx - 1) + 2 * (ny - 1) + (nz - 1)

    @staticmethod
    def scratch(sizes, block, kind):
        ny, nx, nz = sizes
        half = nz // 2
        rest = nz - half
        return [
            pltpu.VMEM((ny, nx, nz) + block, kind),
            pltpu.VMEM((ny, nx, nz) + block, kind),
            pltpu.VMEM((ny - 1, nx, half) + block, kind),
            pltpu.VMEM((nx - 1, ny, rest) + block, kind),
            pltpu.VMEM((nx - 1, half) + block, kind),
            pltpu.VMEM((ny - 1, rest) + block, kind),
            pltpu.VMEM((nz - 1,) + block, kind),
        ]

    def __init__(self, place, source, out, bufs, send, recv, local):
        self.place, self.source, self.out, self.local = place, source, out, local
        self.acc, self.core, self.la, self.lb, self.ma, self.mb, self.last = bufs
        self.links = Links(place, send, recv)
        self.half = place.nz // 2
        self.low, self.high = pl.ds(0, self.half), pl.ds(self.half, place.nz - self.half)

    def own(self):
        p = self.place
        return pltpu.make_async_copy(self.source.at[:, :, :, p.c], self.acc, self.local.at[0])

    def add(self, counts, into, terms):
        total = 1
        for n in counts:
            total *= n

        def body(flat, carry):
            at = []
            for n in reversed(counts):
                at.append(lax.rem(flat, n))
                flat = lax.div(flat, n)
            at = at[::-1]
            where = into(*at)
            value = self.acc[where].astype(f32)
            for ref, index in terms(*at):
                value = value + ref[index].astype(f32)
            self.acc[where] = value.astype(self.acc.dtype)
            return carry

        lax.fori_loop(0, total, body, 0)

    def phase(self, step):
        p, acc = self.place, self.acc
        y, x, z, c = p.y, p.x, p.z, p.c
        half, rest = self.half, p.nz - self.half
        if step == 0:
            self.own().start()
            self.links.start("c", self.source.at[:, :, :, 1 - c], self.core, "c", 1)
        elif step == 1:
            self.own().wait()
            self.links.arrived("c", self.core, "c", 1)
            self.add((p.ny, p.nx, p.nz), lambda *at: at, lambda *at: [(self.core, at)])
            for k in range(1, p.ny):
                self.links.start(("y", k), acc.at[p.shift("y", k), :, self.low], self.la.at[k - 1], "y", k)
            for k in range(1, p.nx):
                self.links.start(("x", k), acc.at[:, p.shift("x", k), self.high], self.lb.at[k - 1], "x", k)
        elif step == 2:
            for k in range(1, p.ny):
                self.links.arrived(("y", k), self.la.at[k - 1], "y", k)
            self.add(
                (p.nx, half), lambda i, j: (y, i, j),
                lambda i, j: [(self.la, (k, i, j)) for k in range(p.ny - 1)],
            )
            for k in range(1, p.nx):
                self.links.start(("yx", k), acc.at[y, p.shift("x", k), self.low], self.ma.at[k - 1], "x", k)
            for k in range(1, p.nx):
                self.links.arrived(("x", k), self.lb.at[k - 1], "x", k)
            self.add(
                (p.ny, rest), lambda i, j: (i, x, half + j),
                lambda i, j: [(self.lb, (k, i, j)) for k in range(p.nx - 1)],
            )
            for k in range(1, p.ny):
                self.links.start(("xy", k), acc.at[p.shift("y", k), x, self.high], self.mb.at[k - 1], "y", k)
        elif step == 3:
            for k in range(1, p.nx):
                self.links.arrived(("yx", k), self.ma.at[k - 1], "x", k)
            for k in range(1, p.ny):
                self.links.arrived(("xy", k), self.mb.at[k - 1], "y", k)
            self.add((half,), lambda j: (y, x, j), lambda j: [(self.ma, (k, j)) for k in range(p.nx - 1)])
            self.add((rest,), lambda j: (y, x, half + j), lambda j: [(self.mb, (k, j)) for k in range(p.ny - 1)])
            for k in range(1, p.nz):
                self.links.start(("z", k), acc.at[y, x, p.shift("z", k)], self.last.at[k - 1], "z", k)
        else:
            for k in range(1, p.nz):
                self.links.arrived(("z", k), self.last.at[k - 1], "z", k)
            value = acc[y, x, z].astype(f32)
            for k in range(p.nz - 1):
                value = value + self.last[k].astype(f32)
            self.out[...] = value
            self.links.drain()


class Transfers:
    def __init__(self, sizes, gathers=(), reduces=()):
        self.sizes = sizes
        self.gathers, self.reduces = list(gathers), list(reduces)
        ny, nx, nz = sizes
        self.lead = (ny, nx, nz, 2)
        blocks = [(r.shape[0] // (ny * nx * nz * 2), r.shape[1]) for r in self.reduces]
        self.args = self.gathers + [r.reshape(self.lead + b) for r, b in zip(self.reduces, blocks)]
        self.in_specs = [VMEM] * len(self.gathers) + [ANY] * len(self.reduces)
        self.out_specs = [ANY] * len(self.gathers) + [VMEM] * len(self.reduces)
        self.shapes = [like(self.lead + g.shape, g.dtype) for g in self.gathers]
        self.shapes += [like(b, f32) for b in blocks]
        self.scratch = []
        for _ in self.gathers:
            self.scratch += [pltpu.SemaphoreType.DMA((Gather.copies(sizes),))] * 2
            self.scratch += [pltpu.SemaphoreType.DMA((1,))]
        for r, b in zip(self.reduces, blocks):
            self.scratch += Reduce.scratch(sizes, b, r.dtype)
            self.scratch += [pltpu.SemaphoreType.DMA((Reduce.copies(sizes),))] * 2
            self.scratch += [pltpu.SemaphoreType.DMA((1,))]

    def build(self, ins, outs, scratch):
        place = Place(self.sizes)
        scratch = list(scratch)
        count = len(self.gathers)
        tasks = []
        for i in range(count):
            tasks.append(Gather(place, ins[i], outs[i], *scratch[3 * i : 3 * i + 3]))
        scratch = scratch[3 * count :]
        for i in range(len(self.reduces)):
            part = scratch[10 * i : 10 * i + 10]
            tasks.append(Reduce(place, ins[count + i], outs[count + i], part[:7], *part[7:]))
        return place, tasks

    def finish(self, outs):
        whole_outs = []
        for out, gathered in zip(outs, self.gathers):
            whole_outs.append(out.reshape((-1,) + gathered.shape[1:]))
        return whole_outs + list(outs[len(self.gathers) :])


def exchange(transfers, order, name, collective_id):
    def body(*refs):
        n_in, n_out = len(transfers.args), len(transfers.shapes)
        place, tasks = transfers.build(refs[:n_in], refs[n_in : n_in + n_out], refs[n_in + n_out :])
        place.enter()
        for task, step in order:
            tasks[task].phase(step)

    outs = pl.pallas_call(
        body,
        in_specs=transfers.in_specs,
        out_specs=transfers.out_specs,
        out_shape=transfers.shapes,
        scratch_shapes=transfers.scratch,
        name=name,
        compiler_params=pltpu.CompilerParams(
            vmem_limit_bytes=60 * 1024 * 1024, collective_id=collective_id, has_side_effects=True
        ),
    )(*transfers.args)
    return transfers.finish(outs)


def staggered(starts, phases=5):
    turns = [(s + p, i, p) for i, s in enumerate(starts) for p in range(phases)]
    return [(i, p) for _, i, p in sorted(turns)]


def tables(clip_row, pad, count):
    frames = clip_row.shape[0]
    size = count // frames
    slots = jnp.arange(frames, dtype=jnp.int32)
    ends = jnp.sum(jnp.where(slots[None, :] <= slots[:, None], clip_row[None, :], 0), axis=1)
    clip_of = jnp.sum((slots[:, None] >= ends[None, :]).astype(jnp.int32), axis=1)
    starts = ends - clip_row
    start_of = jnp.sum(jnp.where(clip_of[:, None] == slots[None, :], starts[None, :], 0), axis=1)
    frame_pos = slots - start_of
    frame = jnp.arange(count, dtype=jnp.int32) // size
    lane = jnp.arange(LANE, dtype=jnp.int32) % HD
    frame_hot = frame[:, None] == lane[None, :]
    own = frame[:, None] == slots[None, :]
    clip_tok = jnp.sum(jnp.where(own, clip_of[None, :], 0), axis=1)
    pos_tok = jnp.sum(jnp.where(own, frame_pos[None, :], 0), axis=1)
    lane_own = lane[:, None] == slots[None, :]
    lane_clip = jnp.sum(jnp.where(lane_own, clip_of[None, :], 0), axis=1)
    lane_pos = jnp.sum(jnp.where(lane_own, frame_pos[None, :], 0), axis=1)
    seen = (
        (clip_tok[:, None] == lane_clip[None, :])
        & (pos_tok[:, None] <= lane_pos[None, :])
        & (pad[:, None] == 1)
    )
    see = jnp.where((lane[None, :] < frames) & ~seen, -1e30, 0.0).astype(bf16)
    quarter = HD // 4
    freq = 10000.0 ** (-jnp.arange(quarter, dtype=f32) / quarter)
    patch = jnp.arange(count, dtype=jnp.int32) % size
    angle = jnp.concatenate(
        [pos_tok.astype(f32)[:, None] * freq[None, :], patch.astype(f32)[:, None] * freq[None, :]],
        axis=1,
    )
    cosine, sine = jnp.cos(angle), jnp.sin(angle)
    cosine = jnp.concatenate([cosine] * 4, axis=1)
    sine = jnp.concatenate([-sine, sine, -sine, sine], axis=1)
    return see, frame_hot.astype(bf16), cosine, sine


def per_device(
    tokens, cotangent, clip_frames, levels, pad_mask, w_mod, b_mod, w_qkv, b_qkv, w_out, b_out,
    w_up, b_up, w_down, b_down, noise_table,
):
    count, width = tokens.shape
    frames = levels.shape[0]
    size = count // frames
    hidden = w_up.shape[1]
    ndev = width // w_up.shape[0]
    me = lax.axis_index("dp") * lax.axis_size("fsdp") + lax.axis_index("fsdp")

    dp, fsdp = lax.axis_size("dp"), lax.axis_size("fsdp")
    sizes = (dp // 2, 2, fsdp // 2)

    biases = [b_mod, b_qkv, b_out, b_up, b_down]
    lengths = [b.shape[0] for b in biases]
    packed = jnp.concatenate([levels.astype(f32)] + [b.astype(f32) for b in biases])
    packed = jnp.pad(packed, (0, 8 * LANE - packed.shape[0])).reshape(8, LANE)
    small, full_qkv = exchange(Transfers(sizes, [packed, w_qkv]), staggered([0, 0]), "gather_in", 1)
    small = small.reshape(ndev, -1)
    all_levels = small[:, :frames].reshape(-1).astype(jnp.int32)
    full_bias, at = [], frames
    for length in lengths:
        full_bias.append(small[:, at : at + length].reshape(1, -1))
        at += length
    bias_mod, bias_qkv, bias_out, bias_up, bias_down = full_bias

    hot = (all_levels[:, None] == jnp.arange(noise_table.shape[1], dtype=jnp.int32)[None, :]).astype(bf16)
    embedded = dot(hot, noise_table, NT)
    cond = jax.nn.silu(embedded).astype(bf16)
    partial = dot(cond, w_mod, NN)
    full_out, full_up, full_down, modulation = exchange(
        Transfers(sizes, [w_out, w_up, w_down], [partial.reshape(ndev * 8, -1)]), staggered([1, 2, 3, 0]), "gather_mod", 2
    )
    modulation = (modulation.reshape(frames, -1) + bias_mod).reshape(frames, 6, width)
    see, frame_hot, cosine, sine = tables(clip_frames[0], pad_mask, count)

    acts = like((count, width), bf16)
    wide = like((count, width), f32)
    tall = like((count, hidden), bf16)
    row = whole((1, width))
    mod_row = pl.BlockSpec((1, 6, width), lambda i: (i, 0, 0))
    mod_all = whole((frames, 6, width))
    rows_bf = by_rows(size, width)
    act_one, query, key, value = run(
        qkv_kernel, frames,
        [rows_bf, mod_row, whole((width, 3 * width)), whole((1, 3 * width)), by_rows(size, LANE), by_rows(size, LANE)],
        [rows_bf] * 4, [acts] * 4, (tokens, modulation, full_qkv, bias_qkv, cosine, sine), name="qkv",
    )
    pair = by_cols(count, LANE)
    table = whole((count, LANE))
    attended, aug = run(
        lambda *refs: attention_forward(*refs, frames=frames), width // LANE,
        [pair, pair, pair, table, table], [pair] * 2, [acts] * 2, (query, key, value, see, frame_hot), name="attf",
    )
    middle, attn, act_two = run(
        project_kernel, frames, [rows_bf, rows_bf, mod_row, whole((width, width)), row], [rows_bf] * 3,
        [wide, acts, acts], (attended, tokens, modulation, full_out, bias_out), name="proj",
    )
    full = whole((count, width))
    step = 512
    cols_h = by_cols(count, step)
    activated, slope = run(
        up_kernel, hidden // step, [full, by_cols(width, step), by_cols(1, step)], [cols_h] * 2, [tall] * 2,
        (act_two, full_up, bias_up), name="up",
    )
    acc = pltpu.VMEM((count, width), f32)
    block_out, d_branch, d_gate_two, bdown = run(
        down_kernel, hidden // width, [by_cols(count, width), by_rows(width, width), row, full, full, mod_all],
        [full, full, whole((frames, width)), row],
        [acts, acts, like((frames, width), f32), like((1, width), f32)],
        (activated, full_down, bias_down, middle, cotangent, modulation), [acc], name="down",
    )
    wdown = run(
        weight_grad_kernel, hidden // step, [cols_h, full], by_rows(step, width), like((hidden, width), bf16),
        (activated, d_branch), name="wdown",
    )
    d_hidden, bup = run(
        hidden_back_kernel, hidden // step, [full, by_rows(step, width), cols_h], [cols_h, by_cols(1, step)],
        [tall, like((1, hidden), f32)], (d_branch, full_down, slope), name="dhid",
    )
    wup = run(
        weight_grad_kernel, hidden // step, [full, cols_h], by_cols(width, step), like((width, hidden), bf16),
        (act_two, d_hidden), name="wup",
    )
    d_middle, d_attn, stat_two, bout = run(
        mlp_back_kernel, hidden // width,
        [by_cols(count, width), by_cols(width, width), full, full, full, mod_all],
        [full, full, whole((frames, 3, width)), row],
        [wide, acts, like((frames, 3, width), f32), like((1, width), f32)],
        (d_hidden, full_up, middle, cotangent, attn, modulation), [acc], name="dact2",
    )
    wout = run(
        weight_grad_kernel, width // step, [by_cols(count, step), full], by_rows(step, width), like((width, width), bf16),
        (attended, d_attn), name="wout",
    )
    d_attended = dot(d_attn, full_out, NT).astype(bf16)
    d_projected, bqkv = run(
        lambda *refs: attention_backward(*refs, frames=frames), width // LANE, [pair] * 6 + [table] * 3,
        [pl.BlockSpec((3, count, LANE), lambda i: (0, 0, i)), pl.BlockSpec((1, 3, LANE), lambda i: (i, 0, 0))],
        [like((3, count, width), bf16), like((width // LANE, 3, LANE), f32)],
        (query, key, value, d_attended, attended, aug, see, cosine, sine), [pltpu.VMEM((count, LANE), f32)], name="attb",
    )
    stacked = pl.BlockSpec((1, count, width), lambda i: (i, 0, 0))
    wqkv = run(
        qkv_grad_kernel, 3, [full, stacked], by_cols(width, width), like((width, 3 * width), bf16),
        (act_one, d_projected), name="wqkv",
    )
    token_grad, stat_one = run(
        input_back_kernel, 3, [stacked, by_cols(width, width), full, full, mod_all], [full, whole((frames, 2, width))],
        [acts, like((frames, 2, width), f32)], (d_projected, full_qkv, tokens, d_middle, modulation), [acc], name="dact1",
    )
    bqkv = jnp.transpose(bqkv, (1, 0, 2)).reshape(1, -1)
    sums = [bqkv, bout, bup, bdown]
    shares = [b.reshape(ndev, -1) for b in sums]
    packed = jnp.concatenate(shares, axis=1)
    bias_len = packed.shape[1]
    packed = jnp.pad(packed, ((0, 0), (0, 8 * LANE - bias_len))).reshape(-1, LANE)
    d_modulation = jnp.concatenate(
        [stat_one[:, 0], stat_one[:, 1], stat_two[:, 0], stat_two[:, 1], stat_two[:, 2], d_gate_two], axis=1
    ).astype(bf16)
    d_mod, bias_sum, wdown_grad, wup_grad, wqkv_grad, wout_grad = exchange(
        Transfers(sizes, [d_modulation.reshape(16, -1)], [packed, wdown, wup, wqkv, wout]),
        staggered([0, 0, 0, 1, 2, 3]), "reduce", 3,
    )
    d_mod = d_mod.reshape(ndev * frames, -1)
    bias_sum = bias_sum.reshape(-1)[:bias_len]
    bias_grads, at = [], 0
    for share in shares:
        bias_grads.append(bias_sum[at : at + share.shape[1]])
        at += share.shape[1]
    wmod_grad = dot(cond, d_mod, TN)
    mine = b_mod.shape[0]
    bmod_grad = jnp.sum(lax.dynamic_slice(d_mod, (0, me * mine), (d_mod.shape[0], mine)).astype(f32), axis=0)
    gate = jax.nn.sigmoid(embedded)
    d_embed = dot(d_mod, w_mod, NT) * gate * (1.0 + embedded * (1.0 - gate))
    table_grad = lax.dot_general(
        d_embed, hot.astype(f32), TN, precision=lax.Precision.HIGHEST, preferred_element_type=f32
    )
    return (
        block_out, token_grad, wmod_grad, bmod_grad, wqkv_grad, bias_grads[0],
        wout_grad, bias_grads[1], wup_grad, bias_grads[2], wdown_grad,
        bias_grads[3], table_grad,
    )


def solution(mesh):
    rows, vec = P(AXES, None), P(AXES)
    return jax.shard_map(
        per_device,
        mesh=mesh,
        in_specs=(rows, rows, rows, vec, vec) + (rows, vec) * 5 + (rows,),
        out_specs=(rows, rows) + (rows, vec) * 5 + (rows,),
        check_vma=False,
    )
```

```python
import jax
import jax.numpy as jnp
from jax import lax
from jax.experimental import pallas as pl
from jax.experimental.pallas import tpu as pltpu
from jax.sharding import PartitionSpec as P

bf16 = jnp.bfloat16
f32 = jnp.float32
AXES = ("dp", "fsdp")
HD = 64
LANE = 128
EPS = 1e-06
NN = (((1,), (0,)), ((), ()))
NT = (((1,), (1,)), ((), ()))
TN = (((0,), (0,)), ((), ()))


def dot(left, right, dims):
    return lax.dot_general(left, right, dims, preferred_element_type=f32)


def lanes(shape):
    return lax.broadcasted_iota(jnp.int32, shape, 1)


def normalize(values):
    centred = values - jnp.mean(values, axis=1, keepdims=True)
    inverse = lax.rsqrt(jnp.mean(centred * centred, axis=1, keepdims=True) + EPS)
    return centred * inverse, inverse


def normalize_back(grad, normed, inverse):
    return inverse * (
        grad
        - jnp.mean(grad, axis=1, keepdims=True)
        - normed * jnp.mean(grad * normed, axis=1, keepdims=True)
    )


def col_sum(values):
    return jnp.sum(values.astype(f32), axis=0, keepdims=True)


def partner(values):
    return jnp.where(
        lanes(values.shape) % HD < HD // 2,
        pltpu.roll(values, LANE - HD // 2, 1),
        pltpu.roll(values, HD // 2, 1),
    )


def carry_lanes(values):
    sub = lanes(values.shape) % HD
    high = values.astype(bf16).astype(f32)
    rest = values - high
    mid = rest.astype(bf16).astype(f32)
    return jnp.where(
        sub == 8, high, jnp.where(sub == 9, mid, jnp.where(sub == 10, rest - mid, 0.0))
    )


def qkv_kernel(x_ref, mod_ref, wa_ref, wb_ref, b_ref, cos_ref, sin_ref, act_ref, q_ref, k_ref, v_ref):
    normed, _ = normalize(x_ref[...].astype(f32))
    act = (normed * (1.0 + mod_ref[0, 1:2, :]) + mod_ref[0, 0:1, :]).astype(bf16)
    act_ref[...] = act
    width = x_ref.shape[1]
    cosine, sine = cos_ref[...], sin_ref[...]
    step = 2 * LANE
    first = wa_ref.shape[1]
    for col in range(0, 3 * width, step):
        w_ref, at = (wa_ref, col) if col < first else (wb_ref, col - first)
        raw = dot(act, w_ref[:, at : at + step], NN) + b_ref[:, col : col + step].astype(f32)
        for sub in range(0, step, LANE):
            part = raw[:, sub : sub + LANE]
            at = (col + sub) % width
            if col < width:
                part = (part * cosine + partner(part) * sine).astype(bf16)
                q_ref[:, at : at + LANE] = (part.astype(f32) * 0.125).astype(bf16)
            elif col < 2 * width:
                k_ref[:, at : at + LANE] = (part * cosine + partner(part) * sine).astype(bf16)
            else:
                v_ref[:, at : at + LANE] = part.astype(bf16)


def attention_forward(q_ref, k_ref, v_ref, see_ref, hot_ref, out_ref, aug_ref, *, frames):
    rows_all = q_ref.shape[0]
    size = rows_all // frames
    low = lanes((rows_all, LANE)) < HD
    low_b = lanes((size, LANE)) < HD
    k, v, see = k_ref[...], v_ref[...], see_ref[...]
    one = jnp.ones_like(v)
    keys = (jnp.where(low, k, see), jnp.where(low, see, k))
    vals = (jnp.where(low, v, one), jnp.where(low, one, v))
    for i in range(frames):
        rows = slice(i * size, (i + 1) * size)
        width = (i + 1) * size
        q, hot = q_ref[rows, :], hot_ref[rows, :]
        query = (jnp.where(low_b, q, hot), jnp.where(low_b, hot, q))
        tops, outs = [], []
        for h in range(2):
            scores = dot(query[h], keys[h][:width], NT)
            top = jnp.max(scores, axis=1, keepdims=True)
            expo = jnp.exp(scores - top).astype(bf16)
            outs.append(dot(expo, vals[h][:width], NN))
            tops.append(top)
        num = jnp.where(low_b, outs[0], outs[1])
        den = jnp.where(low_b, outs[1], outs[0])
        out_ref[rows, :] = (num / pltpu.roll(den, HD, 1)).astype(bf16)
        lse = jnp.where(low_b, tops[1], tops[0]) + jnp.log(den)
        aug_ref[rows, :] = (carry_lanes(-lse) + hot.astype(f32)).astype(bf16)


def project_kernel(att_ref, x_ref, mod_ref, w_ref, b_ref, middle_ref, attn_ref, act_ref):
    attn = dot(att_ref[...], w_ref[...], NN) + b_ref[...].astype(f32)
    attn_ref[...] = attn.astype(bf16)
    middle = x_ref[...].astype(f32) + mod_ref[0, 2:3, :] * attn
    middle_ref[...] = middle
    normed, _ = normalize(middle)
    act_ref[...] = (normed * (1.0 + mod_ref[0, 4:5, :]) + mod_ref[0, 3:4, :]).astype(bf16)


def up_kernel(act_ref, w_ref, b_ref, out_ref, slope_ref):
    hidden = dot(act_ref[...], w_ref[...], NN) + b_ref[...].astype(f32)
    share = 0.5 * (1.0 + lax.erf(hidden * 0.7071067811865476))
    out_ref[...] = (hidden * share).astype(bf16)
    slope = share + hidden * jnp.exp(-0.5 * hidden * hidden) * 0.3989422804014327
    slope_ref[...] = slope.astype(bf16)


def down_kernel(
    act_ref, w_ref, b_ref, mid_ref, cot_ref, mod_ref, out_ref, dbr_ref, gate_ref, sum_ref, acc_ref
):
    step, last = pl.program_id(0), pl.num_programs(0) - 1
    part = dot(act_ref[...], w_ref[...], NN)

    @pl.when(step == 0)
    def _():
        acc_ref[...] = part

    @pl.when(step > 0)
    def _():
        acc_ref[...] += part

    @pl.when(step == last)
    def _():
        frames = mod_ref.shape[0]
        size = acc_ref.shape[0] // frames
        total = jnp.zeros((1, acc_ref.shape[1]), f32)
        for i in range(frames):
            rows = slice(i * size, (i + 1) * size)
            gate = mod_ref[i, 5:6, :]
            branch = acc_ref[rows, :] + b_ref[...].astype(f32)
            out_ref[rows, :] = (mid_ref[rows, :] + gate * branch).astype(bf16)
            upstream = cot_ref[rows, :].astype(f32)
            d_branch = (upstream * gate).astype(bf16)
            dbr_ref[rows, :] = d_branch
            gate_ref[i : i + 1, :] = col_sum(upstream * branch)
            total += col_sum(d_branch)
        sum_ref[...] = total


def hidden_back_kernel(dbr_ref, w_ref, slope_ref, out_ref, sum_ref):
    d_hidden = (dot(dbr_ref[...], w_ref[...], NT) * slope_ref[...].astype(f32)).astype(bf16)
    out_ref[...] = d_hidden
    sum_ref[...] = col_sum(d_hidden)


def mlp_back_kernel(
    dh_ref, w_ref, mid_ref, cot_ref, attn_ref, mod_ref, dmid_ref, datt_ref, stat_ref, sum_ref, acc_ref
):
    step, last = pl.program_id(0), pl.num_programs(0) - 1
    part = dot(dh_ref[...], w_ref[...], NT)

    @pl.when(step == 0)
    def _():
        acc_ref[...] = part

    @pl.when(step > 0)
    def _():
        acc_ref[...] += part

    @pl.when(step == last)
    def _():
        frames = mod_ref.shape[0]
        size = acc_ref.shape[0] // frames
        total = jnp.zeros((1, acc_ref.shape[1]), f32)
        for i in range(frames):
            rows = slice(i * size, (i + 1) * size)
            d_act = acc_ref[rows, :]
            normed, inverse = normalize(mid_ref[rows, :])
            stat_ref[i, 1:2, :] = col_sum(d_act)
            stat_ref[i, 2:3, :] = col_sum(d_act * normed)
            d_middle = cot_ref[rows, :].astype(f32) + normalize_back(
                d_act * (1.0 + mod_ref[i, 4:5, :]), normed, inverse
            )
            dmid_ref[rows, :] = d_middle
            stat_ref[i, 0:1, :] = col_sum(d_middle * attn_ref[rows, :].astype(f32))
            d_attn = (d_middle * mod_ref[i, 2:3, :]).astype(bf16)
            datt_ref[rows, :] = d_attn
            total += col_sum(d_attn)
        sum_ref[...] = total


def attention_backward(
    q_ref, k_ref, v_ref, do_ref, o_ref, aug_ref, see_ref, cos_ref, sin_ref, out_ref, sum_ref, acc_ref, *, frames
):
    rows_all = q_ref.shape[0]
    size = rows_all // frames
    low = lanes((rows_all, LANE)) < HD
    q, aug, grad = q_ref[...], aug_ref[...], do_ref[...]
    prod = grad.astype(f32) * o_ref[...].astype(f32)
    delta_low = jnp.sum(jnp.where(low, prod, 0.0), axis=1, keepdims=True)
    delta_high = jnp.sum(jnp.where(low, 0.0, prod), axis=1, keepdims=True)
    grad_aug = carry_lanes(jnp.where(low, -delta_high, -delta_low)).astype(bf16)
    query = (jnp.where(low, q, aug), jnp.where(low, aug, q))
    upper = (jnp.where(low, grad, grad_aug), jnp.where(low, grad_aug, grad))
    low_b = lanes((size, LANE)) < HD
    sub = lanes((size, LANE)) % HD
    ones = jnp.where((sub >= 8) & (sub <= 10), 1.0, 0.0).astype(bf16)
    sum_k = sum_v = jnp.zeros((1, LANE), f32)
    for j in range(frames):
        rows = slice(j * size, (j + 1) * size)
        start = j * size
        k, v, see = k_ref[rows, :], v_ref[rows, :], see_ref[rows, :] + ones
        keys = (jnp.where(low_b, k, see), jnp.where(low_b, see, k))
        vals = (jnp.where(low_b, v, ones), jnp.where(low_b, ones, v))
        dvs, dks, dqs = [], [], []
        for h in range(2):
            probs = jnp.exp(dot(keys[h], query[h][start:], NT))
            d_scores = (probs * dot(vals[h], upper[h][start:], NT)).astype(bf16)
            dvs.append(dot(probs.astype(bf16), grad[start:], NN))
            dks.append(dot(d_scores, q[start:], NN))
            dqs.append(dot(d_scores, k, TN))
        d_value = jnp.where(low_b, dvs[0], dvs[1]).astype(bf16)
        d_key = jnp.where(low_b, dks[0], dks[1])
        d_key = (d_key * cos_ref[rows, :] - partner(d_key) * sin_ref[rows, :]).astype(bf16)
        out_ref[1, rows, :] = d_key
        out_ref[2, rows, :] = d_value
        sum_k = sum_k + col_sum(d_key)
        sum_v = sum_v + col_sum(d_value)
        d_query = jnp.where(lanes(dqs[0].shape) < HD, dqs[0], dqs[1])
        if j == 0:
            acc_ref[...] = d_query
        else:
            acc_ref[start:, :] += d_query
    d_query = acc_ref[...] * 0.125
    d_query = (d_query * cos_ref[...] - partner(d_query) * sin_ref[...]).astype(bf16)
    out_ref[0] = d_query
    sum_ref[0, 0:1, :] = col_sum(d_query)
    sum_ref[0, 1:2, :] = sum_k
    sum_ref[0, 2:3, :] = sum_v


def input_back_kernel(dp_ref, w_ref, x_ref, dmid_ref, mod_ref, out_ref, stat_ref, acc_ref):
    step, last = pl.program_id(0), pl.num_programs(0) - 1
    part = dot(dp_ref[0], w_ref[0], NT)

    @pl.when(step == 0)
    def _():
        acc_ref[...] = part

    @pl.when(step > 0)
    def _():
        acc_ref[...] += part

    @pl.when(step == last)
    def _():
        frames = mod_ref.shape[0]
        size = acc_ref.shape[0] // frames
        for i in range(frames):
            rows = slice(i * size, (i + 1) * size)
            d_act = acc_ref[rows, :]
            normed, inverse = normalize(x_ref[rows, :].astype(f32))
            stat_ref[i, 0:1, :] = col_sum(d_act)
            stat_ref[i, 1:2, :] = col_sum(d_act * normed)
            back = normalize_back(d_act * (1.0 + mod_ref[i, 1:2, :]), normed, inverse)
            out_ref[rows, :] = (dmid_ref[rows, :] + back).astype(bf16)


def modulation_kernel(small_ref, table_ref, w_ref, part_ref, levels_ref, frames):
    ndev = part_ref.shape[0] * part_ref.shape[1] * part_ref.shape[2] * 2
    rows = levels_ref[...].reshape(ndev, levels_ref.shape[-2], LANE)
    spots = jnp.sum(rows[:, :8], axis=0).astype(jnp.int32)
    count = 2 * frames * ndev
    level = jnp.concatenate([spots[i : i + 1, :] for i in range(count // LANE)], axis=1)
    slot = lax.broadcasted_iota(jnp.int32, (table_ref.shape[1], count), 0)
    hot = jnp.where(slot == level, 1.0, 0.0).astype(bf16)
    embedded = dot(table_ref[...], hot, NN)
    cond = (embedded / (1.0 + jnp.exp(-embedded))).astype(bf16)
    half = part_ref.shape[-1]
    first = lax.broadcasted_iota(jnp.int32, (count, 1), 0) % (2 * frames) < frames
    step = 512
    for col in range(0, half, step):
        low = dot(cond, w_ref[:, col : col + step], TN)
        high = dot(cond, w_ref[:, half + col : half + col + step], TN)
        value = jnp.where(first, low, high)
        part_ref[..., col : col + step] = value.reshape(part_ref.shape[:-1] + (step,))


def weight_grad_kernel(left_ref, right_ref, out_ref):
    out_ref[...] = dot(left_ref[...], right_ref[...], TN).astype(bf16)


def qkv_grad_kernel(left_ref, right_ref, out_ref):
    out_ref[0] = dot(left_ref[...], right_ref[0], TN).astype(bf16)


def like(shape, kind):
    return jax.ShapeDtypeStruct(shape, kind)


def whole(shape):
    return pl.BlockSpec(shape, lambda i: (0,) * len(shape))


def by_rows(size, width):
    return pl.BlockSpec((size, width), lambda i: (i, 0))


def by_cols(height, size):
    return pl.BlockSpec((height, size), lambda i: (0, i))


MESH = pl.DeviceIdType.MESH
ANY = pl.BlockSpec(memory_space=pl.ANY)
VMEM = pl.BlockSpec(memory_space=pltpu.VMEM)
DMA = pltpu.SemaphoreType.DMA


class Place:
    def __init__(self, sizes):
        self.ny, self.nx, self.nz = sizes
        self.half = self.nz // 2
        self.rest = self.nz - self.half
        self.low, self.high = pl.ds(0, self.half), pl.ds(self.half, self.rest)
        self.dp, self.fsdp = lax.axis_index("dp"), lax.axis_index("fsdp")
        self.y, self.x = lax.div(self.dp, self.nx), lax.rem(self.dp, self.nx)
        self.z, self.c = lax.div(self.fsdp, 2), lax.rem(self.fsdp, 2)

        self.shifts, self.devices = {}, {}
        for axis, size in dict(y=self.ny, x=self.nx, z=self.nz, c=2).items():
            for k in range(1, size):
                at = lax.rem(getattr(self, axis) + k, size)
                self.shifts[axis, k] = self.shifts[axis, k - size] = at
                self.devices[axis, k] = dict(
                    y=(at * self.nx + self.x, self.fsdp), x=(self.y * self.nx + at, self.fsdp),
                    z=(self.dp, at * 2 + self.c), c=(self.dp, self.z * 2 + at),
                )[axis]
        self.other = self.shifts["c", 1]

    def shift(self, axis, k):
        return self.shifts[axis, k]

    def device(self, axis, k):
        return self.devices[axis, k]

    def enter(self, axes):
        barrier = pltpu.get_barrier_semaphore()
        sizes = dict(y=self.ny, x=self.nx, z=self.nz, c=2)
        count = 0
        for axis in axes:
            for k in range(1, sizes[axis]):
                count += 1
                pl.semaphore_signal(barrier, inc=1, device_id=self.device(axis, k), device_id_type=MESH)
        pl.semaphore_wait(barrier, count)


class Move:
    ins, in_specs, outs, out_specs, scratch, aliases = (), (), (), (), (), ()

    def bind(self, place, ins, outs, scratch):
        self.place, self.in_refs, self.out_refs, self.refs = place, ins, outs, scratch
        self.slots, self.local_slots, self.legs = {}, {}, []

    def copy(self, key, src, dst, axis, k):
        slot = self.slots.setdefault(key, len(self.slots))
        return pltpu.make_async_remote_copy(
            src_ref=src, dst_ref=dst, send_sem=self.refs[0].at[slot], recv_sem=self.refs[1].at[slot],
            device_id=self.place.device(axis, k), device_id_type=MESH,
        )

    def start(self, items):
        for item in items:
            self.copy(*item).start()

    def arrived(self, key, dst, axis, k):
        self.copy(key, dst, dst, axis, k).wait_recv()

    def drain(self, items):
        for item in items:
            self.copy(*item).wait_send()

    def local(self, key, src, dst):
        slot = self.local_slots.setdefault(key, len(self.local_slots))
        return pltpu.make_async_copy(src, dst, self.refs[2].at[slot])


class Held:
    def __init__(self, shape, kind):
        self.shape, self.dtype, self.ref = shape, kind, None


def legs_copies(sizes):
    ny, nx, nz = sizes
    return (nz - 1) + 4 * (nx - 1) + 4 * (ny - 1) + 1


class Gather(Move):
    def __init__(self, sizes, array, actions, begun=False):
        ny, nx, nz = sizes
        self.begun, self.actions = begun, actions
        self.ins, self.in_specs = [array], [ANY if begun else VMEM]
        shape = array.shape if begun else (ny, nx, nz, 2) + array.shape
        self.outs, self.out_specs = [like(shape, array.dtype)], [ANY]
        self.scratch = [DMA((legs_copies(sizes),)), DMA((legs_copies(sizes),)), DMA((1,))]
        self.aliases = [(0, 0)] if begun else []

    def act(self, what):
        getattr(self, what[:-1])(int(what[-1]))

    def items(self, leg):
        p, full = self.place, self.out_refs[0]
        y, x, z, c = p.y, p.x, p.z, p.c
        d = p.other
        xs, ys, zs = range(1, p.nx), range(1, p.ny), range(1, p.nz)
        back = p.shift
        if leg == 0:
            return [(("z", k), (y, x, z, c), (y, x, back("z", -k), c), "z", k) for k in zs]
        if leg == 1:
            return (
                [(("x", k), (y, x, p.low, c), (y, back("x", -k), p.low, c), "x", k) for k in xs]
                + [(("y", k), (y, x, p.high, c), (back("y", -k), x, p.high, c), "y", k) for k in ys]
                + [("c", (y, x, slice(None), c), (y, x, slice(None), d), "c", 1)]
            )
        every = slice(None)
        if leg == 2:
            return (
                [(("xy", k), (y, every, p.low, c), (back("y", -k), every, p.low, c), "y", k) for k in ys]
                + [(("yx", k), (every, x, p.high, c), (every, back("x", -k), p.high, c), "x", k) for k in xs]
                + [(("cx", k), (y, back("x", -k), p.low, c), (y, back("x", -k), p.low, d), "c", 1) for k in xs]
                + [(("cy", k), (back("y", -k), x, p.high, c), (back("y", -k), x, p.high, d), "c", 1) for k in ys]
            )
        return [
            (("cxy", k), (back("y", -k), every, p.low, c), (back("y", -k), every, p.low, d), "c", 1) for k in ys
        ] + [(("cyx", k), (every, back("x", -k), p.high, c), (every, back("x", -k), p.high, d), "c", 1) for k in xs]

    def own(self):
        p = self.place
        return self.local("own", self.in_refs[0], self.out_refs[0].at[p.y, p.x, p.z, p.c])

    def leaving(self, leg):
        full = self.out_refs[0]
        for key, leaves, _, axis, k in self.items(leg):
            yield key, self.in_refs[0] if leg == 0 else full.at[leaves], full.at[leaves], axis, k

    def start_leg(self, leg):
        self.legs.append(leg)
        if leg == 0:
            self.own().start()
        self.start(self.leaving(leg))

    def wait_leg(self, leg):
        full = self.out_refs[0]
        if leg == 0:
            self.own().wait()
        for key, _, arrives, axis, k in self.items(leg):
            self.arrived(key, full.at[arrives], axis, k)

    def s(self, leg):
        self.start_leg(leg)

    def w(self, leg):
        self.wait_leg(leg)
        for each in self.legs:
            self.drain(self.leaving(each))

    def n(self, leg):
        self.wait_leg(leg)
        self.start_leg(leg + 1)


def add_blocks(into, where, counts, terms):
    total = 1
    for n in counts:
        total *= n

    def body(flat, carry):
        at = []
        for n in reversed(counts):
            at.append(lax.rem(flat, n))
            flat = lax.div(flat, n)
        at = tuple(at[::-1])
        spot = where(*at)
        value = into[spot].astype(f32)
        for ref, index in terms(*at):
            value = value + ref[index].astype(f32)
        into[spot] = value.astype(into.dtype)
        return carry

    lax.fori_loop(0, total, body, 0)


class ReduceCore(Move):
    def __init__(self, sizes, array, actions, part=None):
        self.actions, self.part = actions, part
        ny, nx, nz = sizes
        self.held = array if isinstance(array, Held) else None
        self.ins, self.in_specs = ([], []) if self.held else ([array], [ANY])
        self.outs, self.out_specs = [like((ny, nx, nz) + array.shape[-2:], array.dtype)], [ANY]
        self.scratch = [DMA((1,)), DMA((1,))]

    def act(self, what):
        p = self.place
        source = self.held.ref if self.held else self.in_refs[0]
        source = source if self.part is None else source.at[self.part]
        leaving = [("c", source.at[:, :, :, p.other], self.out_refs[0], "c", 1)]
        if what == "s":
            self.start(leaving)
        else:
            self.arrived("c", self.out_refs[0], "c", 1)
            self.drain(leaving)


class ReduceFirst(Move):
    def __init__(self, sizes, array, core, actions, part=None):
        self.actions, self.part, self.core = actions, part, core
        ny, nx, nz = sizes
        half, rest = nz // 2, nz - nz // 2
        block, kind = array.shape[-2:], array.dtype
        self.held = array if isinstance(array, Held) else None
        self.ins = ([] if self.held else [array]) + ([] if isinstance(core, Move) else [core])
        self.in_specs = [ANY] * len(self.ins)
        self.outs = [
            like((ny - 1, nx, half) + block, kind), like((nx - 1, ny, rest) + block, kind),
            like((nx, half) + block, kind), like((ny, rest) + block, kind),
        ]
        self.out_specs = [ANY] * 4
        remote = DMA((nx + ny - 2,))
        self.scratch = [remote, remote, DMA((4,))] + [pltpu.VMEM((ny, nx, nz) + block, kind)] * 2

    def act(self, what):
        p = self.place
        source = self.held.ref if self.held else self.in_refs[0]
        source = source if self.part is None else source.at[self.part]
        core = self.core.out_refs[0] if isinstance(self.core, Move) else self.in_refs[-1]
        acc, buf = self.refs[3:]
        la, lb, ka, kb = self.out_refs
        loads = [("acc", source.at[:, :, :, p.c], acc), ("buf", core, buf)]
        leaving = [
            (("y", k), acc.at[p.shift("y", k), :, p.low], la.at[k - 1], "y", k) for k in range(1, p.ny)
        ] + [(("x", k), acc.at[:, p.shift("x", k), p.high], lb.at[k - 1], "x", k) for k in range(1, p.nx)]
        keeps = [("ka", acc.at[p.y, :, p.low], ka), ("kb", acc.at[:, p.x, p.high], kb)]
        if what == "l":
            for item in loads:
                self.local(*item).start()
        elif what == "a":
            for item in loads:
                self.local(*item).wait()
            add_blocks(acc, lambda *at: at, (p.ny, p.nx, p.nz), lambda *at: [(buf, at)])
            self.start(leaving)
            for item in keeps:
                self.local(*item).start()
        else:
            for k in range(1, p.ny):
                self.arrived(("y", k), la.at[k - 1], "y", k)
            for k in range(1, p.nx):
                self.arrived(("x", k), lb.at[k - 1], "x", k)
            for item in keeps:
                self.local(*item).wait()
            self.drain(leaving)


class ReduceSecond(Move):
    def __init__(self, sizes, first, actions):
        self.actions, self.first = actions, first
        ny, nx, nz = sizes
        half, rest = nz // 2, nz - nz // 2
        self.inside = isinstance(first, Move)
        arrays = first.outs if self.inside else first
        block, kind = arrays[0].shape[-2:], arrays[0].dtype
        self.ins, self.in_specs = ([], []) if self.inside else (list(arrays), [ANY] * 4)
        self.outs = [
            like((nx - 1, half) + block, kind), like((ny - 1, rest) + block, kind), like((nz,) + block, kind)
        ]
        self.out_specs = [ANY] * 3
        remote = DMA((nx + ny - 2,))
        self.scratch = [remote, remote, DMA((6,))] + [pltpu.VMEM(a.shape, kind) for a in arrays]

    def act(self, what):
        p = self.place
        arrays = self.first.out_refs if self.inside else self.in_refs
        bufs = self.refs[3:]
        la, lb, ka, kb = bufs
        ma, mb, kept = self.out_refs
        loads = [(i, a, b) for i, (a, b) in enumerate(zip(arrays, bufs))]
        leaving = [(("x", k), ka.at[p.shift("x", k)], ma.at[k - 1], "x", k) for k in range(1, p.nx)]
        leaving += [(("y", k), kb.at[p.shift("y", k)], mb.at[k - 1], "y", k) for k in range(1, p.ny)]
        keeps = [("ka", ka.at[p.x], kept.at[p.low]), ("kb", kb.at[p.y], kept.at[p.high])]
        if what == "l":
            for item in loads:
                self.local(*item).start()
        elif what == "a":
            for item in loads:
                self.local(*item).wait()
            add_blocks(ka, lambda *at: at, (p.nx, p.half), lambda i, j: [(la, (k, i, j)) for k in range(p.ny - 1)])
            add_blocks(kb, lambda *at: at, (p.ny, p.rest), lambda i, j: [(lb, (k, i, j)) for k in range(p.nx - 1)])
            self.start(leaving)
            for item in keeps:
                self.local(*item).start()
        else:
            for k in range(1, p.nx):
                self.arrived(("x", k), ma.at[k - 1], "x", k)
            for k in range(1, p.ny):
                self.arrived(("y", k), mb.at[k - 1], "y", k)
            for item in keeps:
                self.local(*item).wait()
            self.drain(leaving)


class ReduceLast(Move):
    def __init__(self, sizes, second, actions):
        self.actions, self.second = actions, second
        ny, nx, nz = sizes
        self.inside = isinstance(second, Move)
        arrays = second.outs if self.inside else second
        block, kind = arrays[0].shape[-2:], arrays[0].dtype
        self.ins, self.in_specs = ([], []) if self.inside else (list(arrays), [ANY] * 3)
        self.outs, self.out_specs = [like(block, f32)], [VMEM]
        self.scratch = [DMA((nz - 1,)), DMA((nz - 1,)), DMA((3,))] + [pltpu.VMEM(a.shape, kind) for a in arrays]
        self.scratch += [pltpu.VMEM((nz - 1,) + block, kind)]

    def act(self, what):
        p = self.place
        arrays = self.second.out_refs if self.inside else self.in_refs
        ma, mb, kept, last = self.refs[3:]
        loads = [(i, a, b) for i, (a, b) in enumerate(zip(arrays, (ma, mb, kept)))]
        leaving = [(("z", k), kept.at[p.shift("z", k)], last.at[k - 1], "z", k) for k in range(1, p.nz)]
        if what == "l":
            for item in loads:
                self.local(*item).start()
        elif what == "a":
            for item in loads:
                self.local(*item).wait()
            add_blocks(kept, lambda j: (j,), (p.half,), lambda j: [(ma, (k, j)) for k in range(p.nx - 1)])
            add_blocks(
                kept, lambda j: (p.half + j,), (p.rest,), lambda j: [(mb, (k, j)) for k in range(p.ny - 1)]
            )
            self.start(leaving)
        else:
            for k in range(1, p.nz):
                self.arrived(("z", k), last.at[k - 1], "z", k)
            value = kept[p.z].astype(f32)
            for k in range(p.nz - 1):
                value = value + last[k].astype(f32)
            self.out_refs[0][...] = value
            self.drain(leaving)


def run(
    kernel, grid, ins, outs, shapes, args, scratch=(), name=None, moves=(), sizes=None, group=None, axes="yxzc", script=None
):
    single = not isinstance(shapes, (list, tuple))
    outs, shapes = ([outs], [shapes]) if single else (list(outs), list(shapes))
    counts = len(ins), len(outs), len(scratch)
    all_ins, all_specs, all_outs = list(args), list(ins), list(shapes)
    all_out_specs, all_scratch, aliases = list(outs), list(scratch), {}
    for move in moves:
        for i, o in move.aliases:
            aliases[len(all_ins) + i] = len(all_outs) + o
        all_ins += list(move.ins)
        all_specs += list(move.in_specs)
        all_outs += list(move.outs)
        all_out_specs += list(move.out_specs)
        all_scratch += list(move.scratch)

    def body(*refs):
        refs = list(refs)

        def take(n):
            part = refs[:n]
            del refs[:n]
            return part

        mine_in = take(counts[0])
        moved_in = [take(len(m.ins)) for m in moves]
        mine_out = take(counts[1])
        moved_out = [take(len(m.outs)) for m in moves]
        mine_scratch = take(counts[2])
        place = Place(sizes) if moves else None
        for move, i, o in zip(moves, moved_in, moved_out):
            move.bind(place, i, o, take(len(move.scratch)))
        step = pl.program_id(0)

        def turn(at):
            for move in moves:
                for when, what in move.actions:
                    if when == at:
                        move.act(what)

        if script is not None:
            place.enter(axes)
            for item in script:
                if isinstance(item, tuple):
                    item[0].act(item[1])
                else:
                    item(mine_in, mine_out, mine_scratch)
            return

        for at in range(grid):
            if any(when == at for m in moves for when, _ in m.actions):

                @pl.when(step == at)
                def _(at=at):
                    if at == 0:
                        place.enter(axes)
                    turn(at)

        kernel(*mine_in, *mine_out, *mine_scratch)
        if moves:

            @pl.when(step == grid - 1)
            def _():
                turn(grid)

    params = dict(vmem_limit_bytes=60 * 1024 * 1024)
    if moves:
        params.update(collective_id=group, has_side_effects=True)
    moved = sum(a.size * a.dtype.itemsize for a in args)
    results = pl.pallas_call(
        body,
        grid=(grid,),
        in_specs=all_specs,
        out_specs=all_out_specs,
        out_shape=all_outs,
        scratch_shapes=all_scratch,
        input_output_aliases=aliases,
        name=name,
        cost_estimate=pl.CostEstimate(flops=0, bytes_accessed=2 * moved, transcendentals=0),
        compiler_params=pltpu.CompilerParams(**params),
    )(*all_ins)
    return results[0] if single and not moves else results


def tables(clip_row, pad, count):
    frames = clip_row.shape[0]
    size = count // frames
    slots = jnp.arange(frames, dtype=jnp.int32)
    ends = jnp.sum(jnp.where(slots[None, :] <= slots[:, None], clip_row[None, :], 0), axis=1)
    clip_of = jnp.sum((slots[:, None] >= ends[None, :]).astype(jnp.int32), axis=1)
    starts = ends - clip_row
    start_of = jnp.sum(jnp.where(clip_of[:, None] == slots[None, :], starts[None, :], 0), axis=1)
    frame_pos = slots - start_of
    frame = jnp.arange(count, dtype=jnp.int32) // size
    lane = jnp.arange(LANE, dtype=jnp.int32) % HD
    frame_hot = frame[:, None] == lane[None, :]
    own = frame[:, None] == slots[None, :]
    clip_tok = jnp.sum(jnp.where(own, clip_of[None, :], 0), axis=1)
    pos_tok = jnp.sum(jnp.where(own, frame_pos[None, :], 0), axis=1)
    lane_own = lane[:, None] == slots[None, :]
    lane_clip = jnp.sum(jnp.where(lane_own, clip_of[None, :], 0), axis=1)
    lane_pos = jnp.sum(jnp.where(lane_own, frame_pos[None, :], 0), axis=1)
    seen = (
        (clip_tok[:, None] == lane_clip[None, :])
        & (pos_tok[:, None] <= lane_pos[None, :])
        & (pad[:, None] == 1)
    )
    see = jnp.where((lane[None, :] < frames) & ~seen, -1e30, 0.0).astype(bf16)
    quarter = HD // 4
    freq = 10000.0 ** (-jnp.arange(quarter, dtype=f32) / quarter)
    patch = jnp.arange(count, dtype=jnp.int32) % size
    angle = jnp.concatenate(
        [pos_tok.astype(f32)[:, None] * freq[None, :], patch.astype(f32)[:, None] * freq[None, :]],
        axis=1,
    )
    cosine, sine = jnp.cos(angle), jnp.sin(angle)
    cosine = jnp.concatenate([cosine] * 4, axis=1)
    sine = jnp.concatenate([-sine, sine, -sine, sine], axis=1)
    return see, frame_hot.astype(bf16), cosine, sine


def per_device(
    tokens, cotangent, clip_frames, levels, pad_mask, w_mod, b_mod, w_qkv, b_qkv, w_out, b_out,
    w_up, b_up, w_down, b_down, noise_table,
):
    count, width = tokens.shape
    frames = levels.shape[0]
    size = count // frames
    hidden = w_up.shape[1]
    ndev = width // w_up.shape[0]
    me = lax.axis_index("dp") * lax.axis_size("fsdp") + lax.axis_index("fsdp")

    dp, fsdp = lax.axis_size("dp"), lax.axis_size("fsdp")
    sizes = (dp // 2, 2, fsdp // 2)
    lead = sizes + (2,)

    def flat(array):
        return array.reshape(-1, array.shape[-1])

    def blocks(array, front=0):
        rows = array.shape[front] // ndev
        return array.reshape(array.shape[:front] + lead + (rows, array.shape[-1]))

    biases = [b_mod, b_qkv, b_out, b_up, b_down]
    lengths = [b.shape[0] for b in biases]
    spots = jnp.arange(8 * LANE, dtype=jnp.int32)
    mine_at = jnp.where(spots // (2 * frames) == me, jnp.tile(levels, spots.shape[0] // frames), 0)
    packed = jnp.concatenate([mine_at.astype(f32)] + [b.astype(f32) for b in biases])
    packed = jnp.pad(packed, (0, 16 * LANE - packed.shape[0])).reshape(16, LANE)
    table_pad = jnp.pad(noise_table, ((0, 0), (0, -noise_table.shape[1] % LANE)))
    split = 3 * width // 2
    part = Held(lead + (2 * frames, w_mod.shape[1] // 2), f32)
    small = Gather(sizes, packed, ())
    qa, qb = Gather(sizes, w_qkv[:, :split], ()), Gather(sizes, w_qkv[:, split:], ())
    out_w, up_w = Gather(sizes, w_out, ()), Gather(sizes, w_up, ())
    mod_c = ReduceCore(sizes, part, ())
    mod_f = ReduceFirst(sizes, part, mod_c, ())
    mod_s = ReduceSecond(sizes, mod_f, ())
    mod_l = ReduceLast(sizes, mod_s, ())

    def add_modulation(ins, _, scratch):
        part.ref = scratch[0]
        load = pltpu.make_async_copy(small.out_refs[0], scratch[1], scratch[2].at[0])
        load.start()
        load.wait()
        modulation_kernel(None, ins[0], ins[1], scratch[0], scratch[1], frames)

    head = run(
        None, 1, [VMEM] * 2, [], [], [table_pad, w_mod],
        [pltpu.VMEM(part.shape, f32), pltpu.VMEM(lead + packed.shape, f32), DMA((1,))], name="head",
        moves=[small, qa, qb, out_w, up_w, mod_c, mod_f, mod_s, mod_l], sizes=sizes, group=1,
        script=[
            (small, "s0"), (qa, "s0"), (qb, "s0"), (small, "n0"), (small, "n1"), (small, "n2"), (small, "w3"),
            (qa, "n0"), (out_w, "s0"), (up_w, "s0"), add_modulation, (mod_c, "s"), (qa, "n1"), (qb, "n0"),
            (mod_c, "w"), (mod_f, "l"), (mod_f, "a"), (qb, "n1"), (mod_f, "w"), (mod_s, "l"), (mod_s, "a"),
            (qa, "n2"), (mod_s, "w"), (mod_l, "l"), (mod_l, "a"), (qb, "n2"), (qa, "w3"), (qb, "w3"),
            (mod_l, "w"), (out_w, "w0"), (up_w, "w0"),
        ],
    )
    small, qa, qb, out_w, up_w = head[:5]
    small = small.reshape(ndev, -1)
    all_levels = jnp.sum(small[:, : 8 * LANE], axis=0).reshape(-1, 2 * frames)[:ndev, :frames]
    all_levels = all_levels.reshape(-1).astype(jnp.int32)
    full_bias, at = [], 8 * LANE
    for length in lengths:
        full_bias.append(small[:, at : at + length].reshape(1, -1))
        at += length
    bias_mod, bias_qkv, bias_out, bias_up, bias_down = full_bias
    modulation = jnp.transpose(head[-1].reshape(2, frames, -1), (1, 0, 2)).reshape(frames, -1)
    modulation = (modulation + bias_mod).reshape(frames, 6, width)
    qkv_a, qkv_b = flat(qa), flat(qb)
    see, frame_hot, cosine, sine = tables(clip_frames[0], pad_mask, count)

    acts = like((count, width), bf16)
    wide = like((count, width), f32)
    tall = like((count, hidden), bf16)
    row = whole((1, width))
    mod_row = pl.BlockSpec((1, 6, width), lambda i: (i, 0, 0))
    mod_all = whole((frames, 6, width))
    rows_bf = by_rows(size, width)
    halves = [whole((width, split))] * 2
    act_one, query, key, value, out_w = run(
        qkv_kernel, frames,
        [rows_bf, mod_row] + halves + [whole((1, 3 * width)), by_rows(size, LANE), by_rows(size, LANE)],
        [rows_bf] * 4, [acts] * 4, (tokens, modulation, qkv_a, qkv_b, bias_qkv, cosine, sine), name="qkv",
        moves=[Gather(sizes, out_w, [(0, "s1"), (1, "n1"), (3, "n2"), (frames, "w3")], True)], sizes=sizes, group=2,
    )
    full_out = flat(out_w)
    pair = by_cols(count, LANE)
    table = whole((count, LANE))
    pairs = width // LANE
    attended, aug, up_w, down_w = run(
        lambda *refs: attention_forward(*refs, frames=frames), pairs,
        [pair, pair, pair, table, table], [pair] * 2, [acts] * 2, (query, key, value, see, frame_hot), name="attf",
        moves=[
            Gather(sizes, up_w, [(0, "s1"), (3, "n1"), (pairs, "w2")], True),
            Gather(sizes, w_down, [(0, "s0"), (pairs, "w0")]),
        ], sizes=sizes, group=3,
    )
    middle, attn, act_two, up_w, down_w = run(
        project_kernel, frames, [rows_bf, rows_bf, mod_row, whole((width, width)), row], [rows_bf] * 3,
        [wide, acts, acts], (attended, tokens, modulation, full_out, bias_out), name="proj",
        moves=[
            Gather(sizes, up_w, [(0, "s3"), (frames, "w3")], True),
            Gather(sizes, down_w, [(0, "s1"), (frames, "w1")], True),
        ], sizes=sizes, group=4,
    )
    full_up = flat(up_w)
    full = whole((count, width))
    step = 512
    tiles = hidden // step
    cols_h = by_cols(count, step)
    activated, slope, down_w = run(
        up_kernel, tiles, [full, by_cols(width, step), by_cols(1, step)], [cols_h] * 2, [tall] * 2,
        (act_two, full_up, bias_up), name="up",
        moves=[Gather(sizes, down_w, [(0, "s2"), (tiles, "n2"), (tiles, "w3")], True)], sizes=sizes, group=5,
    )
    full_down = flat(down_w)
    acc = pltpu.VMEM((count, width), f32)
    deep = hidden // width
    block_out, d_branch, d_gate_two, bdown = run(
        down_kernel, deep, [by_cols(count, width), by_rows(width, width), row, full, full, mod_all],
        [full, full, whole((frames, width)), row],
        [acts, acts, like((frames, width), f32), like((1, width), f32)],
        (activated, full_down, bias_down, middle, cotangent, modulation), [acc], name="down",
    )
    wdown = run(
        weight_grad_kernel, tiles, [cols_h, full], by_rows(step, width), like((hidden, width), bf16),
        (activated, d_branch), name="wdown",
    )
    wdown = blocks(wdown)
    core = ReduceCore(sizes, wdown, [(0, "s"), (tiles, "w")])
    d_hidden, bup, *moved = run(
        hidden_back_kernel, tiles, [full, by_rows(step, width), cols_h], [cols_h, by_cols(1, step)],
        [tall, like((1, hidden), f32)], (d_branch, full_down, slope), name="dhid",
        moves=[core], sizes=sizes, group=6,
    )
    first = ReduceFirst(sizes, wdown, moved[0], [(0, "l"), (1, "a"), (tiles, "w")])
    wup, *moved_down = run(
        weight_grad_kernel, tiles, [full, cols_h], by_cols(width, step), like((width, hidden), bf16),
        (act_two, d_hidden), name="wup", moves=[first], sizes=sizes, group=7,
    )
    wup = blocks(wup)
    second = ReduceSecond(sizes, moved_down, [(0, "l"), (1, "a"), (deep, "w")])
    core = ReduceCore(sizes, wup, [(0, "s"), (deep, "w")])
    d_middle, d_attn, stat_two, bout, *moved = run(
        mlp_back_kernel, deep,
        [by_cols(count, width), by_cols(width, width), full, full, full, mod_all],
        [full, full, whole((frames, 3, width)), row],
        [wide, acts, like((frames, 3, width), f32), like((1, width), f32)],
        (d_hidden, full_up, middle, cotangent, attn, modulation), [acc], name="dact2",
        moves=[second, core], sizes=sizes, group=8,
    )
    moved_down, core_up = moved[:3], moved[3]
    wout = run(
        weight_grad_kernel, width // step, [by_cols(count, step), full], by_rows(step, width), like((width, width), bf16),
        (attended, d_attn), name="wout",
    )
    wout = blocks(wout)
    d_attended = dot(d_attn, full_out, NT).astype(bf16)
    first = ReduceFirst(sizes, wup, core_up, [(0, "l"), (1, "a"), (6, "w")])
    second = ReduceSecond(sizes, first, [(6, "l"), (6, "a"), (pairs, "w")])
    last = ReduceLast(sizes, moved_down, [(0, "l"), (0, "a"), (pairs, "w")])
    core = ReduceCore(sizes, wout, [(0, "s"), (pairs, "w")])
    d_projected, bqkv, *moved = run(
        lambda *refs: attention_backward(*refs, frames=frames), pairs, [pair] * 6 + [table] * 3,
        [pl.BlockSpec((3, count, LANE), lambda i: (0, 0, i)), pl.BlockSpec((1, 3, LANE), lambda i: (i, 0, 0))],
        [like((3, count, width), bf16), like((pairs, 3, LANE), f32)],
        (query, key, value, d_attended, attended, aug, see, cosine, sine), [pltpu.VMEM((count, LANE), f32)], name="attb",
        moves=[last, core, first, second], sizes=sizes, group=9,
    )
    wdown_grad, core_out = moved[:2]
    moved_up = moved[6:]
    stacked = pl.BlockSpec((1, count, width), lambda i: (i, 0, 0))
    last = ReduceLast(sizes, moved_up, [(0, "l"), (0, "a"), (3, "w")])
    first = ReduceFirst(sizes, wout, core_out, [(0, "l"), (1, "a"), (3, "w")])
    wqkv, wup_grad, *moved_out = run(
        qkv_grad_kernel, 3, [full, stacked], pl.BlockSpec((1, width, width), lambda i: (i, 0, 0)),
        like((3, width, width), bf16), (act_one, d_projected), name="wqkv",
        moves=[last, first], sizes=sizes, group=10,
    )
    wqkv = blocks(wqkv, 1)
    core_q = ReduceCore(sizes, wqkv, [(0, "s"), (1, "w")], 0)
    core_k = ReduceCore(sizes, wqkv, [(0, "s"), (2, "w")], 1)
    core_v = ReduceCore(sizes, wqkv, [(0, "s"), (2, "w")], 2)
    first_q = ReduceFirst(sizes, wqkv, core_q, [(1, "l"), (1, "a"), (3, "w")], 0)
    first_k = ReduceFirst(sizes, wqkv, core_k, [(2, "l"), (2, "a"), (3, "w")], 1)
    second = ReduceSecond(sizes, moved_out, [(0, "l"), (0, "a"), (3, "w")])
    token_grad, stat_one, *moved = run(
        input_back_kernel, 3, [stacked, stacked, full, full, mod_all], [full, whole((frames, 2, width))],
        [acts, like((frames, 2, width), f32)],
        (d_projected, jnp.stack([qkv_a[:, :width], jnp.concatenate([qkv_a[:, width:], qkv_b[:, : split - width]], axis=1), qkv_b[:, split - width :]]), tokens, d_middle, modulation), [acc], name="dact1",
        moves=[core_q, core_k, core_v, second, first_q, first_k], sizes=sizes, group=11,
    )
    core_v = moved[2]
    moved_out, moved_q, moved_k = moved[3:6], moved[6:10], moved[10:14]

    bqkv = jnp.transpose(bqkv, (1, 0, 2)).reshape(1, -1)
    shares = [b.reshape(ndev, -1) for b in (bqkv, bout, bup, bdown)]
    packed = jnp.concatenate(shares, axis=1)
    bias_len = packed.shape[1]
    packed = jnp.pad(packed, ((0, 0), (0, 8 * LANE - bias_len))).reshape(-1, LANE)
    packed = blocks(packed)
    d_modulation = jnp.concatenate(
        [stat_one[:, 0], stat_one[:, 1], stat_two[:, 0], stat_two[:, 1], stat_two[:, 2], d_gate_two], axis=1
    ).astype(bf16)
    d_mod = Gather(sizes, d_modulation.reshape(16, -1), ())
    bias_c = ReduceCore(sizes, packed, ())
    bias_f = ReduceFirst(sizes, packed, bias_c, ())
    bias_s = ReduceSecond(sizes, bias_f, ())
    bias_l = ReduceLast(sizes, bias_s, ())
    first_v = ReduceFirst(sizes, wqkv, core_v, (), 2)
    second_q, second_k = ReduceSecond(sizes, moved_q, ()), ReduceSecond(sizes, moved_k, ())
    second_v = ReduceSecond(sizes, first_v, ())
    last_o = ReduceLast(sizes, moved_out, ())
    last_q, last_k, last_v = [ReduceLast(sizes, s, ()) for s in (second_q, second_k, second_v)]
    lasts = [last_o, last_q, last_k, last_v, bias_l]
    tail = run(
        None, 1, [], [], [], [], name="tail",
        moves=[d_mod] + lasts + [bias_c, bias_f, bias_s, first_v, second_q, second_k, second_v], sizes=sizes, group=12,
        script=[
            (d_mod, "s0"), (bias_c, "s"), (last_o, "l"), (second_q, "l"), (second_k, "l"), (first_v, "l"), (last_o, "a"),
            (second_q, "a"), (second_k, "a"), (first_v, "a"), (d_mod, "n0"), (bias_c, "w"), (bias_f, "l"), (bias_f, "a"),
            (second_q, "w"), (last_q, "l"), (last_q, "a"), (second_k, "w"), (last_k, "l"), (last_k, "a"),
            (first_v, "w"), (second_v, "l"), (second_v, "a"), (d_mod, "n1"), (bias_f, "w"), (bias_s, "l"), (bias_s, "a"),
            (second_v, "w"), (last_v, "l"), (last_v, "a"), (d_mod, "n2"), (bias_s, "w"), (bias_l, "l"), (bias_l, "a"),
            (last_o, "w"), (last_q, "w"), (last_k, "w"), (d_mod, "w3"), (bias_l, "w"), (last_v, "w"),
        ],
    )
    d_mod, wout_grad, grad_q, grad_k, grad_v, bias_sum = tail[:6]
    wqkv_grad = jnp.concatenate([grad_q, grad_k, grad_v], axis=1)
    d_mod = d_mod.reshape(ndev * frames, -1)
    bias_sum = bias_sum.reshape(-1)[:bias_len]
    bias_grads, at = [], 0
    for share in shares:
        bias_grads.append(bias_sum[at : at + share.shape[1]])
        at += share.shape[1]
    hot = (all_levels[:, None] == jnp.arange(noise_table.shape[1], dtype=jnp.int32)[None, :]).astype(bf16)
    embedded = dot(hot, noise_table, NT)
    cond = jax.nn.silu(embedded).astype(bf16)
    wmod_grad = dot(cond, d_mod, TN)
    mine = b_mod.shape[0]
    bmod_grad = jnp.sum(lax.dynamic_slice(d_mod, (0, me * mine), (d_mod.shape[0], mine)).astype(f32), axis=0)
    gate = jax.nn.sigmoid(embedded)
    d_embed = dot(d_mod, w_mod, NT) * gate * (1.0 + embedded * (1.0 - gate))
    table_grad = lax.dot_general(
        d_embed, hot.astype(f32), TN, precision=lax.Precision.HIGHEST, preferred_element_type=f32
    )
    return (
        block_out, token_grad, wmod_grad, bmod_grad, wqkv_grad, bias_grads[0], wout_grad, bias_grads[1],
        wup_grad, bias_grads[2], wdown_grad, bias_grads[3], table_grad,
    )


def solution(mesh):
    rows, vec = P(AXES, None), P(AXES)
    return jax.shard_map(
        per_device,
        mesh=mesh,
        in_specs=(rows, rows, rows, vec, vec) + (rows, vec) * 5 + (rows,),
        out_specs=(rows, rows) + (rows, vec) * 5 + (rows,),
        check_vma=False,
    )
```

```python
import jax
import jax.numpy as jnp
from jax import lax
from jax.experimental import pallas as pl
from jax.experimental.pallas import tpu as pltpu
from jax.sharding import PartitionSpec as P

bf16 = jnp.bfloat16
f32 = jnp.float32
AXES = ("dp", "fsdp")
HD = 64
LANE = 128
EPS = 1e-06
NN = (((1,), (0,)), ((), ()))
NT = (((1,), (1,)), ((), ()))
TN = (((0,), (0,)), ((), ()))


def dot(left, right, dims):
    return lax.dot_general(left, right, dims, preferred_element_type=f32)


def lanes(shape):
    return lax.broadcasted_iota(jnp.int32, shape, 1)


def normalize(values):
    centred = values - jnp.mean(values, axis=1, keepdims=True)
    inverse = lax.rsqrt(jnp.mean(centred * centred, axis=1, keepdims=True) + EPS)
    return centred * inverse, inverse


def normalize_back(grad, normed, inverse):
    return inverse * (
        grad
        - jnp.mean(grad, axis=1, keepdims=True)
        - normed * jnp.mean(grad * normed, axis=1, keepdims=True)
    )


def col_sum(values):
    return jnp.sum(values.astype(f32), axis=0, keepdims=True)


def partner(values):
    return jnp.where(
        lanes(values.shape) % HD < HD // 2,
        pltpu.roll(values, LANE - HD // 2, 1),
        pltpu.roll(values, HD // 2, 1),
    )


def carry_lanes(values):
    sub = lanes(values.shape) % HD
    high = values.astype(bf16).astype(f32)
    rest = values - high
    mid = rest.astype(bf16).astype(f32)
    return jnp.where(
        sub == 8, high, jnp.where(sub == 9, mid, jnp.where(sub == 10, rest - mid, 0.0))
    )


def qkv_kernel(x_ref, mod_ref, w_ref, b_ref, cos_ref, sin_ref, act_ref, q_ref, k_ref, v_ref):
    normed, _ = normalize(x_ref[...].astype(f32))
    act = (normed * (1.0 + mod_ref[0, 1:2, :]) + mod_ref[0, 0:1, :]).astype(bf16)
    act_ref[...] = act
    width = x_ref.shape[1]
    cosine, sine = cos_ref[...], sin_ref[...]
    step = 2 * LANE
    for col in range(0, 3 * width, step):
        raw = dot(act, w_ref[:, col : col + step], NN) + b_ref[:, col : col + step].astype(f32)
        for sub in range(0, step, LANE):
            part = raw[:, sub : sub + LANE]
            at = (col + sub) % width
            if col < width:
                part = (part * cosine + partner(part) * sine).astype(bf16)
                q_ref[:, at : at + LANE] = (part.astype(f32) * 0.125).astype(bf16)
            elif col < 2 * width:
                k_ref[:, at : at + LANE] = (part * cosine + partner(part) * sine).astype(bf16)
            else:
                v_ref[:, at : at + LANE] = part.astype(bf16)


def attention_forward(q_ref, k_ref, v_ref, see_ref, hot_ref, out_ref, aug_ref, *, frames):
    rows_all = q_ref.shape[0]
    size = rows_all // frames
    low = lanes((rows_all, LANE)) < HD
    low_b = lanes((size, LANE)) < HD
    k, v, see = k_ref[...], v_ref[...], see_ref[...]
    one = jnp.ones_like(v)
    keys = (jnp.where(low, k, see), jnp.where(low, see, k))
    vals = (jnp.where(low, v, one), jnp.where(low, one, v))
    for i in range(frames):
        rows = slice(i * size, (i + 1) * size)
        width = (i + 1) * size
        q, hot = q_ref[rows, :], hot_ref[rows, :]
        query = (jnp.where(low_b, q, hot), jnp.where(low_b, hot, q))
        tops, outs = [], []
        for h in range(2):
            scores = dot(query[h], keys[h][:width], NT)
            top = jnp.max(scores, axis=1, keepdims=True)
            expo = jnp.exp(scores - top).astype(bf16)
            outs.append(dot(expo, vals[h][:width], NN))
            tops.append(top)
        num = jnp.where(low_b, outs[0], outs[1])
        den = jnp.where(low_b, outs[1], outs[0])
        out_ref[rows, :] = (num / pltpu.roll(den, HD, 1)).astype(bf16)
        lse = jnp.where(low_b, tops[1], tops[0]) + jnp.log(den)
        aug_ref[rows, :] = (carry_lanes(-lse) + hot.astype(f32)).astype(bf16)


def project_kernel(att_ref, x_ref, mod_ref, w_ref, b_ref, middle_ref, attn_ref, act_ref):
    attn = dot(att_ref[...], w_ref[...], NN) + b_ref[...].astype(f32)
    attn_ref[...] = attn.astype(bf16)
    middle = x_ref[...].astype(f32) + mod_ref[0, 2:3, :] * attn
    middle_ref[...] = middle
    normed, _ = normalize(middle)
    act_ref[...] = (normed * (1.0 + mod_ref[0, 4:5, :]) + mod_ref[0, 3:4, :]).astype(bf16)


def up_kernel(act_ref, w_ref, b_ref, out_ref, slope_ref):
    hidden = dot(act_ref[...], w_ref[...], NN) + b_ref[...].astype(f32)
    share = 0.5 * (1.0 + lax.erf(hidden * 0.7071067811865476))
    out_ref[...] = (hidden * share).astype(bf16)
    slope = share + hidden * jnp.exp(-0.5 * hidden * hidden) * 0.3989422804014327
    slope_ref[...] = slope.astype(bf16)


def down_kernel(
    act_ref, w_ref, b_ref, mid_ref, cot_ref, mod_ref, out_ref, dbr_ref, gate_ref, sum_ref, acc_ref
):
    step, last = pl.program_id(0), pl.num_programs(0) - 1
    part = dot(act_ref[...], w_ref[...], NN)

    @pl.when(step == 0)
    def _():
        acc_ref[...] = part

    @pl.when(step > 0)
    def _():
        acc_ref[...] += part

    @pl.when(step == last)
    def _():
        frames = mod_ref.shape[0]
        size = acc_ref.shape[0] // frames
        total = jnp.zeros((1, acc_ref.shape[1]), f32)
        for i in range(frames):
            rows = slice(i * size, (i + 1) * size)
            gate = mod_ref[i, 5:6, :]
            branch = acc_ref[rows, :] + b_ref[...].astype(f32)
            out_ref[rows, :] = (mid_ref[rows, :] + gate * branch).astype(bf16)
            upstream = cot_ref[rows, :].astype(f32)
            d_branch = (upstream * gate).astype(bf16)
            dbr_ref[rows, :] = d_branch
            gate_ref[i : i + 1, :] = col_sum(upstream * branch)
            total += col_sum(d_branch)
        sum_ref[...] = total


def hidden_back_kernel(dbr_ref, w_ref, slope_ref, out_ref, sum_ref):
    d_hidden = (dot(dbr_ref[...], w_ref[...], NT) * slope_ref[...].astype(f32)).astype(bf16)
    out_ref[...] = d_hidden
    sum_ref[...] = col_sum(d_hidden)


def mlp_back_kernel(
    dh_ref, w_ref, mid_ref, cot_ref, attn_ref, mod_ref, dmid_ref, datt_ref, stat_ref, sum_ref, acc_ref
):
    step, last = pl.program_id(0), pl.num_programs(0) - 1
    part = dot(dh_ref[...], w_ref[...], NT)

    @pl.when(step == 0)
    def _():
        acc_ref[...] = part

    @pl.when(step > 0)
    def _():
        acc_ref[...] += part

    @pl.when(step == last)
    def _():
        frames = mod_ref.shape[0]
        size = acc_ref.shape[0] // frames
        total = jnp.zeros((1, acc_ref.shape[1]), f32)
        for i in range(frames):
            rows = slice(i * size, (i + 1) * size)
            d_act = acc_ref[rows, :]
            normed, inverse = normalize(mid_ref[rows, :])
            stat_ref[i, 1:2, :] = col_sum(d_act)
            stat_ref[i, 2:3, :] = col_sum(d_act * normed)
            d_middle = cot_ref[rows, :].astype(f32) + normalize_back(
                d_act * (1.0 + mod_ref[i, 4:5, :]), normed, inverse
            )
            dmid_ref[rows, :] = d_middle
            stat_ref[i, 0:1, :] = col_sum(d_middle * attn_ref[rows, :].astype(f32))
            d_attn = (d_middle * mod_ref[i, 2:3, :]).astype(bf16)
            datt_ref[rows, :] = d_attn
            total += col_sum(d_attn)
        sum_ref[...] = total


def attention_backward(
    q_ref, k_ref, v_ref, do_ref, o_ref, aug_ref, see_ref, cos_ref, sin_ref, out_ref, sum_ref, acc_ref, *, frames
):
    rows_all = q_ref.shape[0]
    size = rows_all // frames
    low = lanes((rows_all, LANE)) < HD
    q, aug, grad = q_ref[...], aug_ref[...], do_ref[...]
    prod = grad.astype(f32) * o_ref[...].astype(f32)
    delta_low = jnp.sum(jnp.where(low, prod, 0.0), axis=1, keepdims=True)
    delta_high = jnp.sum(jnp.where(low, 0.0, prod), axis=1, keepdims=True)
    grad_aug = carry_lanes(jnp.where(low, -delta_high, -delta_low)).astype(bf16)
    query = (jnp.where(low, q, aug), jnp.where(low, aug, q))
    upper = (jnp.where(low, grad, grad_aug), jnp.where(low, grad_aug, grad))
    low_b = lanes((size, LANE)) < HD
    sub = lanes((size, LANE)) % HD
    ones = jnp.where((sub >= 8) & (sub <= 10), 1.0, 0.0).astype(bf16)
    sum_k = sum_v = jnp.zeros((1, LANE), f32)
    for j in range(frames):
        rows = slice(j * size, (j + 1) * size)
        start = j * size
        k, v, see = k_ref[rows, :], v_ref[rows, :], see_ref[rows, :] + ones
        keys = (jnp.where(low_b, k, see), jnp.where(low_b, see, k))
        vals = (jnp.where(low_b, v, ones), jnp.where(low_b, ones, v))
        dvs, dks, dqs = [], [], []
        for h in range(2):
            probs = jnp.exp(dot(keys[h], query[h][start:], NT))
            d_scores = (probs * dot(vals[h], upper[h][start:], NT)).astype(bf16)
            dvs.append(dot(probs.astype(bf16), grad[start:], NN))
            dks.append(dot(d_scores, q[start:], NN))
            dqs.append(dot(d_scores, k, TN))
        d_value = jnp.where(low_b, dvs[0], dvs[1]).astype(bf16)
        d_key = jnp.where(low_b, dks[0], dks[1])
        d_key = (d_key * cos_ref[rows, :] - partner(d_key) * sin_ref[rows, :]).astype(bf16)
        out_ref[1, rows, :] = d_key
        out_ref[2, rows, :] = d_value
        sum_k = sum_k + col_sum(d_key)
        sum_v = sum_v + col_sum(d_value)
        d_query = jnp.where(lanes(dqs[0].shape) < HD, dqs[0], dqs[1])
        if j == 0:
            acc_ref[...] = d_query
        else:
            acc_ref[start:, :] += d_query
    d_query = acc_ref[...] * 0.125
    d_query = (d_query * cos_ref[...] - partner(d_query) * sin_ref[...]).astype(bf16)
    out_ref[0] = d_query
    sum_ref[0, 0:1, :] = col_sum(d_query)
    sum_ref[0, 1:2, :] = sum_k
    sum_ref[0, 2:3, :] = sum_v


def input_back_kernel(dp_ref, w_ref, x_ref, dmid_ref, mod_ref, out_ref, stat_ref, acc_ref):
    step, last = pl.program_id(0), pl.num_programs(0) - 1
    part = dot(dp_ref[0], w_ref[...], NT)

    @pl.when(step == 0)
    def _():
        acc_ref[...] = part

    @pl.when(step > 0)
    def _():
        acc_ref[...] += part

    @pl.when(step == last)
    def _():
        frames = mod_ref.shape[0]
        size = acc_ref.shape[0] // frames
        for i in range(frames):
            rows = slice(i * size, (i + 1) * size)
            d_act = acc_ref[rows, :]
            normed, inverse = normalize(x_ref[rows, :].astype(f32))
            stat_ref[i, 0:1, :] = col_sum(d_act)
            stat_ref[i, 1:2, :] = col_sum(d_act * normed)
            back = normalize_back(d_act * (1.0 + mod_ref[i, 1:2, :]), normed, inverse)
            out_ref[rows, :] = (dmid_ref[rows, :] + back).astype(bf16)


def modulation_kernel(small_ref, table_ref, w_ref, part_ref, levels_ref, frames):
    ndev = part_ref.shape[0] * part_ref.shape[1] * part_ref.shape[2] * 2
    rows = levels_ref[...].reshape(ndev, levels_ref.shape[-2], LANE)
    spots = jnp.sum(rows[:, :8], axis=0).astype(jnp.int32)
    count = 2 * frames * ndev
    level = jnp.concatenate([spots[i : i + 1, :] for i in range(count // LANE)], axis=1)
    slot = lax.broadcasted_iota(jnp.int32, (table_ref.shape[1], count), 0)
    hot = jnp.where(slot == level, 1.0, 0.0).astype(bf16)
    embedded = dot(table_ref[...], hot, NN)
    cond = (embedded / (1.0 + jnp.exp(-embedded))).astype(bf16)
    half = part_ref.shape[-1]
    first = lax.broadcasted_iota(jnp.int32, (count, 1), 0) % (2 * frames) < frames
    step = 512
    for col in range(0, half, step):
        low = dot(cond, w_ref[:, col : col + step], TN)
        high = dot(cond, w_ref[:, half + col : half + col + step], TN)
        value = jnp.where(first, low, high)
        part_ref[..., col : col + step] = value.reshape(part_ref.shape[:-1] + (step,))


def weight_grad_kernel(left_ref, right_ref, out_ref):
    out_ref[...] = dot(left_ref[...], right_ref[...], TN).astype(bf16)


def attended_back_kernel(da_ref, w_ref, att_ref, datt_ref, out_ref):
    datt_ref[...] = dot(da_ref[...], w_ref[...], NT).astype(bf16)
    out_ref[...] = dot(att_ref[...], da_ref[...], TN).astype(bf16)


def qkv_grad_kernel(left_ref, right_ref, out_ref):
    out_ref[0] = dot(left_ref[...], right_ref[0], TN).astype(bf16)


def like(shape, kind):
    return jax.ShapeDtypeStruct(shape, kind)


def whole(shape):
    return pl.BlockSpec(shape, lambda i: (0,) * len(shape))


def by_rows(size, width):
    return pl.BlockSpec((size, width), lambda i: (i, 0))


def by_cols(height, size):
    return pl.BlockSpec((height, size), lambda i: (0, i))


MESH = pl.DeviceIdType.MESH
ANY = pl.BlockSpec(memory_space=pl.ANY)
VMEM = pl.BlockSpec(memory_space=pltpu.VMEM)
DMA = pltpu.SemaphoreType.DMA


class Place:
    def __init__(self, sizes):
        self.ny, self.nx, self.nz = sizes
        self.half = self.nz // 2
        self.rest = self.nz - self.half
        self.low, self.high = pl.ds(0, self.half), pl.ds(self.half, self.rest)
        self.dp, self.fsdp = lax.axis_index("dp"), lax.axis_index("fsdp")
        self.y, self.x = lax.div(self.dp, self.nx), lax.rem(self.dp, self.nx)
        self.z, self.c = lax.div(self.fsdp, 2), lax.rem(self.fsdp, 2)

        self.shifts, self.devices = {}, {}
        for axis, size in dict(y=self.ny, x=self.nx, z=self.nz, c=2).items():
            for k in range(1, size):
                at = lax.rem(getattr(self, axis) + k, size)
                self.shifts[axis, k] = self.shifts[axis, k - size] = at
                self.devices[axis, k] = dict(
                    y=(at * self.nx + self.x, self.fsdp), x=(self.y * self.nx + at, self.fsdp),
                    z=(self.dp, at * 2 + self.c), c=(self.dp, self.z * 2 + at),
                )[axis]
        self.other = self.shifts["c", 1]

    def shift(self, axis, k):
        return self.shifts[axis, k]

    def device(self, axis, k):
        return self.devices[axis, k]

    def enter(self, axes):
        barrier = pltpu.get_barrier_semaphore()
        sizes = dict(y=self.ny, x=self.nx, z=self.nz, c=2)
        count = 0
        for axis in axes:
            for k in range(1, sizes[axis]):
                count += 1
                pl.semaphore_signal(barrier, inc=1, device_id=self.device(axis, k), device_id_type=MESH)
        pl.semaphore_wait(barrier, count)


class Move:
    ins, in_specs, outs, out_specs, scratch, aliases = (), (), (), (), (), ()

    def bind(self, place, ins, outs, scratch):
        self.place, self.in_refs, self.out_refs, self.refs = place, ins, outs, scratch
        self.slots, self.local_slots, self.legs = {}, {}, []

    def copy(self, key, src, dst, axis, k):
        slot = self.slots.setdefault(key, len(self.slots))
        return pltpu.make_async_remote_copy(
            src_ref=src, dst_ref=dst, send_sem=self.refs[0].at[slot], recv_sem=self.refs[1].at[slot],
            device_id=self.place.device(axis, k), device_id_type=MESH,
        )

    def start(self, items):
        for item in items:
            self.copy(*item).start()

    def arrived(self, key, dst, axis, k):
        self.copy(key, dst, dst, axis, k).wait_recv()

    def drain(self, items):
        for item in items:
            self.copy(*item).wait_send()

    def local(self, key, src, dst):
        slot = self.local_slots.setdefault(key, len(self.local_slots))
        return pltpu.make_async_copy(src, dst, self.refs[2].at[slot])


class Held:
    def __init__(self, shape, kind):
        self.shape, self.dtype, self.ref = shape, kind, None


def part_of(ref, part, core):
    if part is None:
        return ref.at[:, :, :, core]
    if isinstance(part, int):
        return ref.at[part, :, :, :, core]
    return ref.at[:, :, :, core, :, part[0] : part[1]]


def block_of(array, part):
    rows, columns = array.shape[-2:]
    return (rows, part[1] - part[0]) if isinstance(part, tuple) else (rows, columns)


def legs_copies(sizes):
    ny, nx, nz = sizes
    return (nz - 1) + 4 * (nx - 1) + 4 * (ny - 1) + 1


class Gather(Move):
    def __init__(self, sizes, array, actions, begun=False):
        ny, nx, nz = sizes
        self.begun, self.actions = begun, actions
        self.ins, self.in_specs = [array], [ANY if begun else VMEM]
        shape = array.shape if begun else (ny, nx, nz, 2) + array.shape
        self.outs, self.out_specs = [like(shape, array.dtype)], [ANY]
        parts = len({what[2:] for _, what in actions}) if actions else 3
        self.scratch = [DMA((legs_copies(sizes) * parts,)), DMA((legs_copies(sizes) * parts,)), DMA((parts,))]
        self.aliases = [(0, 0)] if begun else []

    def act(self, what):
        op, leg, part = what[0], int(what[1]), what[2:]
        if op != "s":
            self.wait_leg(leg, part)
        if op != "w":
            self.start_leg(leg + (op == "n"), part)
        else:
            for each in self.legs:
                if each[1] == part:
                    self.drain(self.leaving(*each))

    def columns(self, part):
        width = self.out_refs[0].shape[-1]
        half = width // 2
        return {"": slice(None), "a": slice(0, half), "b": slice(half, width)}[part]

    def spot(self, index, part):
        return self.out_refs[0].at[index + (slice(None), self.columns(part))]

    def items(self, leg):
        p, full = self.place, self.out_refs[0]
        y, x, z, c = p.y, p.x, p.z, p.c
        d = p.other
        xs, ys, zs = range(1, p.nx), range(1, p.ny), range(1, p.nz)
        back = p.shift
        if leg == 0:
            return [(("z", k), (y, x, z, c), (y, x, back("z", -k), c), "z", k) for k in zs]
        if leg == 1:
            return (
                [(("x", k), (y, x, p.low, c), (y, back("x", -k), p.low, c), "x", k) for k in xs]
                + [(("y", k), (y, x, p.high, c), (back("y", -k), x, p.high, c), "y", k) for k in ys]
                + [("c", (y, x, slice(None), c), (y, x, slice(None), d), "c", 1)]
            )
        every = slice(None)
        if leg == 2:
            return (
                [(("xy", k), (y, every, p.low, c), (back("y", -k), every, p.low, c), "y", k) for k in ys]
                + [(("yx", k), (every, x, p.high, c), (every, back("x", -k), p.high, c), "x", k) for k in xs]
                + [(("cx", k), (y, back("x", -k), p.low, c), (y, back("x", -k), p.low, d), "c", 1) for k in xs]
                + [(("cy", k), (back("y", -k), x, p.high, c), (back("y", -k), x, p.high, d), "c", 1) for k in ys]
            )
        return [
            (("cxy", k), (back("y", -k), every, p.low, c), (back("y", -k), every, p.low, d), "c", 1) for k in ys
        ] + [(("cyx", k), (every, back("x", -k), p.high, c), (every, back("x", -k), p.high, d), "c", 1) for k in xs]

    def own(self, part):
        p = self.place
        mine = self.in_refs[0].at[:, self.columns(part)]
        return self.local(part, mine, self.spot((p.y, p.x, p.z, p.c), part))

    def leaving(self, leg, part):
        for key, leaves, _, axis, k in self.items(leg):
            to = self.spot(leaves, part)
            yield (key, part), self.in_refs[0].at[:, self.columns(part)] if leg == 0 else to, to, axis, k

    def start_leg(self, leg, part):
        self.legs.append((leg, part))
        if leg == 0:
            self.own(part).start()
        self.start(self.leaving(leg, part))

    def wait_leg(self, leg, part):
        if leg == 0:
            self.own(part).wait()
        for key, _, arrives, axis, k in self.items(leg):
            self.arrived((key, part), self.spot(arrives, part), axis, k)


def add_blocks(into, where, counts, terms):
    total = 1
    for n in counts:
        total *= n

    def body(flat, carry):
        at = []
        for n in reversed(counts):
            at.append(lax.rem(flat, n))
            flat = lax.div(flat, n)
        at = tuple(at[::-1])
        spot = where(*at)
        value = into[spot].astype(f32)
        for ref, index in terms(*at):
            value = value + ref[index].astype(f32)
        into[spot] = value.astype(into.dtype)
        return carry

    lax.fori_loop(0, total, body, 0)


class ReduceCore(Move):
    def __init__(self, sizes, array, actions, part=None):
        self.actions, self.part = actions, part
        ny, nx, nz = sizes
        self.held = array if isinstance(array, Held) else None
        self.ins, self.in_specs = ([], []) if self.held else ([array], [ANY])
        self.outs, self.out_specs = [like((ny, nx, nz) + block_of(array, part), array.dtype)], [ANY]
        self.scratch = [DMA((1,)), DMA((1,))]

    def act(self, what):
        p = self.place
        source = self.held.ref if self.held else self.in_refs[0]
        leaving = [("c", part_of(source, self.part, p.other), self.out_refs[0], "c", 1)]
        if what == "s":
            self.start(leaving)
        else:
            self.arrived("c", self.out_refs[0], "c", 1)
            self.drain(leaving)


class ReduceFirst(Move):
    def __init__(self, sizes, array, core, actions, part=None):
        self.actions, self.part, self.core = actions, part, core
        ny, nx, nz = sizes
        half, rest = nz // 2, nz - nz // 2
        block, kind = block_of(array, part), array.dtype
        self.held = array if isinstance(array, Held) else None
        self.ins = ([] if self.held else [array]) + ([] if isinstance(core, Move) else [core])
        self.in_specs = [ANY] * len(self.ins)
        self.outs = [
            like((ny - 1, nx, half) + block, kind), like((nx - 1, ny, rest) + block, kind),
            like((nx, half) + block, kind), like((ny, rest) + block, kind),
        ]
        self.out_specs = [ANY] * 4
        remote = DMA((nx + ny - 2,))
        self.scratch = [remote, remote, DMA((4,))] + [pltpu.VMEM((ny, nx, nz) + block, kind)] * 2

    def act(self, what):
        p = self.place
        source = self.held.ref if self.held else self.in_refs[0]
        core = self.core.out_refs[0] if isinstance(self.core, Move) else self.in_refs[-1]
        acc, buf = self.refs[3:]
        la, lb, ka, kb = self.out_refs
        loads = [("acc", part_of(source, self.part, p.c), acc), ("buf", core, buf)]
        leaving = [
            (("y", k), acc.at[p.shift("y", k), :, p.low], la.at[k - 1], "y", k) for k in range(1, p.ny)
        ] + [(("x", k), acc.at[:, p.shift("x", k), p.high], lb.at[k - 1], "x", k) for k in range(1, p.nx)]
        keeps = [("ka", acc.at[p.y, :, p.low], ka), ("kb", acc.at[:, p.x, p.high], kb)]
        if what == "l":
            for item in loads:
                self.local(*item).start()
        elif what == "a":
            for item in loads:
                self.local(*item).wait()
            add_blocks(acc, lambda *at: at, (p.ny, p.nx, p.nz), lambda *at: [(buf, at)])
            self.start(leaving)
            for item in keeps:
                self.local(*item).start()
        else:
            for k in range(1, p.ny):
                self.arrived(("y", k), la.at[k - 1], "y", k)
            for k in range(1, p.nx):
                self.arrived(("x", k), lb.at[k - 1], "x", k)
            for item in keeps:
                self.local(*item).wait()
            self.drain(leaving)


class ReduceSecond(Move):
    def __init__(self, sizes, first, actions):
        self.actions, self.first = actions, first
        ny, nx, nz = sizes
        half, rest = nz // 2, nz - nz // 2
        self.inside = isinstance(first, Move)
        arrays = first.outs if self.inside else first
        block, kind = arrays[0].shape[-2:], arrays[0].dtype
        self.ins, self.in_specs = ([], []) if self.inside else (list(arrays), [ANY] * 4)
        self.outs = [
            like((nx - 1, half) + block, kind), like((ny - 1, rest) + block, kind), like((nz,) + block, kind)
        ]
        self.out_specs = [ANY] * 3
        remote = DMA((nx + ny - 2,))
        self.scratch = [remote, remote, DMA((6,))] + [pltpu.VMEM(a.shape, kind) for a in arrays]

    def act(self, what):
        p = self.place
        arrays = self.first.out_refs if self.inside else self.in_refs
        bufs = self.refs[3:]
        la, lb, ka, kb = bufs
        ma, mb, kept = self.out_refs
        loads = [(i, a, b) for i, (a, b) in enumerate(zip(arrays, bufs))]
        leaving = [(("x", k), ka.at[p.shift("x", k)], ma.at[k - 1], "x", k) for k in range(1, p.nx)]
        leaving += [(("y", k), kb.at[p.shift("y", k)], mb.at[k - 1], "y", k) for k in range(1, p.ny)]
        keeps = [("ka", ka.at[p.x], kept.at[p.low]), ("kb", kb.at[p.y], kept.at[p.high])]
        if what == "l":
            for item in loads:
                self.local(*item).start()
        elif what == "a":
            for item in loads:
                self.local(*item).wait()
            add_blocks(ka, lambda *at: at, (p.nx, p.half), lambda i, j: [(la, (k, i, j)) for k in range(p.ny - 1)])
            add_blocks(kb, lambda *at: at, (p.ny, p.rest), lambda i, j: [(lb, (k, i, j)) for k in range(p.nx - 1)])
            self.start(leaving)
            for item in keeps:
                self.local(*item).start()
        else:
            for k in range(1, p.nx):
                self.arrived(("x", k), ma.at[k - 1], "x", k)
            for k in range(1, p.ny):
                self.arrived(("y", k), mb.at[k - 1], "y", k)
            for item in keeps:
                self.local(*item).wait()
            self.drain(leaving)


class ReduceLast(Move):
    def __init__(self, sizes, second, actions):
        self.actions, self.second = actions, second
        ny, nx, nz = sizes
        self.inside = isinstance(second, Move)
        arrays = second.outs if self.inside else second
        block, kind = arrays[0].shape[-2:], arrays[0].dtype
        self.ins, self.in_specs = ([], []) if self.inside else (list(arrays), [ANY] * 3)
        self.outs, self.out_specs = [like(block, f32)], [VMEM]
        self.scratch = [DMA((nz - 1,)), DMA((nz - 1,)), DMA((3,))] + [pltpu.VMEM(a.shape, kind) for a in arrays]
        self.scratch += [pltpu.VMEM((nz - 1,) + block, kind)]

    def act(self, what):
        p = self.place
        arrays = self.second.out_refs if self.inside else self.in_refs
        ma, mb, kept, last = self.refs[3:]
        loads = [(i, a, b) for i, (a, b) in enumerate(zip(arrays, (ma, mb, kept)))]
        leaving = [(("z", k), kept.at[p.shift("z", k)], last.at[k - 1], "z", k) for k in range(1, p.nz)]
        if what == "l":
            for item in loads:
                self.local(*item).start()
        elif what == "a":
            for item in loads:
                self.local(*item).wait()
            add_blocks(kept, lambda j: (j,), (p.half,), lambda j: [(ma, (k, j)) for k in range(p.nx - 1)])
            add_blocks(
                kept, lambda j: (p.half + j,), (p.rest,), lambda j: [(mb, (k, j)) for k in range(p.ny - 1)]
            )
            self.start(leaving)
        else:
            for k in range(1, p.nz):
                self.arrived(("z", k), last.at[k - 1], "z", k)
            value = kept[p.z].astype(f32)
            for k in range(p.nz - 1):
                value = value + last[k].astype(f32)
            self.out_refs[0][...] = value
            self.drain(leaving)


def run(
    kernel, grid, ins, outs, shapes, args, scratch=(), name=None, moves=(), sizes=None, group=None, axes="yxzc", script=None
):
    single = not isinstance(shapes, (list, tuple))
    outs, shapes = ([outs], [shapes]) if single else (list(outs), list(shapes))
    counts = len(ins), len(outs), len(scratch)
    all_ins, all_specs, all_outs = list(args), list(ins), list(shapes)
    all_out_specs, all_scratch, aliases = list(outs), list(scratch), {}
    for move in moves:
        for i, o in move.aliases:
            aliases[len(all_ins) + i] = len(all_outs) + o
        all_ins += list(move.ins)
        all_specs += list(move.in_specs)
        all_outs += list(move.outs)
        all_out_specs += list(move.out_specs)
        all_scratch += list(move.scratch)

    def body(*refs):
        refs = list(refs)

        def take(n):
            part = refs[:n]
            del refs[:n]
            return part

        mine_in = take(counts[0])
        moved_in = [take(len(m.ins)) for m in moves]
        mine_out = take(counts[1])
        moved_out = [take(len(m.outs)) for m in moves]
        mine_scratch = take(counts[2])
        place = Place(sizes) if moves else None
        for move, i, o in zip(moves, moved_in, moved_out):
            move.bind(place, i, o, take(len(move.scratch)))
        step = pl.program_id(0)

        def turn(at):
            for move in moves:
                for when, what in move.actions:
                    if when == at:
                        move.act(what)

        if script is not None:
            place.enter(axes)
            for item in script:
                if isinstance(item, tuple):
                    item[0].act(item[1])
                else:
                    item(mine_in, mine_out, mine_scratch)
            return

        for at in range(grid):
            if any(when == at for m in moves for when, _ in m.actions):

                @pl.when(step == at)
                def _(at=at):
                    if at == 0:
                        place.enter(axes)
                    turn(at)

        kernel(*mine_in, *mine_out, *mine_scratch)
        if moves:

            @pl.when(step == grid - 1)
            def _():
                turn(grid)

    params = dict(vmem_limit_bytes=60 * 1024 * 1024)
    if moves:
        params.update(collective_id=group, has_side_effects=True)
    moved = sum(a.size * a.dtype.itemsize for a in args)
    results = pl.pallas_call(
        body,
        grid=(grid,),
        in_specs=all_specs,
        out_specs=all_out_specs,
        out_shape=all_outs,
        scratch_shapes=all_scratch,
        input_output_aliases=aliases,
        name=name,
        cost_estimate=pl.CostEstimate(flops=0, bytes_accessed=2 * moved, transcendentals=0),
        compiler_params=pltpu.CompilerParams(**params),
    )(*all_ins)
    return results[0] if single and not moves else results


def tables(clip_row, pad, count):
    frames = clip_row.shape[0]
    size = count // frames
    slots = jnp.arange(frames, dtype=jnp.int32)
    ends = jnp.sum(jnp.where(slots[None, :] <= slots[:, None], clip_row[None, :], 0), axis=1)
    clip_of = jnp.sum((slots[:, None] >= ends[None, :]).astype(jnp.int32), axis=1)
    starts = ends - clip_row
    start_of = jnp.sum(jnp.where(clip_of[:, None] == slots[None, :], starts[None, :], 0), axis=1)
    frame_pos = slots - start_of
    frame = jnp.arange(count, dtype=jnp.int32) // size
    lane = jnp.arange(LANE, dtype=jnp.int32) % HD
    frame_hot = frame[:, None] == lane[None, :]
    own = frame[:, None] == slots[None, :]
    clip_tok = jnp.sum(jnp.where(own, clip_of[None, :], 0), axis=1)
    pos_tok = jnp.sum(jnp.where(own, frame_pos[None, :], 0), axis=1)
    lane_own = lane[:, None] == slots[None, :]
    lane_clip = jnp.sum(jnp.where(lane_own, clip_of[None, :], 0), axis=1)
    lane_pos = jnp.sum(jnp.where(lane_own, frame_pos[None, :], 0), axis=1)
    seen = (
        (clip_tok[:, None] == lane_clip[None, :])
        & (pos_tok[:, None] <= lane_pos[None, :])
        & (pad[:, None] == 1)
    )
    see = jnp.where((lane[None, :] < frames) & ~seen, -1e30, 0.0).astype(bf16)
    quarter = HD // 4
    freq = 10000.0 ** (-jnp.arange(quarter, dtype=f32) / quarter)
    patch = jnp.arange(count, dtype=jnp.int32) % size
    angle = jnp.concatenate(
        [pos_tok.astype(f32)[:, None] * freq[None, :], patch.astype(f32)[:, None] * freq[None, :]],
        axis=1,
    )
    cosine, sine = jnp.cos(angle), jnp.sin(angle)
    cosine = jnp.concatenate([cosine] * 4, axis=1)
    sine = jnp.concatenate([-sine, sine, -sine, sine], axis=1)
    return see, frame_hot.astype(bf16), cosine, sine


def per_device(
    tokens, cotangent, clip_frames, levels, pad_mask, w_mod, b_mod, w_qkv, b_qkv, w_out, b_out,
    w_up, b_up, w_down, b_down, noise_table,
):
    count, width = tokens.shape
    frames = levels.shape[0]
    size = count // frames
    hidden = w_up.shape[1]
    ndev = width // w_up.shape[0]
    me = lax.axis_index("dp") * lax.axis_size("fsdp") + lax.axis_index("fsdp")

    dp, fsdp = lax.axis_size("dp"), lax.axis_size("fsdp")
    sizes = (dp // 2, 2, fsdp // 2)
    lead = sizes + (2,)

    def flat(array):
        return array.reshape(-1, array.shape[-1])

    def blocks(array, front=0):
        rows = array.shape[front] // ndev
        return array.reshape(array.shape[:front] + lead + (rows, array.shape[-1]))

    biases = [b_mod, b_qkv, b_out, b_up, b_down]
    lengths = [b.shape[0] for b in biases]
    spots = jnp.arange(8 * LANE, dtype=jnp.int32)
    mine_at = jnp.where(spots // (2 * frames) == me, jnp.tile(levels, spots.shape[0] // frames), 0)
    packed = jnp.concatenate([mine_at.astype(f32)] + [b.astype(f32) for b in biases])
    packed = jnp.pad(packed, (0, 16 * LANE - packed.shape[0])).reshape(16, LANE)
    table_pad = jnp.pad(noise_table, ((0, 0), (0, -noise_table.shape[1] % LANE)))
    part = Held(lead + (2 * frames, w_mod.shape[1] // 2), f32)
    small = Gather(sizes, packed, ())
    qkv_w = Gather(sizes, w_qkv, ())
    out_w, up_w = Gather(sizes, w_out, ()), Gather(sizes, w_up, ())
    mod_c = ReduceCore(sizes, part, ())
    mod_f = ReduceFirst(sizes, part, mod_c, ())
    mod_s = ReduceSecond(sizes, mod_f, ())
    mod_l = ReduceLast(sizes, mod_s, ())

    def add_modulation(ins, _, scratch):
        part.ref = scratch[0]
        load = pltpu.make_async_copy(small.out_refs[0], scratch[1], scratch[2].at[0])
        load.start()
        load.wait()
        modulation_kernel(None, ins[0], ins[1], scratch[0], scratch[1], frames)

    head = run(
        None, 1, [VMEM] * 2, [], [], [table_pad, w_mod],
        [pltpu.VMEM(part.shape, f32), pltpu.VMEM(lead + packed.shape, f32), DMA((1,))], name="head",
        moves=[small, qkv_w, out_w, up_w, mod_c, mod_f, mod_s, mod_l], sizes=sizes, group=1,
        script=[
            (small, "s0"), (qkv_w, "s0a"), (qkv_w, "s0b"), (small, "n0"), (small, "n1"), (small, "n2"), (small, "w3"),
            (qkv_w, "n0a"), (out_w, "s0"), (up_w, "s0"), add_modulation, (mod_c, "s"), (qkv_w, "n1a"), (qkv_w, "n0b"),
            (mod_c, "w"), (mod_f, "l"), (mod_f, "a"), (qkv_w, "n1b"), (mod_f, "w"), (mod_s, "l"), (mod_s, "a"),
            (qkv_w, "n2a"), (mod_s, "w"), (mod_l, "l"), (mod_l, "a"), (qkv_w, "n2b"), (qkv_w, "w3a"), (qkv_w, "w3b"),
            (mod_l, "w"), (out_w, "w0"), (up_w, "w0"),
        ],
    )
    small, qkv_w, out_w, up_w = head[:4]
    small = small.reshape(ndev, -1)
    all_levels = jnp.sum(small[:, : 8 * LANE], axis=0).reshape(-1, 2 * frames)[:ndev, :frames]
    all_levels = all_levels.reshape(-1).astype(jnp.int32)
    full_bias, at = [], 8 * LANE
    for length in lengths:
        full_bias.append(small[:, at : at + length].reshape(1, -1))
        at += length
    bias_mod, bias_qkv, bias_out, bias_up, bias_down = full_bias
    modulation = jnp.transpose(head[-1].reshape(2, frames, -1), (1, 0, 2)).reshape(frames, -1)
    modulation = (modulation + bias_mod).reshape(frames, 6, width)
    full_qkv = flat(qkv_w)
    see, frame_hot, cosine, sine = tables(clip_frames[0], pad_mask, count)

    acts = like((count, width), bf16)
    wide = like((count, width), f32)
    tall = like((count, hidden), bf16)
    row = whole((1, width))
    mod_row = pl.BlockSpec((1, 6, width), lambda i: (i, 0, 0))
    mod_all = whole((frames, 6, width))
    rows_bf = by_rows(size, width)
    act_one, query, key, value, out_w, up_w = run(
        qkv_kernel, frames,
        [rows_bf, mod_row, whole((width, 3 * width)), whole((1, 3 * width)), by_rows(size, LANE), by_rows(size, LANE)],
        [rows_bf] * 4, [acts] * 4, (tokens, modulation, full_qkv, bias_qkv, cosine, sine), name="qkv",
        moves=[
            Gather(sizes, out_w, [(0, "s1"), (1, "n1"), (3, "n2"), (frames, "w3")], True),
            Gather(sizes, up_w, [(0, "s1a"), (frames, "w1a")], True),
        ], sizes=sizes, group=2,
    )
    full_out = flat(out_w)
    pair = by_cols(count, LANE)
    table = whole((count, LANE))
    pairs = width // LANE
    attended, aug, up_w, down_w = run(
        lambda *refs: attention_forward(*refs, frames=frames), pairs,
        [pair, pair, pair, table, table], [pair] * 2, [acts] * 2, (query, key, value, see, frame_hot), name="attf",
        moves=[
            Gather(sizes, up_w, [(0, "s2a"), (0, "s1b"), (4, "n2a"), (4, "n1b"), (pairs, "w2b"), (pairs, "w3a")], True),
            Gather(sizes, w_down, [(0, "s0"), (pairs, "w0")]),
        ], sizes=sizes, group=3,
    )
    middle, attn, act_two, up_w, down_w = run(
        project_kernel, frames, [rows_bf, rows_bf, mod_row, whole((width, width)), row], [rows_bf] * 3,
        [wide, acts, acts], (attended, tokens, modulation, full_out, bias_out), name="proj",
        moves=[
            Gather(sizes, up_w, [(0, "s3b"), (frames, "w3b")], True),
            Gather(sizes, down_w, [(0, "s1a"), (frames, "w1a")], True),
        ], sizes=sizes, group=4,
    )
    full_up = flat(up_w)
    full = whole((count, width))
    step = 512
    tiles = hidden // step
    cols_h = by_cols(count, step)
    activated, slope, down_w = run(
        up_kernel, tiles, [full, by_cols(width, step), by_cols(1, step)], [cols_h] * 2, [tall] * 2,
        (act_two, full_up, bias_up), name="up",
        moves=[Gather(sizes, down_w, [(0, "s2a"), (0, "s1b"), (tiles // 2, "n1b"), (tiles - 1, "n2a"), (tiles, "n2b"), (tiles, "w3a"), (tiles, "w3b")], True)], sizes=sizes, group=5,
    )
    full_down = flat(down_w)
    acc = pltpu.VMEM((count, width), f32)
    deep = hidden // width
    block_out, d_branch, d_gate_two, bdown = run(
        down_kernel, deep, [by_cols(count, width), by_rows(width, width), row, full, full, mod_all],
        [full, full, whole((frames, width)), row],
        [acts, acts, like((frames, width), f32), like((1, width), f32)],
        (activated, full_down, bias_down, middle, cotangent, modulation), [acc], name="down",
    )
    wdown = run(
        weight_grad_kernel, tiles, [cols_h, full], by_rows(step, width), like((hidden, width), bf16),
        (activated, d_branch), name="wdown",
    )
    wdown = blocks(wdown)
    low, high = (0, width // 2), (width // 2, width)
    core_a = ReduceCore(sizes, wdown, [(0, "s"), (2, "w")], low)
    core_b = ReduceCore(sizes, wdown, [(0, "s"), (4, "w")], high)
    first_a = ReduceFirst(sizes, wdown, core_a, [(2, "l"), (3, "a"), (tiles, "w")], low)
    d_hidden, bup, *moved = run(
        hidden_back_kernel, tiles, [full, by_rows(step, width), cols_h], [cols_h, by_cols(1, step)],
        [tall, like((1, hidden), f32)], (d_branch, full_down, slope), name="dhid",
        moves=[core_a, core_b, first_a], sizes=sizes, group=6,
    )
    core_b, down_a = moved[1], moved[2:]
    first_b = ReduceFirst(sizes, wdown, core_b, [(0, "l"), (1, "a"), (tiles, "w")], high)
    wup, *down_b = run(
        weight_grad_kernel, tiles, [full, cols_h], by_cols(width, step), like((width, hidden), bf16),
        (act_two, d_hidden), name="wup", moves=[first_b], sizes=sizes, group=7,
    )
    wup = blocks(wup)
    low_u, high_u = (0, hidden // 2), (hidden // 2, hidden)
    second_a = ReduceSecond(sizes, down_a, [(0, "l"), (0, "a"), (2, "w")])
    second_b = ReduceSecond(sizes, down_b, [(0, "l"), (1, "a"), (deep, "w")])
    last_a = ReduceLast(sizes, second_a, [(2, "l"), (2, "a"), (deep, "w")])
    core_a = ReduceCore(sizes, wup, [(0, "s"), (deep, "w")], low_u)
    core_b = ReduceCore(sizes, wup, [(0, "s"), (deep, "w")], high_u)
    d_middle, d_attn, stat_two, bout, *moved = run(
        mlp_back_kernel, deep,
        [by_cols(count, width), by_cols(width, width), full, full, full, mod_all],
        [full, full, whole((frames, 3, width)), row],
        [wide, acts, like((frames, 3, width), f32), like((1, width), f32)],
        (d_hidden, full_up, middle, cotangent, attn, modulation), [acc], name="dact2",
        moves=[second_a, second_b, core_a, core_b, last_a], sizes=sizes, group=8,
    )
    down_b, core_a, core_b, wdown_low = moved[3:6], moved[6], moved[7], moved[8]
    quarter = width // 4
    first_a = ReduceFirst(sizes, wup, core_a, [(0, "l"), (1, "a"), (4, "w")], low_u)
    d_attended, wout, *up_a = run(
        attended_back_kernel, 4, [full, by_rows(quarter, width), by_cols(count, quarter)],
        [by_cols(count, quarter), by_rows(quarter, width)], [acts, like((width, width), bf16)],
        (d_attn, full_out, attended), name="datt", moves=[first_a], sizes=sizes, group=13,
    )
    wout = blocks(wout)
    second_a = ReduceSecond(sizes, up_a, [(0, "l"), (0, "a"), (3, "w")])
    first_b = ReduceFirst(sizes, wup, core_b, [(0, "l"), (1, "a"), (4, "w")], high_u)
    last_b = ReduceLast(sizes, down_b, [(0, "l"), (0, "a"), (pairs, "w")])
    last_a = ReduceLast(sizes, second_a, [(3, "l"), (3, "a"), (pairs, "w")])
    second_b = ReduceSecond(sizes, first_b, [(4, "l"), (4, "a"), (pairs, "w")])
    core = ReduceCore(sizes, wout, [(0, "s"), (5, "w")])
    first = ReduceFirst(sizes, wout, core, [(5, "l"), (5, "a"), (pairs, "w")])
    d_projected, bqkv, *moved = run(
        lambda *refs: attention_backward(*refs, frames=frames), pairs, [pair] * 6 + [table] * 3,
        [pl.BlockSpec((3, count, LANE), lambda i: (0, 0, i)), pl.BlockSpec((1, 3, LANE), lambda i: (i, 0, 0))],
        [like((3, count, width), bf16), like((pairs, 3, LANE), f32)],
        (query, key, value, d_attended, attended, aug, see, cosine, sine), [pltpu.VMEM((count, LANE), f32)], name="attb",
        moves=[second_a, first_b, last_b, last_a, second_b, core, first], sizes=sizes, group=9,
    )
    wdown_high, wup_low, up_b, moved_out = moved[7], moved[8], moved[9:12], moved[13:17]
    wdown_grad = jnp.concatenate([wdown_low, wdown_high], axis=1)
    stacked = pl.BlockSpec((1, count, width), lambda i: (i, 0, 0))
    last = ReduceLast(sizes, up_b, [(0, "l"), (0, "a"), (3, "w")])
    second = ReduceSecond(sizes, moved_out, [(0, "l"), (0, "a"), (3, "w")])
    wqkv, wup_high, *moved_out = run(
        qkv_grad_kernel, 3, [full, stacked], pl.BlockSpec((1, width, width), lambda i: (i, 0, 0)),
        like((3, width, width), bf16), (act_one, d_projected), name="wqkv",
        moves=[last, second], sizes=sizes, group=10,
    )
    wup_grad = jnp.concatenate([wup_low, wup_high], axis=1)
    wqkv = blocks(wqkv, 1)
    core_q = ReduceCore(sizes, wqkv, [(0, "s"), (1, "w")], 0)
    core_k = ReduceCore(sizes, wqkv, [(0, "s"), (1, "w")], 1)
    core_v = ReduceCore(sizes, wqkv, [(0, "s"), (3, "w")], 2)
    first_q = ReduceFirst(sizes, wqkv, core_q, [(1, "l"), (1, "a"), (3, "w")], 0)
    first_k = ReduceFirst(sizes, wqkv, core_k, [(1, "l"), (2, "a"), (3, "w")], 1)
    last_o = ReduceLast(sizes, moved_out, [(0, "l"), (0, "a"), (3, "w")])
    token_grad, stat_one, *moved = run(
        input_back_kernel, 3, [stacked, by_cols(width, width), full, full, mod_all], [full, whole((frames, 2, width))],
        [acts, like((frames, 2, width), f32)],
        (d_projected, full_qkv, tokens, d_middle, modulation), [acc], name="dact1",
        moves=[core_q, core_k, core_v, last_o, first_q, first_k], sizes=sizes, group=11,
    )
    core_v, wout_grad = moved[2], moved[3]
    moved_q, moved_k = moved[4:8], moved[8:12]

    bqkv = jnp.transpose(bqkv, (1, 0, 2)).reshape(1, -1)
    shares = [b.reshape(ndev, -1) for b in (bqkv, bout, bup, bdown)]
    packed = jnp.concatenate(shares, axis=1)
    bias_len = packed.shape[1]
    packed = jnp.pad(packed, ((0, 0), (0, 8 * LANE - bias_len))).reshape(-1, LANE)
    packed = blocks(packed)
    d_modulation = jnp.concatenate(
        [stat_one[:, 0], stat_one[:, 1], stat_two[:, 0], stat_two[:, 1], stat_two[:, 2], d_gate_two], axis=1
    ).astype(bf16)
    d_mod = Gather(sizes, d_modulation.reshape(16, -1), ())
    bias_c = ReduceCore(sizes, packed, ())
    bias_f = ReduceFirst(sizes, packed, bias_c, ())
    bias_s = ReduceSecond(sizes, bias_f, ())
    bias_l = ReduceLast(sizes, bias_s, ())
    first_v = ReduceFirst(sizes, wqkv, core_v, (), 2)
    second_q, second_k = ReduceSecond(sizes, moved_q, ()), ReduceSecond(sizes, moved_k, ())
    second_v = ReduceSecond(sizes, first_v, ())
    last_q, last_k, last_v = [ReduceLast(sizes, s, ()) for s in (second_q, second_k, second_v)]
    lasts = [last_q, last_k, last_v, bias_l]
    tail = run(
        None, 1, [], [], [], [], name="tail",
        moves=[d_mod] + lasts + [bias_c, bias_f, bias_s, first_v, second_q, second_k, second_v], sizes=sizes, group=12,
        script=[
            (d_mod, "s0"), (bias_c, "s"), (second_q, "l"), (second_k, "l"), (first_v, "l"),
            (second_q, "a"), (second_k, "a"), (first_v, "a"), (d_mod, "n0"), (bias_c, "w"), (bias_f, "l"), (bias_f, "a"),
            (second_q, "w"), (last_q, "l"), (last_q, "a"), (second_k, "w"), (last_k, "l"), (last_k, "a"),
            (first_v, "w"), (second_v, "l"), (second_v, "a"), (d_mod, "n1"), (bias_f, "w"), (bias_s, "l"), (bias_s, "a"),
            (second_v, "w"), (last_v, "l"), (last_v, "a"), (d_mod, "n2"), (bias_s, "w"), (bias_l, "l"), (bias_l, "a"),
            (last_q, "w"), (last_k, "w"), (d_mod, "w3"), (bias_l, "w"), (last_v, "w"),
        ],
    )
    d_mod, grad_q, grad_k, grad_v, bias_sum = tail[:5]
    wqkv_grad = jnp.concatenate([grad_q, grad_k, grad_v], axis=1)
    d_mod = d_mod.reshape(ndev * frames, -1)
    bias_sum = bias_sum.reshape(-1)[:bias_len]
    bias_grads, at = [], 0
    for share in shares:
        bias_grads.append(bias_sum[at : at + share.shape[1]])
        at += share.shape[1]
    hot = (all_levels[:, None] == jnp.arange(noise_table.shape[1], dtype=jnp.int32)[None, :]).astype(bf16)
    embedded = dot(hot, noise_table, NT)
    cond = jax.nn.silu(embedded).astype(bf16)
    wmod_grad = dot(cond, d_mod, TN)
    mine = b_mod.shape[0]
    bmod_grad = jnp.sum(lax.dynamic_slice(d_mod, (0, me * mine), (d_mod.shape[0], mine)).astype(f32), axis=0)
    gate = jax.nn.sigmoid(embedded)
    d_embed = dot(d_mod, w_mod, NT) * gate * (1.0 + embedded * (1.0 - gate))
    table_grad = lax.dot_general(
        d_embed, hot.astype(f32), TN, precision=lax.Precision.HIGHEST, preferred_element_type=f32
    )
    return (
        block_out, token_grad, wmod_grad, bmod_grad, wqkv_grad, bias_grads[0], wout_grad, bias_grads[1],
        wup_grad, bias_grads[2], wdown_grad, bias_grads[3], table_grad,
    )


def solution(mesh):
    rows, vec = P(AXES, None), P(AXES)
    return jax.shard_map(
        per_device,
        mesh=mesh,
        in_specs=(rows, rows, rows, vec, vec) + (rows, vec) * 5 + (rows,),
        out_specs=(rows, rows) + (rows, vec) * 5 + (rows,),
        check_vma=False,
    )
```

```python
import jax
import jax.numpy as jnp
from jax import lax
from jax.experimental import pallas as pl
from jax.experimental.pallas import tpu as pltpu
from jax.sharding import PartitionSpec as P

bf16 = jnp.bfloat16
f32 = jnp.float32
AXES = ("dp", "fsdp")
HD = 64
LANE = 128
EPS = 1e-06
NN = (((1,), (0,)), ((), ()))
NT = (((1,), (1,)), ((), ()))
TN = (((0,), (0,)), ((), ()))


def dot(left, right, dims):
    return lax.dot_general(left, right, dims, preferred_element_type=f32)


def lanes(shape):
    return lax.broadcasted_iota(jnp.int32, shape, 1)


def normalize(values):
    centred = values - jnp.mean(values, axis=1, keepdims=True)
    inverse = lax.rsqrt(jnp.mean(centred * centred, axis=1, keepdims=True) + EPS)
    return centred * inverse, inverse


def normalize_back(grad, normed, inverse):
    return inverse * (
        grad
        - jnp.mean(grad, axis=1, keepdims=True)
        - normed * jnp.mean(grad * normed, axis=1, keepdims=True)
    )


def col_sum(values):
    return jnp.sum(values.astype(f32), axis=0, keepdims=True)


def partner(values):
    return jnp.where(
        lanes(values.shape) % HD < HD // 2,
        pltpu.roll(values, LANE - HD // 2, 1),
        pltpu.roll(values, HD // 2, 1),
    )


def carry_lanes(values):
    sub = lanes(values.shape) % HD
    high = values.astype(bf16).astype(f32)
    rest = values - high
    mid = rest.astype(bf16).astype(f32)
    return jnp.where(
        sub == 8, high, jnp.where(sub == 9, mid, jnp.where(sub == 10, rest - mid, 0.0))
    )


def qkv_kernel(x_ref, mod_ref, w_ref, b_ref, cos_ref, sin_ref, act_ref, q_ref, k_ref, v_ref):
    normed, _ = normalize(x_ref[...].astype(f32))
    act = (normed * (1.0 + mod_ref[0, 1:2, :]) + mod_ref[0, 0:1, :]).astype(bf16)
    act_ref[...] = act
    width = x_ref.shape[1]
    cosine, sine = cos_ref[...], sin_ref[...]
    step = 2 * LANE
    for col in range(0, 3 * width, step):
        raw = dot(act, w_ref[:, col : col + step], NN) + b_ref[:, col : col + step].astype(f32)
        for sub in range(0, step, LANE):
            part = raw[:, sub : sub + LANE]
            at = (col + sub) % width
            if col < width:
                part = (part * cosine + partner(part) * sine).astype(bf16)
                q_ref[:, at : at + LANE] = (part.astype(f32) * 0.125).astype(bf16)
            elif col < 2 * width:
                k_ref[:, at : at + LANE] = (part * cosine + partner(part) * sine).astype(bf16)
            else:
                v_ref[:, at : at + LANE] = part.astype(bf16)


def attention_forward(q_ref, k_ref, v_ref, see_ref, hot_ref, out_ref, aug_ref, *, frames):
    rows_all = q_ref.shape[0]
    size = rows_all // frames
    low = lanes((rows_all, LANE)) < HD
    low_b = lanes((size, LANE)) < HD
    k, v, see = k_ref[...], v_ref[...], see_ref[...]
    one = jnp.ones_like(v)
    keys = (jnp.where(low, k, see), jnp.where(low, see, k))
    vals = (jnp.where(low, v, one), jnp.where(low, one, v))
    for i in range(frames):
        rows = slice(i * size, (i + 1) * size)
        width = (i + 1) * size
        q, hot = q_ref[rows, :], hot_ref[rows, :]
        query = (jnp.where(low_b, q, hot), jnp.where(low_b, hot, q))
        tops, outs = [], []
        for h in range(2):
            scores = dot(query[h], keys[h][:width], NT)
            top = jnp.max(scores, axis=1, keepdims=True)
            expo = jnp.exp(scores - top).astype(bf16)
            outs.append(dot(expo, vals[h][:width], NN))
            tops.append(top)
        num = jnp.where(low_b, outs[0], outs[1])
        den = jnp.where(low_b, outs[1], outs[0])
        out_ref[rows, :] = (num / pltpu.roll(den, HD, 1)).astype(bf16)
        lse = jnp.where(low_b, tops[1], tops[0]) + jnp.log(den)
        aug_ref[rows, :] = (carry_lanes(-lse) + hot.astype(f32)).astype(bf16)


def project_kernel(att_ref, x_ref, mod_ref, w_ref, b_ref, middle_ref, attn_ref, act_ref):
    attn = dot(att_ref[...], w_ref[...], NN) + b_ref[...].astype(f32)
    attn_ref[...] = attn.astype(bf16)
    middle = x_ref[...].astype(f32) + mod_ref[0, 2:3, :] * attn
    middle_ref[...] = middle
    normed, _ = normalize(middle)
    act_ref[...] = (normed * (1.0 + mod_ref[0, 4:5, :]) + mod_ref[0, 3:4, :]).astype(bf16)


def up_kernel(act_ref, w_ref, b_ref, out_ref, slope_ref):
    hidden = dot(act_ref[...], w_ref[...], NN) + b_ref[...].astype(f32)
    share = 0.5 * (1.0 + lax.erf(hidden * 0.7071067811865476))
    out_ref[...] = (hidden * share).astype(bf16)
    slope = share + hidden * jnp.exp(-0.5 * hidden * hidden) * 0.3989422804014327
    slope_ref[...] = slope.astype(bf16)


def down_kernel(
    act_ref, w_ref, b_ref, mid_ref, cot_ref, mod_ref, out_ref, dbr_ref, gate_ref, sum_ref, acc_ref
):
    step, last = pl.program_id(0), pl.num_programs(0) - 1
    part = dot(act_ref[...], w_ref[...], NN)

    @pl.when(step == 0)
    def _():
        acc_ref[...] = part

    @pl.when(step > 0)
    def _():
        acc_ref[...] += part

    @pl.when(step == last)
    def _():
        frames = mod_ref.shape[0]
        size = acc_ref.shape[0] // frames
        total = jnp.zeros((1, acc_ref.shape[1]), f32)
        for i in range(frames):
            rows = slice(i * size, (i + 1) * size)
            gate = mod_ref[i, 5:6, :]
            branch = acc_ref[rows, :] + b_ref[...].astype(f32)
            out_ref[rows, :] = (mid_ref[rows, :] + gate * branch).astype(bf16)
            upstream = cot_ref[rows, :].astype(f32)
            d_branch = (upstream * gate).astype(bf16)
            dbr_ref[rows, :] = d_branch
            gate_ref[i : i + 1, :] = col_sum(upstream * branch)
            total += col_sum(d_branch)
        sum_ref[...] = total


def hidden_back_kernel(dbr_ref, w_ref, slope_ref, out_ref, sum_ref):
    d_hidden = (dot(dbr_ref[...], w_ref[...], NT) * slope_ref[...].astype(f32)).astype(bf16)
    out_ref[...] = d_hidden
    sum_ref[...] = col_sum(d_hidden)


def mlp_back_kernel(
    dh_ref, w_ref, mid_ref, cot_ref, attn_ref, mod_ref, dmid_ref, datt_ref, stat_ref, sum_ref, acc_ref, step, last
):
    part = dot(dh_ref[...], w_ref[...], NT)

    @pl.when(step == 0)
    def _():
        acc_ref[...] = part

    @pl.when(step > 0)
    def _():
        acc_ref[...] += part

    @pl.when(step == last)
    def _():
        frames = mod_ref.shape[0]
        size = acc_ref.shape[0] // frames
        total = jnp.zeros((1, acc_ref.shape[1]), f32)
        for i in range(frames):
            rows = slice(i * size, (i + 1) * size)
            d_act = acc_ref[rows, :]
            normed, inverse = normalize(mid_ref[rows, :])
            stat_ref[i, 1:2, :] = col_sum(d_act)
            stat_ref[i, 2:3, :] = col_sum(d_act * normed)
            d_middle = cot_ref[rows, :].astype(f32) + normalize_back(
                d_act * (1.0 + mod_ref[i, 4:5, :]), normed, inverse
            )
            dmid_ref[rows, :] = d_middle
            stat_ref[i, 0:1, :] = col_sum(d_middle * attn_ref[rows, :].astype(f32))
            d_attn = (d_middle * mod_ref[i, 2:3, :]).astype(bf16)
            datt_ref[rows, :] = d_attn
            total += col_sum(d_attn)
        sum_ref[...] = total


def at_columns(ref, index, size):
    return ref.at[:, pl.ds(pl.multiple_of(index * size, size), size)]


def mlp_kernel(
    dbr_ref, wdown_ref, slope_ref, act_ref, wup_ref, mid_ref, cot_ref, attn_ref, mod_ref,
    bup_ref, out_ref, dmid_ref, datt_ref, stat_ref, sum_ref, dh_ref, acc_ref, *, tiles, deep,
):
    step = pl.program_id(0)
    size, wide = dh_ref.shape[1] // tiles, dh_ref.shape[1] // deep

    @pl.when(step < tiles)
    def _():
        hidden_back_kernel(dbr_ref, wdown_ref, slope_ref, at_columns(dh_ref, step, size), bup_ref)

    @pl.when((step >= tiles) & (step < 2 * tiles))
    def _():
        weight_grad_kernel(act_ref, at_columns(dh_ref, step - tiles, size), out_ref)

    @pl.when(step >= 2 * tiles)
    def _():
        mlp_back_kernel(
            at_columns(dh_ref, step - 2 * tiles, wide), wup_ref, mid_ref, cot_ref, attn_ref, mod_ref,
            dmid_ref, datt_ref, stat_ref, sum_ref, acc_ref, step - 2 * tiles, deep - 1,
        )


def attention_back_kernel(
    da_ref, wout_ref, att_ref, q_ref, k_ref, v_ref, o_ref, aug_ref, see_ref, cos_ref, sin_ref, act_ref,
    gout_ref, out_ref, bias_ref, gqkv_ref, do_ref, dp_ref, acc_ref, *, frames, lead, pairs,
):
    step = pl.program_id(0)

    @pl.when(step < lead)
    def _():
        attended_back_kernel(
            da_ref, wout_ref, att_ref, at_columns(do_ref, step, do_ref.shape[1] // lead), gout_ref
        )

    @pl.when((step >= lead) & (step < lead + pairs))
    def _():
        at = step - lead
        attention_backward(
            q_ref, k_ref, v_ref, at_columns(do_ref, at, LANE), o_ref, aug_ref, see_ref, cos_ref, sin_ref,
            out_ref, bias_ref, acc_ref, frames=frames,
        )
        for i in range(3):
            dp_ref[i, :, pl.ds(pl.multiple_of(at * LANE, LANE), LANE)] = out_ref[i]

    @pl.when(step >= lead + pairs)
    def _():
        gqkv_ref[0] = dot(act_ref[...], dp_ref[step - lead - pairs], TN).astype(bf16)


def attention_backward(
    q_ref, k_ref, v_ref, do_ref, o_ref, aug_ref, see_ref, cos_ref, sin_ref, out_ref, sum_ref, acc_ref, *, frames
):
    rows_all = q_ref.shape[0]
    size = rows_all // frames
    low = lanes((rows_all, LANE)) < HD
    q, aug, grad = q_ref[...], aug_ref[...], do_ref[...]
    prod = grad.astype(f32) * o_ref[...].astype(f32)
    delta_low = jnp.sum(jnp.where(low, prod, 0.0), axis=1, keepdims=True)
    delta_high = jnp.sum(jnp.where(low, 0.0, prod), axis=1, keepdims=True)
    grad_aug = carry_lanes(jnp.where(low, -delta_high, -delta_low)).astype(bf16)
    query = (jnp.where(low, q, aug), jnp.where(low, aug, q))
    upper = (jnp.where(low, grad, grad_aug), jnp.where(low, grad_aug, grad))
    low_b = lanes((size, LANE)) < HD
    sub = lanes((size, LANE)) % HD
    ones = jnp.where((sub >= 8) & (sub <= 10), 1.0, 0.0).astype(bf16)
    sum_k = sum_v = jnp.zeros((1, LANE), f32)
    for j in range(frames):
        rows = slice(j * size, (j + 1) * size)
        start = j * size
        k, v, see = k_ref[rows, :], v_ref[rows, :], see_ref[rows, :] + ones
        keys = (jnp.where(low_b, k, see), jnp.where(low_b, see, k))
        vals = (jnp.where(low_b, v, ones), jnp.where(low_b, ones, v))
        dvs, dks, dqs = [], [], []
        for h in range(2):
            probs = jnp.exp(dot(keys[h], query[h][start:], NT))
            d_scores = (probs * dot(vals[h], upper[h][start:], NT)).astype(bf16)
            dvs.append(dot(probs.astype(bf16), grad[start:], NN))
            dks.append(dot(d_scores, q[start:], NN))
            dqs.append(dot(d_scores, k, TN))
        d_value = jnp.where(low_b, dvs[0], dvs[1]).astype(bf16)
        d_key = jnp.where(low_b, dks[0], dks[1])
        d_key = (d_key * cos_ref[rows, :] - partner(d_key) * sin_ref[rows, :]).astype(bf16)
        out_ref[1, rows, :] = d_key
        out_ref[2, rows, :] = d_value
        sum_k = sum_k + col_sum(d_key)
        sum_v = sum_v + col_sum(d_value)
        d_query = jnp.where(lanes(dqs[0].shape) < HD, dqs[0], dqs[1])
        if j == 0:
            acc_ref[...] = d_query
        else:
            acc_ref[start:, :] += d_query
    d_query = acc_ref[...] * 0.125
    d_query = (d_query * cos_ref[...] - partner(d_query) * sin_ref[...]).astype(bf16)
    out_ref[0] = d_query
    sum_ref[0, 0:1, :] = col_sum(d_query)
    sum_ref[0, 1:2, :] = sum_k
    sum_ref[0, 2:3, :] = sum_v


def input_back_kernel(dp_ref, w_ref, x_ref, dmid_ref, mod_ref, out_ref, stat_ref, acc_ref):
    step, last = pl.program_id(0), pl.num_programs(0) - 1
    part = dot(dp_ref[0], w_ref[...], NT)

    @pl.when(step == 0)
    def _():
        acc_ref[...] = part

    @pl.when(step > 0)
    def _():
        acc_ref[...] += part

    @pl.when(step == last)
    def _():
        frames = mod_ref.shape[0]
        size = acc_ref.shape[0] // frames
        for i in range(frames):
            rows = slice(i * size, (i + 1) * size)
            d_act = acc_ref[rows, :]
            normed, inverse = normalize(x_ref[rows, :].astype(f32))
            stat_ref[i, 0:1, :] = col_sum(d_act)
            stat_ref[i, 1:2, :] = col_sum(d_act * normed)
            back = normalize_back(d_act * (1.0 + mod_ref[i, 1:2, :]), normed, inverse)
            out_ref[rows, :] = (dmid_ref[rows, :] + back).astype(bf16)


def modulation_kernel(small_ref, table_ref, w_ref, part_ref, levels_ref, frames):
    ndev = part_ref.shape[0] * part_ref.shape[1] * part_ref.shape[2] * 2
    rows = levels_ref[...].reshape(ndev, levels_ref.shape[-2], LANE)
    spots = jnp.sum(rows[:, :8], axis=0).astype(jnp.int32)
    count = 2 * frames * ndev
    level = jnp.concatenate([spots[i : i + 1, :] for i in range(count // LANE)], axis=1)
    slot = lax.broadcasted_iota(jnp.int32, (table_ref.shape[1], count), 0)
    hot = jnp.where(slot == level, 1.0, 0.0).astype(bf16)
    embedded = dot(table_ref[...], hot, NN)
    cond = (embedded / (1.0 + jnp.exp(-embedded))).astype(bf16)
    half = part_ref.shape[-1]
    first = lax.broadcasted_iota(jnp.int32, (count, 1), 0) % (2 * frames) < frames
    step = 512
    for col in range(0, half, step):
        low = dot(cond, w_ref[:, col : col + step], TN)
        high = dot(cond, w_ref[:, half + col : half + col + step], TN)
        value = jnp.where(first, low, high)
        part_ref[..., col : col + step] = value.reshape(part_ref.shape[:-1] + (step,))


def weight_grad_kernel(left_ref, right_ref, out_ref):
    out_ref[...] = dot(left_ref[...], right_ref[...], TN).astype(bf16)


def attended_back_kernel(da_ref, w_ref, att_ref, datt_ref, out_ref):
    datt_ref[...] = dot(da_ref[...], w_ref[...], NT).astype(bf16)
    out_ref[...] = dot(att_ref[...], da_ref[...], TN).astype(bf16)


def qkv_grad_kernel(left_ref, right_ref, out_ref):
    out_ref[0] = dot(left_ref[...], right_ref[0], TN).astype(bf16)


def like(shape, kind):
    return jax.ShapeDtypeStruct(shape, kind)


def whole(shape):
    return pl.BlockSpec(shape, lambda i: (0,) * len(shape))


def by_rows(size, width):
    return pl.BlockSpec((size, width), lambda i: (i, 0))


def by_cols(height, size):
    return pl.BlockSpec((height, size), lambda i: (0, i))


MESH = pl.DeviceIdType.MESH
ANY = pl.BlockSpec(memory_space=pl.ANY)
VMEM = pl.BlockSpec(memory_space=pltpu.VMEM)
DMA = pltpu.SemaphoreType.DMA


class Place:
    def __init__(self, sizes):
        self.ny, self.nx, self.nz = sizes
        self.half = self.nz // 2
        self.rest = self.nz - self.half
        self.low, self.high = pl.ds(0, self.half), pl.ds(self.half, self.rest)
        self.dp, self.fsdp = lax.axis_index("dp"), lax.axis_index("fsdp")
        self.y, self.x = lax.div(self.dp, self.nx), lax.rem(self.dp, self.nx)
        self.z, self.c = lax.div(self.fsdp, 2), lax.rem(self.fsdp, 2)

        self.shifts, self.devices = {}, {}
        for axis, size in dict(y=self.ny, x=self.nx, z=self.nz, c=2).items():
            for k in range(1, size):
                at = lax.rem(getattr(self, axis) + k, size)
                self.shifts[axis, k] = self.shifts[axis, k - size] = at
                self.devices[axis, k] = dict(
                    y=(at * self.nx + self.x, self.fsdp), x=(self.y * self.nx + at, self.fsdp),
                    z=(self.dp, at * 2 + self.c), c=(self.dp, self.z * 2 + at),
                )[axis]
        self.other = self.shifts["c", 1]

    def shift(self, axis, k):
        return self.shifts[axis, k]

    def device(self, axis, k):
        return self.devices[axis, k]

    def enter(self, axes):
        barrier = pltpu.get_barrier_semaphore()
        sizes = dict(y=self.ny, x=self.nx, z=self.nz, c=2)
        count = 0
        for axis in axes:
            for k in range(1, sizes[axis]):
                count += 1
                pl.semaphore_signal(barrier, inc=1, device_id=self.device(axis, k), device_id_type=MESH)
        pl.semaphore_wait(barrier, count)


class Move:
    ins, in_specs, outs, out_specs, scratch, aliases = (), (), (), (), (), ()

    def bind(self, place, ins, outs, scratch):
        self.place, self.in_refs, self.out_refs, self.refs = place, ins, outs, scratch
        self.slots, self.local_slots, self.legs = {}, {}, []

    def copy(self, key, src, dst, axis, k):
        slot = self.slots.setdefault(key, len(self.slots))
        return pltpu.make_async_remote_copy(
            src_ref=src, dst_ref=dst, send_sem=self.refs[0].at[slot], recv_sem=self.refs[1].at[slot],
            device_id=self.place.device(axis, k), device_id_type=MESH,
        )

    def start(self, items):
        for item in items:
            self.copy(*item).start()

    def arrived(self, key, dst, axis, k):
        self.copy(key, dst, dst, axis, k).wait_recv()

    def drain(self, items):
        for item in items:
            self.copy(*item).wait_send()

    def local(self, key, src, dst):
        slot = self.local_slots.setdefault(key, len(self.local_slots))
        return pltpu.make_async_copy(src, dst, self.refs[2].at[slot])


class Held:
    def __init__(self, shape, kind):
        self.shape, self.dtype, self.ref = shape, kind, None


def part_of(ref, part, core):
    if part is None:
        return ref.at[:, :, :, core]
    if isinstance(part, int):
        return ref.at[part, :, :, :, core]
    return ref.at[:, :, :, core, :, part[0] : part[1]]


def block_of(array, part):
    rows, columns = array.shape[-2:]
    return (rows, part[1] - part[0]) if isinstance(part, tuple) else (rows, columns)


def legs_copies(sizes):
    ny, nx, nz = sizes
    return (nz - 1) + 4 * (nx - 1) + 4 * (ny - 1) + 1


class Gather(Move):
    def __init__(self, sizes, array, actions, begun=False):
        ny, nx, nz = sizes
        self.begun, self.actions = begun, actions
        self.held = array if isinstance(array, Held) else None
        self.ins, self.in_specs = ([], []) if self.held else ([array], [ANY if begun else VMEM])
        shape = array.shape if begun else (ny, nx, nz, 2) + array.shape
        self.outs, self.out_specs = [like(shape, array.dtype)], [ANY]
        parts = len({what[2:] for _, what in actions}) if actions else 3
        self.scratch = [DMA((legs_copies(sizes) * parts,)), DMA((legs_copies(sizes) * parts,)), DMA((parts,))]
        self.aliases = [(0, 0)] if begun else []

    def act(self, what):
        op, leg, part = what[0], int(what[1]), what[2:]
        if op != "s":
            self.wait_leg(leg, part)
        if op != "w":
            self.start_leg(leg + (op == "n"), part)
        else:
            for each in self.legs:
                if each[1] == part:
                    self.drain(self.leaving(*each))

    def columns(self, part):
        width = self.out_refs[0].shape[-1]
        half = width // 2
        return {"": slice(None), "a": slice(0, half), "b": slice(half, width)}[part]

    def spot(self, index, part):
        return self.out_refs[0].at[index + (slice(None), self.columns(part))]

    def items(self, leg):
        p, full = self.place, self.out_refs[0]
        y, x, z, c = p.y, p.x, p.z, p.c
        d = p.other
        xs, ys, zs = range(1, p.nx), range(1, p.ny), range(1, p.nz)
        back = p.shift
        if leg == 0:
            return [(("z", k), (y, x, z, c), (y, x, back("z", -k), c), "z", k) for k in zs]
        if leg == 1:
            return (
                [(("x", k), (y, x, p.low, c), (y, back("x", -k), p.low, c), "x", k) for k in xs]
                + [(("y", k), (y, x, p.high, c), (back("y", -k), x, p.high, c), "y", k) for k in ys]
                + [("c", (y, x, slice(None), c), (y, x, slice(None), d), "c", 1)]
            )
        every = slice(None)
        if leg == 2:
            return (
                [(("xy", k), (y, every, p.low, c), (back("y", -k), every, p.low, c), "y", k) for k in ys]
                + [(("yx", k), (every, x, p.high, c), (every, back("x", -k), p.high, c), "x", k) for k in xs]
                + [(("cx", k), (y, back("x", -k), p.low, c), (y, back("x", -k), p.low, d), "c", 1) for k in xs]
                + [(("cy", k), (back("y", -k), x, p.high, c), (back("y", -k), x, p.high, d), "c", 1) for k in ys]
            )
        return [
            (("cxy", k), (back("y", -k), every, p.low, c), (back("y", -k), every, p.low, d), "c", 1) for k in ys
        ] + [(("cyx", k), (every, back("x", -k), p.high, c), (every, back("x", -k), p.high, d), "c", 1) for k in xs]

    def source(self):
        return self.held.ref if self.held else self.in_refs[0]

    def own(self, part):
        p = self.place
        mine = self.source().at[:, self.columns(part)]
        return self.local(part, mine, self.spot((p.y, p.x, p.z, p.c), part))

    def leaving(self, leg, part):
        for key, leaves, _, axis, k in self.items(leg):
            to = self.spot(leaves, part)
            yield (key, part), self.source().at[:, self.columns(part)] if leg == 0 else to, to, axis, k

    def start_leg(self, leg, part):
        self.legs.append((leg, part))
        if leg == 0:
            self.own(part).start()
        self.start(self.leaving(leg, part))

    def wait_leg(self, leg, part):
        if leg == 0:
            self.own(part).wait()
        for key, _, arrives, axis, k in self.items(leg):
            self.arrived((key, part), self.spot(arrives, part), axis, k)


def add_blocks(into, where, counts, terms):
    total = 1
    for n in counts:
        total *= n

    def body(flat, carry):
        at = []
        for n in reversed(counts):
            at.append(lax.rem(flat, n))
            flat = lax.div(flat, n)
        at = tuple(at[::-1])
        spot = where(*at)
        value = into[spot].astype(f32)
        for ref, index in terms(*at):
            value = value + ref[index].astype(f32)
        into[spot] = value.astype(into.dtype)
        return carry

    lax.fori_loop(0, total, body, 0)


class ReduceCore(Move):
    def __init__(self, sizes, array, actions, part=None):
        self.actions, self.part = actions, part
        ny, nx, nz = sizes
        self.held = array if isinstance(array, Held) else None
        self.ins, self.in_specs = ([], []) if self.held else ([array], [ANY])
        self.outs, self.out_specs = [like((ny, nx, nz) + block_of(array, part), array.dtype)], [ANY]
        self.scratch = [DMA((1,)), DMA((1,))]

    def act(self, what):
        p = self.place
        source = self.held.ref if self.held else self.in_refs[0]
        leaving = [("c", part_of(source, self.part, p.other), self.out_refs[0], "c", 1)]
        if what == "s":
            self.start(leaving)
        else:
            self.arrived("c", self.out_refs[0], "c", 1)
            self.drain(leaving)


class ReduceFirst(Move):
    def __init__(self, sizes, array, core, actions, part=None):
        self.actions, self.part, self.core = actions, part, core
        ny, nx, nz = sizes
        half, rest = nz // 2, nz - nz // 2
        block, kind = block_of(array, part), array.dtype
        self.held = array if isinstance(array, Held) else None
        self.ins = ([] if self.held else [array]) + ([] if isinstance(core, Move) else [core])
        self.in_specs = [ANY] * len(self.ins)
        self.outs = [
            like((ny - 1, nx, half) + block, kind), like((nx - 1, ny, rest) + block, kind),
            like((nx, half) + block, kind), like((ny, rest) + block, kind),
        ]
        self.out_specs = [ANY] * 4
        remote = DMA((nx + ny - 2,))
        self.scratch = [remote, remote, DMA((4,))] + [pltpu.VMEM((ny, nx, nz) + block, kind)] * 2

    def act(self, what):
        p = self.place
        source = self.held.ref if self.held else self.in_refs[0]
        core = self.core.out_refs[0] if isinstance(self.core, Move) else self.in_refs[-1]
        acc, buf = self.refs[3:]
        la, lb, ka, kb = self.out_refs
        loads = [("acc", part_of(source, self.part, p.c), acc), ("buf", core, buf)]
        leaving = [
            (("y", k), acc.at[p.shift("y", k), :, p.low], la.at[k - 1], "y", k) for k in range(1, p.ny)
        ] + [(("x", k), acc.at[:, p.shift("x", k), p.high], lb.at[k - 1], "x", k) for k in range(1, p.nx)]
        keeps = [("ka", acc.at[p.y, :, p.low], ka), ("kb", acc.at[:, p.x, p.high], kb)]
        if what == "l":
            for item in loads:
                self.local(*item).start()
        elif what == "a":
            for item in loads:
                self.local(*item).wait()
            add_blocks(acc, lambda *at: at, (p.ny, p.nx, p.nz), lambda *at: [(buf, at)])
            self.start(leaving)
            for item in keeps:
                self.local(*item).start()
        else:
            for k in range(1, p.ny):
                self.arrived(("y", k), la.at[k - 1], "y", k)
            for k in range(1, p.nx):
                self.arrived(("x", k), lb.at[k - 1], "x", k)
            for item in keeps:
                self.local(*item).wait()
            self.drain(leaving)


class ReduceSecond(Move):
    def __init__(self, sizes, first, actions):
        self.actions, self.first = actions, first
        ny, nx, nz = sizes
        half, rest = nz // 2, nz - nz // 2
        self.inside = isinstance(first, Move)
        arrays = first.outs if self.inside else first
        block, kind = arrays[0].shape[-2:], arrays[0].dtype
        self.ins, self.in_specs = ([], []) if self.inside else (list(arrays), [ANY] * 4)
        self.outs = [
            like((nx - 1, half) + block, kind), like((ny - 1, rest) + block, kind), like((nz,) + block, kind)
        ]
        self.out_specs = [ANY] * 3
        remote = DMA((nx + ny - 2,))
        self.scratch = [remote, remote, DMA((6,))] + [pltpu.VMEM(a.shape, kind) for a in arrays]

    def act(self, what):
        p = self.place
        arrays = self.first.out_refs if self.inside else self.in_refs
        bufs = self.refs[3:]
        la, lb, ka, kb = bufs
        ma, mb, kept = self.out_refs
        loads = [(i, a, b) for i, (a, b) in enumerate(zip(arrays, bufs))]
        leaving = [(("x", k), ka.at[p.shift("x", k)], ma.at[k - 1], "x", k) for k in range(1, p.nx)]
        leaving += [(("y", k), kb.at[p.shift("y", k)], mb.at[k - 1], "y", k) for k in range(1, p.ny)]
        keeps = [("ka", ka.at[p.x], kept.at[p.low]), ("kb", kb.at[p.y], kept.at[p.high])]
        if what == "l":
            for item in loads:
                self.local(*item).start()
        elif what == "a":
            for item in loads:
                self.local(*item).wait()
            add_blocks(ka, lambda *at: at, (p.nx, p.half), lambda i, j: [(la, (k, i, j)) for k in range(p.ny - 1)])
            add_blocks(kb, lambda *at: at, (p.ny, p.rest), lambda i, j: [(lb, (k, i, j)) for k in range(p.nx - 1)])
            self.start(leaving)
            for item in keeps:
                self.local(*item).start()
        else:
            for k in range(1, p.nx):
                self.arrived(("x", k), ma.at[k - 1], "x", k)
            for k in range(1, p.ny):
                self.arrived(("y", k), mb.at[k - 1], "y", k)
            for item in keeps:
                self.local(*item).wait()
            self.drain(leaving)


class ReduceLast(Move):
    def __init__(self, sizes, second, actions):
        self.actions, self.second = actions, second
        ny, nx, nz = sizes
        self.inside = isinstance(second, Move)
        arrays = second.outs if self.inside else second
        block, kind = arrays[0].shape[-2:], arrays[0].dtype
        self.ins, self.in_specs = ([], []) if self.inside else (list(arrays), [ANY] * 3)
        self.outs, self.out_specs = [like(block, f32)], [VMEM]
        self.scratch = [DMA((nz - 1,)), DMA((nz - 1,)), DMA((3,))] + [pltpu.VMEM(a.shape, kind) for a in arrays]
        self.scratch += [pltpu.VMEM((nz - 1,) + block, kind)]

    def act(self, what):
        p = self.place
        arrays = self.second.out_refs if self.inside else self.in_refs
        ma, mb, kept, last = self.refs[3:]
        loads = [(i, a, b) for i, (a, b) in enumerate(zip(arrays, (ma, mb, kept)))]
        leaving = [(("z", k), kept.at[p.shift("z", k)], last.at[k - 1], "z", k) for k in range(1, p.nz)]
        if what == "l":
            for item in loads:
                self.local(*item).start()
        elif what == "a":
            for item in loads:
                self.local(*item).wait()
            add_blocks(kept, lambda j: (j,), (p.half,), lambda j: [(ma, (k, j)) for k in range(p.nx - 1)])
            add_blocks(
                kept, lambda j: (p.half + j,), (p.rest,), lambda j: [(mb, (k, j)) for k in range(p.ny - 1)]
            )
            self.start(leaving)
        else:
            for k in range(1, p.nz):
                self.arrived(("z", k), last.at[k - 1], "z", k)
            value = kept[p.z].astype(f32)
            for k in range(p.nz - 1):
                value = value + last[k].astype(f32)
            self.out_refs[0][...] = value
            self.drain(leaving)


def run(
    kernel, grid, ins, outs, shapes, args, scratch=(), name=None, moves=(), sizes=None, group=None, axes="yxzc", script=None
):
    single = not isinstance(shapes, (list, tuple))
    outs, shapes = ([outs], [shapes]) if single else (list(outs), list(shapes))
    counts = len(ins), len(outs), len(scratch)
    all_ins, all_specs, all_outs = list(args), list(ins), list(shapes)
    all_out_specs, all_scratch, aliases = list(outs), list(scratch), {}
    for move in moves:
        for i, o in move.aliases:
            aliases[len(all_ins) + i] = len(all_outs) + o
        all_ins += list(move.ins)
        all_specs += list(move.in_specs)
        all_outs += list(move.outs)
        all_out_specs += list(move.out_specs)
        all_scratch += list(move.scratch)

    def body(*refs):
        refs = list(refs)

        def take(n):
            part = refs[:n]
            del refs[:n]
            return part

        mine_in = take(counts[0])
        moved_in = [take(len(m.ins)) for m in moves]
        mine_out = take(counts[1])
        moved_out = [take(len(m.outs)) for m in moves]
        mine_scratch = take(counts[2])
        place = Place(sizes) if moves else None
        for move, i, o in zip(moves, moved_in, moved_out):
            move.bind(place, i, o, take(len(move.scratch)))
        step = pl.program_id(0)

        def turn(at):
            for move in moves:
                for when, what in move.actions:
                    if when == at:
                        move.act(what)

        def play():
            for item in script:
                if isinstance(item, tuple):
                    item[0].act(item[1])
                else:
                    item(mine_in, mine_out, mine_scratch)

        if kernel is None:
            place.enter(axes)
            play()
            return

        for at in range(grid):
            if any(when == at for m in moves for when, _ in m.actions):

                @pl.when(step == at)
                def _(at=at):
                    if at == 0:
                        place.enter(axes)
                    turn(at)

        kernel(*mine_in, *mine_out, *mine_scratch)
        if moves:

            @pl.when(step == grid - 1)
            def _():
                turn(grid)
                if script is not None:
                    play()

    params = dict(vmem_limit_bytes=(63 if moves else 60) * 1024 * 1024)
    if moves:
        params.update(collective_id=group, has_side_effects=True)
    moved = sum(a.size * a.dtype.itemsize for a in args)
    results = pl.pallas_call(
        body,
        grid=(grid,),
        in_specs=all_specs,
        out_specs=all_out_specs,
        out_shape=all_outs,
        scratch_shapes=all_scratch,
        input_output_aliases=aliases,
        name=name,
        cost_estimate=pl.CostEstimate(flops=0, bytes_accessed=2 * moved, transcendentals=0),
        compiler_params=pltpu.CompilerParams(**params),
    )(*all_ins)
    return results[0] if single and not moves else results


def tables(clip_row, pad, count):
    frames = clip_row.shape[0]
    size = count // frames
    slots = jnp.arange(frames, dtype=jnp.int32)
    ends = jnp.sum(jnp.where(slots[None, :] <= slots[:, None], clip_row[None, :], 0), axis=1)
    clip_of = jnp.sum((slots[:, None] >= ends[None, :]).astype(jnp.int32), axis=1)
    starts = ends - clip_row
    start_of = jnp.sum(jnp.where(clip_of[:, None] == slots[None, :], starts[None, :], 0), axis=1)
    frame_pos = slots - start_of
    frame = jnp.arange(count, dtype=jnp.int32) // size
    lane = jnp.arange(LANE, dtype=jnp.int32) % HD
    frame_hot = frame[:, None] == lane[None, :]
    own = frame[:, None] == slots[None, :]
    clip_tok = jnp.sum(jnp.where(own, clip_of[None, :], 0), axis=1)
    pos_tok = jnp.sum(jnp.where(own, frame_pos[None, :], 0), axis=1)
    lane_own = lane[:, None] == slots[None, :]
    lane_clip = jnp.sum(jnp.where(lane_own, clip_of[None, :], 0), axis=1)
    lane_pos = jnp.sum(jnp.where(lane_own, frame_pos[None, :], 0), axis=1)
    seen = (
        (clip_tok[:, None] == lane_clip[None, :])
        & (pos_tok[:, None] <= lane_pos[None, :])
        & (pad[:, None] == 1)
    )
    see = jnp.where((lane[None, :] < frames) & ~seen, -1e30, 0.0).astype(bf16)
    quarter = HD // 4
    freq = 10000.0 ** (-jnp.arange(quarter, dtype=f32) / quarter)
    patch = jnp.arange(count, dtype=jnp.int32) % size
    angle = jnp.concatenate(
        [pos_tok.astype(f32)[:, None] * freq[None, :], patch.astype(f32)[:, None] * freq[None, :]],
        axis=1,
    )
    cosine, sine = jnp.cos(angle), jnp.sin(angle)
    cosine = jnp.concatenate([cosine] * 4, axis=1)
    sine = jnp.concatenate([-sine, sine, -sine, sine], axis=1)
    return see, frame_hot.astype(bf16), cosine, sine


def per_device(
    tokens, cotangent, clip_frames, levels, pad_mask, w_mod, b_mod, w_qkv, b_qkv, w_out, b_out,
    w_up, b_up, w_down, b_down, noise_table,
):
    count, width = tokens.shape
    frames = levels.shape[0]
    size = count // frames
    hidden = w_up.shape[1]
    ndev = width // w_up.shape[0]
    me = lax.axis_index("dp") * lax.axis_size("fsdp") + lax.axis_index("fsdp")

    dp, fsdp = lax.axis_size("dp"), lax.axis_size("fsdp")
    sizes = (dp // 2, 2, fsdp // 2)
    lead = sizes + (2,)

    def flat(array):
        return array.reshape(-1, array.shape[-1])

    def blocks(array, front=0):
        rows = array.shape[front] // ndev
        return array.reshape(array.shape[:front] + lead + (rows, array.shape[-1]))

    biases = [b_mod, b_qkv, b_out, b_up, b_down]
    lengths = [b.shape[0] for b in biases]
    spots = jnp.arange(8 * LANE, dtype=jnp.int32)
    mine_at = jnp.where(spots // (2 * frames) == me, jnp.tile(levels, spots.shape[0] // frames), 0)
    packed = jnp.concatenate([mine_at.astype(f32)] + [b.astype(f32) for b in biases])
    packed = jnp.pad(packed, (0, 16 * LANE - packed.shape[0])).reshape(16, LANE)
    table_pad = jnp.pad(noise_table, ((0, 0), (0, -noise_table.shape[1] % LANE)))
    part = Held(lead + (2 * frames, w_mod.shape[1] // 2), f32)
    small = Gather(sizes, packed, ())
    qkv_w = Gather(sizes, w_qkv, ())
    out_w, up_w = Gather(sizes, w_out, ()), Gather(sizes, w_up, ())
    mod_c = ReduceCore(sizes, part, ())
    mod_f = ReduceFirst(sizes, part, mod_c, ())
    mod_s = ReduceSecond(sizes, mod_f, ())
    mod_l = ReduceLast(sizes, mod_s, ())

    def add_modulation(ins, _, scratch):
        part.ref = scratch[0]
        load = pltpu.make_async_copy(small.out_refs[0], scratch[1], scratch[2].at[0])
        load.start()
        load.wait()
        modulation_kernel(None, ins[0], ins[1], scratch[0], scratch[1], frames)

    head = run(
        None, 1, [VMEM] * 2, [], [], [table_pad, w_mod],
        [pltpu.VMEM(part.shape, f32), pltpu.VMEM(lead + packed.shape, f32), DMA((1,))], name="head",
        moves=[small, qkv_w, out_w, up_w, mod_c, mod_f, mod_s, mod_l], sizes=sizes, group=1,
        script=[
            (small, "s0"), (qkv_w, "s0a"), (qkv_w, "s0b"), (small, "n0"), (small, "n1"), (small, "n2"), (small, "w3"),
            (qkv_w, "n0a"), (out_w, "s0"), (up_w, "s0"), add_modulation, (mod_c, "s"), (qkv_w, "n1a"), (qkv_w, "n0b"),
            (mod_c, "w"), (mod_f, "l"), (mod_f, "a"), (qkv_w, "n1b"), (mod_f, "w"), (mod_s, "l"), (mod_s, "a"),
            (qkv_w, "n2a"), (mod_s, "w"), (mod_l, "l"), (mod_l, "a"), (qkv_w, "n2b"), (qkv_w, "w3a"), (qkv_w, "w3b"),
            (mod_l, "w"), (out_w, "w0"), (up_w, "w0"),
        ],
    )
    small, qkv_w, out_w, up_w = head[:4]
    small = small.reshape(ndev, -1)
    all_levels = jnp.sum(small[:, : 8 * LANE], axis=0).reshape(-1, 2 * frames)[:ndev, :frames]
    all_levels = all_levels.reshape(-1).astype(jnp.int32)
    full_bias, at = [], 8 * LANE
    for length in lengths:
        full_bias.append(small[:, at : at + length].reshape(1, -1))
        at += length
    bias_mod, bias_qkv, bias_out, bias_up, bias_down = full_bias
    modulation = jnp.transpose(head[-1].reshape(2, frames, -1), (1, 0, 2)).reshape(frames, -1)
    modulation = (modulation + bias_mod).reshape(frames, 6, width)
    full_qkv = flat(qkv_w)
    see, frame_hot, cosine, sine = tables(clip_frames[0], pad_mask, count)

    acts = like((count, width), bf16)
    wide = like((count, width), f32)
    tall = like((count, hidden), bf16)
    row = whole((1, width))
    mod_row = pl.BlockSpec((1, 6, width), lambda i: (i, 0, 0))
    mod_all = whole((frames, 6, width))
    rows_bf = by_rows(size, width)
    act_one, query, key, value, out_w, up_w = run(
        qkv_kernel, frames,
        [rows_bf, mod_row, whole((width, 3 * width)), whole((1, 3 * width)), by_rows(size, LANE), by_rows(size, LANE)],
        [rows_bf] * 4, [acts] * 4, (tokens, modulation, full_qkv, bias_qkv, cosine, sine), name="qkv",
        moves=[
            Gather(sizes, out_w, [(0, "s1"), (1, "n1"), (frames, "n2"), (frames, "w3")], True),
            Gather(sizes, up_w, [(0, "s1a"), (frames, "w1a")], True),
        ], sizes=sizes, group=2,
    )
    full_out = flat(out_w)
    pair = by_cols(count, LANE)
    table = whole((count, LANE))
    pairs = width // LANE
    attended, aug, up_w, down_w = run(
        lambda *refs: attention_forward(*refs, frames=frames), pairs,
        [pair, pair, pair, table, table], [pair] * 2, [acts] * 2, (query, key, value, see, frame_hot), name="attf",
        moves=[
            Gather(sizes, up_w, [(0, "s1b"), (0, "s2a"), (3, "n1b"), (6, "n2a"), (pairs, "w2b"), (pairs, "w3a")], True),
            Gather(sizes, w_down, [(0, "s0"), (pairs, "w0")]),
        ], sizes=sizes, group=3,
    )
    middle, attn, act_two, up_w, down_w = run(
        project_kernel, frames, [rows_bf, rows_bf, mod_row, whole((width, width)), row], [rows_bf] * 3,
        [wide, acts, acts], (attended, tokens, modulation, full_out, bias_out), name="proj",
        moves=[
            Gather(sizes, up_w, [(0, "s3b"), (frames, "w3b")], True),
            Gather(sizes, down_w, [(0, "s1a"), (frames, "w1a")], True),
        ], sizes=sizes, group=4,
    )
    full_up = flat(up_w)
    full = whole((count, width))
    step = 512
    tiles = hidden // step
    cols_h = by_cols(count, step)
    activated, slope, down_w = run(
        up_kernel, tiles, [full, by_cols(width, step), by_cols(1, step)], [cols_h] * 2, [tall] * 2,
        (act_two, full_up, bias_up), name="up",
        moves=[Gather(sizes, down_w, [(0, "s1b"), (0, "s2a"), (tiles // 2, "n1b"), (tiles, "n2a"), (tiles, "n2b"), (tiles, "w3a"), (tiles, "w3b")], True)], sizes=sizes, group=5,
    )
    full_down = flat(down_w)
    acc = pltpu.VMEM((count, width), f32)
    deep = hidden // width
    block_out, d_branch, d_gate_two, bdown = run(
        down_kernel, deep, [by_cols(count, width), by_rows(width, width), row, full, full, mod_all],
        [full, full, whole((frames, width)), row],
        [acts, acts, like((frames, width), f32), like((1, width), f32)],
        (activated, full_down, bias_down, middle, cotangent, modulation), [acc], name="down",
    )
    wdown = run(
        weight_grad_kernel, tiles, [cols_h, full], by_rows(step, width), like((hidden, width), bf16),
        (activated, d_branch), name="wdown",
    )
    wdown = blocks(wdown)
    stacked = pl.BlockSpec((1, count, width), lambda i: (i, 0, 0))
    def turn(start, count, index):
        return lambda i: index(jnp.clip(i - start, 0, count - 1))

    def held(shape):
        return pl.BlockSpec(shape, lambda i: (0,) * len(shape), pipeline_mode=pl.Buffered(1))

    once = held((count, width))
    mod_once = held((frames, 6, width))
    halves = ((0, width // 2), (width // 2, width))
    steps = 2 * tiles + deep
    cores = [ReduceCore(sizes, wdown, [(0, "s"), (2 + 2 * i, "w")], h) for i, h in enumerate(halves)]
    firsts = [
        ReduceFirst(sizes, wdown, cores[0], [(2, "l"), (3, "a"), (9, "w")], halves[0]),
        ReduceFirst(sizes, wdown, cores[1], [(4, "l"), (5, "a"), (2 * tiles - 1, "w")], halves[1]),
    ]
    seconds = [
        ReduceSecond(sizes, firsts[0], [(9, "l"), (10, "a"), (2 * tiles + 1, "w")]),
        ReduceSecond(sizes, firsts[1], [(2 * tiles - 1, "l"), (2 * tiles, "a"), (steps, "w")]),
    ]
    last_a = ReduceLast(sizes, seconds[0], [(2 * tiles + 1, "l"), (2 * tiles + 1, "a"), (steps, "w")])
    bup, wup, d_middle, d_attn, stat_two, bout, *moved = run(
        lambda *refs: mlp_kernel(*refs, tiles=tiles, deep=deep), steps,
        [
            once, pl.BlockSpec((step, width), turn(0, tiles, lambda i: (i, 0))),
            pl.BlockSpec((count, step), turn(0, tiles, lambda i: (0, i))), once,
            pl.BlockSpec((width, width), turn(2 * tiles, deep, lambda i: (0, i))), once, once, once, mod_once,
        ],
        [
            pl.BlockSpec((1, step), turn(0, tiles, lambda i: (0, i))),
            pl.BlockSpec((width, step), turn(tiles, tiles, lambda i: (0, i))),
            once, once, held((frames, 3, width)), held((1, width)),
        ],
        [
            like((1, hidden), f32), like((width, hidden), bf16), wide, acts, like((frames, 3, width), f32),
            like((1, width), f32),
        ],
        (d_branch, full_down, slope, act_two, full_up, middle, cotangent, attn, modulation),
        [pltpu.VMEM((count, hidden), bf16), acc], name="mlpb",
        moves=cores + firsts + seconds + [last_a], sizes=sizes, group=6,
    )
    down_b, wdown_low = moved[13:16], moved[16]
    wup = blocks(wup)
    halves = ((0, hidden // 2), (hidden // 2, hidden))
    quarters = 4
    quarter = width // quarters
    steps = quarters + pairs + 3
    cores = [ReduceCore(sizes, wup, [(0, "s"), (2 + i, "w")], h) for i, h in enumerate(halves)]
    firsts = [
        ReduceFirst(sizes, wup, cores[0], [(2, "l"), (3, "a"), (7, "w")], halves[0]),
        ReduceFirst(sizes, wup, cores[1], [(3, "l"), (4, "a"), (9, "w")], halves[1]),
    ]
    seconds = [
        ReduceSecond(sizes, firsts[0], [(7, "l"), (7, "a"), (10, "w")]),
        ReduceSecond(sizes, firsts[1], [(9, "l"), (9, "a"), (12, "w")]),
    ]
    last_b = ReduceLast(sizes, down_b, [(0, "l"), (1, "a"), (5, "w")])
    last_a = ReduceLast(sizes, seconds[0], [(10, "l"), (10, "a"), (steps, "w")])
    pair_b = pl.BlockSpec((count, LANE), turn(quarters, pairs, lambda i: (0, i)))
    table_once = held((count, LANE))
    wout, d_projected, bqkv, wqkv, *moved = run(
        lambda *refs: attention_back_kernel(*refs, frames=frames, lead=quarters, pairs=pairs), steps,
        [
            once, pl.BlockSpec((quarter, width), turn(0, quarters, lambda i: (i, 0))),
            pl.BlockSpec((count, quarter), turn(0, quarters, lambda i: (0, i))),
        ] + [pair_b] * 5 + [table_once] * 3 + [once],
        [
            pl.BlockSpec((quarter, width), turn(0, quarters, lambda i: (i, 0))),
            pl.BlockSpec((3, count, LANE), turn(quarters, pairs, lambda i: (0, 0, i))),
            pl.BlockSpec((1, 3, LANE), turn(quarters, pairs, lambda i: (i, 0, 0))),
            pl.BlockSpec((1, width, width), turn(quarters + pairs, 3, lambda i: (i, 0, 0))),
        ],
        [
            like((width, width), bf16), like((3, count, width), bf16), like((pairs, 3, LANE), f32),
            like((3, width, width), bf16),
        ],
        (d_attn, full_out, attended, query, key, value, attended, aug, see, cosine, sine, act_one),
        [pltpu.VMEM((count, width), bf16), pltpu.VMEM((3, count, width), bf16), pltpu.VMEM((count, LANE), f32)],
        name="attb", moves=[last_b] + cores + firsts + seconds + [last_a], sizes=sizes, group=7,
    )
    wdown_high, up_b, wup_low = moved[0], moved[14:17], moved[17]
    wdown_grad = jnp.concatenate([wdown_low, wdown_high], axis=1)
    wout, wqkv = blocks(wout), blocks(wqkv, 1)

    bqkv = jnp.transpose(bqkv, (1, 0, 2)).reshape(1, -1)
    shares = [b.reshape(ndev, -1) for b in (bqkv, bout, bup, bdown)]
    packed = jnp.concatenate(shares, axis=1)
    bias_len = packed.shape[1]
    packed = jnp.pad(packed, ((0, 0), (0, 8 * LANE - bias_len))).reshape(-1, LANE)
    packed = blocks(packed)
    mod_block = Held((6 * frames, width), bf16)
    d_mod = Gather(sizes, mod_block, ())
    bc = ReduceCore(sizes, packed, ())
    bf = ReduceFirst(sizes, packed, bc, ())
    bs = ReduceSecond(sizes, bf, ())
    bl = ReduceLast(sizes, bs, ())
    chunks = [(wqkv, 0), (wqkv, 1), (wqkv, 2), (wout, None)]
    marks = [(1, 1), (1, 2), (3, 3), (3, 3)]
    cores, firsts, seconds, lasts = [], [], [], []
    for (array, part), (at, then) in zip(chunks, marks):
        cores.append(ReduceCore(sizes, array, [(0, "s")] + [(at, "w")] * (at < 3), part))
        firsts.append(ReduceFirst(sizes, array, cores[-1], [(at, "l"), (then, "a")] if at < 3 else (), part))
        seconds.append(ReduceSecond(sizes, firsts[-1], ()))
        lasts.append(ReduceLast(sizes, seconds[-1], ()))
    last_b = ReduceLast(sizes, up_b, [(0, "l"), (0, "a"), (3, "w")])

    def pack_modulation(ins, outs, scratch):
        one, two, gate = outs[1], ins[5], ins[6]
        parts = [one[:, 0, :], one[:, 1, :], two[:, 0, :], two[:, 1, :], two[:, 2, :], gate[...]]
        scratch[1][...] = jnp.concatenate(parts, axis=0).astype(bf16)

    def set_block(refs):
        mod_block.ref = refs[-1]
        input_back_kernel(*refs[:5], *refs[7:9], refs[9])

    (cq, ck, cv, co), (fq, fk, fv, fo), (sq, sk, sv, so), (lq, lk, lv, lo) = cores, firsts, seconds, lasts
    token_grad, stat_one, *moved = run(
        lambda *refs: set_block(refs), 3,
        [stacked, by_cols(width, width), once, once, mod_once, held((frames, 3, width)), held((frames, width))],
        [once, held((frames, 2, width))],
        [acts, like((frames, 2, width), f32)],
        (d_projected, full_qkv, tokens, d_middle, modulation, stat_two, d_gate_two),
        [acc, pltpu.VMEM(mod_block.shape, bf16)], name="dact1",
        moves=[d_mod] + lasts + [last_b, bl] + cores + firsts + seconds + [bc, bf, bs], sizes=sizes, group=8,
        script=[
            (cv, "w"), (fv, "l"), (co, "w"), (fo, "l"), (bc, "s"), (fv, "a"), (fo, "a"), pack_modulation, (d_mod, "s0"),
            (fq, "w"), (sq, "l"), (sq, "a"), (bc, "w"), (bf, "l"), (bf, "a"), (fk, "w"), (sk, "l"), (sk, "a"),
            (d_mod, "n0"), (sq, "w"), (lq, "l"), (lq, "a"), (bf, "w"), (bs, "l"), (bs, "a"),
            (fv, "w"), (sv, "l"), (sv, "a"), (sk, "w"), (lk, "l"), (lk, "a"), (d_mod, "n1"), (bs, "w"), (bl, "l"), (bl, "a"),
            (fo, "w"), (so, "l"), (so, "a"), (sv, "w"), (lv, "l"), (lv, "a"), (d_mod, "n2"),
            (so, "w"), (lo, "l"), (lo, "a"), (d_mod, "w3"), (lq, "w"), (lk, "w"), (bl, "w"), (lv, "w"), (lo, "w"),
        ],
    )
    d_mod, grad_q, grad_k, grad_v, wout_grad, wup_high, bias_sum = moved[:7]
    wup_grad = jnp.concatenate([wup_low, wup_high], axis=1)
    wqkv_grad = jnp.concatenate([grad_q, grad_k, grad_v], axis=1)
    d_mod = jnp.transpose(d_mod.reshape(ndev, 6, frames, width), (0, 2, 1, 3))
    d_mod = d_mod.reshape(ndev * frames, -1)
    bias_sum = bias_sum.reshape(-1)[:bias_len]
    bias_grads, at = [], 0
    for share in shares:
        bias_grads.append(bias_sum[at : at + share.shape[1]])
        at += share.shape[1]
    hot = (all_levels[:, None] == jnp.arange(noise_table.shape[1], dtype=jnp.int32)[None, :]).astype(bf16)
    embedded = dot(hot, noise_table, NT)
    cond = jax.nn.silu(embedded).astype(bf16)
    wmod_grad = dot(cond, d_mod, TN)
    mine = b_mod.shape[0]
    bmod_grad = jnp.sum(lax.dynamic_slice(d_mod, (0, me * mine), (d_mod.shape[0], mine)).astype(f32), axis=0)
    gate = jax.nn.sigmoid(embedded)
    d_embed = dot(d_mod, w_mod, NT) * gate * (1.0 + embedded * (1.0 - gate))
    table_grad = lax.dot_general(
        d_embed, hot.astype(f32), TN, precision=lax.Precision.HIGHEST, preferred_element_type=f32
    )
    return (
        block_out, token_grad, wmod_grad, bmod_grad, wqkv_grad, bias_grads[0], wout_grad, bias_grads[1],
        wup_grad, bias_grads[2], wdown_grad, bias_grads[3], table_grad,
    )


def solution(mesh):
    rows, vec = P(AXES, None), P(AXES)
    return jax.shard_map(
        per_device,
        mesh=mesh,
        in_specs=(rows, rows, rows, vec, vec) + (rows, vec) * 5 + (rows,),
        out_specs=(rows, rows) + (rows, vec) * 5 + (rows,),
        check_vma=False,
    )
```

```python
import jax
import jax.numpy as jnp
from jax import lax
from jax.experimental import pallas as pl
from jax.experimental.pallas import tpu as pltpu
from jax.sharding import PartitionSpec as P

bf16 = jnp.bfloat16
f32 = jnp.float32
AXES = ("dp", "fsdp")
HD = 64
LANE = 128
EPS = 1e-06
NN = (((1,), (0,)), ((), ()))
NT = (((1,), (1,)), ((), ()))
TN = (((0,), (0,)), ((), ()))


def dot(left, right, dims):
    return lax.dot_general(left, right, dims, preferred_element_type=f32)


def lanes(shape):
    return lax.broadcasted_iota(jnp.int32, shape, 1)


def normalize(values):
    centred = values - jnp.mean(values, axis=1, keepdims=True)
    inverse = lax.rsqrt(jnp.mean(centred * centred, axis=1, keepdims=True) + EPS)
    return centred * inverse, inverse


def normalize_back(grad, normed, inverse):
    return inverse * (
        grad
        - jnp.mean(grad, axis=1, keepdims=True)
        - normed * jnp.mean(grad * normed, axis=1, keepdims=True)
    )


def col_sum(values):
    return jnp.sum(values.astype(f32), axis=0, keepdims=True)


def partner(values):
    return jnp.where(
        lanes(values.shape) % HD < HD // 2,
        pltpu.roll(values, LANE - HD // 2, 1),
        pltpu.roll(values, HD // 2, 1),
    )


def carry_lanes(values):
    sub = lanes(values.shape) % HD
    high = values.astype(bf16).astype(f32)
    rest = values - high
    mid = rest.astype(bf16).astype(f32)
    return jnp.where(
        sub == 8, high, jnp.where(sub == 9, mid, jnp.where(sub == 10, rest - mid, 0.0))
    )


def qkv_kernel(x_ref, mod_ref, w_ref, b_ref, cos_ref, sin_ref, act_ref, q_ref, k_ref, v_ref):
    normed, _ = normalize(x_ref[...].astype(f32))
    act = (normed * (1.0 + mod_ref[0, 1:2, :]) + mod_ref[0, 0:1, :]).astype(bf16)
    act_ref[...] = act
    width = x_ref.shape[1]
    cosine, sine = cos_ref[...], sin_ref[...]
    step = 2 * LANE
    for col in range(0, 3 * width, step):
        raw = dot(act, w_ref[:, col : col + step], NN) + b_ref[:, col : col + step].astype(f32)
        for sub in range(0, step, LANE):
            part = raw[:, sub : sub + LANE]
            at = (col + sub) % width
            if col < width:
                part = (part * cosine + partner(part) * sine).astype(bf16)
                q_ref[:, at : at + LANE] = (part.astype(f32) * 0.125).astype(bf16)
            elif col < 2 * width:
                k_ref[:, at : at + LANE] = (part * cosine + partner(part) * sine).astype(bf16)
            else:
                v_ref[:, at : at + LANE] = part.astype(bf16)


def attention_forward(q_ref, k_ref, v_ref, see_ref, hot_ref, out_ref, aug_ref, *, frames):
    rows_all = q_ref.shape[0]
    size = rows_all // frames
    low = lanes((rows_all, LANE)) < HD
    low_b = lanes((size, LANE)) < HD
    k, v, see = k_ref[...], v_ref[...], see_ref[...]
    one = jnp.ones_like(v)
    keys = (jnp.where(low, k, see), jnp.where(low, see, k))
    vals = (jnp.where(low, v, one), jnp.where(low, one, v))
    for i in range(frames):
        rows = slice(i * size, (i + 1) * size)
        width = (i + 1) * size
        q, hot = q_ref[rows, :], hot_ref[rows, :]
        query = (jnp.where(low_b, q, hot), jnp.where(low_b, hot, q))
        tops, outs = [], []
        for h in range(2):
            scores = dot(query[h], keys[h][:width], NT)
            top = jnp.max(scores, axis=1, keepdims=True)
            expo = jnp.exp(scores - top).astype(bf16)
            outs.append(dot(expo, vals[h][:width], NN))
            tops.append(top)
        num = jnp.where(low_b, outs[0], outs[1])
        den = jnp.where(low_b, outs[1], outs[0])
        out_ref[rows, :] = (num / pltpu.roll(den, HD, 1)).astype(bf16)
        lse = jnp.where(low_b, tops[1], tops[0]) + jnp.log(den)
        aug_ref[rows, :] = (carry_lanes(-lse) + hot.astype(f32)).astype(bf16)


def project_kernel(att_ref, x_ref, mod_ref, w_ref, b_ref, middle_ref, attn_ref, act_ref):
    attn = dot(att_ref[...], w_ref[...].reshape(-1, w_ref.shape[-1]), NN) + b_ref[...].astype(f32)
    attn_ref[...] = attn.astype(bf16)
    middle = x_ref[...].astype(f32) + mod_ref[0, 2:3, :] * attn
    middle_ref[...] = middle
    normed, _ = normalize(middle)
    act_ref[...] = (normed * (1.0 + mod_ref[0, 4:5, :]) + mod_ref[0, 3:4, :]).astype(bf16)


def up_kernel(act_ref, w_ref, b_ref, out_ref, slope_ref):
    hidden = dot(act_ref[...], w_ref[...].reshape(-1, w_ref.shape[-1]), NN) + b_ref[...].astype(f32)
    share = 0.5 * (1.0 + lax.erf(hidden * 0.7071067811865476))
    out_ref[...] = (hidden * share).astype(bf16)
    slope = share + hidden * jnp.exp(-0.5 * hidden * hidden) * 0.3989422804014327
    slope_ref[...] = slope.astype(bf16)


def down_kernel(
    act_ref, w_ref, b_ref, mid_ref, cot_ref, mod_ref, out_ref, dbr_ref, gate_ref, sum_ref, acc_ref
):
    step, last = pl.program_id(0), pl.num_programs(0) - 1
    part = dot(act_ref[...], w_ref[...], NN)

    @pl.when(step == 0)
    def _():
        acc_ref[...] = part

    @pl.when(step > 0)
    def _():
        acc_ref[...] += part

    @pl.when(step == last)
    def _():
        frames = mod_ref.shape[0]
        size = acc_ref.shape[0] // frames
        total = jnp.zeros((1, acc_ref.shape[1]), f32)
        for i in range(frames):
            rows = slice(i * size, (i + 1) * size)
            gate = mod_ref[i, 5:6, :]
            branch = acc_ref[rows, :] + b_ref[...].astype(f32)
            out_ref[rows, :] = (mid_ref[rows, :] + gate * branch).astype(bf16)
            upstream = cot_ref[rows, :].astype(f32)
            d_branch = (upstream * gate).astype(bf16)
            dbr_ref[rows, :] = d_branch
            gate_ref[i : i + 1, :] = col_sum(upstream * branch)
            total += col_sum(d_branch)
        sum_ref[...] = total


def hidden_back_kernel(dbr_ref, w_ref, slope_ref, out_ref, sum_ref):
    d_hidden = (dot(dbr_ref[...], w_ref[...], NT) * slope_ref[...].astype(f32)).astype(bf16)
    out_ref[...] = d_hidden
    sum_ref[...] = col_sum(d_hidden)


def mlp_back_kernel(
    dh_ref, w_ref, mid_ref, cot_ref, attn_ref, mod_ref, dmid_ref, datt_ref, stat_ref, sum_ref, acc_ref, step, last
):
    part = dot(dh_ref[...], w_ref[...], NT)

    @pl.when(step == 0)
    def _():
        acc_ref[...] = part

    @pl.when(step > 0)
    def _():
        acc_ref[...] += part

    @pl.when(step == last)
    def _():
        frames = mod_ref.shape[0]
        size = acc_ref.shape[0] // frames
        total = jnp.zeros((1, acc_ref.shape[1]), f32)
        for i in range(frames):
            rows = slice(i * size, (i + 1) * size)
            d_act = acc_ref[rows, :]
            normed, inverse = normalize(mid_ref[rows, :])
            stat_ref[i, 1:2, :] = col_sum(d_act)
            stat_ref[i, 2:3, :] = col_sum(d_act * normed)
            d_middle = cot_ref[rows, :].astype(f32) + normalize_back(
                d_act * (1.0 + mod_ref[i, 4:5, :]), normed, inverse
            )
            dmid_ref[rows, :] = d_middle
            stat_ref[i, 0:1, :] = col_sum(d_middle * attn_ref[rows, :].astype(f32))
            d_attn = (d_middle * mod_ref[i, 2:3, :]).astype(bf16)
            datt_ref[rows, :] = d_attn
            total += col_sum(d_attn)
        sum_ref[...] = total


def at_columns(ref, index, size):
    return ref.at[:, pl.ds(pl.multiple_of(index * size, size), size)]


def mlp_kernel(
    dbr_ref, wdown_ref, slope_ref, act_ref, wup_ref, mid_ref, cot_ref, attn_ref, mod_ref,
    bup_ref, out_ref, dmid_ref, datt_ref, stat_ref, sum_ref, dh_ref, acc_ref, *, tiles, deep,
):
    step = pl.program_id(0)
    size, wide = dh_ref.shape[1] // tiles, dh_ref.shape[1] // deep

    @pl.when(step < tiles)
    def _():
        hidden_back_kernel(dbr_ref, wdown_ref, slope_ref, at_columns(dh_ref, step, size), bup_ref)

    @pl.when((step >= tiles) & (step < 2 * tiles))
    def _():
        weight_grad_kernel(act_ref, at_columns(dh_ref, step - tiles, size), out_ref)

    @pl.when(step >= 2 * tiles)
    def _():
        mlp_back_kernel(
            at_columns(dh_ref, step - 2 * tiles, wide), wup_ref, mid_ref, cot_ref, attn_ref, mod_ref,
            dmid_ref, datt_ref, stat_ref, sum_ref, acc_ref, step - 2 * tiles, deep - 1,
        )


def attention_back_kernel(
    da_ref, wout_ref, att_ref, q_ref, k_ref, v_ref, o_ref, aug_ref, see_ref, cos_ref, sin_ref, act_ref,
    gout_ref, out_ref, bias_ref, gqkv_ref, do_ref, dp_ref, acc_ref, *, frames, lead, pairs,
):
    step = pl.program_id(0)

    @pl.when(step < lead)
    def _():
        attended_back_kernel(
            da_ref, wout_ref, att_ref, at_columns(do_ref, step, do_ref.shape[1] // lead), gout_ref
        )

    @pl.when((step >= lead) & (step < lead + pairs))
    def _():
        at = step - lead
        attention_backward(
            q_ref, k_ref, v_ref, at_columns(do_ref, at, LANE), o_ref, aug_ref, see_ref, cos_ref, sin_ref,
            out_ref, bias_ref, acc_ref, frames=frames,
        )
        for i in range(3):
            dp_ref[i, :, pl.ds(pl.multiple_of(at * LANE, LANE), LANE)] = out_ref[i]

    @pl.when(step >= lead + pairs)
    def _():
        gqkv_ref[0] = dot(act_ref[...], dp_ref[step - lead - pairs], TN).astype(bf16)


def forward_kernel(
    x_ref, mod_ref, w_ref, b_ref, cos_ref, sin_ref, see_ref, hot_ref, again_ref, mod_again_ref, bout_ref, bup_ref,
    act_ref, q_ref, k_ref, v_ref, att_ref, aug_ref, middle_ref, attn_ref, act_two_ref, up_ref, slope_ref,
    q_all, k_all, v_all, att_all, act_all, *, frames, pairs, tiles, gathers,
):
    step = pl.program_id(0)
    size = x_ref.shape[0]
    marks = (frames, frames + pairs, 2 * frames + pairs)

    @pl.when(step < marks[0])
    def _():
        qkv_kernel(x_ref, mod_ref, w_ref, b_ref, cos_ref, sin_ref, act_ref, q_ref, k_ref, v_ref)
        rows = pl.ds(pl.multiple_of(step * size, size), size)
        for ref, every in ((q_ref, q_all), (k_ref, k_all), (v_ref, v_all)):
            every[rows, :] = ref[...]

    @pl.when((step >= marks[0]) & (step < marks[1]))
    def _():
        at = step - marks[0]
        q, k, v = [at_columns(ref, at, LANE) for ref in (q_all, k_all, v_all)]
        attention_forward(q, k, v, see_ref, hot_ref, att_ref, aug_ref, frames=frames)
        att_all[:, pl.ds(pl.multiple_of(at * LANE, LANE), LANE)] = att_ref[...]

    @pl.when((step >= marks[1]) & (step < marks[2]))
    def _():
        rows = pl.ds(pl.multiple_of((step - marks[1]) * size, size), size)
        weight = gathers[0].refs[3]
        project_kernel(
            att_all.at[rows, :], again_ref, mod_again_ref, weight, bout_ref, middle_ref, attn_ref, act_two_ref
        )
        act_all[rows, :] = act_two_ref[...]

    @pl.when(step >= marks[2])
    def _():
        width = up_ref.shape[1]
        at = pl.multiple_of((step - marks[2]) * width, width)
        up_kernel(act_all, gathers[1].refs[3].at[:, :, :, :, :, pl.ds(at, width)], bup_ref, up_ref, slope_ref)


def attention_backward(
    q_ref, k_ref, v_ref, do_ref, o_ref, aug_ref, see_ref, cos_ref, sin_ref, out_ref, sum_ref, acc_ref, *, frames
):
    rows_all = q_ref.shape[0]
    size = rows_all // frames
    low = lanes((rows_all, LANE)) < HD
    q, aug, grad = q_ref[...], aug_ref[...], do_ref[...]
    prod = grad.astype(f32) * o_ref[...].astype(f32)
    delta_low = jnp.sum(jnp.where(low, prod, 0.0), axis=1, keepdims=True)
    delta_high = jnp.sum(jnp.where(low, 0.0, prod), axis=1, keepdims=True)
    grad_aug = carry_lanes(jnp.where(low, -delta_high, -delta_low)).astype(bf16)
    query = (jnp.where(low, q, aug), jnp.where(low, aug, q))
    upper = (jnp.where(low, grad, grad_aug), jnp.where(low, grad_aug, grad))
    low_b = lanes((size, LANE)) < HD
    sub = lanes((size, LANE)) % HD
    ones = jnp.where((sub >= 8) & (sub <= 10), 1.0, 0.0).astype(bf16)
    sum_k = sum_v = jnp.zeros((1, LANE), f32)
    for j in range(frames):
        rows = slice(j * size, (j + 1) * size)
        start = j * size
        k, v, see = k_ref[rows, :], v_ref[rows, :], see_ref[rows, :] + ones
        keys = (jnp.where(low_b, k, see), jnp.where(low_b, see, k))
        vals = (jnp.where(low_b, v, ones), jnp.where(low_b, ones, v))
        dvs, dks, dqs = [], [], []
        for h in range(2):
            probs = jnp.exp(dot(keys[h], query[h][start:], NT))
            d_scores = (probs * dot(vals[h], upper[h][start:], NT)).astype(bf16)
            dvs.append(dot(probs.astype(bf16), grad[start:], NN))
            dks.append(dot(d_scores, q[start:], NN))
            dqs.append(dot(d_scores, k, TN))
        d_value = jnp.where(low_b, dvs[0], dvs[1]).astype(bf16)
        d_key = jnp.where(low_b, dks[0], dks[1])
        d_key = (d_key * cos_ref[rows, :] - partner(d_key) * sin_ref[rows, :]).astype(bf16)
        out_ref[1, rows, :] = d_key
        out_ref[2, rows, :] = d_value
        sum_k = sum_k + col_sum(d_key)
        sum_v = sum_v + col_sum(d_value)
        d_query = jnp.where(lanes(dqs[0].shape) < HD, dqs[0], dqs[1])
        if j == 0:
            acc_ref[...] = d_query
        else:
            acc_ref[start:, :] += d_query
    d_query = acc_ref[...] * 0.125
    d_query = (d_query * cos_ref[...] - partner(d_query) * sin_ref[...]).astype(bf16)
    out_ref[0] = d_query
    sum_ref[0, 0:1, :] = col_sum(d_query)
    sum_ref[0, 1:2, :] = sum_k
    sum_ref[0, 2:3, :] = sum_v


def input_back_kernel(dp_ref, w_ref, x_ref, dmid_ref, mod_ref, out_ref, stat_ref, acc_ref):
    step, last = pl.program_id(0), pl.num_programs(0) - 1
    part = dot(dp_ref[0], w_ref[...], NT)

    @pl.when(step == 0)
    def _():
        acc_ref[...] = part

    @pl.when(step > 0)
    def _():
        acc_ref[...] += part

    @pl.when(step == last)
    def _():
        frames = mod_ref.shape[0]
        size = acc_ref.shape[0] // frames
        for i in range(frames):
            rows = slice(i * size, (i + 1) * size)
            d_act = acc_ref[rows, :]
            normed, inverse = normalize(x_ref[rows, :].astype(f32))
            stat_ref[i, 0:1, :] = col_sum(d_act)
            stat_ref[i, 1:2, :] = col_sum(d_act * normed)
            back = normalize_back(d_act * (1.0 + mod_ref[i, 1:2, :]), normed, inverse)
            out_ref[rows, :] = (dmid_ref[rows, :] + back).astype(bf16)


def modulation_kernel(small_ref, table_ref, w_ref, part_ref, levels_ref, frames):
    ndev = part_ref.shape[0] * part_ref.shape[1] * part_ref.shape[2] * 2
    rows = levels_ref[...].reshape(ndev, levels_ref.shape[-2], LANE)
    spots = jnp.sum(rows[:, :8], axis=0).astype(jnp.int32)
    count = 2 * frames * ndev
    level = jnp.concatenate([spots[i : i + 1, :] for i in range(count // LANE)], axis=1)
    slot = lax.broadcasted_iota(jnp.int32, (table_ref.shape[1], count), 0)
    hot = jnp.where(slot == level, 1.0, 0.0).astype(bf16)
    embedded = dot(table_ref[...], hot, NN)
    cond = (embedded / (1.0 + jnp.exp(-embedded))).astype(bf16)
    half = part_ref.shape[-1]
    first = lax.broadcasted_iota(jnp.int32, (count, 1), 0) % (2 * frames) < frames
    step = 512
    for col in range(0, half, step):
        low = dot(cond, w_ref[:, col : col + step], TN)
        high = dot(cond, w_ref[:, half + col : half + col + step], TN)
        value = jnp.where(first, low, high)
        part_ref[..., col : col + step] = value.reshape(part_ref.shape[:-1] + (step,)).astype(part_ref.dtype)


def weight_grad_kernel(left_ref, right_ref, out_ref):
    out_ref[...] = dot(left_ref[...], right_ref[...], TN).astype(bf16)


def attended_back_kernel(da_ref, w_ref, att_ref, datt_ref, out_ref):
    datt_ref[...] = dot(da_ref[...], w_ref[...], NT).astype(bf16)
    out_ref[...] = dot(att_ref[...], da_ref[...], TN).astype(bf16)


def qkv_grad_kernel(left_ref, right_ref, out_ref):
    out_ref[0] = dot(left_ref[...], right_ref[0], TN).astype(bf16)


def like(shape, kind):
    return jax.ShapeDtypeStruct(shape, kind)


def whole(shape):
    return pl.BlockSpec(shape, lambda i: (0,) * len(shape))


def by_rows(size, width):
    return pl.BlockSpec((size, width), lambda i: (i, 0))


def by_cols(height, size):
    return pl.BlockSpec((height, size), lambda i: (0, i))


MESH = pl.DeviceIdType.MESH
ANY = pl.BlockSpec(memory_space=pl.ANY)
VMEM = pl.BlockSpec(memory_space=pltpu.VMEM)
DMA = pltpu.SemaphoreType.DMA


class Place:
    def __init__(self, sizes):
        self.ny, self.nx, self.nz = sizes
        self.half = self.nz // 2
        self.rest = self.nz - self.half
        self.low, self.high = pl.ds(0, self.half), pl.ds(self.half, self.rest)
        self.dp, self.fsdp = lax.axis_index("dp"), lax.axis_index("fsdp")
        self.y, self.x = lax.div(self.dp, self.nx), lax.rem(self.dp, self.nx)
        self.z, self.c = lax.div(self.fsdp, 2), lax.rem(self.fsdp, 2)

        self.shifts, self.devices = {}, {}
        for axis, size in dict(y=self.ny, x=self.nx, z=self.nz, c=2).items():
            for k in range(1, size):
                at = lax.rem(getattr(self, axis) + k, size)
                self.shifts[axis, k] = self.shifts[axis, k - size] = at
                self.devices[axis, k] = dict(
                    y=(at * self.nx + self.x, self.fsdp), x=(self.y * self.nx + at, self.fsdp),
                    z=(self.dp, at * 2 + self.c), c=(self.dp, self.z * 2 + at),
                )[axis]
        self.other = self.shifts["c", 1]
        self.nd, self.nf = self.ny * self.nx, self.nz * 2
        for k in range(1, self.nd):
            at = lax.rem(self.dp + k, self.nd)
            self.shifts["d", k] = self.shifts["d", k - self.nd] = at
            self.devices["d", k] = (at, self.fsdp)
        for k in range(1, self.nf):
            at = lax.rem(self.fsdp + k, self.nf)
            self.shifts["f", k] = self.shifts["f", k - self.nf] = at
            self.devices["f", k] = (self.dp, at)

    def shift(self, axis, k):
        return self.shifts[axis, k]

    def device(self, axis, k):
        return self.devices[axis, k]

    def enter(self, axes):
        barrier = pltpu.get_barrier_semaphore()
        sizes = dict(y=self.ny, x=self.nx, z=self.nz, c=2, d=self.nd, f=self.nf)
        count = 0
        for axis in axes:
            for k in range(1, sizes[axis]):
                count += 1
                pl.semaphore_signal(barrier, inc=1, device_id=self.device(axis, k), device_id_type=MESH)
        pl.semaphore_wait(barrier, count)


class Move:
    ins, in_specs, outs, out_specs, scratch, aliases = (), (), (), (), (), ()

    def bind(self, place, ins, outs, scratch):
        self.place, self.in_refs, self.out_refs, self.refs = place, ins, outs, scratch
        self.slots, self.local_slots, self.legs = {}, {}, []

    def copy(self, key, src, dst, axis, k):
        slot = self.slots.setdefault(key, len(self.slots))
        return pltpu.make_async_remote_copy(
            src_ref=src, dst_ref=dst, send_sem=self.refs[0].at[slot], recv_sem=self.refs[1].at[slot],
            device_id=self.place.device(axis, k), device_id_type=MESH,
        )

    def start(self, items):
        for item in items:
            self.copy(*item).start()

    def arrived(self, key, dst, axis, k):
        self.copy(key, dst, dst, axis, k).wait_recv()

    def drain(self, items):
        for item in items:
            self.copy(*item).wait_send()

    def local(self, key, src, dst):
        slot = self.local_slots.setdefault(key, len(self.local_slots))
        return pltpu.make_async_copy(src, dst, self.refs[2].at[slot])


class Held:
    def __init__(self, shape, kind):
        self.shape, self.dtype, self.ref = shape, kind, None


def part_of(ref, part, core):
    if part is None:
        return ref.at[:, :, :, core]
    if isinstance(part, int):
        return ref.at[part, :, :, :, core]
    return ref.at[:, :, :, core, :, part[0] : part[1]]


def block_of(array, part):
    rows, columns = array.shape[-2:]
    return (rows, part[1] - part[0]) if isinstance(part, tuple) else (rows, columns)


def legs_copies(sizes):
    ny, nx, nz = sizes
    return (nz - 1) + 4 * (nx - 1) + 4 * (ny - 1) + 1


class Gather(Move):
    def __init__(self, sizes, array, actions, begun=False, shard=None, load=False):
        ny, nx, nz = sizes
        self.begun, self.actions = begun, actions
        self.held = array if isinstance(array, Held) else None
        self.ins, self.in_specs = ([], []) if self.held else ([array], [ANY if begun else VMEM])
        if shard is not None:
            self.ins, self.in_specs = [array, shard], [ANY, VMEM]
        shape = array.shape if begun else (ny, nx, nz, 2) + array.shape
        self.outs, self.out_specs = [like(shape, array.dtype)], [ANY]
        parts = len({what[2:] for _, what in actions}) if actions else 3
        self.scratch = [DMA((legs_copies(sizes) * parts,)), DMA((legs_copies(sizes) * parts,)), DMA((parts + 3,))]
        if load:
            self.scratch.append(pltpu.VMEM(shape, array.dtype))
        self.aliases = [(0, 0)] if begun else []

    def act(self, what):
        if what[0] in "ld":
            part = what[1:]
            copy = self.local(("load", part), self.spot((slice(None),) * 4, part), self.held_part(part))
            return copy.start() if what[0] == "l" else copy.wait()
        op, leg, part = what[0], int(what[1]), what[2:]
        if op != "s":
            self.wait_leg(leg, part)
        if op != "w":
            self.start_leg(leg + (op == "n"), part)
        else:
            for each in self.legs:
                if each[1] == part:
                    self.drain(self.leaving(*each))

    def columns(self, part):
        width = self.out_refs[0].shape[-1]
        half = width // 2
        return {"": slice(None), "a": slice(0, half), "b": slice(half, width)}[part]

    def held_part(self, part):
        return self.refs[3].at[:, :, :, :, :, self.columns(part)]

    def spot(self, index, part):
        return self.out_refs[0].at[index + (slice(None), self.columns(part))]

    def items(self, leg):
        p, full = self.place, self.out_refs[0]
        y, x, z, c = p.y, p.x, p.z, p.c
        d = p.other
        xs, ys, zs = range(1, p.nx), range(1, p.ny), range(1, p.nz)
        back = p.shift
        if leg == 0:
            return [(("z", k), (y, x, z, c), (y, x, back("z", -k), c), "z", k) for k in zs]
        if leg == 1:
            return (
                [(("x", k), (y, x, p.low, c), (y, back("x", -k), p.low, c), "x", k) for k in xs]
                + [(("y", k), (y, x, p.high, c), (back("y", -k), x, p.high, c), "y", k) for k in ys]
                + [("c", (y, x, slice(None), c), (y, x, slice(None), d), "c", 1)]
            )
        every = slice(None)
        if leg == 2:
            return (
                [(("xy", k), (y, every, p.low, c), (back("y", -k), every, p.low, c), "y", k) for k in ys]
                + [(("yx", k), (every, x, p.high, c), (every, back("x", -k), p.high, c), "x", k) for k in xs]
                + [(("cx", k), (y, back("x", -k), p.low, c), (y, back("x", -k), p.low, d), "c", 1) for k in xs]
                + [(("cy", k), (back("y", -k), x, p.high, c), (back("y", -k), x, p.high, d), "c", 1) for k in ys]
            )
        return [
            (("cxy", k), (back("y", -k), every, p.low, c), (back("y", -k), every, p.low, d), "c", 1) for k in ys
        ] + [(("cyx", k), (every, back("x", -k), p.high, c), (every, back("x", -k), p.high, d), "c", 1) for k in xs]

    def source(self):
        return self.held.ref if self.held else self.in_refs[-1]

    def own(self, part):
        p = self.place
        mine = self.source().at[:, self.columns(part)]
        return self.local(part, mine, self.spot((p.y, p.x, p.z, p.c), part))

    def leaving(self, leg, part):
        for key, leaves, _, axis, k in self.items(leg):
            to = self.spot(leaves, part)
            yield (key, part), self.source().at[:, self.columns(part)] if leg == 0 else to, to, axis, k

    def start_leg(self, leg, part):
        self.legs.append((leg, part))
        if leg == 0:
            self.own(part).start()
        self.start(self.leaving(leg, part))

    def wait_leg(self, leg, part):
        if leg == 0:
            self.own(part).wait()
        for key, _, arrives, axis, k in self.items(leg):
            self.arrived((key, part), self.spot(arrives, part), axis, k)


class Spread(Move):
    def __init__(self, sizes, array):
        ny, nx, nz = sizes
        self.ins, self.in_specs = [array], [VMEM]
        self.outs, self.out_specs = [like((ny * nx, 2 * nz) + array.shape, array.dtype)], [ANY]
        count = DMA((ny * nx + 2 * nz - 2,))
        self.scratch, self.actions = [count, count, DMA((1,))], ()

    def act(self, what):
        p, full = self.place, self.out_refs[0]
        own = ("own", self.in_refs[0], full.at[p.dp, p.fsdp])
        along = [(("f", k), self.in_refs[0], full.at[p.dp, p.fsdp], "f", k) for k in range(1, p.nf)]
        across = [(("d", k), full.at[p.dp], full.at[p.dp], "d", k) for k in range(1, p.nd)]
        if what == "0":
            self.local(*own).start()
            self.start(along)
        elif what == "1":
            self.local(*own).wait()
            for k in range(1, p.nf):
                self.arrived(("f", k), full.at[p.dp, p.shift("f", -k)], "f", k)
            self.start(across)
        else:
            for k in range(1, p.nd):
                self.arrived(("d", k), full.at[p.shift("d", -k)], "d", k)
            self.drain(along + across)


def add_blocks(into, where, counts, terms):
    total = 1
    for n in counts:
        total *= n

    def body(flat, carry):
        at = []
        for n in reversed(counts):
            at.append(lax.rem(flat, n))
            flat = lax.div(flat, n)
        at = tuple(at[::-1])
        spot = where(*at)
        value = into[spot].astype(f32)
        for ref, index in terms(*at):
            value = value + ref[index].astype(f32)
        into[spot] = value.astype(into.dtype)
        return carry

    lax.fori_loop(0, total, body, 0)


class Reduce(Move):
    def __init__(self, sizes, array, actions, part=None):
        self.actions, self.part = actions, part
        ny, nx, nz = sizes
        half, rest = nz // 2, nz - nz // 2
        block, kind = block_of(array, part), array.dtype
        self.held = array if isinstance(array, Held) else None
        self.ins, self.in_specs = ([], []) if self.held else ([array], [ANY])
        self.outs, self.out_specs = [like(block, f32)], [VMEM]
        shapes = [
            (ny, nx, nz), (ny, nx, nz), (ny - 1, nx, half), (nx - 1, ny, rest), (nx - 1, half), (ny - 1, rest), (nz - 1,)
        ]
        count = DMA((1 + 2 * (nx - 1) + 2 * (ny - 1) + nz - 1,))
        self.scratch = [count, count, DMA((1,))] + [pltpu.VMEM(a + block, kind) for a in shapes]

    def act(self, what):
        p, stage = self.place, int(what)
        y, x, z = p.y, p.x, p.z
        source = self.held.ref if self.held else self.in_refs[0]
        acc, core, la, lb, ma, mb, last = self.refs[3:]
        own = ("own", part_of(source, self.part, p.c), acc)
        xs, ys, zs = range(1, p.nx), range(1, p.ny), range(1, p.nz)

        def leaving(at):
            if at == 0:
                return [("c", part_of(source, self.part, p.other), core, "c", 1)]
            if at == 1:
                return [(("y", k), acc.at[p.shift("y", k), :, p.low], la.at[k - 1], "y", k) for k in ys] + [
                    (("x", k), acc.at[:, p.shift("x", k), p.high], lb.at[k - 1], "x", k) for k in xs
                ]
            if at == 2:
                return [(("yx", k), acc.at[y, p.shift("x", k), p.low], ma.at[k - 1], "x", k) for k in xs] + [
                    (("xy", k), acc.at[p.shift("y", k), x, p.high], mb.at[k - 1], "y", k) for k in ys
                ]
            return [(("z", k), acc.at[y, x, p.shift("z", k)], last.at[k - 1], "z", k) for k in zs]

        if stage > 0:
            for key, _, to, axis, k in leaving(stage - 1):
                self.arrived(key, to, axis, k)
        if stage == 0:
            self.local(*own).start()
        elif stage == 1:
            self.local(*own).wait()
            add_blocks(acc, lambda *at: at, (p.ny, p.nx, p.nz), lambda *at: [(core, at)])
        elif stage == 2:
            add_blocks(
                acc, lambda i, j: (y, i, j), (p.nx, p.half), lambda i, j: [(la, (k, i, j)) for k in range(p.ny - 1)]
            )
            add_blocks(
                acc, lambda i, j: (i, x, p.half + j), (p.ny, p.rest),
                lambda i, j: [(lb, (k, i, j)) for k in range(p.nx - 1)],
            )
        elif stage == 3:
            add_blocks(acc, lambda j: (y, x, j), (p.half,), lambda j: [(ma, (k, j)) for k in range(p.nx - 1)])
            add_blocks(
                acc, lambda j: (y, x, p.half + j), (p.rest,), lambda j: [(mb, (k, j)) for k in range(p.ny - 1)]
            )
        if stage < 4:
            self.start(leaving(stage))
        else:
            value = acc[y, x, z].astype(f32)
            for k in range(p.nz - 1):
                value = value + last[k].astype(f32)
            self.out_refs[0][...] = value
            for at in range(4):
                self.drain(leaving(at))


class ReduceCore(Move):
    def __init__(self, sizes, array, actions, part=None):
        self.actions, self.part = actions, part
        ny, nx, nz = sizes
        self.held = array if isinstance(array, Held) else None
        self.ins, self.in_specs = ([], []) if self.held else ([array], [ANY])
        self.outs, self.out_specs = [like((ny, nx, nz) + block_of(array, part), array.dtype)], [ANY]
        self.scratch = [DMA((1,)), DMA((1,))]

    def act(self, what):
        p = self.place
        source = self.held.ref if self.held else self.in_refs[0]
        leaving = [("c", part_of(source, self.part, p.other), self.out_refs[0], "c", 1)]
        if what == "s":
            self.start(leaving)
        else:
            self.arrived("c", self.out_refs[0], "c", 1)
            self.drain(leaving)


class ReduceFirst(Move):
    def __init__(self, sizes, array, core, actions, part=None):
        self.actions, self.part, self.core = actions, part, core
        ny, nx, nz = sizes
        half, rest = nz // 2, nz - nz // 2
        block, kind = block_of(array, part), array.dtype
        self.held = array if isinstance(array, Held) else None
        self.ins = ([] if self.held else [array]) + ([] if isinstance(core, Move) else [core])
        self.in_specs = [ANY] * len(self.ins)
        self.outs = [
            like((ny - 1, nx, half) + block, kind), like((nx - 1, ny, rest) + block, kind),
            like((nx, half) + block, kind), like((ny, rest) + block, kind),
        ]
        self.out_specs = [ANY] * 4
        remote = DMA((nx + ny - 2,))
        self.scratch = [remote, remote, DMA((4,))] + [pltpu.VMEM((ny, nx, nz) + block, kind)] * 2

    def act(self, what):
        p = self.place
        source = self.held.ref if self.held else self.in_refs[0]
        core = self.core.out_refs[0] if isinstance(self.core, Move) else self.in_refs[-1]
        acc, buf = self.refs[3:]
        la, lb, ka, kb = self.out_refs
        loads = [("acc", part_of(source, self.part, p.c), acc), ("buf", core, buf)]
        leaving = [
            (("y", k), acc.at[p.shift("y", k), :, p.low], la.at[k - 1], "y", k) for k in range(1, p.ny)
        ] + [(("x", k), acc.at[:, p.shift("x", k), p.high], lb.at[k - 1], "x", k) for k in range(1, p.nx)]
        keeps = [("ka", acc.at[p.y, :, p.low], ka), ("kb", acc.at[:, p.x, p.high], kb)]
        if what == "l":
            for item in loads:
                self.local(*item).start()
        elif what == "a":
            for item in loads:
                self.local(*item).wait()
            add_blocks(acc, lambda *at: at, (p.ny, p.nx, p.nz), lambda *at: [(buf, at)])
            self.start(leaving)
            for item in keeps:
                self.local(*item).start()
        else:
            for k in range(1, p.ny):
                self.arrived(("y", k), la.at[k - 1], "y", k)
            for k in range(1, p.nx):
                self.arrived(("x", k), lb.at[k - 1], "x", k)
            for item in keeps:
                self.local(*item).wait()
            self.drain(leaving)


class ReduceSecond(Move):
    def __init__(self, sizes, first, actions):
        self.actions, self.first = actions, first
        ny, nx, nz = sizes
        half, rest = nz // 2, nz - nz // 2
        self.inside = isinstance(first, Move)
        arrays = first.outs if self.inside else first
        block, kind = arrays[0].shape[-2:], arrays[0].dtype
        self.ins, self.in_specs = ([], []) if self.inside else (list(arrays), [ANY] * 4)
        self.outs = [
            like((nx - 1, half) + block, kind), like((ny - 1, rest) + block, kind), like((nz,) + block, kind)
        ]
        self.out_specs = [ANY] * 3
        remote = DMA((nx + ny - 2,))
        self.scratch = [remote, remote, DMA((6,))] + [pltpu.VMEM(a.shape, kind) for a in arrays]

    def act(self, what):
        p = self.place
        arrays = self.first.out_refs if self.inside else self.in_refs
        bufs = self.refs[3:]
        la, lb, ka, kb = bufs
        ma, mb, kept = self.out_refs
        loads = [(i, a, b) for i, (a, b) in enumerate(zip(arrays, bufs))]
        leaving = [(("x", k), ka.at[p.shift("x", k)], ma.at[k - 1], "x", k) for k in range(1, p.nx)]
        leaving += [(("y", k), kb.at[p.shift("y", k)], mb.at[k - 1], "y", k) for k in range(1, p.ny)]
        keeps = [("ka", ka.at[p.x], kept.at[p.low]), ("kb", kb.at[p.y], kept.at[p.high])]
        if what == "l":
            for item in loads:
                self.local(*item).start()
        elif what == "a":
            for item in loads:
                self.local(*item).wait()
            add_blocks(ka, lambda *at: at, (p.nx, p.half), lambda i, j: [(la, (k, i, j)) for k in range(p.ny - 1)])
            add_blocks(kb, lambda *at: at, (p.ny, p.rest), lambda i, j: [(lb, (k, i, j)) for k in range(p.nx - 1)])
            self.start(leaving)
            for item in keeps:
                self.local(*item).start()
        else:
            for k in range(1, p.nx):
                self.arrived(("x", k), ma.at[k - 1], "x", k)
            for k in range(1, p.ny):
                self.arrived(("y", k), mb.at[k - 1], "y", k)
            for item in keeps:
                self.local(*item).wait()
            self.drain(leaving)


class ReduceLast(Move):
    def __init__(self, sizes, second, actions):
        self.actions, self.second = actions, second
        ny, nx, nz = sizes
        self.inside = isinstance(second, Move)
        arrays = second.outs if self.inside else second
        block, kind = arrays[0].shape[-2:], arrays[0].dtype
        self.ins, self.in_specs = ([], []) if self.inside else (list(arrays), [ANY] * 3)
        self.outs, self.out_specs = [like(block, f32)], [VMEM]
        self.scratch = [DMA((nz - 1,)), DMA((nz - 1,)), DMA((3,))] + [pltpu.VMEM(a.shape, kind) for a in arrays]
        self.scratch += [pltpu.VMEM((nz - 1,) + block, kind)]

    def act(self, what):
        p = self.place
        arrays = self.second.out_refs if self.inside else self.in_refs
        ma, mb, kept, last = self.refs[3:]
        loads = [(i, a, b) for i, (a, b) in enumerate(zip(arrays, (ma, mb, kept)))]
        leaving = [(("z", k), kept.at[p.shift("z", k)], last.at[k - 1], "z", k) for k in range(1, p.nz)]
        if what == "l":
            for item in loads:
                self.local(*item).start()
        elif what == "a":
            for item in loads:
                self.local(*item).wait()
            add_blocks(kept, lambda j: (j,), (p.half,), lambda j: [(ma, (k, j)) for k in range(p.nx - 1)])
            add_blocks(
                kept, lambda j: (p.half + j,), (p.rest,), lambda j: [(mb, (k, j)) for k in range(p.ny - 1)]
            )
            self.start(leaving)
        else:
            for k in range(1, p.nz):
                self.arrived(("z", k), last.at[k - 1], "z", k)
            value = kept[p.z].astype(f32)
            for k in range(p.nz - 1):
                value = value + last[k].astype(f32)
            self.out_refs[0][...] = value
            self.drain(leaving)


def run(
    kernel, grid, ins, outs, shapes, args, scratch=(), name=None, moves=(), sizes=None, group=None, axes="yxzc", script=None
):
    single = not isinstance(shapes, (list, tuple))
    outs, shapes = ([outs], [shapes]) if single else (list(outs), list(shapes))
    counts = len(ins), len(outs), len(scratch)
    all_ins, all_specs, all_outs = list(args), list(ins), list(shapes)
    all_out_specs, all_scratch, aliases = list(outs), list(scratch), {}
    for move in moves:
        for i, o in move.aliases:
            aliases[len(all_ins) + i] = len(all_outs) + o
        all_ins += list(move.ins)
        all_specs += list(move.in_specs)
        all_outs += list(move.outs)
        all_out_specs += list(move.out_specs)
        all_scratch += list(move.scratch)

    def body(*refs):
        refs = list(refs)

        def take(n):
            part = refs[:n]
            del refs[:n]
            return part

        mine_in = take(counts[0])
        moved_in = [take(len(m.ins)) for m in moves]
        mine_out = take(counts[1])
        moved_out = [take(len(m.outs)) for m in moves]
        mine_scratch = take(counts[2])
        place = Place(sizes) if moves else None
        for move, i, o in zip(moves, moved_in, moved_out):
            move.bind(place, i, o, take(len(move.scratch)))
        step = pl.program_id(0)

        def turn(at):
            for move in moves:
                for when, what in move.actions:
                    if when == at:
                        move.act(what)

        def play():
            for item in script:
                if isinstance(item, tuple):
                    item[0].act(item[1])
                else:
                    item(mine_in, mine_out, mine_scratch)

        if kernel is None:
            place.enter(axes)
            play()
            return

        for at in range(grid):
            if any(when == at for m in moves for when, _ in m.actions):

                @pl.when(step == at)
                def _(at=at):
                    if at == 0:
                        place.enter(axes)
                    turn(at)

        kernel(*mine_in, *mine_out, *mine_scratch)
        if moves:

            @pl.when(step == grid - 1)
            def _():
                turn(grid)
                if script is not None:
                    play()

    params = dict(vmem_limit_bytes=(63 if moves else 60) * 1024 * 1024)
    if moves:
        params.update(collective_id=group, has_side_effects=True)
    moved = sum(a.size * a.dtype.itemsize for a in args)
    results = pl.pallas_call(
        body,
        grid=(grid,),
        in_specs=all_specs,
        out_specs=all_out_specs,
        out_shape=all_outs,
        scratch_shapes=all_scratch,
        input_output_aliases=aliases,
        name=name,
        cost_estimate=pl.CostEstimate(flops=0, bytes_accessed=2 * moved, transcendentals=0),
        compiler_params=pltpu.CompilerParams(**params),
    )(*all_ins)
    return results[0] if single and not moves else results


def tables(clip_row, pad, count):
    frames = clip_row.shape[0]
    size = count // frames
    slots = jnp.arange(frames, dtype=jnp.int32)
    ends = jnp.sum(jnp.where(slots[None, :] <= slots[:, None], clip_row[None, :], 0), axis=1)
    clip_of = jnp.sum((slots[:, None] >= ends[None, :]).astype(jnp.int32), axis=1)
    starts = ends - clip_row
    start_of = jnp.sum(jnp.where(clip_of[:, None] == slots[None, :], starts[None, :], 0), axis=1)
    frame_pos = slots - start_of
    frame = jnp.arange(count, dtype=jnp.int32) // size
    lane = jnp.arange(LANE, dtype=jnp.int32) % HD
    frame_hot = frame[:, None] == lane[None, :]
    own = frame[:, None] == slots[None, :]
    clip_tok = jnp.sum(jnp.where(own, clip_of[None, :], 0), axis=1)
    pos_tok = jnp.sum(jnp.where(own, frame_pos[None, :], 0), axis=1)
    lane_own = lane[:, None] == slots[None, :]
    lane_clip = jnp.sum(jnp.where(lane_own, clip_of[None, :], 0), axis=1)
    lane_pos = jnp.sum(jnp.where(lane_own, frame_pos[None, :], 0), axis=1)
    seen = (
        (clip_tok[:, None] == lane_clip[None, :])
        & (pos_tok[:, None] <= lane_pos[None, :])
        & (pad[:, None] == 1)
    )
    see = jnp.where((lane[None, :] < frames) & ~seen, -1e30, 0.0).astype(bf16)
    quarter = HD // 4
    freq = 10000.0 ** (-jnp.arange(quarter, dtype=f32) / quarter)
    patch = jnp.arange(count, dtype=jnp.int32) % size
    angle = jnp.concatenate(
        [pos_tok.astype(f32)[:, None] * freq[None, :], patch.astype(f32)[:, None] * freq[None, :]],
        axis=1,
    )
    cosine, sine = jnp.cos(angle), jnp.sin(angle)
    cosine = jnp.concatenate([cosine] * 4, axis=1)
    sine = jnp.concatenate([-sine, sine, -sine, sine], axis=1)
    return see, frame_hot.astype(bf16), cosine, sine


def per_device(
    tokens, cotangent, clip_frames, levels, pad_mask, w_mod, b_mod, w_qkv, b_qkv, w_out, b_out,
    w_up, b_up, w_down, b_down, noise_table,
):
    count, width = tokens.shape
    frames = levels.shape[0]
    size = count // frames
    hidden = w_up.shape[1]
    ndev = width // w_up.shape[0]
    me = lax.axis_index("dp") * lax.axis_size("fsdp") + lax.axis_index("fsdp")

    dp, fsdp = lax.axis_size("dp"), lax.axis_size("fsdp")
    sizes = (dp // 2, 2, fsdp // 2)
    lead = sizes + (2,)

    def flat(array):
        return array.reshape(-1, array.shape[-1])

    def blocks(array, front=0):
        rows = array.shape[front] // ndev
        return array.reshape(array.shape[:front] + lead + (rows, array.shape[-1]))

    biases = [b_mod, b_qkv, b_out, b_up, b_down]
    lengths = [b.shape[0] for b in biases]
    spots = jnp.arange(8 * LANE, dtype=jnp.int32)
    mine_at = jnp.where(spots // (2 * frames) == me, jnp.tile(levels, spots.shape[0] // frames), 0)
    packed = jnp.concatenate([mine_at.astype(f32)] + [b.astype(f32) for b in biases])
    packed = jnp.pad(packed, (0, 16 * LANE - packed.shape[0])).reshape(16, LANE)
    table_pad = jnp.pad(noise_table, ((0, 0), (0, -noise_table.shape[1] % LANE)))
    part = Held(lead + (2 * frames, w_mod.shape[1] // 2), bf16)
    small = Spread(sizes, packed)
    qkv_w = Gather(sizes, w_qkv, ())
    out_w, up_w = Gather(sizes, w_out, ()), Gather(sizes, w_up, ())
    mod_sum = Reduce(sizes, part, ())

    def add_modulation(ins, _, scratch):
        part.ref = scratch[0]
        load = pltpu.make_async_copy(small.out_refs[0], scratch[1], scratch[2].at[0])
        load.start()
        load.wait()
        modulation_kernel(None, ins[0], ins[1], scratch[0], scratch[1], frames)

    head = run(
        None, 1, [VMEM] * 2, [], [], [table_pad, w_mod],
        [pltpu.VMEM(part.shape, bf16), pltpu.VMEM(small.outs[0].shape, f32), DMA((1,))], name="head",
        moves=[small, qkv_w, out_w, up_w, mod_sum], sizes=sizes, group=1, axes="df",
        script=[
            (small, "0"), (qkv_w, "s0a"), (qkv_w, "s0b"), (out_w, "s0"), (small, "1"), (small, "2"), add_modulation,
            (mod_sum, "0"), (qkv_w, "n0a"), (mod_sum, "1"), (qkv_w, "n0b"), (mod_sum, "2"), (qkv_w, "n1a"), (mod_sum, "3"),
            (up_w, "s0a"), (qkv_w, "n1b"), (mod_sum, "4"), (qkv_w, "n2a"), (qkv_w, "n2b"), (qkv_w, "w3a"), (qkv_w, "w3b"),
            (out_w, "w0"), (up_w, "w0a"),
        ],
    )
    small, qkv_w, out_w, up_w = head[:4]
    small = small.reshape(ndev, -1)
    all_levels = jnp.sum(small[:, : 8 * LANE], axis=0).reshape(-1, 2 * frames)[:ndev, :frames]
    all_levels = all_levels.reshape(-1).astype(jnp.int32)
    full_bias, at = [], 8 * LANE
    for length in lengths:
        full_bias.append(small[:, at : at + length].reshape(1, -1))
        at += length
    bias_mod, bias_qkv, bias_out, bias_up, bias_down = full_bias
    modulation = jnp.transpose(head[-1].reshape(2, frames, -1), (1, 0, 2)).reshape(frames, -1)
    modulation = (modulation + bias_mod).reshape(frames, 6, width)
    full_qkv = flat(qkv_w)
    see, frame_hot, cosine, sine = tables(clip_frames[0], pad_mask, count)

    acts = like((count, width), bf16)
    wide = like((count, width), f32)
    tall = like((count, hidden), bf16)
    row = whole((1, width))
    mod_row = pl.BlockSpec((1, 6, width), lambda i: (i, 0, 0))
    mod_all = whole((frames, 6, width))
    rows_bf = by_rows(size, width)
    def turn(start, count, index):
        return lambda i: index(jnp.clip(i - start, 0, count - 1))

    def held(shape):
        return pl.BlockSpec(shape, lambda i: (0,) * len(shape), pipeline_mode=pl.Buffered(1))

    pairs = width // LANE
    step = 512
    tiles = hidden // step
    m1, m2 = frames + pairs, 2 * frames + pairs
    steps = m2 + tiles
    rows_one = pl.BlockSpec((size, width), turn(0, frames, lambda i: (i, 0)))
    rows_two = pl.BlockSpec((size, width), turn(m1, frames, lambda i: (i, 0)))
    lanes_one = pl.BlockSpec((size, LANE), turn(0, frames, lambda i: (i, 0)))
    pair_one = pl.BlockSpec((count, LANE), turn(frames, pairs, lambda i: (0, i)))
    cols_one = pl.BlockSpec((count, step), turn(m2, tiles, lambda i: (0, i)))
    move_out = Gather(
        sizes, out_w, [(0, "s1"), (4, "n1"), (8, "n2"), (9, "w3"), (9, "l"), (m1, "d")], True, load=True
    )
    move_up = Gather(
        sizes, up_w,
        [
            (0, "s1a"), (0, "s0b"), (2, "n1a"), (5, "n0b"), (6, "n2a"), (7, "w3a"), (7, "la"), (9, "n1b"), (m2, "da"),
            (m2 + 1, "n2b"), (m2 + 2, "w3b"), (m2 + 2, "lb"), (m2 + tiles // 2, "db"),
        ], True, w_up, True,
    )
    move_down = Gather(
        sizes, w_down,
        [
            (1, "s0a"), (1, "s0b"), (8, "n0a"), (11, "n0b"), (11, "n1a"), (m2 + 3, "n1b"), (steps, "n2a"), (steps, "n2b"),
            (steps, "w3a"), (steps, "w3b"),
        ],
    )
    act_one, query, key, value, attended, aug, middle, attn, act_two, activated, slope, *moved = run(
        lambda *refs: forward_kernel(*refs, frames=frames, pairs=pairs, tiles=tiles, gathers=(move_out, move_up)), steps,
        [
            rows_one, pl.BlockSpec((1, 6, width), turn(0, frames, lambda i: (i, 0, 0))), held((width, 3 * width)),
            held((1, 3 * width)), lanes_one, lanes_one, held((count, LANE)), held((count, LANE)), rows_two,
            pl.BlockSpec((1, 6, width), turn(m1, frames, lambda i: (i, 0, 0))), held((1, width)),
            pl.BlockSpec((1, step), turn(m2, tiles, lambda i: (0, i))),
        ],
        [rows_one] * 4 + [pair_one] * 2 + [rows_two] * 3 + [cols_one] * 2,
        [acts] * 6 + [wide, acts, acts] + [tall] * 2,
        (
            tokens, modulation, full_qkv, bias_qkv, cosine, sine, see, frame_hot, tokens, modulation, bias_out, bias_up,
        ),
        [pltpu.VMEM((count, width), bf16)] * 5, name="fwd",
        moves=[move_out, move_up, move_down], sizes=sizes, group=2,
    )
    full_out, full_up, full_down = [flat(w) for w in moved]
    full = whole((count, width))
    cols_h = by_cols(count, step)
    acc = pltpu.VMEM((count, width), f32)
    deep = hidden // width
    block_out, d_branch, d_gate_two, bdown = run(
        down_kernel, deep, [by_cols(count, width), by_rows(width, width), row, full, full, mod_all],
        [full, full, whole((frames, width)), row],
        [acts, acts, like((frames, width), f32), like((1, width), f32)],
        (activated, full_down, bias_down, middle, cotangent, modulation), [acc], name="down",
    )
    wdown = run(
        weight_grad_kernel, tiles, [cols_h, full], by_rows(step, width), like((hidden, width), bf16),
        (activated, d_branch), name="wdown",
    )
    wdown = blocks(wdown)
    stacked = pl.BlockSpec((1, count, width), lambda i: (i, 0, 0))
    once = held((count, width))
    mod_once = held((frames, 6, width))
    halves = ((0, width // 2), (width // 2, width))
    steps = 2 * tiles + deep
    cores = [ReduceCore(sizes, wdown, [(0, "s"), (2 + 2 * i, "w")], h) for i, h in enumerate(halves)]
    firsts = [
        ReduceFirst(sizes, wdown, cores[0], [(2, "l"), (3, "a"), (9, "w")], halves[0]),
        ReduceFirst(sizes, wdown, cores[1], [(4, "l"), (5, "a"), (2 * tiles - 1, "w")], halves[1]),
    ]
    seconds = [
        ReduceSecond(sizes, firsts[0], [(9, "l"), (10, "a"), (2 * tiles + 1, "w")]),
        ReduceSecond(sizes, firsts[1], [(2 * tiles - 1, "l"), (2 * tiles, "a"), (steps, "w")]),
    ]
    last_a = ReduceLast(sizes, seconds[0], [(2 * tiles + 1, "l"), (2 * tiles + 1, "a"), (steps, "w")])
    bup, wup, d_middle, d_attn, stat_two, bout, *moved = run(
        lambda *refs: mlp_kernel(*refs, tiles=tiles, deep=deep), steps,
        [
            once, pl.BlockSpec((step, width), turn(0, tiles, lambda i: (i, 0))),
            pl.BlockSpec((count, step), turn(0, tiles, lambda i: (0, i))), once,
            pl.BlockSpec((width, width), turn(2 * tiles, deep, lambda i: (0, i))), once, once, once, mod_once,
        ],
        [
            pl.BlockSpec((1, step), turn(0, tiles, lambda i: (0, i))),
            pl.BlockSpec((width, step), turn(tiles, tiles, lambda i: (0, i))),
            once, once, held((frames, 3, width)), held((1, width)),
        ],
        [
            like((1, hidden), f32), like((width, hidden), bf16), wide, acts, like((frames, 3, width), f32),
            like((1, width), f32),
        ],
        (d_branch, full_down, slope, act_two, full_up, middle, cotangent, attn, modulation),
        [pltpu.VMEM((count, hidden), bf16), acc], name="mlpb",
        moves=cores + firsts + seconds + [last_a], sizes=sizes, group=6,
    )
    down_b, wdown_low = moved[13:16], moved[16]
    wup = blocks(wup)
    halves = ((0, hidden // 2), (hidden // 2, hidden))
    quarters = 4
    quarter = width // quarters
    steps = quarters + pairs + 3
    cores = [ReduceCore(sizes, wup, [(0, "s"), (2 + i, "w")], h) for i, h in enumerate(halves)]
    firsts = [
        ReduceFirst(sizes, wup, cores[0], [(2, "l"), (3, "a"), (7, "w")], halves[0]),
        ReduceFirst(sizes, wup, cores[1], [(3, "l"), (4, "a"), (9, "w")], halves[1]),
    ]
    seconds = [
        ReduceSecond(sizes, firsts[0], [(7, "l"), (7, "a"), (10, "w")]),
        ReduceSecond(sizes, firsts[1], [(9, "l"), (9, "a"), (12, "w")]),
    ]
    last_b = ReduceLast(sizes, down_b, [(0, "l"), (1, "a"), (5, "w")])
    last_a = ReduceLast(sizes, seconds[0], [(10, "l"), (10, "a"), (steps, "w")])
    pair_b = pl.BlockSpec((count, LANE), turn(quarters, pairs, lambda i: (0, i)))
    table_once = held((count, LANE))
    wout, d_projected, bqkv, wqkv, *moved = run(
        lambda *refs: attention_back_kernel(*refs, frames=frames, lead=quarters, pairs=pairs), steps,
        [
            once, pl.BlockSpec((quarter, width), turn(0, quarters, lambda i: (i, 0))),
            pl.BlockSpec((count, quarter), turn(0, quarters, lambda i: (0, i))),
        ] + [pair_b] * 5 + [table_once] * 3 + [once],
        [
            pl.BlockSpec((quarter, width), turn(0, quarters, lambda i: (i, 0))),
            pl.BlockSpec((3, count, LANE), turn(quarters, pairs, lambda i: (0, 0, i))),
            pl.BlockSpec((1, 3, LANE), turn(quarters, pairs, lambda i: (i, 0, 0))),
            pl.BlockSpec((1, width, width), turn(quarters + pairs, 3, lambda i: (i, 0, 0))),
        ],
        [
            like((width, width), bf16), like((3, count, width), bf16), like((pairs, 3, LANE), f32),
            like((3, width, width), bf16),
        ],
        (d_attn, full_out, attended, query, key, value, attended, aug, see, cosine, sine, act_one),
        [pltpu.VMEM((count, width), bf16), pltpu.VMEM((3, count, width), bf16), pltpu.VMEM((count, LANE), f32)],
        name="attb", moves=[last_b] + cores + firsts + seconds + [last_a], sizes=sizes, group=7,
    )
    wdown_high, up_b, wup_low = moved[0], moved[14:17], moved[17]
    wdown_grad = jnp.concatenate([wdown_low, wdown_high], axis=1)
    wout, wqkv = blocks(wout), blocks(wqkv, 1)

    bqkv = jnp.transpose(bqkv, (1, 0, 2)).reshape(1, -1)
    shares = [b.reshape(ndev, -1) for b in (bqkv, bout, bup, bdown)]
    packed = jnp.concatenate(shares, axis=1)
    bias_len = packed.shape[1]
    packed = jnp.pad(packed, ((0, 0), (0, 8 * LANE - bias_len))).reshape(-1, LANE)
    packed = blocks(packed)
    mod_block = Held((6 * frames, width), bf16)
    d_mod = Gather(sizes, mod_block, ())
    sums, bias = [], Reduce(sizes, packed, ())
    for i in range(3):
        sums.append(Reduce(sizes, wqkv, [(0, "0"), (1 + i // 2, "1")] + [(2, "2")] * (i == 0), i))
    halves = ((0, width // 2), (width // 2, width))
    sums += [Reduce(sizes, wout, [(0, "0")], h) for h in halves]
    last_b = ReduceLast(sizes, up_b, [(0, "l"), (0, "a"), (3, "w")])

    def pack_modulation(ins, outs, scratch):
        one, two, gate = outs[1], ins[5], ins[6]
        parts = [one[:, 0, :], one[:, 1, :], two[:, 0, :], two[:, 1, :], two[:, 2, :], gate[...]]
        scratch[1][...] = jnp.concatenate(parts, axis=0).astype(bf16)

    def set_block(refs):
        mod_block.ref = refs[-1]
        input_back_kernel(*refs[:5], *refs[7:9], refs[9])

    q, k, v, oa, ob = sums
    token_grad, stat_one, *moved = run(
        lambda *refs: set_block(refs), 3,
        [stacked, by_cols(width, width), once, once, mod_once, held((frames, 3, width)), held((frames, width))],
        [once, held((frames, 2, width))],
        [acts, like((frames, 2, width), f32)],
        (d_projected, full_qkv, tokens, d_middle, modulation, stat_two, d_gate_two),
        [acc, pltpu.VMEM(mod_block.shape, bf16)], name="dact1",
        moves=[d_mod] + sums + [last_b, bias], sizes=sizes, group=8, axes="yxzc",
        script=[
            (oa, "1"), (ob, "1"), (bias, "0"), pack_modulation, (d_mod, "s0"), (k, "2"), (q, "3"), (bias, "1"),
            (v, "2"), (k, "3"), (d_mod, "n0"), (oa, "2"), (bias, "2"), (ob, "2"), (v, "3"), (q, "4"), (d_mod, "n1"),
            (bias, "3"), (oa, "3"), (ob, "3"), (k, "4"), (d_mod, "n2"), (bias, "4"), (v, "4"), (d_mod, "w3"),
            (oa, "4"), (ob, "4"),
        ],
    )
    d_mod, grad_q, grad_k, grad_v, wout_low, wout_high, wup_high, bias_sum = moved[:8]
    wout_grad = jnp.concatenate([wout_low, wout_high], axis=1)
    wup_grad = jnp.concatenate([wup_low, wup_high], axis=1)
    wqkv_grad = jnp.concatenate([grad_q, grad_k, grad_v], axis=1)
    d_mod = jnp.transpose(d_mod.reshape(ndev, 6, frames, width), (0, 2, 1, 3))
    d_mod = d_mod.reshape(ndev * frames, -1)
    bias_sum = bias_sum.reshape(-1)[:bias_len]
    bias_grads, at = [], 0
    for share in shares:
        bias_grads.append(bias_sum[at : at + share.shape[1]])
        at += share.shape[1]
    hot = (all_levels[:, None] == jnp.arange(noise_table.shape[1], dtype=jnp.int32)[None, :]).astype(bf16)
    embedded = dot(hot, noise_table, NT)
    cond = jax.nn.silu(embedded).astype(bf16)
    wmod_grad = dot(cond, d_mod, TN)
    mine = b_mod.shape[0]
    bmod_grad = jnp.sum(lax.dynamic_slice(d_mod, (0, me * mine), (d_mod.shape[0], mine)).astype(f32), axis=0)
    gate = jax.nn.sigmoid(embedded)
    d_embed = dot(d_mod, w_mod, NT) * gate * (1.0 + embedded * (1.0 - gate))
    table_grad = lax.dot_general(
        d_embed, hot.astype(f32), TN, precision=lax.Precision.HIGHEST, preferred_element_type=f32
    )
    return (
        block_out, token_grad, wmod_grad, bmod_grad, wqkv_grad, bias_grads[0], wout_grad, bias_grads[1],
        wup_grad, bias_grads[2], wdown_grad, bias_grads[3], table_grad,
    )


def solution(mesh):
    rows, vec = P(AXES, None), P(AXES)
    return jax.shard_map(
        per_device,
        mesh=mesh,
        in_specs=(rows, rows, rows, vec, vec) + (rows, vec) * 5 + (rows,),
        out_specs=(rows, rows) + (rows, vec) * 5 + (rows,),
        check_vma=False,
    )
```

```python
import jax
import jax.numpy as jnp
from jax import lax
from jax.experimental import pallas as pl
from jax.experimental.pallas import tpu as pltpu
from jax.sharding import PartitionSpec as P

bf16 = jnp.bfloat16
f32 = jnp.float32
AXES = ("dp", "fsdp")
HD = 64
LANE = 128
EPS = 1e-06
NN = (((1,), (0,)), ((), ()))
NT = (((1,), (1,)), ((), ()))
TN = (((0,), (0,)), ((), ()))


def dot(left, right, dims):
    return lax.dot_general(left, right, dims, preferred_element_type=f32)


def lanes(shape):
    return lax.broadcasted_iota(jnp.int32, shape, 1)


def normalize(values):
    centred = values - jnp.mean(values, axis=1, keepdims=True)
    inverse = lax.rsqrt(jnp.mean(centred * centred, axis=1, keepdims=True) + EPS)
    return centred * inverse, inverse


def normalize_back(grad, normed, inverse):
    return inverse * (
        grad
        - jnp.mean(grad, axis=1, keepdims=True)
        - normed * jnp.mean(grad * normed, axis=1, keepdims=True)
    )


def col_sum(values):
    return jnp.sum(values.astype(f32), axis=0, keepdims=True)


def partner(values):
    return jnp.where(
        lanes(values.shape) % HD < HD // 2,
        pltpu.roll(values, LANE - HD // 2, 1),
        pltpu.roll(values, HD // 2, 1),
    )


def carry_lanes(values):
    sub = lanes(values.shape) % HD
    high = values.astype(bf16).astype(f32)
    rest = values - high
    mid = rest.astype(bf16).astype(f32)
    return jnp.where(
        sub == 8, high, jnp.where(sub == 9, mid, jnp.where(sub == 10, rest - mid, 0.0))
    )


def qkv_kernel(x_ref, mod_ref, w_ref, b_ref, cos_ref, sin_ref, act_ref, q_ref, k_ref, v_ref):
    normed, _ = normalize(x_ref[...].astype(f32))
    act = (normed * (1.0 + mod_ref[0, 1:2, :]) + mod_ref[0, 0:1, :]).astype(bf16)
    act_ref[...] = act
    width = x_ref.shape[1]
    cosine, sine = cos_ref[...], sin_ref[...]
    step = 2 * LANE
    for col in range(0, 3 * width, step):
        raw = dot(act, w_ref[:, col : col + step], NN) + b_ref[:, col : col + step].astype(f32)
        for sub in range(0, step, LANE):
            part = raw[:, sub : sub + LANE]
            at = (col + sub) % width
            if col < width:
                part = (part * cosine + partner(part) * sine).astype(bf16)
                q_ref[:, at : at + LANE] = (part.astype(f32) * 0.125).astype(bf16)
            elif col < 2 * width:
                k_ref[:, at : at + LANE] = (part * cosine + partner(part) * sine).astype(bf16)
            else:
                v_ref[:, at : at + LANE] = part.astype(bf16)


def attention_forward(q_ref, k_ref, v_ref, see_ref, hot_ref, out_ref, aug_ref, *, frames):
    rows_all = q_ref.shape[0]
    size = rows_all // frames
    low = lanes((rows_all, LANE)) < HD
    low_b = lanes((size, LANE)) < HD
    k, v, see = k_ref[...], v_ref[...], see_ref[...]
    one = jnp.ones_like(v)
    keys = (jnp.where(low, k, see), jnp.where(low, see, k))
    vals = (jnp.where(low, v, one), jnp.where(low, one, v))
    for i in range(frames):
        rows = slice(i * size, (i + 1) * size)
        width = (i + 1) * size
        q, hot = q_ref[rows, :], hot_ref[rows, :]
        query = (jnp.where(low_b, q, hot), jnp.where(low_b, hot, q))
        tops, outs = [], []
        for h in range(2):
            scores = dot(query[h], keys[h][:width], NT)
            top = jnp.max(scores, axis=1, keepdims=True)
            expo = jnp.exp(scores - top).astype(bf16)
            outs.append(dot(expo, vals[h][:width], NN))
            tops.append(top)
        num = jnp.where(low_b, outs[0], outs[1])
        den = jnp.where(low_b, outs[1], outs[0])
        out_ref[rows, :] = (num / pltpu.roll(den, HD, 1)).astype(bf16)
        lse = jnp.where(low_b, tops[1], tops[0]) + jnp.log(den)
        aug_ref[rows, :] = (carry_lanes(-lse) + hot.astype(f32)).astype(bf16)


def project_kernel(att_ref, x_ref, mod_ref, w_ref, b_ref, middle_ref, attn_ref, act_ref):
    attn = dot(att_ref[...], w_ref[...].reshape(-1, w_ref.shape[-1]), NN) + b_ref[...].astype(f32)
    attn_ref[...] = attn.astype(bf16)
    middle = x_ref[...].astype(f32) + mod_ref[0, 2:3, :] * attn
    middle_ref[...] = middle
    normed, _ = normalize(middle)
    act_ref[...] = (normed * (1.0 + mod_ref[0, 4:5, :]) + mod_ref[0, 3:4, :]).astype(bf16)


def up_kernel(act_ref, w_ref, b_ref, out_ref, slope_ref):
    hidden = dot(act_ref[...], w_ref[...].reshape(-1, w_ref.shape[-1]), NN) + b_ref[...].astype(f32)
    share = 0.5 * (1.0 + lax.erf(hidden * 0.7071067811865476))
    out_ref[...] = (hidden * share).astype(bf16)
    slope = share + hidden * jnp.exp(-0.5 * hidden * hidden) * 0.3989422804014327
    slope_ref[...] = slope.astype(bf16)


def down_kernel(
    act_ref, w_ref, b_ref, mid_ref, cot_ref, mod_ref, out_ref, dbr_ref, gate_ref, sum_ref, acc_ref
):
    step, last = pl.program_id(0), pl.num_programs(0) - 1
    part = dot(act_ref[...], w_ref[...], NN)

    @pl.when(step == 0)
    def _():
        acc_ref[...] = part

    @pl.when(step > 0)
    def _():
        acc_ref[...] += part

    @pl.when(step == last)
    def _():
        frames = mod_ref.shape[0]
        size = acc_ref.shape[0] // frames
        total = jnp.zeros((1, acc_ref.shape[1]), f32)
        for i in range(frames):
            rows = slice(i * size, (i + 1) * size)
            gate = mod_ref[i, 5:6, :]
            branch = acc_ref[rows, :] + b_ref[...].astype(f32)
            out_ref[rows, :] = (mid_ref[rows, :] + gate * branch).astype(bf16)
            upstream = cot_ref[rows, :].astype(f32)
            d_branch = (upstream * gate).astype(bf16)
            dbr_ref[rows, :] = d_branch
            gate_ref[i : i + 1, :] = col_sum(upstream * branch)
            total += col_sum(d_branch)
        sum_ref[...] = total


def hidden_back_kernel(dbr_ref, w_ref, slope_ref, out_ref, sum_ref):
    d_hidden = (dot(dbr_ref[...], w_ref[...], NT) * slope_ref[...].astype(f32)).astype(bf16)
    out_ref[...] = d_hidden
    sum_ref[...] = col_sum(d_hidden)


def mlp_back_kernel(
    dh_ref, w_ref, mid_ref, cot_ref, attn_ref, mod_ref, dmid_ref, datt_ref, stat_ref, sum_ref, acc_ref, step, last
):
    part = dot(dh_ref[...], w_ref[...], NT)

    @pl.when(step == 0)
    def _():
        acc_ref[...] = part

    @pl.when(step > 0)
    def _():
        acc_ref[...] += part

    @pl.when(step == last)
    def _():
        frames = mod_ref.shape[0]
        size = acc_ref.shape[0] // frames
        total = jnp.zeros((1, acc_ref.shape[1]), f32)
        for i in range(frames):
            rows = slice(i * size, (i + 1) * size)
            d_act = acc_ref[rows, :]
            normed, inverse = normalize(mid_ref[rows, :])
            stat_ref[i, 1:2, :] = col_sum(d_act)
            stat_ref[i, 2:3, :] = col_sum(d_act * normed)
            d_middle = cot_ref[rows, :].astype(f32) + normalize_back(
                d_act * (1.0 + mod_ref[i, 4:5, :]), normed, inverse
            )
            dmid_ref[rows, :] = d_middle
            stat_ref[i, 0:1, :] = col_sum(d_middle * attn_ref[rows, :].astype(f32))
            d_attn = (d_middle * mod_ref[i, 2:3, :]).astype(bf16)
            datt_ref[rows, :] = d_attn
            total += col_sum(d_attn)
        sum_ref[...] = total


def at_columns(ref, index, size):
    return ref.at[:, pl.ds(pl.multiple_of(index * size, size), size)]


def mlp_kernel(
    dbr_ref, wdown_ref, slope_ref, act_ref, wup_ref, mid_ref, cot_ref, attn_ref, mod_ref,
    bup_ref, out_ref, dmid_ref, datt_ref, stat_ref, sum_ref, dh_ref, acc_ref, mid_all, cot_all, attn_all, sems,
    *, tiles, deep,
):
    step = pl.program_id(0)
    size, wide = dh_ref.shape[1] // tiles, dh_ref.shape[1] // deep
    late = [
        (mid_ref, mid_all, sems.at[0]), (cot_ref, cot_all, sems.at[1]), (attn_ref, attn_all, sems.at[2])
    ]

    @pl.when(step == 1)
    def _():
        for item in late:
            pltpu.make_async_copy(*item).start()

    @pl.when(step == 2 * tiles)
    def _():
        for item in late:
            pltpu.make_async_copy(*item).wait()

    @pl.when(step < tiles)
    def _():
        hidden_back_kernel(dbr_ref, wdown_ref, slope_ref, at_columns(dh_ref, step, size), bup_ref)

    @pl.when((step >= tiles) & (step < 2 * tiles))
    def _():
        weight_grad_kernel(act_ref, at_columns(dh_ref, step - tiles, size), out_ref)

    @pl.when(step >= 2 * tiles)
    def _():
        mlp_back_kernel(
            at_columns(dh_ref, step - 2 * tiles, wide), wup_ref, mid_all, cot_all, attn_all, mod_ref,
            dmid_ref, datt_ref, stat_ref, sum_ref, acc_ref, step - 2 * tiles, deep - 1,
        )


def attention_back_kernel(
    da_ref, wout_ref, att_ref, q_ref, k_ref, v_ref, o_ref, aug_ref, see_ref, cos_ref, sin_ref, act_ref,
    gout_ref, out_ref, bias_ref, gqkv_ref, do_ref, dp_ref, acc_ref, *, frames, lead, pairs,
):
    step = pl.program_id(0)

    @pl.when(step < lead)
    def _():
        attended_back_kernel(
            da_ref, wout_ref, att_ref, at_columns(do_ref, step, do_ref.shape[1] // lead), gout_ref
        )

    @pl.when((step >= lead) & (step < lead + pairs))
    def _():
        at = step - lead
        attention_backward(
            q_ref, k_ref, v_ref, at_columns(do_ref, at, LANE), o_ref, aug_ref, see_ref, cos_ref, sin_ref,
            out_ref, bias_ref, acc_ref, frames=frames,
        )
        for i in range(3):
            dp_ref[i, :, pl.ds(pl.multiple_of(at * LANE, LANE), LANE)] = out_ref[i]

    @pl.when(step >= lead + pairs)
    def _():
        gqkv_ref[0] = dot(act_ref[...], dp_ref[step - lead - pairs], TN).astype(bf16)


def forward_kernel(
    x_ref, mod_ref, w_ref, b_ref, cos_ref, sin_ref, see_ref, hot_ref, again_ref, mod_again_ref, bout_ref, bup_ref,
    act_ref, q_ref, k_ref, v_ref, att_ref, aug_ref, middle_ref, attn_ref, act_two_ref, up_ref, slope_ref,
    q_all, k_all, v_all, att_all, act_all, *, frames, pairs, tiles, gathers,
):
    step = pl.program_id(0)
    size = x_ref.shape[0]
    marks = (frames, frames + pairs, 2 * frames + pairs)

    @pl.when(step < marks[0])
    def _():
        qkv_kernel(x_ref, mod_ref, w_ref, b_ref, cos_ref, sin_ref, act_ref, q_ref, k_ref, v_ref)
        rows = pl.ds(pl.multiple_of(step * size, size), size)
        for ref, every in ((q_ref, q_all), (k_ref, k_all), (v_ref, v_all)):
            every[rows, :] = ref[...]

    @pl.when((step >= marks[0]) & (step < marks[1]))
    def _():
        at = step - marks[0]
        q, k, v = [at_columns(ref, at, LANE) for ref in (q_all, k_all, v_all)]
        attention_forward(q, k, v, see_ref, hot_ref, att_ref, aug_ref, frames=frames)
        att_all[:, pl.ds(pl.multiple_of(at * LANE, LANE), LANE)] = att_ref[...]

    @pl.when((step >= marks[1]) & (step < marks[2]))
    def _():
        rows = pl.ds(pl.multiple_of((step - marks[1]) * size, size), size)
        weight = gathers[0].refs[3]
        project_kernel(
            att_all.at[rows, :], again_ref, mod_again_ref, weight, bout_ref, middle_ref, attn_ref, act_two_ref
        )
        act_all[rows, :] = act_two_ref[...]

    @pl.when(step >= marks[2])
    def _():
        width = up_ref.shape[1]
        at = pl.multiple_of((step - marks[2]) * width, width)
        up_kernel(act_all, gathers[1].refs[3].at[:, :, :, :, :, pl.ds(at, width)], bup_ref, up_ref, slope_ref)


def attention_backward(
    q_ref, k_ref, v_ref, do_ref, o_ref, aug_ref, see_ref, cos_ref, sin_ref, out_ref, sum_ref, acc_ref, *, frames
):
    rows_all = q_ref.shape[0]
    size = rows_all // frames
    low = lanes((rows_all, LANE)) < HD
    q, aug, grad = q_ref[...], aug_ref[...], do_ref[...]
    prod = grad.astype(f32) * o_ref[...].astype(f32)
    delta_low = jnp.sum(jnp.where(low, prod, 0.0), axis=1, keepdims=True)
    delta_high = jnp.sum(jnp.where(low, 0.0, prod), axis=1, keepdims=True)
    grad_aug = carry_lanes(jnp.where(low, -delta_high, -delta_low)).astype(bf16)
    query = (jnp.where(low, q, aug), jnp.where(low, aug, q))
    upper = (jnp.where(low, grad, grad_aug), jnp.where(low, grad_aug, grad))
    low_b = lanes((size, LANE)) < HD
    sub = lanes((size, LANE)) % HD
    ones = jnp.where((sub >= 8) & (sub <= 10), 1.0, 0.0).astype(bf16)
    sum_k = sum_v = jnp.zeros((1, LANE), f32)
    for j in range(frames):
        rows = slice(j * size, (j + 1) * size)
        start = j * size
        k, v, see = k_ref[rows, :], v_ref[rows, :], see_ref[rows, :] + ones
        keys = (jnp.where(low_b, k, see), jnp.where(low_b, see, k))
        vals = (jnp.where(low_b, v, ones), jnp.where(low_b, ones, v))
        dvs, dks, dqs = [], [], []
        for h in range(2):
            probs = jnp.exp(dot(keys[h], query[h][start:], NT))
            d_scores = (probs * dot(vals[h], upper[h][start:], NT)).astype(bf16)
            dvs.append(dot(probs.astype(bf16), grad[start:], NN))
            dks.append(dot(d_scores, q[start:], NN))
            dqs.append(dot(d_scores, k, TN))
        d_value = jnp.where(low_b, dvs[0], dvs[1]).astype(bf16)
        d_key = jnp.where(low_b, dks[0], dks[1])
        d_key = (d_key * cos_ref[rows, :] - partner(d_key) * sin_ref[rows, :]).astype(bf16)
        out_ref[1, rows, :] = d_key
        out_ref[2, rows, :] = d_value
        sum_k = sum_k + col_sum(d_key)
        sum_v = sum_v + col_sum(d_value)
        d_query = jnp.where(lanes(dqs[0].shape) < HD, dqs[0], dqs[1])
        if j == 0:
            acc_ref[...] = d_query
        else:
            acc_ref[start:, :] += d_query
    d_query = acc_ref[...] * 0.125
    d_query = (d_query * cos_ref[...] - partner(d_query) * sin_ref[...]).astype(bf16)
    out_ref[0] = d_query
    sum_ref[0, 0:1, :] = col_sum(d_query)
    sum_ref[0, 1:2, :] = sum_k
    sum_ref[0, 2:3, :] = sum_v


def input_back_kernel(dp_ref, w_ref, x_ref, dmid_ref, mod_ref, out_ref, stat_ref, acc_ref):
    step, last = pl.program_id(0), pl.num_programs(0) - 1
    part = dot(dp_ref[0], w_ref[...], NT)

    @pl.when(step == 0)
    def _():
        acc_ref[...] = part

    @pl.when(step > 0)
    def _():
        acc_ref[...] += part

    @pl.when(step == last)
    def _():
        frames = mod_ref.shape[0]
        size = acc_ref.shape[0] // frames
        for i in range(frames):
            rows = slice(i * size, (i + 1) * size)
            d_act = acc_ref[rows, :]
            normed, inverse = normalize(x_ref[rows, :].astype(f32))
            stat_ref[i, 0:1, :] = col_sum(d_act)
            stat_ref[i, 1:2, :] = col_sum(d_act * normed)
            back = normalize_back(d_act * (1.0 + mod_ref[i, 1:2, :]), normed, inverse)
            out_ref[rows, :] = (dmid_ref[rows, :] + back).astype(bf16)


def modulation_kernel(small_ref, table_ref, w_ref, part_ref, levels_ref, frames):
    ndev = part_ref.shape[0] * part_ref.shape[1] * part_ref.shape[2] * 2
    rows = levels_ref[...].reshape(ndev, levels_ref.shape[-2], LANE)
    spots = jnp.sum(rows[:, :8], axis=0).astype(jnp.int32)
    count = 2 * frames * ndev
    level = jnp.concatenate([spots[i : i + 1, :] for i in range(count // LANE)], axis=1)
    slot = lax.broadcasted_iota(jnp.int32, (table_ref.shape[1], count), 0)
    hot = jnp.where(slot == level, 1.0, 0.0).astype(bf16)
    embedded = dot(table_ref[...], hot, NN)
    cond = (embedded / (1.0 + jnp.exp(-embedded))).astype(bf16)
    half = part_ref.shape[-1]
    first = lax.broadcasted_iota(jnp.int32, (count, 1), 0) % (2 * frames) < frames
    step = 512
    for col in range(0, half, step):
        low = dot(cond, w_ref[:, col : col + step], TN)
        high = dot(cond, w_ref[:, half + col : half + col + step], TN)
        value = jnp.where(first, low, high)
        part_ref[..., col : col + step] = value.reshape(part_ref.shape[:-1] + (step,)).astype(part_ref.dtype)


def weight_grad_kernel(left_ref, right_ref, out_ref):
    out_ref[...] = dot(left_ref[...], right_ref[...], TN).astype(bf16)


def attended_back_kernel(da_ref, w_ref, att_ref, datt_ref, out_ref):
    datt_ref[...] = dot(da_ref[...], w_ref[...], NT).astype(bf16)
    out_ref[...] = dot(att_ref[...], da_ref[...], TN).astype(bf16)


def qkv_grad_kernel(left_ref, right_ref, out_ref):
    out_ref[0] = dot(left_ref[...], right_ref[0], TN).astype(bf16)


def like(shape, kind):
    return jax.ShapeDtypeStruct(shape, kind)


def whole(shape):
    return pl.BlockSpec(shape, lambda i: (0,) * len(shape))


def by_rows(size, width):
    return pl.BlockSpec((size, width), lambda i: (i, 0))


def by_cols(height, size):
    return pl.BlockSpec((height, size), lambda i: (0, i))


MESH = pl.DeviceIdType.MESH
ANY = pl.BlockSpec(memory_space=pl.ANY)
VMEM = pl.BlockSpec(memory_space=pltpu.VMEM)
DMA = pltpu.SemaphoreType.DMA


class Place:
    def __init__(self, sizes):
        self.ny, self.nx, self.nz = sizes
        self.half = self.nz // 2
        self.rest = self.nz - self.half
        self.low, self.high = pl.ds(0, self.half), pl.ds(self.half, self.rest)
        self.dp, self.fsdp = lax.axis_index("dp"), lax.axis_index("fsdp")
        self.y, self.x = lax.div(self.dp, self.nx), lax.rem(self.dp, self.nx)
        self.z, self.c = lax.div(self.fsdp, 2), lax.rem(self.fsdp, 2)

        self.shifts, self.devices = {}, {}
        for axis, size in dict(y=self.ny, x=self.nx, z=self.nz, c=2).items():
            for k in range(1, size):
                at = lax.rem(getattr(self, axis) + k, size)
                self.shifts[axis, k] = self.shifts[axis, k - size] = at
                self.devices[axis, k] = dict(
                    y=(at * self.nx + self.x, self.fsdp), x=(self.y * self.nx + at, self.fsdp),
                    z=(self.dp, at * 2 + self.c), c=(self.dp, self.z * 2 + at),
                )[axis]
        self.other = self.shifts["c", 1]
        self.nd, self.nf = self.ny * self.nx, self.nz * 2
        for k in range(1, self.nd):
            at = lax.rem(self.dp + k, self.nd)
            self.shifts["d", k] = self.shifts["d", k - self.nd] = at
            self.devices["d", k] = (at, self.fsdp)
        for k in range(1, self.nf):
            at = lax.rem(self.fsdp + k, self.nf)
            self.shifts["f", k] = self.shifts["f", k - self.nf] = at
            self.devices["f", k] = (self.dp, at)

    def shift(self, axis, k):
        return self.shifts[axis, k]

    def device(self, axis, k):
        return self.devices[axis, k]

    def enter(self, axes):
        barrier = pltpu.get_barrier_semaphore()
        sizes = dict(y=self.ny, x=self.nx, z=self.nz, c=2, d=self.nd, f=self.nf)
        count = 0
        for axis in axes:
            for k in range(1, sizes[axis]):
                count += 1
                pl.semaphore_signal(barrier, inc=1, device_id=self.device(axis, k), device_id_type=MESH)
        pl.semaphore_wait(barrier, count)


class Move:
    ins, in_specs, outs, out_specs, scratch, aliases = (), (), (), (), (), ()

    def bind(self, place, ins, outs, scratch):
        self.place, self.in_refs, self.out_refs, self.refs = place, ins, outs, scratch
        self.slots, self.local_slots, self.legs = {}, {}, []

    def copy(self, key, src, dst, axis, k):
        slot = self.slots.setdefault(key, len(self.slots))
        return pltpu.make_async_remote_copy(
            src_ref=src, dst_ref=dst, send_sem=self.refs[0].at[slot], recv_sem=self.refs[1].at[slot],
            device_id=self.place.device(axis, k), device_id_type=MESH,
        )

    def start(self, items):
        for item in items:
            self.copy(*item).start()

    def arrived(self, key, dst, axis, k):
        self.copy(key, dst, dst, axis, k).wait_recv()

    def drain(self, items):
        for item in items:
            self.copy(*item).wait_send()

    def local(self, key, src, dst):
        slot = self.local_slots.setdefault(key, len(self.local_slots))
        return pltpu.make_async_copy(src, dst, self.refs[2].at[slot])


class Held:
    def __init__(self, shape, kind):
        self.shape, self.dtype, self.ref = shape, kind, None


def part_of(ref, part, core):
    if part is None:
        return ref.at[:, :, :, core]
    if isinstance(part, int):
        return ref.at[part, :, :, :, core]
    return ref.at[:, :, :, core, :, part[0] : part[1]]


def block_of(array, part):
    rows, columns = array.shape[-2:]
    return (rows, part[1] - part[0]) if isinstance(part, tuple) else (rows, columns)


def legs_copies(sizes):
    ny, nx, nz = sizes
    return (nz - 1) + 4 * (nx - 1) + 4 * (ny - 1) + 1


class Gather(Move):
    def __init__(self, sizes, array, actions, begun=False, shard=None, load=False):
        ny, nx, nz = sizes
        self.begun, self.actions = begun, actions
        self.held = array if isinstance(array, Held) else None
        self.ins, self.in_specs = ([], []) if self.held else ([array], [ANY if begun else VMEM])
        if shard is not None:
            self.ins, self.in_specs = [array, shard], [ANY, VMEM]
        shape = array.shape if begun else (ny, nx, nz, 2) + array.shape
        self.outs, self.out_specs = [like(shape, array.dtype)], [ANY]
        parts = len({what[2:] for _, what in actions}) if actions else 3
        self.scratch = [DMA((legs_copies(sizes) * parts,)), DMA((legs_copies(sizes) * parts,)), DMA((parts + 3,))]
        if load:
            self.scratch.append(pltpu.VMEM(shape, array.dtype))
        self.aliases = [(0, 0)] if begun else []

    def act(self, what):
        if what[0] in "ld":
            part = what[1:]
            copy = self.local(("load", part), self.spot((slice(None),) * 4, part), self.held_part(part))
            return copy.start() if what[0] == "l" else copy.wait()
        op, leg, part = what[0], int(what[1]), what[2:]
        if op != "s":
            self.wait_leg(leg, part)
        if op != "w":
            self.start_leg(leg + (op == "n"), part)
        else:
            for each in self.legs:
                if each[1] == part:
                    self.drain(self.leaving(*each))

    def columns(self, part):
        width = self.out_refs[0].shape[-1]
        half = width // 2
        return {"": slice(None), "a": slice(0, half), "b": slice(half, width)}[part]

    def held_part(self, part):
        return self.refs[3].at[:, :, :, :, :, self.columns(part)]

    def spot(self, index, part):
        return self.out_refs[0].at[index + (slice(None), self.columns(part))]

    def items(self, leg):
        p, full = self.place, self.out_refs[0]
        y, x, z, c = p.y, p.x, p.z, p.c
        d = p.other
        xs, ys, zs = range(1, p.nx), range(1, p.ny), range(1, p.nz)
        back = p.shift
        if leg == 0:
            return [(("z", k), (y, x, z, c), (y, x, back("z", -k), c), "z", k) for k in zs]
        if leg == 1:
            return (
                [(("x", k), (y, x, p.low, c), (y, back("x", -k), p.low, c), "x", k) for k in xs]
                + [(("y", k), (y, x, p.high, c), (back("y", -k), x, p.high, c), "y", k) for k in ys]
                + [("c", (y, x, slice(None), c), (y, x, slice(None), d), "c", 1)]
            )
        every = slice(None)
        if leg == 2:
            return (
                [(("xy", k), (y, every, p.low, c), (back("y", -k), every, p.low, c), "y", k) for k in ys]
                + [(("yx", k), (every, x, p.high, c), (every, back("x", -k), p.high, c), "x", k) for k in xs]
                + [(("cx", k), (y, back("x", -k), p.low, c), (y, back("x", -k), p.low, d), "c", 1) for k in xs]
                + [(("cy", k), (back("y", -k), x, p.high, c), (back("y", -k), x, p.high, d), "c", 1) for k in ys]
            )
        return [
            (("cxy", k), (back("y", -k), every, p.low, c), (back("y", -k), every, p.low, d), "c", 1) for k in ys
        ] + [(("cyx", k), (every, back("x", -k), p.high, c), (every, back("x", -k), p.high, d), "c", 1) for k in xs]

    def source(self):
        return self.held.ref if self.held else self.in_refs[-1]

    def own(self, part):
        p = self.place
        mine = self.source().at[:, self.columns(part)]
        return self.local(part, mine, self.spot((p.y, p.x, p.z, p.c), part))

    def leaving(self, leg, part):
        for key, leaves, _, axis, k in self.items(leg):
            to = self.spot(leaves, part)
            yield (key, part), self.source().at[:, self.columns(part)] if leg == 0 else to, to, axis, k

    def start_leg(self, leg, part):
        self.legs.append((leg, part))
        if leg == 0:
            self.own(part).start()
        self.start(self.leaving(leg, part))

    def wait_leg(self, leg, part):
        if leg == 0:
            self.own(part).wait()
        for key, _, arrives, axis, k in self.items(leg):
            self.arrived((key, part), self.spot(arrives, part), axis, k)


class Spread(Move):
    def __init__(self, sizes, array):
        ny, nx, nz = sizes
        self.ins, self.in_specs = [array], [VMEM]
        self.outs, self.out_specs = [like((ny * nx, 2 * nz) + array.shape, array.dtype)], [ANY]
        count = DMA((ny * nx + 2 * nz - 2,))
        self.scratch, self.actions = [count, count, DMA((1,))], ()

    def act(self, what):
        p, full = self.place, self.out_refs[0]
        own = ("own", self.in_refs[0], full.at[p.dp, p.fsdp])
        along = [(("f", k), self.in_refs[0], full.at[p.dp, p.fsdp], "f", k) for k in range(1, p.nf)]
        across = [(("d", k), full.at[p.dp], full.at[p.dp], "d", k) for k in range(1, p.nd)]
        if what == "0":
            self.local(*own).start()
            self.start(along)
        elif what == "1":
            self.local(*own).wait()
            for k in range(1, p.nf):
                self.arrived(("f", k), full.at[p.dp, p.shift("f", -k)], "f", k)
            self.start(across)
        else:
            for k in range(1, p.nd):
                self.arrived(("d", k), full.at[p.shift("d", -k)], "d", k)
            self.drain(along + across)


def add_blocks(into, where, counts, terms):
    total = 1
    for n in counts:
        total *= n

    def body(flat, carry):
        at = []
        for n in reversed(counts):
            at.append(lax.rem(flat, n))
            flat = lax.div(flat, n)
        at = tuple(at[::-1])
        spot = where(*at)
        value = into[spot].astype(f32)
        for ref, index in terms(*at):
            value = value + ref[index].astype(f32)
        into[spot] = value.astype(into.dtype)
        return carry

    lax.fori_loop(0, total, body, 0)


class Reduce(Move):
    def __init__(self, sizes, array, actions, part=None, into=None):
        self.actions, self.part, self.into = actions, part, into
        ny, nx, nz = sizes
        half, rest = nz // 2, nz - nz // 2
        block, kind = block_of(array, part), array.dtype
        self.held = array if isinstance(array, Held) else None
        self.ins, self.in_specs = ([], []) if self.held else ([array], [ANY])
        self.outs, self.out_specs = ([like(block, f32)], [VMEM]) if into is None else ([], [])
        shapes = [
            (ny, nx, nz), (ny, nx, nz), (ny - 1, nx, half), (nx - 1, ny, rest), (nx - 1, half), (ny - 1, rest), (nz - 1,)
        ]
        count = DMA((1 + 2 * (nx - 1) + 2 * (ny - 1) + nz - 1,))
        self.scratch = [count, count, DMA((1,))] + [pltpu.VMEM(a + block, kind) for a in shapes]

    def act(self, what):
        p, stage = self.place, int(what)
        y, x, z = p.y, p.x, p.z
        source = self.held.ref if self.held else self.in_refs[0]
        acc, core, la, lb, ma, mb, last = self.refs[3:]
        own = ("own", part_of(source, self.part, p.c), acc)
        xs, ys, zs = range(1, p.nx), range(1, p.ny), range(1, p.nz)

        def leaving(at):
            if at == 0:
                return [("c", part_of(source, self.part, p.other), core, "c", 1)]
            if at == 1:
                return [(("y", k), acc.at[p.shift("y", k), :, p.low], la.at[k - 1], "y", k) for k in ys] + [
                    (("x", k), acc.at[:, p.shift("x", k), p.high], lb.at[k - 1], "x", k) for k in xs
                ]
            if at == 2:
                return [(("yx", k), acc.at[y, p.shift("x", k), p.low], ma.at[k - 1], "x", k) for k in xs] + [
                    (("xy", k), acc.at[p.shift("y", k), x, p.high], mb.at[k - 1], "y", k) for k in ys
                ]
            return [(("z", k), acc.at[y, x, p.shift("z", k)], last.at[k - 1], "z", k) for k in zs]

        if stage > 0:
            for key, _, to, axis, k in leaving(stage - 1):
                self.arrived(key, to, axis, k)
        if stage == 0:
            self.local(*own).start()
        elif stage == 1:
            self.local(*own).wait()
            add_blocks(acc, lambda *at: at, (p.ny, p.nx, p.nz), lambda *at: [(core, at)])
        elif stage == 2:
            add_blocks(
                acc, lambda i, j: (y, i, j), (p.nx, p.half), lambda i, j: [(la, (k, i, j)) for k in range(p.ny - 1)]
            )
            add_blocks(
                acc, lambda i, j: (i, x, p.half + j), (p.ny, p.rest),
                lambda i, j: [(lb, (k, i, j)) for k in range(p.nx - 1)],
            )
        elif stage == 3:
            add_blocks(acc, lambda j: (y, x, j), (p.half,), lambda j: [(ma, (k, j)) for k in range(p.nx - 1)])
            add_blocks(
                acc, lambda j: (y, x, p.half + j), (p.rest,), lambda j: [(mb, (k, j)) for k in range(p.ny - 1)]
            )
        if stage < 4:
            self.start(leaving(stage))
        else:
            value = acc[y, x, z].astype(f32)
            for k in range(p.nz - 1):
                value = value + last[k].astype(f32)
            if self.into is None:
                self.out_refs[0][...] = value
            else:
                held, start = self.into
                held.ref[:, start : start + value.shape[1]] = value
            for at in range(4):
                self.drain(leaving(at))


class ReduceCore(Move):
    def __init__(self, sizes, array, actions, part=None):
        self.actions, self.part = actions, part
        ny, nx, nz = sizes
        self.held = array if isinstance(array, Held) else None
        self.ins, self.in_specs = ([], []) if self.held else ([array], [ANY])
        self.outs, self.out_specs = [like((ny, nx, nz) + block_of(array, part), array.dtype)], [ANY]
        self.scratch = [DMA((1,)), DMA((1,))]

    def act(self, what):
        p = self.place
        source = self.held.ref if self.held else self.in_refs[0]
        leaving = [("c", part_of(source, self.part, p.other), self.out_refs[0], "c", 1)]
        if what == "s":
            self.start(leaving)
        else:
            self.arrived("c", self.out_refs[0], "c", 1)
            self.drain(leaving)


class ReduceFirst(Move):
    def __init__(self, sizes, array, core, actions, part=None):
        self.actions, self.part, self.core = actions, part, core
        ny, nx, nz = sizes
        half, rest = nz // 2, nz - nz // 2
        block, kind = block_of(array, part), array.dtype
        self.held = array if isinstance(array, Held) else None
        self.ins = ([] if self.held else [array]) + ([] if isinstance(core, Move) else [core])
        self.in_specs = [ANY] * len(self.ins)
        self.outs = [
            like((ny - 1, nx, half) + block, kind), like((nx - 1, ny, rest) + block, kind),
            like((nx, half) + block, kind), like((ny, rest) + block, kind),
        ]
        self.out_specs = [ANY] * 4
        remote = DMA((nx + ny - 2,))
        self.scratch = [remote, remote, DMA((4,))] + [pltpu.VMEM((ny, nx, nz) + block, kind)] * 2

    def act(self, what):
        p = self.place
        source = self.held.ref if self.held else self.in_refs[0]
        core = self.core.out_refs[0] if isinstance(self.core, Move) else self.in_refs[-1]
        acc, buf = self.refs[3:]
        la, lb, ka, kb = self.out_refs
        loads = [("acc", part_of(source, self.part, p.c), acc), ("buf", core, buf)]
        leaving = [
            (("y", k), acc.at[p.shift("y", k), :, p.low], la.at[k - 1], "y", k) for k in range(1, p.ny)
        ] + [(("x", k), acc.at[:, p.shift("x", k), p.high], lb.at[k - 1], "x", k) for k in range(1, p.nx)]
        keeps = [("ka", acc.at[p.y, :, p.low], ka), ("kb", acc.at[:, p.x, p.high], kb)]
        if what == "l":
            for item in loads:
                self.local(*item).start()
        elif what == "a":
            for item in loads:
                self.local(*item).wait()
            add_blocks(acc, lambda *at: at, (p.ny, p.nx, p.nz), lambda *at: [(buf, at)])
            self.start(leaving)
            for item in keeps:
                self.local(*item).start()
        else:
            for k in range(1, p.ny):
                self.arrived(("y", k), la.at[k - 1], "y", k)
            for k in range(1, p.nx):
                self.arrived(("x", k), lb.at[k - 1], "x", k)
            for item in keeps:
                self.local(*item).wait()
            self.drain(leaving)


class ReduceSecond(Move):
    def __init__(self, sizes, first, actions):
        self.actions, self.first = actions, first
        ny, nx, nz = sizes
        half, rest = nz // 2, nz - nz // 2
        self.inside = isinstance(first, Move)
        arrays = first.outs if self.inside else first
        block, kind = arrays[0].shape[-2:], arrays[0].dtype
        self.ins, self.in_specs = ([], []) if self.inside else (list(arrays), [ANY] * 4)
        self.outs = [
            like((nx - 1, half) + block, kind), like((ny - 1, rest) + block, kind), like((nz,) + block, kind)
        ]
        self.out_specs = [ANY] * 3
        remote = DMA((nx + ny - 2,))
        self.scratch = [remote, remote, DMA((6,))] + [pltpu.VMEM(a.shape, kind) for a in arrays]

    def act(self, what):
        p = self.place
        arrays = self.first.out_refs if self.inside else self.in_refs
        bufs = self.refs[3:]
        la, lb, ka, kb = bufs
        ma, mb, kept = self.out_refs
        loads = [(i, a, b) for i, (a, b) in enumerate(zip(arrays, bufs))]
        leaving = [(("x", k), ka.at[p.shift("x", k)], ma.at[k - 1], "x", k) for k in range(1, p.nx)]
        leaving += [(("y", k), kb.at[p.shift("y", k)], mb.at[k - 1], "y", k) for k in range(1, p.ny)]
        keeps = [("ka", ka.at[p.x], kept.at[p.low]), ("kb", kb.at[p.y], kept.at[p.high])]
        if what == "l":
            for item in loads:
                self.local(*item).start()
        elif what == "a":
            for item in loads:
                self.local(*item).wait()
            add_blocks(ka, lambda *at: at, (p.nx, p.half), lambda i, j: [(la, (k, i, j)) for k in range(p.ny - 1)])
            add_blocks(kb, lambda *at: at, (p.ny, p.rest), lambda i, j: [(lb, (k, i, j)) for k in range(p.nx - 1)])
            self.start(leaving)
            for item in keeps:
                self.local(*item).start()
        else:
            for k in range(1, p.nx):
                self.arrived(("x", k), ma.at[k - 1], "x", k)
            for k in range(1, p.ny):
                self.arrived(("y", k), mb.at[k - 1], "y", k)
            for item in keeps:
                self.local(*item).wait()
            self.drain(leaving)


class ReduceLast(Move):
    def __init__(self, sizes, second, actions):
        self.actions, self.second = actions, second
        ny, nx, nz = sizes
        self.inside = isinstance(second, Move)
        arrays = second.outs if self.inside else second
        block, kind = arrays[0].shape[-2:], arrays[0].dtype
        self.ins, self.in_specs = ([], []) if self.inside else (list(arrays), [ANY] * 3)
        self.outs, self.out_specs = [like(block, f32)], [VMEM]
        self.scratch = [DMA((nz - 1,)), DMA((nz - 1,)), DMA((3,))] + [pltpu.VMEM(a.shape, kind) for a in arrays]
        self.scratch += [pltpu.VMEM((nz - 1,) + block, kind)]

    def act(self, what):
        p = self.place
        arrays = self.second.out_refs if self.inside else self.in_refs
        ma, mb, kept, last = self.refs[3:]
        loads = [(i, a, b) for i, (a, b) in enumerate(zip(arrays, (ma, mb, kept)))]
        leaving = [(("z", k), kept.at[p.shift("z", k)], last.at[k - 1], "z", k) for k in range(1, p.nz)]
        if what == "l":
            for item in loads:
                self.local(*item).start()
        elif what == "a":
            for item in loads:
                self.local(*item).wait()
            add_blocks(kept, lambda j: (j,), (p.half,), lambda j: [(ma, (k, j)) for k in range(p.nx - 1)])
            add_blocks(
                kept, lambda j: (p.half + j,), (p.rest,), lambda j: [(mb, (k, j)) for k in range(p.ny - 1)]
            )
            self.start(leaving)
        else:
            for k in range(1, p.nz):
                self.arrived(("z", k), last.at[k - 1], "z", k)
            value = kept[p.z].astype(f32)
            for k in range(p.nz - 1):
                value = value + last[k].astype(f32)
            self.out_refs[0][...] = value
            self.drain(leaving)


def run(
    kernel, grid, ins, outs, shapes, args, scratch=(), name=None, moves=(), sizes=None, group=None, axes="yxzc", script=None
):
    single = not isinstance(shapes, (list, tuple))
    outs, shapes = ([outs], [shapes]) if single else (list(outs), list(shapes))
    counts = len(ins), len(outs), len(scratch)
    all_ins, all_specs, all_outs = list(args), list(ins), list(shapes)
    all_out_specs, all_scratch, aliases = list(outs), list(scratch), {}
    for move in moves:
        for i, o in move.aliases:
            aliases[len(all_ins) + i] = len(all_outs) + o
        all_ins += list(move.ins)
        all_specs += list(move.in_specs)
        all_outs += list(move.outs)
        all_out_specs += list(move.out_specs)
        all_scratch += list(move.scratch)

    def body(*refs):
        refs = list(refs)

        def take(n):
            part = refs[:n]
            del refs[:n]
            return part

        mine_in = take(counts[0])
        moved_in = [take(len(m.ins)) for m in moves]
        mine_out = take(counts[1])
        moved_out = [take(len(m.outs)) for m in moves]
        mine_scratch = take(counts[2])
        place = Place(sizes) if moves else None
        for move, i, o in zip(moves, moved_in, moved_out):
            move.bind(place, i, o, take(len(move.scratch)))
        step = pl.program_id(0)

        def turn(at):
            for move in moves:
                for when, what in move.actions:
                    if when == at:
                        move.act(what)

        def play():
            for item in script:
                if isinstance(item, tuple):
                    item[0].act(item[1])
                else:
                    item(mine_in, mine_out, mine_scratch)

        if kernel is None:
            place.enter(axes)
            play()
            return

        for at in range(grid):
            if any(when == at for m in moves for when, _ in m.actions):

                @pl.when(step == at)
                def _(at=at):
                    if at == 0:
                        place.enter(axes)
                    turn(at)

        kernel(*mine_in, *mine_out, *mine_scratch)
        if moves:

            @pl.when(step == grid - 1)
            def _():
                turn(grid)
                if script is not None:
                    play()

    params = dict(vmem_limit_bytes=(63 if moves else 60) * 1024 * 1024)
    if moves:
        params.update(collective_id=group, has_side_effects=True)
    moved = sum(a.size * a.dtype.itemsize for a in args)
    results = pl.pallas_call(
        body,
        grid=(grid,),
        in_specs=all_specs,
        out_specs=all_out_specs,
        out_shape=all_outs,
        scratch_shapes=all_scratch,
        input_output_aliases=aliases,
        name=name,
        cost_estimate=pl.CostEstimate(flops=0, bytes_accessed=2 * moved, transcendentals=0),
        compiler_params=pltpu.CompilerParams(**params),
    )(*all_ins)
    return results[0] if single and not moves else results


def tables(clip_row, pad, count):
    frames = clip_row.shape[0]
    size = count // frames
    slots = jnp.arange(frames, dtype=jnp.int32)
    ends = jnp.sum(jnp.where(slots[None, :] <= slots[:, None], clip_row[None, :], 0), axis=1)
    clip_of = jnp.sum((slots[:, None] >= ends[None, :]).astype(jnp.int32), axis=1)
    starts = ends - clip_row
    start_of = jnp.sum(jnp.where(clip_of[:, None] == slots[None, :], starts[None, :], 0), axis=1)
    frame_pos = slots - start_of
    frame = jnp.arange(count, dtype=jnp.int32) // size
    lane = jnp.arange(LANE, dtype=jnp.int32) % HD
    frame_hot = frame[:, None] == lane[None, :]
    own = frame[:, None] == slots[None, :]
    clip_tok = jnp.sum(jnp.where(own, clip_of[None, :], 0), axis=1)
    pos_tok = jnp.sum(jnp.where(own, frame_pos[None, :], 0), axis=1)
    lane_own = lane[:, None] == slots[None, :]
    lane_clip = jnp.sum(jnp.where(lane_own, clip_of[None, :], 0), axis=1)
    lane_pos = jnp.sum(jnp.where(lane_own, frame_pos[None, :], 0), axis=1)
    seen = (
        (clip_tok[:, None] == lane_clip[None, :])
        & (pos_tok[:, None] <= lane_pos[None, :])
        & (pad[:, None] == 1)
    )
    see = jnp.where((lane[None, :] < frames) & ~seen, -1e30, 0.0).astype(bf16)
    quarter = HD // 4
    freq = 10000.0 ** (-jnp.arange(quarter, dtype=f32) / quarter)
    patch = jnp.arange(count, dtype=jnp.int32) % size
    angle = jnp.concatenate(
        [pos_tok.astype(f32)[:, None] * freq[None, :], patch.astype(f32)[:, None] * freq[None, :]],
        axis=1,
    )
    cosine, sine = jnp.cos(angle), jnp.sin(angle)
    cosine = jnp.concatenate([cosine] * 4, axis=1)
    sine = jnp.concatenate([-sine, sine, -sine, sine], axis=1)
    return see, frame_hot.astype(bf16), cosine, sine


def per_device(
    tokens, cotangent, clip_frames, levels, pad_mask, w_mod, b_mod, w_qkv, b_qkv, w_out, b_out,
    w_up, b_up, w_down, b_down, noise_table,
):
    count, width = tokens.shape
    frames = levels.shape[0]
    size = count // frames
    hidden = w_up.shape[1]
    ndev = width // w_up.shape[0]
    me = lax.axis_index("dp") * lax.axis_size("fsdp") + lax.axis_index("fsdp")

    dp, fsdp = lax.axis_size("dp"), lax.axis_size("fsdp")
    sizes = (dp // 2, 2, fsdp // 2)
    lead = sizes + (2,)

    def flat(array):
        return array.reshape(-1, array.shape[-1])

    def blocks(array, front=0):
        rows = array.shape[front] // ndev
        return array.reshape(array.shape[:front] + lead + (rows, array.shape[-1]))

    biases = [b_mod, b_qkv, b_out, b_up, b_down]
    lengths = [b.shape[0] for b in biases]
    spots = jnp.arange(8 * LANE, dtype=jnp.int32)
    mine_at = jnp.where(spots // (2 * frames) == me, jnp.tile(levels, spots.shape[0] // frames), 0)
    packed = jnp.concatenate([mine_at.astype(f32)] + [b.astype(f32) for b in biases])
    packed = jnp.pad(packed, (0, 16 * LANE - packed.shape[0])).reshape(16, LANE)
    table_pad = jnp.pad(noise_table, ((0, 0), (0, -noise_table.shape[1] % LANE)))
    part = Held(lead + (2 * frames, w_mod.shape[1] // 2), f32)
    small = Spread(sizes, packed)
    qkv_w = Gather(sizes, w_qkv, ())
    out_w, up_w = Gather(sizes, w_out, ()), Gather(sizes, w_up, ())
    mod_sum = Reduce(sizes, part, ())

    def add_modulation(ins, _, scratch):
        part.ref = scratch[0]
        load = pltpu.make_async_copy(small.out_refs[0], scratch[1], scratch[2].at[0])
        load.start()
        load.wait()
        modulation_kernel(None, ins[0], ins[1], scratch[0], scratch[1], frames)

    head = run(
        None, 1, [VMEM] * 2, [], [], [table_pad, w_mod],
        [pltpu.VMEM(part.shape, f32), pltpu.VMEM(small.outs[0].shape, f32), DMA((1,))], name="head",
        moves=[small, qkv_w, out_w, up_w, mod_sum], sizes=sizes, group=1, axes="df",
        script=[
            (small, "0"), (qkv_w, "s0a"), (qkv_w, "s0b"), (out_w, "s0"), (small, "1"), (small, "2"), add_modulation,
            (mod_sum, "0"), (qkv_w, "n0a"), (mod_sum, "1"), (qkv_w, "n0b"), (mod_sum, "2"), (qkv_w, "n1a"), (mod_sum, "3"),
            (up_w, "s0a"), (qkv_w, "n1b"), (mod_sum, "4"), (qkv_w, "n2a"), (qkv_w, "n2b"), (qkv_w, "w3a"), (qkv_w, "w3b"),
            (out_w, "w0"), (up_w, "w0a"),
        ],
    )
    small, qkv_w, out_w, up_w = head[:4]
    small = small.reshape(ndev, -1)
    all_levels = jnp.sum(small[:, : 8 * LANE], axis=0).reshape(-1, 2 * frames)[:ndev, :frames]
    all_levels = all_levels.reshape(-1).astype(jnp.int32)
    full_bias, at = [], 8 * LANE
    for length in lengths:
        full_bias.append(small[:, at : at + length].reshape(1, -1))
        at += length
    bias_mod, bias_qkv, bias_out, bias_up, bias_down = full_bias
    modulation = jnp.transpose(head[-1].reshape(2, frames, -1), (1, 0, 2)).reshape(frames, -1)
    modulation = (modulation + bias_mod).reshape(frames, 6, width)
    full_qkv = flat(qkv_w)
    see, frame_hot, cosine, sine = tables(clip_frames[0], pad_mask, count)

    acts = like((count, width), bf16)
    wide = like((count, width), f32)
    tall = like((count, hidden), bf16)
    row = whole((1, width))
    mod_row = pl.BlockSpec((1, 6, width), lambda i: (i, 0, 0))
    mod_all = whole((frames, 6, width))
    rows_bf = by_rows(size, width)
    def turn(start, count, index):
        return lambda i: index(jnp.clip(i - start, 0, count - 1))

    def held(shape):
        return pl.BlockSpec(shape, lambda i: (0,) * len(shape), pipeline_mode=pl.Buffered(1))

    pairs = width // LANE
    step = 512
    tiles = hidden // step
    m1, m2 = frames + pairs, 2 * frames + pairs
    steps = m2 + tiles
    rows_one = pl.BlockSpec((size, width), turn(0, frames, lambda i: (i, 0)))
    rows_two = pl.BlockSpec((size, width), turn(m1, frames, lambda i: (i, 0)))
    lanes_one = pl.BlockSpec((size, LANE), turn(0, frames, lambda i: (i, 0)))
    pair_one = pl.BlockSpec((count, LANE), turn(frames, pairs, lambda i: (0, i)))
    cols_one = pl.BlockSpec((count, step), turn(m2, tiles, lambda i: (0, i)))
    move_out = Gather(
        sizes, out_w, [(0, "s1"), (4, "n1"), (8, "n2"), (9, "w3"), (9, "l"), (m1, "d")], True, load=True
    )
    move_up = Gather(
        sizes, up_w,
        [
            (0, "s1a"), (0, "s0b"), (2, "n1a"), (5, "n0b"), (6, "n2a"), (7, "w3a"), (7, "la"), (9, "n1b"), (m2, "da"),
            (m2 + 1, "n2b"), (m2 + 2, "w3b"), (m2 + 2, "lb"), (m2 + tiles // 2, "db"),
        ], True, w_up, True,
    )
    move_down = Gather(
        sizes, w_down,
        [
            (1, "s0a"), (1, "s0b"), (8, "n0a"), (11, "n0b"), (11, "n1a"), (m2 + 3, "n1b"), (steps, "n2a"), (steps, "n2b"),
            (steps, "w3a"), (steps, "w3b"),
        ],
    )
    act_one, query, key, value, attended, aug, middle, attn, act_two, activated, slope, *moved = run(
        lambda *refs: forward_kernel(*refs, frames=frames, pairs=pairs, tiles=tiles, gathers=(move_out, move_up)), steps,
        [
            rows_one, pl.BlockSpec((1, 6, width), turn(0, frames, lambda i: (i, 0, 0))), held((width, 3 * width)),
            held((1, 3 * width)), lanes_one, lanes_one, held((count, LANE)), held((count, LANE)), rows_two,
            pl.BlockSpec((1, 6, width), turn(m1, frames, lambda i: (i, 0, 0))), held((1, width)),
            pl.BlockSpec((1, step), turn(m2, tiles, lambda i: (0, i))),
        ],
        [rows_one] * 4 + [pair_one] * 2 + [rows_two] * 3 + [cols_one] * 2,
        [acts] * 6 + [wide, acts, acts] + [tall] * 2,
        (
            tokens, modulation, full_qkv, bias_qkv, cosine, sine, see, frame_hot, tokens, modulation, bias_out, bias_up,
        ),
        [pltpu.VMEM((count, width), bf16)] * 5, name="fwd",
        moves=[move_out, move_up, move_down], sizes=sizes, group=2,
    )
    full_out, full_up, full_down = [flat(w) for w in moved]
    full = whole((count, width))
    cols_h = by_cols(count, step)
    acc = pltpu.VMEM((count, width), f32)
    deep = hidden // width
    block_out, d_branch, d_gate_two, bdown = run(
        down_kernel, deep, [by_cols(count, width), by_rows(width, width), row, full, full, mod_all],
        [full, full, whole((frames, width)), row],
        [acts, acts, like((frames, width), f32), like((1, width), f32)],
        (activated, full_down, bias_down, middle, cotangent, modulation), [acc], name="down",
    )
    wdown = run(
        weight_grad_kernel, tiles, [cols_h, full], by_rows(step, width), like((hidden, width), bf16),
        (activated, d_branch), name="wdown",
    )
    wdown = blocks(wdown)
    stacked = pl.BlockSpec((1, count, width), lambda i: (i, 0, 0))
    once = held((count, width))
    mod_once = held((frames, 6, width))
    halves = ((0, width // 2), (width // 2, width))
    steps = 2 * tiles + deep
    sum_a = Reduce(
        sizes, wdown, [(0, "0"), (2, "1"), (tiles, "2"), (2 * tiles, "3"), (steps, "4")], halves[0]
    )
    core = ReduceCore(sizes, wdown, [(0, "s"), (3, "w")], halves[1])
    first = ReduceFirst(sizes, wdown, core, [(3, "l"), (4, "a"), (2 * tiles - 1, "w")], halves[1])
    second = ReduceSecond(sizes, first, [(2 * tiles - 1, "l"), (2 * tiles, "a"), (steps, "w")])
    bup, wup, d_middle, d_attn, stat_two, bout, *moved = run(
        lambda *refs: mlp_kernel(*refs, tiles=tiles, deep=deep), steps,
        [
            once, pl.BlockSpec((step, width), turn(0, tiles, lambda i: (i, 0))),
            pl.BlockSpec((count, step), turn(0, tiles, lambda i: (0, i))), once,
            pl.BlockSpec((width, width), turn(2 * tiles, deep, lambda i: (0, i))), ANY, ANY, ANY, mod_once,
        ],
        [
            pl.BlockSpec((1, step), turn(0, tiles, lambda i: (0, i))),
            pl.BlockSpec((width, step), turn(tiles, tiles, lambda i: (0, i))),
            once, once, held((frames, 3, width)), held((1, width)),
        ],
        [
            like((1, hidden), f32), like((width, hidden), bf16), wide, acts, like((frames, 3, width), f32),
            like((1, width), f32),
        ],
        (d_branch, full_down, slope, act_two, full_up, middle, cotangent, attn, modulation),
        [
            pltpu.VMEM((count, hidden), bf16), acc, acc, pltpu.VMEM((count, width), bf16),
            pltpu.VMEM((count, width), bf16), DMA((3,)),
        ],
        name="mlpb", moves=[sum_a, core, first, second], sizes=sizes, group=6,
    )
    wdown_low, down_b = moved[0], moved[6:9]
    wup = blocks(wup)
    halves = ((0, hidden // 2), (hidden // 2, hidden))
    quarters = 4
    quarter = width // quarters
    steps = quarters + pairs + 3
    sum_a = Reduce(sizes, wup, [(0, "0"), (2, "1"), (6, "2"), (9, "3"), (steps, "4")], halves[0])
    core = ReduceCore(sizes, wup, [(0, "s"), (3, "w")], halves[1])
    first = ReduceFirst(sizes, wup, core, [(3, "l"), (4, "a"), (9, "w")], halves[1])
    second = ReduceSecond(sizes, first, [(9, "l"), (9, "a"), (12, "w")])
    last_b = ReduceLast(sizes, down_b, [(0, "l"), (1, "a"), (5, "w")])
    pair_b = pl.BlockSpec((count, LANE), turn(quarters, pairs, lambda i: (0, i)))
    table_once = held((count, LANE))
    wout, d_projected, bqkv, wqkv, *moved = run(
        lambda *refs: attention_back_kernel(*refs, frames=frames, lead=quarters, pairs=pairs), steps,
        [
            once, pl.BlockSpec((quarter, width), turn(0, quarters, lambda i: (i, 0))),
            pl.BlockSpec((count, quarter), turn(0, quarters, lambda i: (0, i))),
        ] + [pair_b] * 5 + [table_once] * 3 + [once],
        [
            pl.BlockSpec((quarter, width), turn(0, quarters, lambda i: (i, 0))),
            pl.BlockSpec((3, count, LANE), turn(quarters, pairs, lambda i: (0, 0, i))),
            pl.BlockSpec((1, 3, LANE), turn(quarters, pairs, lambda i: (i, 0, 0))),
            pl.BlockSpec((1, width, width), turn(quarters + pairs, 3, lambda i: (i, 0, 0))),
        ],
        [
            like((width, width), bf16), like((3, count, width), bf16), like((pairs, 3, LANE), f32),
            like((3, width, width), bf16),
        ],
        (d_attn, full_out, attended, query, key, value, attended, aug, see, cosine, sine, act_one),
        [pltpu.VMEM((count, width), bf16), pltpu.VMEM((3, count, width), bf16), pltpu.VMEM((count, LANE), f32)],
        name="attb", moves=[last_b, sum_a, core, first, second], sizes=sizes, group=7,
    )
    wdown_high, wup_low, up_b = moved[0], moved[1], moved[7:10]
    wdown_grad = jnp.concatenate([wdown_low, wdown_high], axis=1)
    wout, wqkv = blocks(wout), blocks(wqkv, 1)

    bqkv = jnp.transpose(bqkv, (1, 0, 2)).reshape(1, -1)
    shares = [b.reshape(ndev, -1) for b in (bqkv, bout, bup, bdown)]
    packed = jnp.concatenate(shares, axis=1)
    bias_len = packed.shape[1]
    packed = jnp.pad(packed, ((0, 0), (0, 8 * LANE - bias_len))).reshape(-1, LANE)
    packed = blocks(packed)
    mod_block = Held((6 * frames, width), bf16)
    d_mod = Gather(sizes, mod_block, ())
    bias = Reduce(sizes, packed, ())
    qkv_out, out_out = Held((width // ndev, 3 * width), f32), Held((width // ndev, width), f32)
    marks = ([(0, "0"), (0, "1"), (1, "2"), (2, "3")], [(0, "0"), (0, "1"), (2, "2")], [(0, "0"), (1, "1")])
    q, k, v = [Reduce(sizes, wqkv, marks[i], i, (qkv_out, i * width)) for i in range(3)]
    halves = ((0, width // 2), (width // 2, width))
    oa = Reduce(sizes, wout, [(0, "0"), (2, "1")], halves[0], (out_out, 0))
    ob = Reduce(sizes, wout, [(0, "0")], halves[1], (out_out, width // 2))
    last_b = ReduceLast(sizes, up_b, [(0, "l"), (0, "a"), (3, "w")])

    def pack_modulation(ins, outs, scratch):
        one, two, gate = outs[1], ins[5], ins[6]
        parts = [one[:, 0, :], one[:, 1, :], two[:, 0, :], two[:, 1, :], two[:, 2, :], gate[...]]
        mod_block.ref = scratch[1]
        qkv_out.ref, out_out.ref = outs[2:]
        scratch[1][...] = jnp.concatenate(parts, axis=0).astype(bf16)

    def set_block(refs):
        input_back_kernel(*refs[:5], *refs[7:9], refs[11])

    token_grad, stat_one, wqkv_grad, wout_grad, *moved = run(
        lambda *refs: set_block(refs), 3,
        [stacked, by_cols(width, width), once, once, mod_once, held((frames, 3, width)), held((frames, width))],
        [once, held((frames, 2, width)), VMEM, VMEM],
        [acts, like((frames, 2, width), f32), like(qkv_out.shape, f32), like(out_out.shape, f32)],
        (d_projected, full_qkv, tokens, d_middle, modulation, stat_two, d_gate_two),
        [acc, pltpu.VMEM(mod_block.shape, bf16)], name="dact1",
        moves=[d_mod, q, k, v, oa, ob, last_b, bias], sizes=sizes, group=8,
        script=[
            (bias, "0"), pack_modulation, (d_mod, "s0"), (v, "2"), (k, "3"), (ob, "1"), (bias, "1"), (oa, "2"), (v, "3"),
            (d_mod, "n0"), (ob, "2"), (bias, "2"), (oa, "3"), (ob, "3"), (d_mod, "n1"), (bias, "3"), (q, "4"), (k, "4"),
            (d_mod, "n2"), (bias, "4"), (v, "4"), (d_mod, "w3"), (oa, "4"), (ob, "4"),
        ],
    )
    d_mod, wup_high, bias_sum = moved
    wup_grad = jnp.concatenate([wup_low, wup_high], axis=1)
    d_mod = jnp.transpose(d_mod.reshape(ndev, 6, frames, width), (0, 2, 1, 3))
    d_mod = d_mod.reshape(ndev * frames, -1)
    bias_sum = bias_sum.reshape(-1)[:bias_len]
    bias_grads, at = [], 0
    for share in shares:
        bias_grads.append(bias_sum[at : at + share.shape[1]])
        at += share.shape[1]
    hot = (all_levels[:, None] == jnp.arange(noise_table.shape[1], dtype=jnp.int32)[None, :]).astype(bf16)
    embedded = dot(hot, noise_table, NT)
    cond = jax.nn.silu(embedded).astype(bf16)
    wmod_grad = dot(cond, d_mod, TN)
    mine = b_mod.shape[0]
    bmod_grad = jnp.sum(lax.dynamic_slice(d_mod, (0, me * mine), (d_mod.shape[0], mine)).astype(f32), axis=0)
    gate = jax.nn.sigmoid(embedded)
    d_embed = dot(d_mod, w_mod, NT) * gate * (1.0 + embedded * (1.0 - gate))
    table_grad = lax.dot_general(
        d_embed, hot.astype(f32), TN, precision=lax.Precision.HIGHEST, preferred_element_type=f32
    )
    return (
        block_out, token_grad, wmod_grad, bmod_grad, wqkv_grad, bias_grads[0], wout_grad, bias_grads[1],
        wup_grad, bias_grads[2], wdown_grad, bias_grads[3], table_grad,
    )


def solution(mesh):
    rows, vec = P(AXES, None), P(AXES)
    return jax.shard_map(
        per_device,
        mesh=mesh,
        in_specs=(rows, rows, rows, vec, vec) + (rows, vec) * 5 + (rows,),
        out_specs=(rows, rows) + (rows, vec) * 5 + (rows,),
        check_vma=False,
    )
```

```python
import jax
import jax.numpy as jnp
from jax import lax
from jax.experimental import pallas as pl
from jax.experimental.pallas import tpu as pltpu
from jax.sharding import PartitionSpec as P

bf16 = jnp.bfloat16
f32 = jnp.float32
AXES = ("dp", "fsdp")
HD = 64
LANE = 128
EPS = 1e-06
NN = (((1,), (0,)), ((), ()))
NT = (((1,), (1,)), ((), ()))
TN = (((0,), (0,)), ((), ()))


def dot(left, right, dims):
    return lax.dot_general(left, right, dims, preferred_element_type=f32)


def lanes(shape):
    return lax.broadcasted_iota(jnp.int32, shape, 1)


def normalize(values):
    centred = values - jnp.mean(values, axis=1, keepdims=True)
    inverse = lax.rsqrt(jnp.mean(centred * centred, axis=1, keepdims=True) + EPS)
    return centred * inverse, inverse


def normalize_back(grad, normed, inverse):
    return inverse * (
        grad
        - jnp.mean(grad, axis=1, keepdims=True)
        - normed * jnp.mean(grad * normed, axis=1, keepdims=True)
    )


def col_sum(values):
    return jnp.sum(values.astype(f32), axis=0, keepdims=True)


def partner(values):
    return jnp.where(
        lanes(values.shape) % HD < HD // 2,
        pltpu.roll(values, LANE - HD // 2, 1),
        pltpu.roll(values, HD // 2, 1),
    )


def carry_lanes(values):
    sub = lanes(values.shape) % HD
    high = values.astype(bf16).astype(f32)
    rest = values - high
    mid = rest.astype(bf16).astype(f32)
    return jnp.where(
        sub == 8, high, jnp.where(sub == 9, mid, jnp.where(sub == 10, rest - mid, 0.0))
    )


def qkv_kernel(x_ref, mod_ref, w_ref, b_ref, cos_ref, sin_ref, act_ref, q_ref, k_ref, v_ref):
    normed, _ = normalize(x_ref[...].astype(f32))
    act = (normed * (1.0 + mod_ref[0, 1:2, :]) + mod_ref[0, 0:1, :]).astype(bf16)
    act_ref[...] = act
    width = x_ref.shape[1]
    cosine, sine = cos_ref[...], sin_ref[...]
    step = 2 * LANE
    for col in range(0, 3 * width, step):
        raw = dot(act, w_ref[:, col : col + step], NN) + b_ref[:, col : col + step].astype(f32)
        for sub in range(0, step, LANE):
            part = raw[:, sub : sub + LANE]
            at = (col + sub) % width
            if col < width:
                part = (part * cosine + partner(part) * sine).astype(bf16)
                q_ref[:, at : at + LANE] = (part.astype(f32) * 0.125).astype(bf16)
            elif col < 2 * width:
                k_ref[:, at : at + LANE] = (part * cosine + partner(part) * sine).astype(bf16)
            else:
                v_ref[:, at : at + LANE] = part.astype(bf16)


def attention_forward(q_ref, k_ref, v_ref, see_ref, hot_ref, out_ref, aug_ref, *, frames):
    rows_all = q_ref.shape[0]
    size = rows_all // frames
    low = lanes((rows_all, LANE)) < HD
    low_b = lanes((size, LANE)) < HD
    k, v, see = k_ref[...], v_ref[...], see_ref[...]
    one = jnp.ones_like(v)
    keys = (jnp.where(low, k, see), jnp.where(low, see, k))
    vals = (jnp.where(low, v, one), jnp.where(low, one, v))
    for i in range(frames):
        rows = slice(i * size, (i + 1) * size)
        width = (i + 1) * size
        q, hot = q_ref[rows, :], hot_ref[rows, :]
        query = (jnp.where(low_b, q, hot), jnp.where(low_b, hot, q))
        tops, outs = [], []
        for h in range(2):
            scores = dot(query[h], keys[h][:width], NT)
            top = jnp.max(scores, axis=1, keepdims=True)
            expo = jnp.exp(scores - top).astype(bf16)
            outs.append(dot(expo, vals[h][:width], NN))
            tops.append(top)
        num = jnp.where(low_b, outs[0], outs[1])
        den = jnp.where(low_b, outs[1], outs[0])
        out_ref[rows, :] = (num / pltpu.roll(den, HD, 1)).astype(bf16)
        lse = jnp.where(low_b, tops[1], tops[0]) + jnp.log(den)
        aug_ref[rows, :] = (carry_lanes(-lse) + hot.astype(f32)).astype(bf16)


def project_kernel(att_ref, x_ref, mod_ref, w_ref, b_ref, middle_ref, attn_ref, act_ref):
    attn = dot(att_ref[...], w_ref[...].reshape(-1, w_ref.shape[-1]), NN) + b_ref[...].astype(f32)
    attn_ref[...] = attn.astype(bf16)
    middle = x_ref[...].astype(f32) + mod_ref[0, 2:3, :] * attn
    middle_ref[...] = middle
    normed, _ = normalize(middle)
    act_ref[...] = (normed * (1.0 + mod_ref[0, 4:5, :]) + mod_ref[0, 3:4, :]).astype(bf16)


def up_kernel(act_ref, w_ref, b_ref, out_ref, slope_ref):
    hidden = dot(act_ref[...], w_ref[...].reshape(-1, w_ref.shape[-1]), NN) + b_ref[...].astype(f32)
    share = 0.5 * (1.0 + lax.erf(hidden * 0.7071067811865476))
    out_ref[...] = (hidden * share).astype(bf16)
    slope = share + hidden * jnp.exp(-0.5 * hidden * hidden) * 0.3989422804014327
    slope_ref[...] = slope.astype(bf16)


def down_kernel(
    act_ref, w_ref, b_ref, mid_ref, cot_ref, mod_ref, out_ref, dbr_ref, gate_ref, sum_ref, acc_ref
):
    step, last = pl.program_id(0), pl.num_programs(0) - 1
    part = dot(act_ref[...], w_ref[...], NN)

    @pl.when(step == 0)
    def _():
        acc_ref[...] = part

    @pl.when(step > 0)
    def _():
        acc_ref[...] += part

    @pl.when(step == last)
    def _():
        frames = mod_ref.shape[0]
        size = acc_ref.shape[0] // frames
        total = jnp.zeros((1, acc_ref.shape[1]), f32)
        for i in range(frames):
            rows = slice(i * size, (i + 1) * size)
            gate = mod_ref[i, 5:6, :]
            branch = acc_ref[rows, :] + b_ref[...].astype(f32)
            out_ref[rows, :] = (mid_ref[rows, :] + gate * branch).astype(bf16)
            upstream = cot_ref[rows, :].astype(f32)
            d_branch = (upstream * gate).astype(bf16)
            dbr_ref[rows, :] = d_branch
            gate_ref[i : i + 1, :] = col_sum(upstream * branch)
            total += col_sum(d_branch)
        sum_ref[...] = total


def hidden_back_kernel(dbr_ref, w_ref, slope_ref, out_ref, sum_ref):
    d_hidden = (dot(dbr_ref[...], w_ref[...], NT) * slope_ref[...].astype(f32)).astype(bf16)
    out_ref[...] = d_hidden
    sum_ref[...] = col_sum(d_hidden)


def mlp_back_kernel(
    dh_ref, w_ref, mid_ref, cot_ref, attn_ref, mod_ref, dmid_ref, datt_ref, stat_ref, sum_ref, acc_ref, step, last
):
    part = dot(dh_ref[...], w_ref[...], NT)

    @pl.when(step == 0)
    def _():
        acc_ref[...] = part

    @pl.when(step > 0)
    def _():
        acc_ref[...] += part

    @pl.when(step == last)
    def _():
        frames = mod_ref.shape[0]
        size = acc_ref.shape[0] // frames
        total = jnp.zeros((1, acc_ref.shape[1]), f32)
        for i in range(frames):
            rows = slice(i * size, (i + 1) * size)
            d_act = acc_ref[rows, :]
            normed, inverse = normalize(mid_ref[rows, :])
            stat_ref[i, 1:2, :] = col_sum(d_act)
            stat_ref[i, 2:3, :] = col_sum(d_act * normed)
            d_middle = cot_ref[rows, :].astype(f32) + normalize_back(
                d_act * (1.0 + mod_ref[i, 4:5, :]), normed, inverse
            )
            dmid_ref[rows, :] = d_middle
            stat_ref[i, 0:1, :] = col_sum(d_middle * attn_ref[rows, :].astype(f32))
            d_attn = (d_middle * mod_ref[i, 2:3, :]).astype(bf16)
            datt_ref[rows, :] = d_attn
            total += col_sum(d_attn)
        sum_ref[...] = total


def at_columns(ref, index, size):
    return ref.at[:, pl.ds(pl.multiple_of(index * size, size), size)]


def mlp_kernel(
    dbr_ref, wdown_ref, slope_ref, act_ref, wup_ref, mid_ref, cot_ref, attn_ref, mod_ref,
    bup_ref, out_ref, dmid_ref, datt_ref, stat_ref, sum_ref, dh_ref, acc_ref, mid_all, cot_all, attn_all, sems,
    *, tiles, deep,
):
    step = pl.program_id(0)
    size, wide = dh_ref.shape[1] // tiles, dh_ref.shape[1] // deep
    late = [
        (mid_ref, mid_all, sems.at[0]), (cot_ref, cot_all, sems.at[1]), (attn_ref, attn_all, sems.at[2])
    ]

    @pl.when(step == 1)
    def _():
        for item in late:
            pltpu.make_async_copy(*item).start()

    @pl.when(step == 2 * tiles)
    def _():
        for item in late:
            pltpu.make_async_copy(*item).wait()

    @pl.when(step < tiles)
    def _():
        hidden_back_kernel(dbr_ref, wdown_ref, slope_ref, at_columns(dh_ref, step, size), bup_ref)

    @pl.when((step >= tiles) & (step < 2 * tiles))
    def _():
        weight_grad_kernel(act_ref, at_columns(dh_ref, step - tiles, size), out_ref)

    @pl.when(step >= 2 * tiles)
    def _():
        mlp_back_kernel(
            at_columns(dh_ref, step - 2 * tiles, wide), wup_ref, mid_all, cot_all, attn_all, mod_ref,
            dmid_ref, datt_ref, stat_ref, sum_ref, acc_ref, step - 2 * tiles, deep - 1,
        )


def attention_back_kernel(
    da_ref, wout_ref, att_ref, q_ref, k_ref, v_ref, o_ref, aug_ref, see_ref, cos_ref, sin_ref, act_ref,
    gout_ref, out_ref, bias_ref, gqkv_ref, do_ref, dp_ref, acc_ref, *, frames, lead, pairs,
):
    step = pl.program_id(0)

    @pl.when(step < lead)
    def _():
        attended_back_kernel(
            da_ref, wout_ref, att_ref, at_columns(do_ref, step, do_ref.shape[1] // lead), gout_ref
        )

    @pl.when((step >= lead) & (step < lead + pairs))
    def _():
        at = step - lead
        attention_backward(
            q_ref, k_ref, v_ref, at_columns(do_ref, at, LANE), o_ref, aug_ref, see_ref, cos_ref, sin_ref,
            out_ref, bias_ref, acc_ref, frames=frames,
        )
        for i in range(3):
            dp_ref[i, :, pl.ds(pl.multiple_of(at * LANE, LANE), LANE)] = out_ref[i]

    @pl.when(step >= lead + pairs)
    def _():
        gqkv_ref[0] = dot(act_ref[...], dp_ref[step - lead - pairs], TN).astype(bf16)


def forward_kernel(
    x_ref, mod_ref, w_ref, b_ref, cos_ref, sin_ref, see_ref, hot_ref, again_ref, mod_again_ref, bout_ref, bup_ref,
    act_ref, q_ref, k_ref, v_ref, att_ref, aug_ref, middle_ref, attn_ref, act_two_ref, up_ref, slope_ref,
    q_all, k_all, v_all, att_all, act_all, *, frames, pairs, tiles, gathers,
):
    step = pl.program_id(0)
    size = x_ref.shape[0]
    marks = (frames, frames + pairs, 2 * frames + pairs)

    @pl.when(step < marks[0])
    def _():
        qkv_kernel(x_ref, mod_ref, w_ref, b_ref, cos_ref, sin_ref, act_ref, q_ref, k_ref, v_ref)
        rows = pl.ds(pl.multiple_of(step * size, size), size)
        for ref, every in ((q_ref, q_all), (k_ref, k_all), (v_ref, v_all)):
            every[rows, :] = ref[...]

    @pl.when((step >= marks[0]) & (step < marks[1]))
    def _():
        at = step - marks[0]
        q, k, v = [at_columns(ref, at, LANE) for ref in (q_all, k_all, v_all)]
        attention_forward(q, k, v, see_ref, hot_ref, att_ref, aug_ref, frames=frames)
        att_all[:, pl.ds(pl.multiple_of(at * LANE, LANE), LANE)] = att_ref[...]

    @pl.when((step >= marks[1]) & (step < marks[2]))
    def _():
        rows = pl.ds(pl.multiple_of((step - marks[1]) * size, size), size)
        weight = gathers[0].refs[3]
        project_kernel(
            att_all.at[rows, :], again_ref, mod_again_ref, weight, bout_ref, middle_ref, attn_ref, act_two_ref
        )
        act_all[rows, :] = act_two_ref[...]

    @pl.when(step >= marks[2])
    def _():
        width = up_ref.shape[1]
        at = pl.multiple_of((step - marks[2]) * width, width)
        up_kernel(act_all, gathers[1].refs[3].at[:, :, :, :, :, pl.ds(at, width)], bup_ref, up_ref, slope_ref)


def attention_backward(
    q_ref, k_ref, v_ref, do_ref, o_ref, aug_ref, see_ref, cos_ref, sin_ref, out_ref, sum_ref, acc_ref, *, frames
):
    rows_all = q_ref.shape[0]
    size = rows_all // frames
    low = lanes((rows_all, LANE)) < HD
    q, aug, grad = q_ref[...], aug_ref[...], do_ref[...]
    prod = grad.astype(f32) * o_ref[...].astype(f32)
    delta_low = jnp.sum(jnp.where(low, prod, 0.0), axis=1, keepdims=True)
    delta_high = jnp.sum(jnp.where(low, 0.0, prod), axis=1, keepdims=True)
    grad_aug = carry_lanes(jnp.where(low, -delta_high, -delta_low)).astype(bf16)
    query = (jnp.where(low, q, aug), jnp.where(low, aug, q))
    upper = (jnp.where(low, grad, grad_aug), jnp.where(low, grad_aug, grad))
    low_b = lanes((size, LANE)) < HD
    sub = lanes((size, LANE)) % HD
    ones = jnp.where((sub >= 8) & (sub <= 10), 1.0, 0.0).astype(bf16)
    sum_k = sum_v = jnp.zeros((1, LANE), f32)
    for j in range(frames):
        rows = slice(j * size, (j + 1) * size)
        start = j * size
        k, v, see = k_ref[rows, :], v_ref[rows, :], see_ref[rows, :] + ones
        keys = (jnp.where(low_b, k, see), jnp.where(low_b, see, k))
        vals = (jnp.where(low_b, v, ones), jnp.where(low_b, ones, v))
        dvs, dks, dqs = [], [], []
        for h in range(2):
            probs = jnp.exp(dot(keys[h], query[h][start:], NT))
            d_scores = (probs * dot(vals[h], upper[h][start:], NT)).astype(bf16)
            dvs.append(dot(probs.astype(bf16), grad[start:], NN))
            dks.append(dot(d_scores, q[start:], NN))
            dqs.append(dot(d_scores, k, TN))
        d_value = jnp.where(low_b, dvs[0], dvs[1]).astype(bf16)
        d_key = jnp.where(low_b, dks[0], dks[1])
        d_key = (d_key * cos_ref[rows, :] - partner(d_key) * sin_ref[rows, :]).astype(bf16)
        out_ref[1, rows, :] = d_key
        out_ref[2, rows, :] = d_value
        sum_k = sum_k + col_sum(d_key)
        sum_v = sum_v + col_sum(d_value)
        d_query = jnp.where(lanes(dqs[0].shape) < HD, dqs[0], dqs[1])
        if j == 0:
            acc_ref[...] = d_query
        else:
            acc_ref[start:, :] += d_query
    d_query = acc_ref[...] * 0.125
    d_query = (d_query * cos_ref[...] - partner(d_query) * sin_ref[...]).astype(bf16)
    out_ref[0] = d_query
    sum_ref[0, 0:1, :] = col_sum(d_query)
    sum_ref[0, 1:2, :] = sum_k
    sum_ref[0, 2:3, :] = sum_v


def input_back_kernel(dp_ref, w_ref, x_ref, dmid_ref, mod_ref, out_ref, stat_ref, acc_ref):
    step, last = pl.program_id(0), pl.num_programs(0) - 1
    part = dot(dp_ref[0], w_ref[...], NT)

    @pl.when(step == 0)
    def _():
        acc_ref[...] = part

    @pl.when(step > 0)
    def _():
        acc_ref[...] += part

    @pl.when(step == last)
    def _():
        frames = mod_ref.shape[0]
        size = acc_ref.shape[0] // frames
        for i in range(frames):
            rows = slice(i * size, (i + 1) * size)
            d_act = acc_ref[rows, :]
            normed, inverse = normalize(x_ref[rows, :].astype(f32))
            stat_ref[i, 0:1, :] = col_sum(d_act)
            stat_ref[i, 1:2, :] = col_sum(d_act * normed)
            back = normalize_back(d_act * (1.0 + mod_ref[i, 1:2, :]), normed, inverse)
            out_ref[rows, :] = (dmid_ref[rows, :] + back).astype(bf16)


def modulation_kernel(small_ref, table_ref, w_ref, part_ref, levels_ref, frames):
    ndev = part_ref.shape[0] * part_ref.shape[1] * part_ref.shape[2] * 2
    rows = levels_ref[...].reshape(ndev, levels_ref.shape[-2], LANE)
    spots = jnp.sum(rows[:, :8], axis=0).astype(jnp.int32)
    count = 2 * frames * ndev
    level = jnp.concatenate([spots[i : i + 1, :] for i in range(count // LANE)], axis=1)
    slot = lax.broadcasted_iota(jnp.int32, (table_ref.shape[1], count), 0)
    hot = jnp.where(slot == level, 1.0, 0.0).astype(bf16)
    embedded = dot(table_ref[...], hot, NN)
    cond = (embedded / (1.0 + jnp.exp(-embedded))).astype(bf16)
    half = part_ref.shape[-1]
    first = lax.broadcasted_iota(jnp.int32, (count, 1), 0) % (2 * frames) < frames
    step = 512
    for col in range(0, half, step):
        low = dot(cond, w_ref[:, col : col + step], TN)
        high = dot(cond, w_ref[:, half + col : half + col + step], TN)
        value = jnp.where(first, low, high)
        part_ref[..., col : col + step] = value.reshape(part_ref.shape[:-1] + (step,)).astype(part_ref.dtype)


def weight_grad_kernel(left_ref, right_ref, out_ref):
    out_ref[...] = dot(left_ref[...], right_ref[...], TN).astype(bf16)


def attended_back_kernel(da_ref, w_ref, att_ref, datt_ref, out_ref):
    datt_ref[...] = dot(da_ref[...], w_ref[...], NT).astype(bf16)
    out_ref[...] = dot(att_ref[...], da_ref[...], TN).astype(bf16)


def qkv_grad_kernel(left_ref, right_ref, out_ref):
    out_ref[0] = dot(left_ref[...], right_ref[0], TN).astype(bf16)


def like(shape, kind):
    return jax.ShapeDtypeStruct(shape, kind)


def whole(shape):
    return pl.BlockSpec(shape, lambda i: (0,) * len(shape))


def by_rows(size, width):
    return pl.BlockSpec((size, width), lambda i: (i, 0))


def by_cols(height, size):
    return pl.BlockSpec((height, size), lambda i: (0, i))


MESH = pl.DeviceIdType.MESH
ANY = pl.BlockSpec(memory_space=pl.ANY)
VMEM = pl.BlockSpec(memory_space=pltpu.VMEM)
DMA = pltpu.SemaphoreType.DMA


class Place:
    def __init__(self, sizes):
        self.ny, self.nx, self.nz = sizes
        self.half = self.nz // 2
        self.rest = self.nz - self.half
        self.low, self.high = pl.ds(0, self.half), pl.ds(self.half, self.rest)
        self.dp, self.fsdp = lax.axis_index("dp"), lax.axis_index("fsdp")
        self.y, self.x = lax.div(self.dp, self.nx), lax.rem(self.dp, self.nx)
        self.z, self.c = lax.div(self.fsdp, 2), lax.rem(self.fsdp, 2)

        self.shifts, self.devices = {}, {}
        for axis, size in dict(y=self.ny, x=self.nx, z=self.nz, c=2).items():
            for k in range(1, size):
                at = lax.rem(getattr(self, axis) + k, size)
                self.shifts[axis, k] = self.shifts[axis, k - size] = at
                self.devices[axis, k] = dict(
                    y=(at * self.nx + self.x, self.fsdp), x=(self.y * self.nx + at, self.fsdp),
                    z=(self.dp, at * 2 + self.c), c=(self.dp, self.z * 2 + at),
                )[axis]
        self.other = self.shifts["c", 1]
        self.nd, self.nf = self.ny * self.nx, self.nz * 2
        for k in range(1, self.nd):
            at = lax.rem(self.dp + k, self.nd)
            self.shifts["d", k] = self.shifts["d", k - self.nd] = at
            self.devices["d", k] = (at, self.fsdp)
        for k in range(1, self.nf):
            at = lax.rem(self.fsdp + k, self.nf)
            self.shifts["f", k] = self.shifts["f", k - self.nf] = at
            self.devices["f", k] = (self.dp, at)

    def shift(self, axis, k):
        return self.shifts[axis, k]

    def device(self, axis, k):
        return self.devices[axis, k]

    def enter(self, axes):
        barrier = pltpu.get_barrier_semaphore()
        sizes = dict(y=self.ny, x=self.nx, z=self.nz, c=2, d=self.nd, f=self.nf)
        count = 0
        for axis in axes:
            for k in range(1, sizes[axis]):
                count += 1
                pl.semaphore_signal(barrier, inc=1, device_id=self.device(axis, k), device_id_type=MESH)
        pl.semaphore_wait(barrier, count)


class Move:
    ins, in_specs, outs, out_specs, scratch, aliases = (), (), (), (), (), ()

    def bind(self, place, ins, outs, scratch):
        self.place, self.in_refs, self.out_refs, self.refs = place, ins, outs, scratch
        self.slots, self.local_slots, self.legs = {}, {}, []

    def copy(self, key, src, dst, axis, k):
        slot = self.slots.setdefault(key, len(self.slots))
        return pltpu.make_async_remote_copy(
            src_ref=src, dst_ref=dst, send_sem=self.refs[0].at[slot], recv_sem=self.refs[1].at[slot],
            device_id=self.place.device(axis, k), device_id_type=MESH,
        )

    def start(self, items):
        for item in items:
            self.copy(*item).start()

    def arrived(self, key, dst, axis, k):
        self.copy(key, dst, dst, axis, k).wait_recv()

    def drain(self, items):
        for item in items:
            self.copy(*item).wait_send()

    def local(self, key, src, dst):
        slot = self.local_slots.setdefault(key, len(self.local_slots))
        return pltpu.make_async_copy(src, dst, self.refs[2].at[slot])


class Held:
    def __init__(self, shape, kind):
        self.shape, self.dtype, self.ref = shape, kind, None


def part_of(ref, part, core):
    if part is None:
        return ref.at[:, :, :, core]
    if isinstance(part, int):
        return ref.at[part, :, :, :, core]
    return ref.at[:, :, :, core, :, part[0] : part[1]]


def block_of(array, part):
    rows, columns = array.shape[-2:]
    return (rows, part[1] - part[0]) if isinstance(part, tuple) else (rows, columns)


def legs_copies(sizes):
    ny, nx, nz = sizes
    return (nz - 1) + 4 * (nx - 1) + 4 * (ny - 1) + 1


class Gather(Move):
    def __init__(self, sizes, array, actions, begun=False, shard=None, load=False):
        ny, nx, nz = sizes
        self.begun, self.actions = begun, actions
        self.held = array if isinstance(array, Held) else None
        self.ins, self.in_specs = ([], []) if self.held else ([array], [ANY if begun else VMEM])
        if shard is not None:
            self.ins, self.in_specs = [array, shard], [ANY, VMEM]
        shape = array.shape if begun else (ny, nx, nz, 2) + array.shape
        self.outs, self.out_specs = [like(shape, array.dtype)], [ANY]
        parts = len({what[2:] for _, what in actions}) if actions else 3
        self.scratch = [DMA((legs_copies(sizes) * parts,)), DMA((legs_copies(sizes) * parts,)), DMA((parts + 3,))]
        if load:
            self.scratch.append(pltpu.VMEM(shape, array.dtype))
        self.aliases = [(0, 0)] if begun else []

    def act(self, what):
        if what[0] in "ld":
            part = what[1:]
            copy = self.local(("load", part), self.spot((slice(None),) * 4, part), self.held_part(part))
            return copy.start() if what[0] == "l" else copy.wait()
        op, leg, part = what[0], int(what[1]), what[2:]
        if op != "s":
            self.wait_leg(leg, part)
        if op != "w":
            self.start_leg(leg + (op == "n"), part)
        else:
            for each in self.legs:
                if each[1] == part:
                    self.drain(self.leaving(*each))

    def columns(self, part):
        width = self.out_refs[0].shape[-1]
        half = width // 2
        return {"": slice(None), "a": slice(0, half), "b": slice(half, width)}[part]

    def held_part(self, part):
        return self.refs[3].at[:, :, :, :, :, self.columns(part)]

    def spot(self, index, part):
        return self.out_refs[0].at[index + (slice(None), self.columns(part))]

    def items(self, leg):
        p, full = self.place, self.out_refs[0]
        y, x, z, c = p.y, p.x, p.z, p.c
        d = p.other
        xs, ys, zs = range(1, p.nx), range(1, p.ny), range(1, p.nz)
        back = p.shift
        if leg == 0:
            return [(("z", k), (y, x, z, c), (y, x, back("z", -k), c), "z", k) for k in zs]
        if leg == 1:
            return (
                [(("x", k), (y, x, p.low, c), (y, back("x", -k), p.low, c), "x", k) for k in xs]
                + [(("y", k), (y, x, p.high, c), (back("y", -k), x, p.high, c), "y", k) for k in ys]
                + [("c", (y, x, slice(None), c), (y, x, slice(None), d), "c", 1)]
            )
        every = slice(None)
        if leg == 2:
            return (
                [(("xy", k), (y, every, p.low, c), (back("y", -k), every, p.low, c), "y", k) for k in ys]
                + [(("yx", k), (every, x, p.high, c), (every, back("x", -k), p.high, c), "x", k) for k in xs]
                + [(("cx", k), (y, back("x", -k), p.low, c), (y, back("x", -k), p.low, d), "c", 1) for k in xs]
                + [(("cy", k), (back("y", -k), x, p.high, c), (back("y", -k), x, p.high, d), "c", 1) for k in ys]
            )
        return [
            (("cxy", k), (back("y", -k), every, p.low, c), (back("y", -k), every, p.low, d), "c", 1) for k in ys
        ] + [(("cyx", k), (every, back("x", -k), p.high, c), (every, back("x", -k), p.high, d), "c", 1) for k in xs]

    def source(self):
        return self.held.ref if self.held else self.in_refs[-1]

    def own(self, part):
        p = self.place
        mine = self.source().at[:, self.columns(part)]
        return self.local(part, mine, self.spot((p.y, p.x, p.z, p.c), part))

    def leaving(self, leg, part):
        for key, leaves, _, axis, k in self.items(leg):
            to = self.spot(leaves, part)
            yield (key, part), self.source().at[:, self.columns(part)] if leg == 0 else to, to, axis, k

    def start_leg(self, leg, part):
        self.legs.append((leg, part))
        if leg == 0:
            self.own(part).start()
        self.start(self.leaving(leg, part))

    def wait_leg(self, leg, part):
        if leg == 0:
            self.own(part).wait()
        for key, _, arrives, axis, k in self.items(leg):
            self.arrived((key, part), self.spot(arrives, part), axis, k)


class Spread(Move):
    def __init__(self, sizes, array):
        ny, nx, nz = sizes
        self.ins, self.in_specs = [array], [VMEM]
        self.outs, self.out_specs = [like((ny * nx, 2 * nz) + array.shape, array.dtype)], [ANY]
        count = DMA((ny * nx + 2 * nz - 2,))
        self.scratch, self.actions = [count, count, DMA((1,))], ()

    def act(self, what):
        p, full = self.place, self.out_refs[0]
        own = ("own", self.in_refs[0], full.at[p.dp, p.fsdp])
        along = [(("f", k), self.in_refs[0], full.at[p.dp, p.fsdp], "f", k) for k in range(1, p.nf)]
        across = [(("d", k), full.at[p.dp], full.at[p.dp], "d", k) for k in range(1, p.nd)]
        if what == "0":
            self.local(*own).start()
            self.start(along)
        elif what == "1":
            self.local(*own).wait()
            for k in range(1, p.nf):
                self.arrived(("f", k), full.at[p.dp, p.shift("f", -k)], "f", k)
            self.start(across)
        else:
            for k in range(1, p.nd):
                self.arrived(("d", k), full.at[p.shift("d", -k)], "d", k)
            self.drain(along + across)


def add_blocks(into, where, counts, terms):
    total = 1
    for n in counts:
        total *= n

    def body(flat, carry):
        at = []
        for n in reversed(counts):
            at.append(lax.rem(flat, n))
            flat = lax.div(flat, n)
        at = tuple(at[::-1])
        spot = where(*at)
        value = into[spot].astype(f32)
        for ref, index in terms(*at):
            value = value + ref[index].astype(f32)
        into[spot] = value.astype(into.dtype)
        return carry

    lax.fori_loop(0, total, body, 0)


class Reduce(Move):
    def __init__(self, sizes, array, actions, part=None, into=None):
        self.actions, self.part, self.into = actions, part, into
        ny, nx, nz = sizes
        half, rest = nz // 2, nz - nz // 2
        block, kind = block_of(array, part), array.dtype
        self.held = array if isinstance(array, Held) else None
        self.ins, self.in_specs = ([], []) if self.held else ([array], [ANY])
        self.outs, self.out_specs = ([like(block, f32)], [VMEM]) if into is None else ([], [])
        shapes = [
            (ny, nx, nz), (ny, nx, nz), (ny - 1, nx, half), (nx - 1, ny, rest), (nx - 1, half), (ny - 1, rest), (nz - 1,)
        ]
        count = DMA((1 + 2 * (nx - 1) + 2 * (ny - 1) + nz - 1,))
        self.scratch = [count, count, DMA((1,))] + [pltpu.VMEM(a + block, kind) for a in shapes]

    def act(self, what):
        p, stage = self.place, int(what)
        y, x, z = p.y, p.x, p.z
        source = self.held.ref if self.held else self.in_refs[0]
        acc, core, la, lb, ma, mb, last = self.refs[3:]
        own = ("own", part_of(source, self.part, p.c), acc)
        xs, ys, zs = range(1, p.nx), range(1, p.ny), range(1, p.nz)

        def leaving(at):
            if at == 0:
                return [("c", part_of(source, self.part, p.other), core, "c", 1)]
            if at == 1:
                return [(("y", k), acc.at[p.shift("y", k), :, p.low], la.at[k - 1], "y", k) for k in ys] + [
                    (("x", k), acc.at[:, p.shift("x", k), p.high], lb.at[k - 1], "x", k) for k in xs
                ]
            if at == 2:
                return [(("yx", k), acc.at[y, p.shift("x", k), p.low], ma.at[k - 1], "x", k) for k in xs] + [
                    (("xy", k), acc.at[p.shift("y", k), x, p.high], mb.at[k - 1], "y", k) for k in ys
                ]
            return [(("z", k), acc.at[y, x, p.shift("z", k)], last.at[k - 1], "z", k) for k in zs]

        if stage > 0:
            for key, _, to, axis, k in leaving(stage - 1):
                self.arrived(key, to, axis, k)
        if stage == 0:
            self.local(*own).start()
        elif stage == 1:
            self.local(*own).wait()
            add_blocks(acc, lambda *at: at, (p.ny, p.nx, p.nz), lambda *at: [(core, at)])
        elif stage == 2:
            add_blocks(
                acc, lambda i, j: (y, i, j), (p.nx, p.half), lambda i, j: [(la, (k, i, j)) for k in range(p.ny - 1)]
            )
            add_blocks(
                acc, lambda i, j: (i, x, p.half + j), (p.ny, p.rest),
                lambda i, j: [(lb, (k, i, j)) for k in range(p.nx - 1)],
            )
        elif stage == 3:
            add_blocks(acc, lambda j: (y, x, j), (p.half,), lambda j: [(ma, (k, j)) for k in range(p.nx - 1)])
            add_blocks(
                acc, lambda j: (y, x, p.half + j), (p.rest,), lambda j: [(mb, (k, j)) for k in range(p.ny - 1)]
            )
        if stage < 4:
            self.start(leaving(stage))
        else:
            value = acc[y, x, z].astype(f32)
            for k in range(p.nz - 1):
                value = value + last[k].astype(f32)
            if self.into is None:
                self.out_refs[0][...] = value
            else:
                held, start = self.into
                held.ref[:, start : start + value.shape[1]] = value
            for at in range(4):
                self.drain(leaving(at))


class ReduceCore(Move):
    def __init__(self, sizes, array, actions, part=None):
        self.actions, self.part = actions, part
        ny, nx, nz = sizes
        self.held = array if isinstance(array, Held) else None
        self.ins, self.in_specs = ([], []) if self.held else ([array], [ANY])
        self.outs, self.out_specs = [like((ny, nx, nz) + block_of(array, part), array.dtype)], [ANY]
        self.scratch = [DMA((1,)), DMA((1,))]

    def act(self, what):
        p = self.place
        source = self.held.ref if self.held else self.in_refs[0]
        leaving = [("c", part_of(source, self.part, p.other), self.out_refs[0], "c", 1)]
        if what == "s":
            self.start(leaving)
        else:
            self.arrived("c", self.out_refs[0], "c", 1)
            self.drain(leaving)


class ReduceFirst(Move):
    def __init__(self, sizes, array, core, actions, part=None):
        self.actions, self.part, self.core = actions, part, core
        ny, nx, nz = sizes
        half, rest = nz // 2, nz - nz // 2
        block, kind = block_of(array, part), array.dtype
        self.held = array if isinstance(array, Held) else None
        self.ins = ([] if self.held else [array]) + ([] if isinstance(core, Move) else [core])
        self.in_specs = [ANY] * len(self.ins)
        self.outs = [
            like((ny - 1, nx, half) + block, kind), like((nx - 1, ny, rest) + block, kind),
            like((nx, half) + block, kind), like((ny, rest) + block, kind),
        ]
        self.out_specs = [ANY] * 4
        remote = DMA((nx + ny - 2,))
        self.scratch = [remote, remote, DMA((4,))] + [pltpu.VMEM((ny, nx, nz) + block, kind)] * 2

    def act(self, what):
        p = self.place
        source = self.held.ref if self.held else self.in_refs[0]
        core = self.core.out_refs[0] if isinstance(self.core, Move) else self.in_refs[-1]
        acc, buf = self.refs[3:]
        la, lb, ka, kb = self.out_refs
        loads = [("acc", part_of(source, self.part, p.c), acc), ("buf", core, buf)]
        leaving = [
            (("y", k), acc.at[p.shift("y", k), :, p.low], la.at[k - 1], "y", k) for k in range(1, p.ny)
        ] + [(("x", k), acc.at[:, p.shift("x", k), p.high], lb.at[k - 1], "x", k) for k in range(1, p.nx)]
        keeps = [("ka", acc.at[p.y, :, p.low], ka), ("kb", acc.at[:, p.x, p.high], kb)]
        if what == "l":
            for item in loads:
                self.local(*item).start()
        elif what == "a":
            for item in loads:
                self.local(*item).wait()
            add_blocks(acc, lambda *at: at, (p.ny, p.nx, p.nz), lambda *at: [(buf, at)])
            self.start(leaving)
            for item in keeps:
                self.local(*item).start()
        else:
            for k in range(1, p.ny):
                self.arrived(("y", k), la.at[k - 1], "y", k)
            for k in range(1, p.nx):
                self.arrived(("x", k), lb.at[k - 1], "x", k)
            for item in keeps:
                self.local(*item).wait()
            self.drain(leaving)


class ReduceSecond(Move):
    def __init__(self, sizes, first, actions):
        self.actions, self.first = actions, first
        ny, nx, nz = sizes
        half, rest = nz // 2, nz - nz // 2
        self.inside = isinstance(first, Move)
        arrays = first.outs if self.inside else first
        block, kind = arrays[0].shape[-2:], arrays[0].dtype
        self.ins, self.in_specs = ([], []) if self.inside else (list(arrays), [ANY] * 4)
        self.outs = [
            like((nx - 1, half) + block, kind), like((ny - 1, rest) + block, kind), like((nz,) + block, kind)
        ]
        self.out_specs = [ANY] * 3
        remote = DMA((nx + ny - 2,))
        self.scratch = [remote, remote, DMA((6,))] + [pltpu.VMEM(a.shape, kind) for a in arrays]

    def act(self, what):
        p = self.place
        arrays = self.first.out_refs if self.inside else self.in_refs
        bufs = self.refs[3:]
        la, lb, ka, kb = bufs
        ma, mb, kept = self.out_refs
        loads = [(i, a, b) for i, (a, b) in enumerate(zip(arrays, bufs))]
        leaving = [(("x", k), ka.at[p.shift("x", k)], ma.at[k - 1], "x", k) for k in range(1, p.nx)]
        leaving += [(("y", k), kb.at[p.shift("y", k)], mb.at[k - 1], "y", k) for k in range(1, p.ny)]
        keeps = [("ka", ka.at[p.x], kept.at[p.low]), ("kb", kb.at[p.y], kept.at[p.high])]
        if what == "l":
            for item in loads:
                self.local(*item).start()
        elif what == "a":
            for item in loads:
                self.local(*item).wait()
            add_blocks(ka, lambda *at: at, (p.nx, p.half), lambda i, j: [(la, (k, i, j)) for k in range(p.ny - 1)])
            add_blocks(kb, lambda *at: at, (p.ny, p.rest), lambda i, j: [(lb, (k, i, j)) for k in range(p.nx - 1)])
            self.start(leaving)
            for item in keeps:
                self.local(*item).start()
        else:
            for k in range(1, p.nx):
                self.arrived(("x", k), ma.at[k - 1], "x", k)
            for k in range(1, p.ny):
                self.arrived(("y", k), mb.at[k - 1], "y", k)
            for item in keeps:
                self.local(*item).wait()
            self.drain(leaving)


class ReduceLast(Move):
    def __init__(self, sizes, second, actions):
        self.actions, self.second = actions, second
        ny, nx, nz = sizes
        self.inside = isinstance(second, Move)
        arrays = second.outs if self.inside else second
        block, kind = arrays[0].shape[-2:], arrays[0].dtype
        self.ins, self.in_specs = ([], []) if self.inside else (list(arrays), [ANY] * 3)
        self.outs, self.out_specs = [like(block, f32)], [VMEM]
        self.scratch = [DMA((nz - 1,)), DMA((nz - 1,)), DMA((3,))] + [pltpu.VMEM(a.shape, kind) for a in arrays]
        self.scratch += [pltpu.VMEM((nz - 1,) + block, kind)]

    def act(self, what):
        p = self.place
        arrays = self.second.out_refs if self.inside else self.in_refs
        ma, mb, kept, last = self.refs[3:]
        loads = [(i, a, b) for i, (a, b) in enumerate(zip(arrays, (ma, mb, kept)))]
        leaving = [(("z", k), kept.at[p.shift("z", k)], last.at[k - 1], "z", k) for k in range(1, p.nz)]
        if what == "l":
            for item in loads:
                self.local(*item).start()
        elif what == "a":
            for item in loads:
                self.local(*item).wait()
            add_blocks(kept, lambda j: (j,), (p.half,), lambda j: [(ma, (k, j)) for k in range(p.nx - 1)])
            add_blocks(
                kept, lambda j: (p.half + j,), (p.rest,), lambda j: [(mb, (k, j)) for k in range(p.ny - 1)]
            )
            self.start(leaving)
        else:
            for k in range(1, p.nz):
                self.arrived(("z", k), last.at[k - 1], "z", k)
            value = kept[p.z].astype(f32)
            for k in range(p.nz - 1):
                value = value + last[k].astype(f32)
            self.out_refs[0][...] = value
            self.drain(leaving)


def run(
    kernel, grid, ins, outs, shapes, args, scratch=(), name=None, moves=(), sizes=None, group=None, axes="yxzc", script=None
):
    single = not isinstance(shapes, (list, tuple))
    outs, shapes = ([outs], [shapes]) if single else (list(outs), list(shapes))
    counts = len(ins), len(outs), len(scratch)
    all_ins, all_specs, all_outs = list(args), list(ins), list(shapes)
    all_out_specs, all_scratch, aliases = list(outs), list(scratch), {}
    for move in moves:
        for i, o in move.aliases:
            aliases[len(all_ins) + i] = len(all_outs) + o
        all_ins += list(move.ins)
        all_specs += list(move.in_specs)
        all_outs += list(move.outs)
        all_out_specs += list(move.out_specs)
        all_scratch += list(move.scratch)

    def body(*refs):
        refs = list(refs)

        def take(n):
            part = refs[:n]
            del refs[:n]
            return part

        mine_in = take(counts[0])
        moved_in = [take(len(m.ins)) for m in moves]
        mine_out = take(counts[1])
        moved_out = [take(len(m.outs)) for m in moves]
        mine_scratch = take(counts[2])
        place = Place(sizes) if moves else None
        for move, i, o in zip(moves, moved_in, moved_out):
            move.bind(place, i, o, take(len(move.scratch)))
        step = pl.program_id(0)

        def turn(at):
            for move in moves:
                for when, what in move.actions:
                    if when == at:
                        move.act(what)

        def play():
            for item in script:
                if isinstance(item, tuple):
                    item[0].act(item[1])
                else:
                    item(mine_in, mine_out, mine_scratch)

        if kernel is None:
            place.enter(axes)
            play()
            return

        for at in range(grid):
            if any(when == at for m in moves for when, _ in m.actions):

                @pl.when(step == at)
                def _(at=at):
                    if at == 0:
                        place.enter(axes)
                    turn(at)

        kernel(*mine_in, *mine_out, *mine_scratch)
        if moves:

            @pl.when(step == grid - 1)
            def _():
                turn(grid)
                if script is not None:
                    play()

    params = dict(vmem_limit_bytes=(63 if moves else 60) * 1024 * 1024)
    if moves:
        params.update(collective_id=group, has_side_effects=True)
    moved = sum(a.size * a.dtype.itemsize for a in args)
    results = pl.pallas_call(
        body,
        grid=(grid,),
        in_specs=all_specs,
        out_specs=all_out_specs,
        out_shape=all_outs,
        scratch_shapes=all_scratch,
        input_output_aliases=aliases,
        name=name,
        cost_estimate=pl.CostEstimate(flops=0, bytes_accessed=2 * moved, transcendentals=0),
        compiler_params=pltpu.CompilerParams(**params),
    )(*all_ins)
    return results[0] if single and not moves else results


def tables(clip_row, pad, count):
    frames = clip_row.shape[0]
    size = count // frames
    slots = jnp.arange(frames, dtype=jnp.int32)
    ends = jnp.sum(jnp.where(slots[None, :] <= slots[:, None], clip_row[None, :], 0), axis=1)
    clip_of = jnp.sum((slots[:, None] >= ends[None, :]).astype(jnp.int32), axis=1)
    starts = ends - clip_row
    start_of = jnp.sum(jnp.where(clip_of[:, None] == slots[None, :], starts[None, :], 0), axis=1)
    frame_pos = slots - start_of
    frame = jnp.arange(count, dtype=jnp.int32) // size
    lane = jnp.arange(LANE, dtype=jnp.int32) % HD
    frame_hot = frame[:, None] == lane[None, :]
    own = frame[:, None] == slots[None, :]
    clip_tok = jnp.sum(jnp.where(own, clip_of[None, :], 0), axis=1)
    pos_tok = jnp.sum(jnp.where(own, frame_pos[None, :], 0), axis=1)
    lane_own = lane[:, None] == slots[None, :]
    lane_clip = jnp.sum(jnp.where(lane_own, clip_of[None, :], 0), axis=1)
    lane_pos = jnp.sum(jnp.where(lane_own, frame_pos[None, :], 0), axis=1)
    seen = (
        (clip_tok[:, None] == lane_clip[None, :])
        & (pos_tok[:, None] <= lane_pos[None, :])
        & (pad[:, None] == 1)
    )
    see = jnp.where((lane[None, :] < frames) & ~seen, -1e30, 0.0).astype(bf16)
    quarter = HD // 4
    freq = 10000.0 ** (-jnp.arange(quarter, dtype=f32) / quarter)
    patch = jnp.arange(count, dtype=jnp.int32) % size
    angle = jnp.concatenate(
        [pos_tok.astype(f32)[:, None] * freq[None, :], patch.astype(f32)[:, None] * freq[None, :]],
        axis=1,
    )
    cosine, sine = jnp.cos(angle), jnp.sin(angle)
    cosine = jnp.concatenate([cosine] * 4, axis=1)
    sine = jnp.concatenate([-sine, sine, -sine, sine], axis=1)
    return see, frame_hot.astype(bf16), cosine, sine


def per_device(
    tokens, cotangent, clip_frames, levels, pad_mask, w_mod, b_mod, w_qkv, b_qkv, w_out, b_out,
    w_up, b_up, w_down, b_down, noise_table,
):
    count, width = tokens.shape
    frames = levels.shape[0]
    size = count // frames
    hidden = w_up.shape[1]
    ndev = width // w_up.shape[0]
    me = lax.axis_index("dp") * lax.axis_size("fsdp") + lax.axis_index("fsdp")

    dp, fsdp = lax.axis_size("dp"), lax.axis_size("fsdp")
    sizes = (dp // 2, 2, fsdp // 2)
    lead = sizes + (2,)

    def flat(array):
        return array.reshape(-1, array.shape[-1])

    def blocks(array, front=0):
        rows = array.shape[front] // ndev
        return array.reshape(array.shape[:front] + lead + (rows, array.shape[-1]))

    biases = [b_mod, b_qkv, b_out, b_up, b_down]
    lengths = [b.shape[0] for b in biases]
    spots = jnp.arange(8 * LANE, dtype=jnp.int32)
    mine_at = jnp.where(spots // (2 * frames) == me, jnp.tile(levels, spots.shape[0] // frames), 0)
    packed = jnp.concatenate([mine_at.astype(f32)] + [b.astype(f32) for b in biases])
    packed = jnp.pad(packed, (0, 16 * LANE - packed.shape[0])).reshape(16, LANE)
    part = Held(lead + (2 * frames, w_mod.shape[1] // 2), f32)
    small = Spread(sizes, packed)
    qkv_w = Gather(sizes, w_qkv, ())
    out_w, up_w = Gather(sizes, w_out, ()), Gather(sizes, w_up, ())
    mod_sum = Reduce(sizes, part, ())

    def add_modulation(ins, _, scratch):
        part.ref = scratch[0]
        load = pltpu.make_async_copy(small.out_refs[0], scratch[1], scratch[2].at[0])
        load.start()
        load.wait()
        modulation_kernel(None, ins[0], ins[1], scratch[0], scratch[1], frames)

    head = run(
        None, 1, [VMEM] * 2, [], [], [noise_table, w_mod],
        [pltpu.VMEM(part.shape, f32), pltpu.VMEM(small.outs[0].shape, f32), DMA((1,))], name="head",
        moves=[small, qkv_w, out_w, up_w, mod_sum], sizes=sizes, group=1, axes="df",
        script=[
            (small, "0"), (qkv_w, "s0a"), (qkv_w, "s0b"), (out_w, "s0"), (small, "1"), (small, "2"), add_modulation,
            (mod_sum, "0"), (qkv_w, "n0a"), (mod_sum, "1"), (qkv_w, "n0b"), (mod_sum, "2"), (qkv_w, "n1a"), (mod_sum, "3"),
            (up_w, "s0a"), (qkv_w, "n1b"), (mod_sum, "4"), (qkv_w, "n2a"), (qkv_w, "n2b"), (qkv_w, "w3a"), (qkv_w, "w3b"),
            (out_w, "w0"), (up_w, "w0a"),
        ],
    )
    small, qkv_w, out_w, up_w = head[:4]
    small = small.reshape(ndev, -1)
    all_levels = jnp.sum(small[:, : 8 * LANE], axis=0).reshape(-1, 2 * frames)[:ndev, :frames]
    all_levels = all_levels.reshape(-1).astype(jnp.int32)
    full_bias, at = [], 8 * LANE
    for length in lengths:
        full_bias.append(small[:, at : at + length].reshape(1, -1))
        at += length
    bias_mod, bias_qkv, bias_out, bias_up, bias_down = full_bias
    modulation = jnp.transpose(head[-1].reshape(2, frames, -1), (1, 0, 2)).reshape(frames, -1)
    modulation = (modulation + bias_mod).reshape(frames, 6, width)
    full_qkv = flat(qkv_w)
    see, frame_hot, cosine, sine = tables(clip_frames[0], pad_mask, count)

    acts = like((count, width), bf16)
    wide = like((count, width), f32)
    tall = like((count, hidden), bf16)
    row = whole((1, width))
    mod_row = pl.BlockSpec((1, 6, width), lambda i: (i, 0, 0))
    mod_all = whole((frames, 6, width))
    rows_bf = by_rows(size, width)
    def turn(start, count, index):
        return lambda i: index(jnp.clip(i - start, 0, count - 1))

    def held(shape):
        return pl.BlockSpec(shape, lambda i: (0,) * len(shape), pipeline_mode=pl.Buffered(1))

    pairs = width // LANE
    step = 512
    tiles = hidden // step
    m1, m2 = frames + pairs, 2 * frames + pairs
    steps = m2 + tiles
    rows_one = pl.BlockSpec((size, width), turn(0, frames, lambda i: (i, 0)))
    rows_two = pl.BlockSpec((size, width), turn(m1, frames, lambda i: (i, 0)))
    lanes_one = pl.BlockSpec((size, LANE), turn(0, frames, lambda i: (i, 0)))
    pair_one = pl.BlockSpec((count, LANE), turn(frames, pairs, lambda i: (0, i)))
    cols_one = pl.BlockSpec((count, step), turn(m2, tiles, lambda i: (0, i)))
    move_out = Gather(
        sizes, out_w, [(0, "s1"), (3, "n1"), (8, "n2"), (9, "w3"), (9, "l"), (m1, "d")], True, load=True
    )
    move_up = Gather(
        sizes, up_w,
        [
            (0, "s1a"), (0, "s0b"), (2, "n1a"), (5, "n0b"), (7, "n2a"), (8, "w3a"), (8, "la"), (9, "n1b"), (m2, "da"),
            (m2 + 1, "n2b"), (m2 + 2, "w3b"), (m2 + 2, "lb"), (m2 + tiles // 2, "db"),
        ], True, w_up, True,
    )
    move_down = Gather(
        sizes, w_down,
        [
            (1, "s0a"), (1, "s0b"), (8, "n0a"), (11, "n0b"), (11, "n1a"), (m2 + 3, "n1b"), (steps, "n2a"), (steps, "n2b"),
            (steps, "w3a"), (steps, "w3b"),
        ],
    )
    act_one, query, key, value, attended, aug, middle, attn, act_two, activated, slope, *moved = run(
        lambda *refs: forward_kernel(*refs, frames=frames, pairs=pairs, tiles=tiles, gathers=(move_out, move_up)), steps,
        [
            rows_one, pl.BlockSpec((1, 6, width), turn(0, frames, lambda i: (i, 0, 0))), held((width, 3 * width)),
            held((1, 3 * width)), lanes_one, lanes_one, held((count, LANE)), held((count, LANE)), rows_two,
            pl.BlockSpec((1, 6, width), turn(m1, frames, lambda i: (i, 0, 0))), held((1, width)),
            pl.BlockSpec((1, step), turn(m2, tiles, lambda i: (0, i))),
        ],
        [rows_one] * 4 + [pair_one] * 2 + [rows_two] * 3 + [cols_one] * 2,
        [acts] * 6 + [wide, acts, acts] + [tall] * 2,
        (
            tokens, modulation, full_qkv, bias_qkv, cosine, sine, see, frame_hot, tokens, modulation, bias_out, bias_up,
        ),
        [pltpu.VMEM((count, width), bf16)] * 5, name="fwd",
        moves=[move_out, move_up, move_down], sizes=sizes, group=2,
    )
    full_out, full_up, full_down = [flat(w) for w in moved]
    full = whole((count, width))
    cols_h = by_cols(count, step)
    acc = pltpu.VMEM((count, width), f32)
    deep = hidden // width
    block_out, d_branch, d_gate_two, bdown = run(
        down_kernel, deep, [by_cols(count, width), by_rows(width, width), row, full, full, mod_all],
        [full, full, whole((frames, width)), row],
        [acts, acts, like((frames, width), f32), like((1, width), f32)],
        (activated, full_down, bias_down, middle, cotangent, modulation), [acc], name="down",
    )
    wdown = run(
        weight_grad_kernel, tiles, [cols_h, full], by_rows(step, width), like((hidden, width), bf16),
        (activated, d_branch), name="wdown",
    )
    wdown = blocks(wdown)
    stacked = pl.BlockSpec((1, count, width), lambda i: (i, 0, 0))
    once = held((count, width))
    mod_once = held((frames, 6, width))
    halves = ((0, width // 2), (width // 2, width))
    steps = 2 * tiles + deep
    sum_a = Reduce(
        sizes, wdown, [(0, "0"), (2, "1"), (tiles + 1, "2"), (2 * tiles + 2, "3"), (steps, "4")], halves[0]
    )
    core = ReduceCore(sizes, wdown, [(0, "s"), (3, "w")], halves[1])
    first = ReduceFirst(sizes, wdown, core, [(3, "l"), (4, "a"), (2 * tiles, "w")], halves[1])
    second = ReduceSecond(sizes, first, [(2 * tiles, "l"), (2 * tiles + 1, "a"), (steps, "w")])
    bup, wup, d_middle, d_attn, stat_two, bout, *moved = run(
        lambda *refs: mlp_kernel(*refs, tiles=tiles, deep=deep), steps,
        [
            once, pl.BlockSpec((step, width), turn(0, tiles, lambda i: (i, 0))),
            pl.BlockSpec((count, step), turn(0, tiles, lambda i: (0, i))), once,
            pl.BlockSpec((width, width), turn(2 * tiles, deep, lambda i: (0, i))), ANY, ANY, ANY, mod_once,
        ],
        [
            pl.BlockSpec((1, step), turn(0, tiles, lambda i: (0, i))),
            pl.BlockSpec((width, step), turn(tiles, tiles, lambda i: (0, i))),
            once, once, held((frames, 3, width)), held((1, width)),
        ],
        [
            like((1, hidden), f32), like((width, hidden), bf16), wide, acts, like((frames, 3, width), f32),
            like((1, width), f32),
        ],
        (d_branch, full_down, slope, act_two, full_up, middle, cotangent, attn, modulation),
        [
            pltpu.VMEM((count, hidden), bf16), acc, acc, pltpu.VMEM((count, width), bf16),
            pltpu.VMEM((count, width), bf16), DMA((3,)),
        ],
        name="mlpb", moves=[sum_a, core, first, second], sizes=sizes, group=6,
    )
    wdown_low, down_b = moved[0], moved[6:9]
    wup = blocks(wup)
    halves = ((0, hidden // 2), (hidden // 2, hidden))
    quarters = 4
    quarter = width // quarters
    steps = quarters + pairs + 3
    sum_a = Reduce(sizes, wup, [(0, "0"), (2, "1"), (7, "2"), (11, "3"), (steps, "4")], halves[0])
    core = ReduceCore(sizes, wup, [(0, "s"), (3, "w")], halves[1])
    first = ReduceFirst(sizes, wup, core, [(3, "l"), (5, "a"), (11, "w")], halves[1])
    second = ReduceSecond(sizes, first, [(11, "l"), (12, "a"), (steps, "w")])
    last_b = ReduceLast(sizes, down_b, [(0, "l"), (1, "a"), (9, "w")])
    pair_b = pl.BlockSpec((count, LANE), turn(quarters, pairs, lambda i: (0, i)))
    table_once = held((count, LANE))
    wout, d_projected, bqkv, wqkv, *moved = run(
        lambda *refs: attention_back_kernel(*refs, frames=frames, lead=quarters, pairs=pairs), steps,
        [
            once, pl.BlockSpec((quarter, width), turn(0, quarters, lambda i: (i, 0))),
            pl.BlockSpec((count, quarter), turn(0, quarters, lambda i: (0, i))),
        ] + [pair_b] * 5 + [table_once] * 3 + [once],
        [
            pl.BlockSpec((quarter, width), turn(0, quarters, lambda i: (i, 0))),
            pl.BlockSpec((3, count, LANE), turn(quarters, pairs, lambda i: (0, 0, i))),
            pl.BlockSpec((1, 3, LANE), turn(quarters, pairs, lambda i: (i, 0, 0))),
            pl.BlockSpec((1, width, width), turn(quarters + pairs, 3, lambda i: (i, 0, 0))),
        ],
        [
            like((width, width), bf16), like((3, count, width), bf16), like((pairs, 3, LANE), f32),
            like((3, width, width), bf16),
        ],
        (d_attn, full_out, attended, query, key, value, attended, aug, see, cosine, sine, act_one),
        [pltpu.VMEM((count, width), bf16), pltpu.VMEM((3, count, width), bf16), pltpu.VMEM((count, LANE), f32)],
        name="attb", moves=[last_b, sum_a, core, first, second], sizes=sizes, group=7,
    )
    wdown_high, wup_low, up_b = moved[0], moved[1], moved[7:10]
    wdown_grad = jnp.concatenate([wdown_low, wdown_high], axis=1)
    wout, wqkv = blocks(wout), blocks(wqkv, 1)

    bqkv = jnp.transpose(bqkv, (1, 0, 2)).reshape(1, -1)
    shares = [b.reshape(ndev, -1) for b in (bqkv, bout, bup, bdown)]
    packed = jnp.concatenate(shares, axis=1)
    bias_len = packed.shape[1]
    packed = jnp.pad(packed, ((0, 0), (0, 8 * LANE - bias_len))).reshape(-1, LANE)
    packed = blocks(packed)
    mod_block = Held((6 * frames, width), bf16)
    d_mod = Gather(sizes, mod_block, ())
    bias = Reduce(sizes, packed, ())
    qkv_out, out_out = Held((width // ndev, 3 * width), f32), Held((width // ndev, width), f32)
    marks = ([(0, "0"), (0, "1"), (1, "2"), (2, "3")], [(0, "0"), (0, "1"), (2, "2")], [(0, "0"), (1, "1")])
    q, k, v = [Reduce(sizes, wqkv, marks[i], i, (qkv_out, i * width)) for i in range(3)]
    halves = ((0, width // 2), (width // 2, width))
    oa = Reduce(sizes, wout, [(0, "0"), (2, "1")], halves[0], (out_out, 0))
    ob = Reduce(sizes, wout, [(0, "0")], halves[1], (out_out, width // 2))
    last_b = ReduceLast(sizes, up_b, [(0, "l"), (0, "a"), (3, "w")])

    def pack_modulation(ins, outs, scratch):
        one, two, gate = outs[1], ins[5], ins[6]
        parts = [one[:, 0, :], one[:, 1, :], two[:, 0, :], two[:, 1, :], two[:, 2, :], gate[...]]
        mod_block.ref = scratch[1]
        qkv_out.ref, out_out.ref = outs[2:]
        scratch[1][...] = jnp.concatenate(parts, axis=0).astype(bf16)

    def set_block(refs):
        input_back_kernel(*refs[:5], *refs[7:9], refs[11])

    token_grad, stat_one, wqkv_grad, wout_grad, *moved = run(
        lambda *refs: set_block(refs), 3,
        [stacked, by_cols(width, width), once, once, mod_once, held((frames, 3, width)), held((frames, width))],
        [once, held((frames, 2, width)), VMEM, VMEM],
        [acts, like((frames, 2, width), f32), like(qkv_out.shape, f32), like(out_out.shape, f32)],
        (d_projected, full_qkv, tokens, d_middle, modulation, stat_two, d_gate_two),
        [acc, pltpu.VMEM(mod_block.shape, bf16)], name="dact1",
        moves=[d_mod, q, k, v, oa, ob, last_b, bias], sizes=sizes, group=8,
        script=[
            (bias, "0"), pack_modulation, (d_mod, "s0"), (v, "2"), (k, "3"), (ob, "1"), (bias, "1"), (oa, "2"), (v, "3"),
            (d_mod, "n0"), (ob, "2"), (bias, "2"), (oa, "3"), (ob, "3"), (d_mod, "n1"), (bias, "3"), (q, "4"), (k, "4"),
            (d_mod, "n2"), (bias, "4"), (v, "4"), (d_mod, "w3"), (oa, "4"), (ob, "4"),
        ],
    )
    d_mod, wup_high, bias_sum = moved
    wup_grad = jnp.concatenate([wup_low, wup_high], axis=1)
    d_mod = jnp.transpose(d_mod.reshape(ndev, 6, frames, width), (0, 2, 1, 3))
    d_mod = d_mod.reshape(ndev * frames, -1)
    bias_sum = bias_sum.reshape(-1)[:bias_len]
    bias_grads, at = [], 0
    for share in shares:
        bias_grads.append(bias_sum[at : at + share.shape[1]])
        at += share.shape[1]
    hot = (all_levels[:, None] == jnp.arange(noise_table.shape[1], dtype=jnp.int32)[None, :]).astype(bf16)
    embedded = dot(hot, noise_table, NT)
    cond = jax.nn.silu(embedded).astype(bf16)
    wmod_grad = dot(cond, d_mod, TN)
    mine = b_mod.shape[0]
    bmod_grad = jnp.sum(lax.dynamic_slice(d_mod, (0, me * mine), (d_mod.shape[0], mine)).astype(f32), axis=0)
    gate = jax.nn.sigmoid(embedded)
    d_embed = dot(d_mod, w_mod, NT) * gate * (1.0 + embedded * (1.0 - gate))
    table_grad = lax.dot_general(
        d_embed, hot.astype(f32), TN, precision=lax.Precision.HIGHEST, preferred_element_type=f32
    )
    return (
        block_out, token_grad, wmod_grad, bmod_grad, wqkv_grad, bias_grads[0], wout_grad, bias_grads[1],
        wup_grad, bias_grads[2], wdown_grad, bias_grads[3], table_grad,
    )


def solution(mesh):
    rows, vec = P(AXES, None), P(AXES)
    return jax.shard_map(
        per_device,
        mesh=mesh,
        in_specs=(rows, rows, rows, vec, vec) + (rows, vec) * 5 + (rows,),
        out_specs=(rows, rows) + (rows, vec) * 5 + (rows,),
        check_vma=False,
    )
```

```python
import jax
import jax.numpy as jnp
from jax import lax
from jax.experimental import pallas as pl
from jax.experimental.pallas import tpu as pltpu
from jax.sharding import PartitionSpec as P

bf16 = jnp.bfloat16
f32 = jnp.float32
AXES = ("dp", "fsdp")
HD = 64
LANE = 128
EPS = 1e-06
NN = (((1,), (0,)), ((), ()))
NT = (((1,), (1,)), ((), ()))
TN = (((0,), (0,)), ((), ()))


def dot(left, right, dims):
    return lax.dot_general(left, right, dims, preferred_element_type=f32)


def lanes(shape):
    return lax.broadcasted_iota(jnp.int32, shape, 1)


def normalize(values):
    centred = values - jnp.mean(values, axis=1, keepdims=True)
    inverse = lax.rsqrt(jnp.mean(centred * centred, axis=1, keepdims=True) + EPS)
    return centred * inverse, inverse


def normalize_back(grad, normed, inverse):
    return inverse * (
        grad
        - jnp.mean(grad, axis=1, keepdims=True)
        - normed * jnp.mean(grad * normed, axis=1, keepdims=True)
    )


def col_sum(values):
    return jnp.sum(values.astype(f32), axis=0, keepdims=True)


def partner(values):
    return jnp.where(
        lanes(values.shape) % HD < HD // 2,
        pltpu.roll(values, LANE - HD // 2, 1),
        pltpu.roll(values, HD // 2, 1),
    )


def carry_lanes(values):
    sub = lanes(values.shape) % HD
    high = values.astype(bf16).astype(f32)
    rest = values - high
    mid = rest.astype(bf16).astype(f32)
    return jnp.where(
        sub == 8, high, jnp.where(sub == 9, mid, jnp.where(sub == 10, rest - mid, 0.0))
    )


def qkv_kernel(x_ref, mod_ref, w_ref, b_ref, cos_ref, sin_ref, act_ref, q_ref, k_ref, v_ref):
    normed, _ = normalize(x_ref[...].astype(f32))
    act = (normed * (1.0 + mod_ref[0, 1:2, :]) + mod_ref[0, 0:1, :]).astype(bf16)
    act_ref[...] = act
    width = x_ref.shape[1]
    cosine, sine = cos_ref[...], sin_ref[...]
    step = 2 * LANE
    for col in range(0, 3 * width, step):
        raw = dot(act, w_ref[:, col : col + step], NN) + b_ref[:, col : col + step].astype(f32)
        for sub in range(0, step, LANE):
            part = raw[:, sub : sub + LANE]
            at = (col + sub) % width
            if col < width:
                part = (part * cosine + partner(part) * sine).astype(bf16)
                q_ref[:, at : at + LANE] = (part.astype(f32) * 0.125).astype(bf16)
            elif col < 2 * width:
                k_ref[:, at : at + LANE] = (part * cosine + partner(part) * sine).astype(bf16)
            else:
                v_ref[:, at : at + LANE] = part.astype(bf16)


def attention_forward(q_ref, k_ref, v_ref, see_ref, hot_ref, out_ref, aug_ref, *, frames):
    rows_all = q_ref.shape[0]
    size = rows_all // frames
    low = lanes((rows_all, LANE)) < HD
    low_b = lanes((size, LANE)) < HD
    k, v, see = k_ref[...], v_ref[...], see_ref[...]
    one = jnp.ones_like(v)
    keys = (jnp.where(low, k, see), jnp.where(low, see, k))
    vals = (jnp.where(low, v, one), jnp.where(low, one, v))
    for i in range(frames):
        rows = slice(i * size, (i + 1) * size)
        width = (i + 1) * size
        q, hot = q_ref[rows, :], hot_ref[rows, :]
        query = (jnp.where(low_b, q, hot), jnp.where(low_b, hot, q))
        tops, outs = [], []
        for h in range(2):
            scores = dot(query[h], keys[h][:width], NT)
            top = jnp.max(scores, axis=1, keepdims=True)
            expo = jnp.exp(scores - top).astype(bf16)
            outs.append(dot(expo, vals[h][:width], NN))
            tops.append(top)
        num = jnp.where(low_b, outs[0], outs[1])
        den = jnp.where(low_b, outs[1], outs[0])
        out_ref[rows, :] = (num / pltpu.roll(den, HD, 1)).astype(bf16)
        lse = jnp.where(low_b, tops[1], tops[0]) + jnp.log(den)
        aug_ref[rows, :] = (carry_lanes(-lse) + hot.astype(f32)).astype(bf16)


def project_kernel(att_ref, x_ref, mod_ref, w_ref, b_ref, middle_ref, attn_ref, act_ref):
    attn = dot(att_ref[...], w_ref[...].reshape(-1, w_ref.shape[-1]), NN) + b_ref[...].astype(f32)
    attn_ref[...] = attn.astype(bf16)
    middle = x_ref[...].astype(f32) + mod_ref[0, 2:3, :] * attn
    middle_ref[...] = middle
    normed, _ = normalize(middle)
    act_ref[...] = (normed * (1.0 + mod_ref[0, 4:5, :]) + mod_ref[0, 3:4, :]).astype(bf16)


def up_kernel(act_ref, w_ref, b_ref, out_ref, slope_ref):
    hidden = dot(act_ref[...], w_ref[...].reshape(-1, w_ref.shape[-1]), NN) + b_ref[...].astype(f32)
    share = 0.5 * (1.0 + lax.erf(hidden * 0.7071067811865476))
    out_ref[...] = (hidden * share).astype(bf16)
    slope = share + hidden * jnp.exp(-0.5 * hidden * hidden) * 0.3989422804014327
    slope_ref[...] = slope.astype(bf16)


def down_kernel(
    act_ref, w_ref, b_ref, mid_ref, cot_ref, mod_ref, out_ref, dbr_ref, gate_ref, sum_ref, acc_ref
):
    step, last = pl.program_id(0), pl.num_programs(0) - 1
    part = dot(act_ref[...], w_ref[...], NN)

    @pl.when(step == 0)
    def _():
        acc_ref[...] = part

    @pl.when(step > 0)
    def _():
        acc_ref[...] += part

    @pl.when(step == last)
    def _():
        frames = mod_ref.shape[0]
        size = acc_ref.shape[0] // frames
        total = jnp.zeros((1, acc_ref.shape[1]), f32)
        for i in range(frames):
            rows = slice(i * size, (i + 1) * size)
            gate = mod_ref[i, 5:6, :]
            branch = acc_ref[rows, :] + b_ref[...].astype(f32)
            out_ref[rows, :] = (mid_ref[rows, :] + gate * branch).astype(bf16)
            upstream = cot_ref[rows, :].astype(f32)
            d_branch = (upstream * gate).astype(bf16)
            dbr_ref[rows, :] = d_branch
            gate_ref[i : i + 1, :] = col_sum(upstream * branch)
            total += col_sum(d_branch)
        sum_ref[...] = total


def hidden_back_kernel(dbr_ref, w_ref, slope_ref, out_ref, sum_ref):
    d_hidden = (dot(dbr_ref[...], w_ref[...], NT) * slope_ref[...].astype(f32)).astype(bf16)
    out_ref[...] = d_hidden
    sum_ref[...] = col_sum(d_hidden)


def mlp_back_kernel(
    dh_ref, w_ref, mid_ref, cot_ref, attn_ref, mod_ref, dmid_ref, datt_ref, stat_ref, sum_ref, acc_ref, step, last
):
    part = dot(dh_ref[...], w_ref[...], NT)

    @pl.when(step == 0)
    def _():
        acc_ref[...] = part

    @pl.when(step > 0)
    def _():
        acc_ref[...] += part

    @pl.when(step == last)
    def _():
        frames = mod_ref.shape[0]
        size = acc_ref.shape[0] // frames
        total = jnp.zeros((1, acc_ref.shape[1]), f32)
        for i in range(frames):
            rows = slice(i * size, (i + 1) * size)
            d_act = acc_ref[rows, :]
            normed, inverse = normalize(mid_ref[rows, :])
            stat_ref[i, 1:2, :] = col_sum(d_act)
            stat_ref[i, 2:3, :] = col_sum(d_act * normed)
            d_middle = cot_ref[rows, :].astype(f32) + normalize_back(
                d_act * (1.0 + mod_ref[i, 4:5, :]), normed, inverse
            )
            dmid_ref[rows, :] = d_middle
            stat_ref[i, 0:1, :] = col_sum(d_middle * attn_ref[rows, :].astype(f32))
            d_attn = (d_middle * mod_ref[i, 2:3, :]).astype(bf16)
            datt_ref[rows, :] = d_attn
            total += col_sum(d_attn)
        sum_ref[...] = total


def at_columns(ref, index, size):
    return ref.at[:, pl.ds(pl.multiple_of(index * size, size), size)]


def mlp_kernel(
    dbr_ref, wdown_ref, slope_ref, act_ref, wup_ref, mid_ref, cot_ref, attn_ref, mod_ref,
    bup_ref, out_ref, dmid_ref, datt_ref, stat_ref, sum_ref, dh_ref, acc_ref, mid_all, cot_all, attn_all, sems,
    *, tiles, deep,
):
    step = pl.program_id(0)
    size, wide = dh_ref.shape[1] // tiles, dh_ref.shape[1] // deep
    late = [
        (mid_ref, mid_all, sems.at[0]), (cot_ref, cot_all, sems.at[1]), (attn_ref, attn_all, sems.at[2])
    ]

    @pl.when(step == 1)
    def _():
        for item in late:
            pltpu.make_async_copy(*item).start()

    @pl.when(step == 2 * tiles)
    def _():
        for item in late:
            pltpu.make_async_copy(*item).wait()

    @pl.when(step < tiles)
    def _():
        hidden_back_kernel(dbr_ref, wdown_ref, slope_ref, at_columns(dh_ref, step, size), bup_ref)

    @pl.when((step >= tiles) & (step < 2 * tiles))
    def _():
        weight_grad_kernel(act_ref, at_columns(dh_ref, step - tiles, size), out_ref)

    @pl.when(step >= 2 * tiles)
    def _():
        mlp_back_kernel(
            at_columns(dh_ref, step - 2 * tiles, wide), wup_ref, mid_all, cot_all, attn_all, mod_ref,
            dmid_ref, datt_ref, stat_ref, sum_ref, acc_ref, step - 2 * tiles, deep - 1,
        )


def attention_back_kernel(
    da_ref, wout_ref, att_ref, q_ref, k_ref, v_ref, o_ref, aug_ref, see_ref, cos_ref, sin_ref, act_ref,
    gout_ref, out_ref, bias_ref, gqkv_ref, do_ref, dp_ref, acc_ref, *, frames, lead, pairs,
):
    step = pl.program_id(0)

    @pl.when(step < lead)
    def _():
        attended_back_kernel(
            da_ref, wout_ref, att_ref, at_columns(do_ref, step, do_ref.shape[1] // lead), gout_ref
        )

    @pl.when((step >= lead) & (step < lead + pairs))
    def _():
        at = step - lead
        attention_backward(
            q_ref, k_ref, v_ref, at_columns(do_ref, at, LANE), o_ref, aug_ref, see_ref, cos_ref, sin_ref,
            out_ref, bias_ref, acc_ref, frames=frames,
        )
        for i in range(3):
            dp_ref[i, :, pl.ds(pl.multiple_of(at * LANE, LANE), LANE)] = out_ref[i]

    @pl.when(step >= lead + pairs)
    def _():
        gqkv_ref[0] = dot(act_ref[...], dp_ref[step - lead - pairs], TN).astype(bf16)


def forward_kernel(
    x_ref, mod_ref, w_ref, b_ref, cos_ref, sin_ref, see_ref, hot_ref, again_ref, mod_again_ref, bout_ref, bup_ref,
    act_ref, q_ref, k_ref, v_ref, att_ref, aug_ref, middle_ref, attn_ref, act_two_ref, up_ref, slope_ref,
    q_all, k_all, v_all, att_all, act_all, *, frames, pairs, tiles, gathers,
):
    step = pl.program_id(0)
    size = x_ref.shape[0]
    marks = (frames, frames + pairs, 2 * frames + pairs)

    @pl.when(step < marks[0])
    def _():
        qkv_kernel(x_ref, mod_ref, w_ref, b_ref, cos_ref, sin_ref, act_ref, q_ref, k_ref, v_ref)
        rows = pl.ds(pl.multiple_of(step * size, size), size)
        for ref, every in ((q_ref, q_all), (k_ref, k_all), (v_ref, v_all)):
            every[rows, :] = ref[...]

    @pl.when((step >= marks[0]) & (step < marks[1]))
    def _():
        at = step - marks[0]
        q, k, v = [at_columns(ref, at, LANE) for ref in (q_all, k_all, v_all)]
        attention_forward(q, k, v, see_ref, hot_ref, att_ref, aug_ref, frames=frames)
        att_all[:, pl.ds(pl.multiple_of(at * LANE, LANE), LANE)] = att_ref[...]

    @pl.when((step >= marks[1]) & (step < marks[2]))
    def _():
        rows = pl.ds(pl.multiple_of((step - marks[1]) * size, size), size)
        weight = gathers[0].refs[3]
        project_kernel(
            att_all.at[rows, :], again_ref, mod_again_ref, weight, bout_ref, middle_ref, attn_ref, act_two_ref
        )
        act_all[rows, :] = act_two_ref[...]

    @pl.when(step >= marks[2])
    def _():
        width = up_ref.shape[1]
        at = pl.multiple_of((step - marks[2]) * width, width)
        up_kernel(act_all, gathers[1].refs[3].at[:, :, :, :, :, pl.ds(at, width)], bup_ref, up_ref, slope_ref)


def attention_backward(
    q_ref, k_ref, v_ref, do_ref, o_ref, aug_ref, see_ref, cos_ref, sin_ref, out_ref, sum_ref, acc_ref, *, frames
):
    rows_all = q_ref.shape[0]
    size = rows_all // frames
    low = lanes((rows_all, LANE)) < HD
    q, aug, grad = q_ref[...], aug_ref[...], do_ref[...]
    prod = grad.astype(f32) * o_ref[...].astype(f32)
    delta_low = jnp.sum(jnp.where(low, prod, 0.0), axis=1, keepdims=True)
    delta_high = jnp.sum(jnp.where(low, 0.0, prod), axis=1, keepdims=True)
    grad_aug = carry_lanes(jnp.where(low, -delta_high, -delta_low)).astype(bf16)
    query = (jnp.where(low, q, aug), jnp.where(low, aug, q))
    upper = (jnp.where(low, grad, grad_aug), jnp.where(low, grad_aug, grad))
    low_b = lanes((size, LANE)) < HD
    sub = lanes((size, LANE)) % HD
    ones = jnp.where((sub >= 8) & (sub <= 10), 1.0, 0.0).astype(bf16)
    sum_k = sum_v = jnp.zeros((1, LANE), f32)
    for j in range(frames):
        rows = slice(j * size, (j + 1) * size)
        start = j * size
        k, v, see = k_ref[rows, :], v_ref[rows, :], see_ref[rows, :] + ones
        keys = (jnp.where(low_b, k, see), jnp.where(low_b, see, k))
        vals = (jnp.where(low_b, v, ones), jnp.where(low_b, ones, v))
        dvs, dks, dqs = [], [], []
        for h in range(2):
            probs = jnp.exp(dot(keys[h], query[h][start:], NT))
            d_scores = (probs * dot(vals[h], upper[h][start:], NT)).astype(bf16)
            dvs.append(dot(probs.astype(bf16), grad[start:], NN))
            dks.append(dot(d_scores, q[start:], NN))
            dqs.append(dot(d_scores, k, TN))
        d_value = jnp.where(low_b, dvs[0], dvs[1]).astype(bf16)
        d_key = jnp.where(low_b, dks[0], dks[1])
        d_key = (d_key * cos_ref[rows, :] - partner(d_key) * sin_ref[rows, :]).astype(bf16)
        out_ref[1, rows, :] = d_key
        out_ref[2, rows, :] = d_value
        sum_k = sum_k + col_sum(d_key)
        sum_v = sum_v + col_sum(d_value)
        d_query = jnp.where(lanes(dqs[0].shape) < HD, dqs[0], dqs[1])
        if j == 0:
            acc_ref[...] = d_query
        else:
            acc_ref[start:, :] += d_query
    d_query = acc_ref[...] * 0.125
    d_query = (d_query * cos_ref[...] - partner(d_query) * sin_ref[...]).astype(bf16)
    out_ref[0] = d_query
    sum_ref[0, 0:1, :] = col_sum(d_query)
    sum_ref[0, 1:2, :] = sum_k
    sum_ref[0, 2:3, :] = sum_v


def input_back_kernel(dp_ref, w_ref, x_ref, dmid_ref, mod_ref, out_ref, stat_ref, acc_ref):
    step, last = pl.program_id(0), pl.num_programs(0) - 1
    part = dot(dp_ref[0], w_ref[...], NT)

    @pl.when(step == 0)
    def _():
        acc_ref[...] = part

    @pl.when(step > 0)
    def _():
        acc_ref[...] += part

    @pl.when(step == last)
    def _():
        frames = mod_ref.shape[0]
        size = acc_ref.shape[0] // frames
        for i in range(frames):
            rows = slice(i * size, (i + 1) * size)
            d_act = acc_ref[rows, :]
            normed, inverse = normalize(x_ref[rows, :].astype(f32))
            stat_ref[i, 0:1, :] = col_sum(d_act)
            stat_ref[i, 1:2, :] = col_sum(d_act * normed)
            back = normalize_back(d_act * (1.0 + mod_ref[i, 1:2, :]), normed, inverse)
            out_ref[rows, :] = (dmid_ref[rows, :] + back).astype(bf16)


def modulation_kernel(small_ref, table_ref, w_ref, part_ref, levels_ref, frames):
    ndev = part_ref.shape[0] * part_ref.shape[1] * part_ref.shape[2] * 2
    rows = levels_ref[...].reshape(ndev, levels_ref.shape[-2], LANE)
    spots = jnp.sum(rows[:, :8], axis=0).astype(jnp.int32)
    count = 2 * frames * ndev
    level = jnp.concatenate([spots[i : i + 1, :] for i in range(count // LANE)], axis=1)
    slot = lax.broadcasted_iota(jnp.int32, (table_ref.shape[1], count), 0)
    hot = jnp.where(slot == level, 1.0, 0.0).astype(bf16)
    embedded = dot(table_ref[...], hot, NN)
    cond = (embedded / (1.0 + jnp.exp(-embedded))).astype(bf16)
    half = part_ref.shape[-1]
    first = lax.broadcasted_iota(jnp.int32, (count, 1), 0) % (2 * frames) < frames
    step = 512
    for col in range(0, half, step):
        low = dot(cond, w_ref[:, col : col + step], TN)
        high = dot(cond, w_ref[:, half + col : half + col + step], TN)
        value = jnp.where(first, low, high)
        part_ref[..., col : col + step] = value.reshape(part_ref.shape[:-1] + (step,)).astype(part_ref.dtype)


def weight_grad_kernel(left_ref, right_ref, out_ref):
    out_ref[...] = dot(left_ref[...], right_ref[...], TN).astype(bf16)


def attended_back_kernel(da_ref, w_ref, att_ref, datt_ref, out_ref):
    datt_ref[...] = dot(da_ref[...], w_ref[...], NT).astype(bf16)
    out_ref[...] = dot(att_ref[...], da_ref[...], TN).astype(bf16)


def qkv_grad_kernel(left_ref, right_ref, out_ref):
    out_ref[0] = dot(left_ref[...], right_ref[0], TN).astype(bf16)


def like(shape, kind):
    return jax.ShapeDtypeStruct(shape, kind)


def whole(shape):
    return pl.BlockSpec(shape, lambda i: (0,) * len(shape))


def by_rows(size, width):
    return pl.BlockSpec((size, width), lambda i: (i, 0))


def by_cols(height, size):
    return pl.BlockSpec((height, size), lambda i: (0, i))


MESH = pl.DeviceIdType.MESH
ANY = pl.BlockSpec(memory_space=pl.ANY)
VMEM = pl.BlockSpec(memory_space=pltpu.VMEM)
DMA = pltpu.SemaphoreType.DMA


class Place:
    def __init__(self, sizes):
        self.ny, self.nx, self.nz = sizes
        self.half = self.nz // 2
        self.rest = self.nz - self.half
        self.low, self.high = pl.ds(0, self.half), pl.ds(self.half, self.rest)
        self.dp, self.fsdp = lax.axis_index("dp"), lax.axis_index("fsdp")
        self.y, self.x = lax.div(self.dp, self.nx), lax.rem(self.dp, self.nx)
        self.z, self.c = lax.div(self.fsdp, 2), lax.rem(self.fsdp, 2)

        self.shifts, self.devices = {}, {}
        for axis, size in dict(y=self.ny, x=self.nx, z=self.nz, c=2).items():
            for k in range(1, size):
                at = lax.rem(getattr(self, axis) + k, size)
                self.shifts[axis, k] = self.shifts[axis, k - size] = at
                self.devices[axis, k] = dict(
                    y=(at * self.nx + self.x, self.fsdp), x=(self.y * self.nx + at, self.fsdp),
                    z=(self.dp, at * 2 + self.c), c=(self.dp, self.z * 2 + at),
                )[axis]
        self.other = self.shifts["c", 1]
        self.nd, self.nf = self.ny * self.nx, self.nz * 2
        for k in range(1, self.nd):
            at = lax.rem(self.dp + k, self.nd)
            self.shifts["d", k] = self.shifts["d", k - self.nd] = at
            self.devices["d", k] = (at, self.fsdp)
        for k in range(1, self.nf):
            at = lax.rem(self.fsdp + k, self.nf)
            self.shifts["f", k] = self.shifts["f", k - self.nf] = at
            self.devices["f", k] = (self.dp, at)

    def shift(self, axis, k):
        return self.shifts[axis, k]

    def device(self, axis, k):
        return self.devices[axis, k]

    def enter(self, axes):
        barrier = pltpu.get_barrier_semaphore()
        sizes = dict(y=self.ny, x=self.nx, z=self.nz, c=2, d=self.nd, f=self.nf)
        count = 0
        for axis in axes:
            for k in range(1, sizes[axis]):
                count += 1
                pl.semaphore_signal(barrier, inc=1, device_id=self.device(axis, k), device_id_type=MESH)
        pl.semaphore_wait(barrier, count)


class Move:
    ins, in_specs, outs, out_specs, scratch, aliases = (), (), (), (), (), ()

    def bind(self, place, ins, outs, scratch):
        self.place, self.in_refs, self.out_refs, self.refs = place, ins, outs, scratch
        self.slots, self.local_slots, self.legs = {}, {}, []

    def copy(self, key, src, dst, axis, k):
        slot = self.slots.setdefault(key, len(self.slots))
        return pltpu.make_async_remote_copy(
            src_ref=src, dst_ref=dst, send_sem=self.refs[0].at[slot], recv_sem=self.refs[1].at[slot],
            device_id=self.place.device(axis, k), device_id_type=MESH,
        )

    def start(self, items):
        for item in items:
            self.copy(*item).start()

    def arrived(self, key, dst, axis, k):
        self.copy(key, dst, dst, axis, k).wait_recv()

    def drain(self, items):
        for item in items:
            self.copy(*item).wait_send()

    def local(self, key, src, dst):
        slot = self.local_slots.setdefault(key, len(self.local_slots))
        return pltpu.make_async_copy(src, dst, self.refs[2].at[slot])


class Held:
    def __init__(self, shape, kind):
        self.shape, self.dtype, self.ref = shape, kind, None


def part_of(ref, part, core):
    if part is None:
        return ref.at[:, :, :, core]
    if isinstance(part, int):
        return ref.at[part, :, :, :, core]
    return ref.at[:, :, :, core, :, part[0] : part[1]]


def block_of(array, part):
    rows, columns = array.shape[-2:]
    return (rows, part[1] - part[0]) if isinstance(part, tuple) else (rows, columns)


def legs_copies(sizes):
    ny, nx, nz = sizes
    return (nz - 1) + 4 * (nx - 1) + 4 * (ny - 1) + 1


class Gather(Move):
    def __init__(self, sizes, array, actions, begun=False, shard=None, load=False):
        ny, nx, nz = sizes
        self.begun, self.actions = begun, actions
        self.held = array if isinstance(array, Held) else None
        self.ins, self.in_specs = ([], []) if self.held else ([array], [ANY if begun else VMEM])
        if shard is not None:
            self.ins, self.in_specs = [array, shard], [ANY, VMEM]
        shape = array.shape if begun else (ny, nx, nz, 2) + array.shape
        self.outs, self.out_specs = [like(shape, array.dtype)], [ANY]
        parts = len({what[2:] for _, what in actions}) if actions else 3
        self.scratch = [DMA((legs_copies(sizes) * parts,)), DMA((legs_copies(sizes) * parts,)), DMA((parts + 3,))]
        if load:
            self.scratch.append(pltpu.VMEM(shape, array.dtype))
        self.aliases = [(0, 0)] if begun else []

    def act(self, what):
        if what[0] in "ld":
            part = what[1:]
            copy = self.local(("load", part), self.spot((slice(None),) * 4, part), self.held_part(part))
            return copy.start() if what[0] == "l" else copy.wait()
        op, leg, part = what[0], int(what[1]), what[2:]
        if op != "s":
            self.wait_leg(leg, part)
        if op != "w":
            self.start_leg(leg + (op == "n"), part)
        else:
            for each in self.legs:
                if each[1] == part:
                    self.drain(self.leaving(*each))

    def columns(self, part):
        width = self.out_refs[0].shape[-1]
        half = width // 2
        return {"": slice(None), "a": slice(0, half), "b": slice(half, width)}[part]

    def held_part(self, part):
        return self.refs[3].at[:, :, :, :, :, self.columns(part)]

    def spot(self, index, part):
        return self.out_refs[0].at[index + (slice(None), self.columns(part))]

    def items(self, leg):
        p, full = self.place, self.out_refs[0]
        y, x, z, c = p.y, p.x, p.z, p.c
        d = p.other
        xs, ys, zs = range(1, p.nx), range(1, p.ny), range(1, p.nz)
        back = p.shift
        if leg == 0:
            return [(("z", k), (y, x, z, c), (y, x, back("z", -k), c), "z", k) for k in zs]
        if leg == 1:
            return (
                [(("x", k), (y, x, p.low, c), (y, back("x", -k), p.low, c), "x", k) for k in xs]
                + [(("y", k), (y, x, p.high, c), (back("y", -k), x, p.high, c), "y", k) for k in ys]
                + [("c", (y, x, slice(None), c), (y, x, slice(None), d), "c", 1)]
            )
        every = slice(None)
        if leg == 2:
            return (
                [(("xy", k), (y, every, p.low, c), (back("y", -k), every, p.low, c), "y", k) for k in ys]
                + [(("yx", k), (every, x, p.high, c), (every, back("x", -k), p.high, c), "x", k) for k in xs]
                + [(("cx", k), (y, back("x", -k), p.low, c), (y, back("x", -k), p.low, d), "c", 1) for k in xs]
                + [(("cy", k), (back("y", -k), x, p.high, c), (back("y", -k), x, p.high, d), "c", 1) for k in ys]
            )
        return [
            (("cxy", k), (back("y", -k), every, p.low, c), (back("y", -k), every, p.low, d), "c", 1) for k in ys
        ] + [(("cyx", k), (every, back("x", -k), p.high, c), (every, back("x", -k), p.high, d), "c", 1) for k in xs]

    def source(self):
        return self.held.ref if self.held else self.in_refs[-1]

    def own(self, part):
        p = self.place
        mine = self.source().at[:, self.columns(part)]
        return self.local(part, mine, self.spot((p.y, p.x, p.z, p.c), part))

    def leaving(self, leg, part):
        for key, leaves, _, axis, k in self.items(leg):
            to = self.spot(leaves, part)
            yield (key, part), self.source().at[:, self.columns(part)] if leg == 0 else to, to, axis, k

    def start_leg(self, leg, part):
        self.legs.append((leg, part))
        if leg == 0:
            self.own(part).start()
        self.start(self.leaving(leg, part))

    def wait_leg(self, leg, part):
        if leg == 0:
            self.own(part).wait()
        for key, _, arrives, axis, k in self.items(leg):
            self.arrived((key, part), self.spot(arrives, part), axis, k)


class Spread(Move):
    def __init__(self, sizes, array):
        ny, nx, nz = sizes
        self.ins, self.in_specs = [array], [VMEM]
        self.outs, self.out_specs = [like((ny * nx, 2 * nz) + array.shape, array.dtype)], [ANY]
        count = DMA((ny * nx + 2 * nz - 2,))
        self.scratch, self.actions = [count, count, DMA((1,))], ()

    def act(self, what):
        p, full = self.place, self.out_refs[0]
        own = ("own", self.in_refs[0], full.at[p.dp, p.fsdp])
        along = [(("f", k), self.in_refs[0], full.at[p.dp, p.fsdp], "f", k) for k in range(1, p.nf)]
        across = [(("d", k), full.at[p.dp], full.at[p.dp], "d", k) for k in range(1, p.nd)]
        if what == "0":
            self.local(*own).start()
            self.start(along)
        elif what == "1":
            self.local(*own).wait()
            for k in range(1, p.nf):
                self.arrived(("f", k), full.at[p.dp, p.shift("f", -k)], "f", k)
            self.start(across)
        else:
            for k in range(1, p.nd):
                self.arrived(("d", k), full.at[p.shift("d", -k)], "d", k)
            self.drain(along + across)


def add_blocks(into, where, counts, terms):
    total = 1
    for n in counts:
        total *= n

    def body(flat, carry):
        at = []
        for n in reversed(counts):
            at.append(lax.rem(flat, n))
            flat = lax.div(flat, n)
        at = tuple(at[::-1])
        spot = where(*at)
        value = into[spot].astype(f32)
        for ref, index in terms(*at):
            value = value + ref[index].astype(f32)
        into[spot] = value.astype(into.dtype)
        return carry

    lax.fori_loop(0, total, body, 0)


class Reduce(Move):
    def __init__(self, sizes, array, actions, part=None, into=None):
        self.actions, self.part, self.into = actions, part, into
        ny, nx, nz = sizes
        half, rest = nz // 2, nz - nz // 2
        block, kind = block_of(array, part), array.dtype
        self.held = array if isinstance(array, Held) else None
        self.ins, self.in_specs = ([], []) if self.held else ([array], [ANY])
        self.outs, self.out_specs = ([like(block, f32)], [VMEM]) if into is None else ([], [])
        shapes = [
            (ny, nx, nz), (ny, nx, nz), (ny - 1, nx, half), (nx - 1, ny, rest), (nx - 1, half), (ny - 1, rest), (nz - 1,)
        ]
        count = DMA((1 + 2 * (nx - 1) + 2 * (ny - 1) + nz - 1,))
        self.scratch = [count, count, DMA((1,))] + [pltpu.VMEM(a + block, kind) for a in shapes]

    def act(self, what):
        p, stage = self.place, int(what)
        y, x, z = p.y, p.x, p.z
        source = self.held.ref if self.held else self.in_refs[0]
        acc, core, la, lb, ma, mb, last = self.refs[3:]
        own = ("own", part_of(source, self.part, p.c), acc)
        xs, ys, zs = range(1, p.nx), range(1, p.ny), range(1, p.nz)

        def leaving(at):
            if at == 0:
                return [("c", part_of(source, self.part, p.other), core, "c", 1)]
            if at == 1:
                return [(("y", k), acc.at[p.shift("y", k), :, p.low], la.at[k - 1], "y", k) for k in ys] + [
                    (("x", k), acc.at[:, p.shift("x", k), p.high], lb.at[k - 1], "x", k) for k in xs
                ]
            if at == 2:
                return [(("yx", k), acc.at[y, p.shift("x", k), p.low], ma.at[k - 1], "x", k) for k in xs] + [
                    (("xy", k), acc.at[p.shift("y", k), x, p.high], mb.at[k - 1], "y", k) for k in ys
                ]
            return [(("z", k), acc.at[y, x, p.shift("z", k)], last.at[k - 1], "z", k) for k in zs]

        if stage > 0:
            for key, _, to, axis, k in leaving(stage - 1):
                self.arrived(key, to, axis, k)
        if stage == 0:
            self.local(*own).start()
        elif stage == 1:
            self.local(*own).wait()
            add_blocks(acc, lambda *at: at, (p.ny, p.nx, p.nz), lambda *at: [(core, at)])
        elif stage == 2:
            add_blocks(
                acc, lambda i, j: (y, i, j), (p.nx, p.half), lambda i, j: [(la, (k, i, j)) for k in range(p.ny - 1)]
            )
            add_blocks(
                acc, lambda i, j: (i, x, p.half + j), (p.ny, p.rest),
                lambda i, j: [(lb, (k, i, j)) for k in range(p.nx - 1)],
            )
        elif stage == 3:
            add_blocks(acc, lambda j: (y, x, j), (p.half,), lambda j: [(ma, (k, j)) for k in range(p.nx - 1)])
            add_blocks(
                acc, lambda j: (y, x, p.half + j), (p.rest,), lambda j: [(mb, (k, j)) for k in range(p.ny - 1)]
            )
        if stage < 4:
            self.start(leaving(stage))
        else:
            value = acc[y, x, z].astype(f32)
            for k in range(p.nz - 1):
                value = value + last[k].astype(f32)
            if self.into is None:
                self.out_refs[0][...] = value
            else:
                held, start = self.into
                held.ref[:, start : start + value.shape[1]] = value
            for at in range(4):
                self.drain(leaving(at))


class ReduceCore(Move):
    def __init__(self, sizes, array, actions, part=None):
        self.actions, self.part = actions, part
        ny, nx, nz = sizes
        self.held = array if isinstance(array, Held) else None
        self.ins, self.in_specs = ([], []) if self.held else ([array], [ANY])
        self.outs, self.out_specs = [like((ny, nx, nz) + block_of(array, part), array.dtype)], [ANY]
        self.scratch = [DMA((1,)), DMA((1,))]

    def act(self, what):
        p = self.place
        source = self.held.ref if self.held else self.in_refs[0]
        leaving = [("c", part_of(source, self.part, p.other), self.out_refs[0], "c", 1)]
        if what == "s":
            self.start(leaving)
        else:
            self.arrived("c", self.out_refs[0], "c", 1)
            self.drain(leaving)


class ReduceFirst(Move):
    def __init__(self, sizes, array, core, actions, part=None):
        self.actions, self.part, self.core = actions, part, core
        ny, nx, nz = sizes
        half, rest = nz // 2, nz - nz // 2
        block, kind = block_of(array, part), array.dtype
        self.held = array if isinstance(array, Held) else None
        self.ins = ([] if self.held else [array]) + ([] if isinstance(core, Move) else [core])
        self.in_specs = [ANY] * len(self.ins)
        self.outs = [
            like((ny - 1, nx, half) + block, kind), like((nx - 1, ny, rest) + block, kind),
            like((nx, half) + block, kind), like((ny, rest) + block, kind),
        ]
        self.out_specs = [ANY] * 4
        remote = DMA((nx + ny - 2,))
        self.scratch = [remote, remote, DMA((4,))] + [pltpu.VMEM((ny, nx, nz) + block, kind)] * 2

    def act(self, what):
        p = self.place
        source = self.held.ref if self.held else self.in_refs[0]
        core = self.core.out_refs[0] if isinstance(self.core, Move) else self.in_refs[-1]
        acc, buf = self.refs[3:]
        la, lb, ka, kb = self.out_refs
        loads = [("acc", part_of(source, self.part, p.c), acc), ("buf", core, buf)]
        leaving = [
            (("y", k), acc.at[p.shift("y", k), :, p.low], la.at[k - 1], "y", k) for k in range(1, p.ny)
        ] + [(("x", k), acc.at[:, p.shift("x", k), p.high], lb.at[k - 1], "x", k) for k in range(1, p.nx)]
        keeps = [("ka", acc.at[p.y, :, p.low], ka), ("kb", acc.at[:, p.x, p.high], kb)]
        if what == "l":
            for item in loads:
                self.local(*item).start()
        elif what == "a":
            for item in loads:
                self.local(*item).wait()
            add_blocks(acc, lambda *at: at, (p.ny, p.nx, p.nz), lambda *at: [(buf, at)])
            self.start(leaving)
            for item in keeps:
                self.local(*item).start()
        else:
            for k in range(1, p.ny):
                self.arrived(("y", k), la.at[k - 1], "y", k)
            for k in range(1, p.nx):
                self.arrived(("x", k), lb.at[k - 1], "x", k)
            for item in keeps:
                self.local(*item).wait()
            self.drain(leaving)


class ReduceSecond(Move):
    def __init__(self, sizes, first, actions):
        self.actions, self.first = actions, first
        ny, nx, nz = sizes
        half, rest = nz // 2, nz - nz // 2
        self.inside = isinstance(first, Move)
        arrays = first.outs if self.inside else first
        block, kind = arrays[0].shape[-2:], arrays[0].dtype
        self.ins, self.in_specs = ([], []) if self.inside else (list(arrays), [ANY] * 4)
        self.outs = [
            like((nx - 1, half) + block, kind), like((ny - 1, rest) + block, kind), like((nz,) + block, kind)
        ]
        self.out_specs = [ANY] * 3
        remote = DMA((nx + ny - 2,))
        self.scratch = [remote, remote, DMA((6,))] + [pltpu.VMEM(a.shape, kind) for a in arrays]

    def act(self, what):
        p = self.place
        arrays = self.first.out_refs if self.inside else self.in_refs
        bufs = self.refs[3:]
        la, lb, ka, kb = bufs
        ma, mb, kept = self.out_refs
        loads = [(i, a, b) for i, (a, b) in enumerate(zip(arrays, bufs))]
        leaving = [(("x", k), ka.at[p.shift("x", k)], ma.at[k - 1], "x", k) for k in range(1, p.nx)]
        leaving += [(("y", k), kb.at[p.shift("y", k)], mb.at[k - 1], "y", k) for k in range(1, p.ny)]
        keeps = [("ka", ka.at[p.x], kept.at[p.low]), ("kb", kb.at[p.y], kept.at[p.high])]
        if what == "l":
            for item in loads:
                self.local(*item).start()
        elif what == "a":
            for item in loads:
                self.local(*item).wait()
            add_blocks(ka, lambda *at: at, (p.nx, p.half), lambda i, j: [(la, (k, i, j)) for k in range(p.ny - 1)])
            add_blocks(kb, lambda *at: at, (p.ny, p.rest), lambda i, j: [(lb, (k, i, j)) for k in range(p.nx - 1)])
            self.start(leaving)
            for item in keeps:
                self.local(*item).start()
        else:
            for k in range(1, p.nx):
                self.arrived(("x", k), ma.at[k - 1], "x", k)
            for k in range(1, p.ny):
                self.arrived(("y", k), mb.at[k - 1], "y", k)
            for item in keeps:
                self.local(*item).wait()
            self.drain(leaving)


class ReduceLast(Move):
    def __init__(self, sizes, second, actions):
        self.actions, self.second = actions, second
        ny, nx, nz = sizes
        self.inside = isinstance(second, Move)
        arrays = second.outs if self.inside else second
        block, kind = arrays[0].shape[-2:], arrays[0].dtype
        self.ins, self.in_specs = ([], []) if self.inside else (list(arrays), [ANY] * 3)
        self.outs, self.out_specs = [like(block, f32)], [VMEM]
        self.scratch = [DMA((nz - 1,)), DMA((nz - 1,)), DMA((3,))] + [pltpu.VMEM(a.shape, kind) for a in arrays]
        self.scratch += [pltpu.VMEM((nz - 1,) + block, kind)]

    def act(self, what):
        p = self.place
        arrays = self.second.out_refs if self.inside else self.in_refs
        ma, mb, kept, last = self.refs[3:]
        loads = [(i, a, b) for i, (a, b) in enumerate(zip(arrays, (ma, mb, kept)))]
        leaving = [(("z", k), kept.at[p.shift("z", k)], last.at[k - 1], "z", k) for k in range(1, p.nz)]
        if what == "l":
            for item in loads:
                self.local(*item).start()
        elif what == "a":
            for item in loads:
                self.local(*item).wait()
            add_blocks(kept, lambda j: (j,), (p.half,), lambda j: [(ma, (k, j)) for k in range(p.nx - 1)])
            add_blocks(
                kept, lambda j: (p.half + j,), (p.rest,), lambda j: [(mb, (k, j)) for k in range(p.ny - 1)]
            )
            self.start(leaving)
        else:
            for k in range(1, p.nz):
                self.arrived(("z", k), last.at[k - 1], "z", k)
            value = kept[p.z].astype(f32)
            for k in range(p.nz - 1):
                value = value + last[k].astype(f32)
            self.out_refs[0][...] = value
            self.drain(leaving)


def run(
    kernel, grid, ins, outs, shapes, args, scratch=(), name=None, moves=(), sizes=None, group=None, axes="yxzc", script=None
):
    single = not isinstance(shapes, (list, tuple))
    outs, shapes = ([outs], [shapes]) if single else (list(outs), list(shapes))
    counts = len(ins), len(outs), len(scratch)
    all_ins, all_specs, all_outs = list(args), list(ins), list(shapes)
    all_out_specs, all_scratch, aliases = list(outs), list(scratch), {}
    for move in moves:
        for i, o in move.aliases:
            aliases[len(all_ins) + i] = len(all_outs) + o
        all_ins += list(move.ins)
        all_specs += list(move.in_specs)
        all_outs += list(move.outs)
        all_out_specs += list(move.out_specs)
        all_scratch += list(move.scratch)

    def body(*refs):
        refs = list(refs)

        def take(n):
            part = refs[:n]
            del refs[:n]
            return part

        mine_in = take(counts[0])
        moved_in = [take(len(m.ins)) for m in moves]
        mine_out = take(counts[1])
        moved_out = [take(len(m.outs)) for m in moves]
        mine_scratch = take(counts[2])
        place = Place(sizes) if moves else None
        for move, i, o in zip(moves, moved_in, moved_out):
            move.bind(place, i, o, take(len(move.scratch)))
        step = pl.program_id(0)

        def turn(at):
            for move in moves:
                for when, what in move.actions:
                    if when == at:
                        move.act(what)

        def play():
            for item in script:
                if isinstance(item, tuple):
                    item[0].act(item[1])
                else:
                    item(mine_in, mine_out, mine_scratch)

        if kernel is None:
            place.enter(axes)
            play()
            return

        for at in range(grid):
            if any(when == at for m in moves for when, _ in m.actions):

                @pl.when(step == at)
                def _(at=at):
                    if at == 0:
                        place.enter(axes)
                    turn(at)

        kernel(*mine_in, *mine_out, *mine_scratch)
        if moves:

            @pl.when(step == grid - 1)
            def _():
                turn(grid)
                if script is not None:
                    play()

    params = dict(vmem_limit_bytes=(63 if moves else 60) * 1024 * 1024)
    if moves:
        params.update(collective_id=group, has_side_effects=True)
    moved = sum(a.size * a.dtype.itemsize for a in args)
    results = pl.pallas_call(
        body,
        grid=(grid,),
        in_specs=all_specs,
        out_specs=all_out_specs,
        out_shape=all_outs,
        scratch_shapes=all_scratch,
        input_output_aliases=aliases,
        name=name,
        cost_estimate=pl.CostEstimate(flops=0, bytes_accessed=2 * moved, transcendentals=0),
        compiler_params=pltpu.CompilerParams(**params),
    )(*all_ins)
    return results[0] if single and not moves else results


def tables(clip_row, pad, count):
    frames = clip_row.shape[0]
    size = count // frames
    slots = jnp.arange(frames, dtype=jnp.int32)
    ends = jnp.sum(jnp.where(slots[None, :] <= slots[:, None], clip_row[None, :], 0), axis=1)
    clip_of = jnp.sum((slots[:, None] >= ends[None, :]).astype(jnp.int32), axis=1)
    starts = ends - clip_row
    start_of = jnp.sum(jnp.where(clip_of[:, None] == slots[None, :], starts[None, :], 0), axis=1)
    frame_pos = slots - start_of
    frame = jnp.arange(count, dtype=jnp.int32) // size
    lane = jnp.arange(LANE, dtype=jnp.int32) % HD
    frame_hot = frame[:, None] == lane[None, :]
    own = frame[:, None] == slots[None, :]
    clip_tok = jnp.sum(jnp.where(own, clip_of[None, :], 0), axis=1)
    pos_tok = jnp.sum(jnp.where(own, frame_pos[None, :], 0), axis=1)
    lane_own = lane[:, None] == slots[None, :]
    lane_clip = jnp.sum(jnp.where(lane_own, clip_of[None, :], 0), axis=1)
    lane_pos = jnp.sum(jnp.where(lane_own, frame_pos[None, :], 0), axis=1)
    seen = (
        (clip_tok[:, None] == lane_clip[None, :])
        & (pos_tok[:, None] <= lane_pos[None, :])
        & (pad[:, None] == 1)
    )
    see = jnp.where((lane[None, :] < frames) & ~seen, -1e30, 0.0).astype(bf16)
    quarter = HD // 4
    freq = 10000.0 ** (-jnp.arange(quarter, dtype=f32) / quarter)
    patch = jnp.arange(count, dtype=jnp.int32) % size
    angle = jnp.concatenate(
        [pos_tok.astype(f32)[:, None] * freq[None, :], patch.astype(f32)[:, None] * freq[None, :]],
        axis=1,
    )
    cosine, sine = jnp.cos(angle), jnp.sin(angle)
    cosine = jnp.concatenate([cosine] * 4, axis=1)
    sine = jnp.concatenate([-sine, sine, -sine, sine], axis=1)
    return see, frame_hot.astype(bf16), cosine, sine


def per_device(
    tokens, cotangent, clip_frames, levels, pad_mask, w_mod, b_mod, w_qkv, b_qkv, w_out, b_out,
    w_up, b_up, w_down, b_down, noise_table,
):
    count, width = tokens.shape
    frames = levels.shape[0]
    size = count // frames
    hidden = w_up.shape[1]
    ndev = width // w_up.shape[0]
    me = lax.axis_index("dp") * lax.axis_size("fsdp") + lax.axis_index("fsdp")

    dp, fsdp = lax.axis_size("dp"), lax.axis_size("fsdp")
    sizes = (dp // 2, 2, fsdp // 2)
    lead = sizes + (2,)

    def flat(array):
        return array.reshape(-1, array.shape[-1])

    def blocks(array, front=0):
        rows = array.shape[front] // ndev
        return array.reshape(array.shape[:front] + lead + (rows, array.shape[-1]))

    biases = [b_mod, b_qkv, b_out, b_up, b_down]
    lengths = [b.shape[0] for b in biases]
    spots = jnp.arange(8 * LANE, dtype=jnp.int32)
    mine_at = jnp.where(spots // (2 * frames) == me, jnp.tile(levels, spots.shape[0] // frames), 0)
    packed = jnp.concatenate([mine_at.astype(f32)] + [b.astype(f32) for b in biases])
    packed = jnp.pad(packed, (0, 16 * LANE - packed.shape[0])).reshape(16, LANE)
    part = Held(lead + (2 * frames, w_mod.shape[1] // 2), f32)
    small = Spread(sizes, packed)
    qkv_w = Gather(sizes, w_qkv, ())
    out_w, up_w = Gather(sizes, w_out, ()), Gather(sizes, w_up, ())
    mod_sum = Reduce(sizes, part, ())

    def add_modulation(ins, _, scratch):
        part.ref = scratch[0]
        load = pltpu.make_async_copy(small.out_refs[0], scratch[1], scratch[2].at[0])
        load.start()
        load.wait()
        modulation_kernel(None, ins[0], ins[1], scratch[0], scratch[1], frames)

    head = run(
        None, 1, [VMEM] * 2, [], [], [noise_table, w_mod],
        [pltpu.VMEM(part.shape, f32), pltpu.VMEM(small.outs[0].shape, f32), DMA((1,))], name="head",
        moves=[small, qkv_w, out_w, up_w, mod_sum], sizes=sizes, group=1, axes="df",
        script=[
            (small, "0"), (qkv_w, "s0a"), (qkv_w, "s0b"), (out_w, "s0"), (small, "1"), (small, "2"), add_modulation,
            (mod_sum, "0"), (qkv_w, "n0a"), (mod_sum, "1"), (qkv_w, "n0b"), (mod_sum, "2"), (qkv_w, "n1a"), (mod_sum, "3"),
            (up_w, "s0a"), (qkv_w, "n1b"), (mod_sum, "4"), (qkv_w, "n2a"), (qkv_w, "n2b"), (qkv_w, "w3a"), (qkv_w, "w3b"),
            (out_w, "w0"), (up_w, "w0a"),
        ],
    )
    small, qkv_w, out_w, up_w = head[:4]
    small = small.reshape(ndev, -1)
    all_levels = jnp.sum(small[:, : 8 * LANE], axis=0).reshape(-1, 2 * frames)[:ndev, :frames]
    all_levels = all_levels.reshape(-1).astype(jnp.int32)
    full_bias, at = [], 8 * LANE
    for length in lengths:
        full_bias.append(small[:, at : at + length].reshape(1, -1))
        at += length
    bias_mod, bias_qkv, bias_out, bias_up, bias_down = full_bias
    modulation = jnp.transpose(head[-1].reshape(2, frames, -1), (1, 0, 2)).reshape(frames, -1)
    modulation = (modulation + bias_mod).reshape(frames, 6, width)
    full_qkv = flat(qkv_w)
    see, frame_hot, cosine, sine = tables(clip_frames[0], pad_mask, count)

    acts = like((count, width), bf16)
    wide = like((count, width), f32)
    tall = like((count, hidden), bf16)
    row = whole((1, width))
    mod_row = pl.BlockSpec((1, 6, width), lambda i: (i, 0, 0))
    mod_all = whole((frames, 6, width))
    rows_bf = by_rows(size, width)
    def turn(start, count, index):
        return lambda i: index(jnp.clip(i - start, 0, count - 1))

    def held(shape):
        return pl.BlockSpec(shape, lambda i: (0,) * len(shape), pipeline_mode=pl.Buffered(1))

    pairs = width // LANE
    step = 512
    tiles = hidden // step
    m1, m2 = frames + pairs, 2 * frames + pairs
    steps = m2 + tiles
    rows_one = pl.BlockSpec((size, width), turn(0, frames, lambda i: (i, 0)))
    rows_two = pl.BlockSpec((size, width), turn(m1, frames, lambda i: (i, 0)))
    lanes_one = pl.BlockSpec((size, LANE), turn(0, frames, lambda i: (i, 0)))
    pair_one = pl.BlockSpec((count, LANE), turn(frames, pairs, lambda i: (0, i)))
    cols_one = pl.BlockSpec((count, step), turn(m2, tiles, lambda i: (0, i)))
    move_out = Gather(
        sizes, out_w, [(0, "s1"), (3, "n1"), (8, "n2"), (9, "w3"), (9, "l"), (m1, "d")], True, load=True
    )
    move_up = Gather(
        sizes, up_w,
        [
            (0, "s1a"), (0, "s0b"), (2, "n1a"), (5, "n0b"), (7, "n2a"), (8, "w3a"), (8, "la"), (9, "n1b"), (m2, "da"),
            (m2 + 1, "n2b"), (m2 + 2, "w3b"), (m2 + 2, "lb"), (m2 + tiles // 2, "db"),
        ], True, w_up, True,
    )
    move_down = Gather(
        sizes, w_down,
        [
            (1, "s0a"), (1, "s0b"), (8, "n0a"), (11, "n0b"), (11, "n1a"), (m2 + 3, "n1b"), (steps, "n2a"), (steps, "n2b"),
            (steps, "w3a"), (steps, "w3b"),
        ],
    )
    act_one, query, key, value, attended, aug, middle, attn, act_two, activated, slope, *moved = run(
        lambda *refs: forward_kernel(*refs, frames=frames, pairs=pairs, tiles=tiles, gathers=(move_out, move_up)), steps,
        [
            rows_one, pl.BlockSpec((1, 6, width), turn(0, frames, lambda i: (i, 0, 0))), held((width, 3 * width)),
            held((1, 3 * width)), lanes_one, lanes_one, held((count, LANE)), held((count, LANE)), rows_two,
            pl.BlockSpec((1, 6, width), turn(m1, frames, lambda i: (i, 0, 0))), held((1, width)),
            pl.BlockSpec((1, step), turn(m2, tiles, lambda i: (0, i))),
        ],
        [rows_one] * 4 + [pair_one] * 2 + [rows_two] * 3 + [cols_one] * 2,
        [acts] * 6 + [wide, acts, acts] + [tall] * 2,
        (
            tokens, modulation, full_qkv, bias_qkv, cosine, sine, see, frame_hot, tokens, modulation, bias_out, bias_up,
        ),
        [pltpu.VMEM((count, width), bf16)] * 5, name="fwd",
        moves=[move_out, move_up, move_down], sizes=sizes, group=2,
    )
    full_out, full_up, full_down = [flat(w) for w in moved]
    full = whole((count, width))
    cols_h = by_cols(count, step)
    acc = pltpu.VMEM((count, width), f32)
    deep = hidden // width
    block_out, d_branch, d_gate_two, bdown = run(
        down_kernel, deep, [by_cols(count, width), by_rows(width, width), row, full, full, mod_all],
        [full, full, whole((frames, width)), row],
        [acts, acts, like((frames, width), f32), like((1, width), f32)],
        (activated, full_down, bias_down, middle, cotangent, modulation), [acc], name="down",
    )
    wdown = run(
        weight_grad_kernel, tiles, [cols_h, full], by_rows(step, width), like((hidden, width), bf16),
        (activated, d_branch), name="wdown",
    )
    wdown = blocks(wdown)
    stacked = pl.BlockSpec((1, count, width), lambda i: (i, 0, 0))
    once = held((count, width))
    mod_once = held((frames, 6, width))
    halves = ((0, width // 2), (width // 2, width))
    steps = 2 * tiles + deep
    sum_a = Reduce(
        sizes, wdown, [(0, "0"), (2, "1"), (tiles + 1, "2"), (2 * tiles + 2, "3"), (steps, "4")], halves[0]
    )
    core = ReduceCore(sizes, wdown, [(0, "s"), (3, "w")], halves[1])
    first = ReduceFirst(sizes, wdown, core, [(3, "l"), (4, "a"), (2 * tiles, "w")], halves[1])
    second = ReduceSecond(sizes, first, [(2 * tiles, "l"), (2 * tiles + 1, "a"), (steps, "w")])
    bup, wup, d_middle, d_attn, stat_two, bout, *moved = run(
        lambda *refs: mlp_kernel(*refs, tiles=tiles, deep=deep), steps,
        [
            once, pl.BlockSpec((step, width), turn(0, tiles, lambda i: (i, 0))),
            pl.BlockSpec((count, step), turn(0, tiles, lambda i: (0, i))), once,
            pl.BlockSpec((width, width), turn(2 * tiles, deep, lambda i: (0, i))), ANY, ANY, ANY, mod_once,
        ],
        [
            pl.BlockSpec((1, step), turn(0, tiles, lambda i: (0, i))),
            pl.BlockSpec((width, step), turn(tiles, tiles, lambda i: (0, i))),
            once, once, held((frames, 3, width)), held((1, width)),
        ],
        [
            like((1, hidden), f32), like((width, hidden), bf16), wide, acts, like((frames, 3, width), f32),
            like((1, width), f32),
        ],
        (d_branch, full_down, slope, act_two, full_up, middle, cotangent, attn, modulation),
        [
            pltpu.VMEM((count, hidden), bf16), acc, acc, pltpu.VMEM((count, width), bf16),
            pltpu.VMEM((count, width), bf16), DMA((3,)),
        ],
        name="mlpb", moves=[sum_a, core, first, second], sizes=sizes, group=6,
    )
    wdown_low, down_b = moved[0], moved[6:9]
    wup = blocks(wup)
    halves = ((0, hidden // 2), (hidden // 2, hidden))
    quarters = 4
    quarter = width // quarters
    steps = quarters + pairs + 3
    sum_a = Reduce(sizes, wup, [(0, "0"), (2, "1"), (7, "2"), (11, "3"), (steps, "4")], halves[0])
    core = ReduceCore(sizes, wup, [(0, "s"), (3, "w")], halves[1])
    first = ReduceFirst(sizes, wup, core, [(3, "l"), (5, "a"), (11, "w")], halves[1])
    second = ReduceSecond(sizes, first, [(11, "l"), (12, "a"), (steps, "w")])
    last_b = ReduceLast(sizes, down_b, [(0, "l"), (1, "a"), (9, "w")])
    pair_b = pl.BlockSpec((count, LANE), turn(quarters, pairs, lambda i: (0, i)))
    table_once = held((count, LANE))
    wout, d_projected, bqkv, wqkv, *moved = run(
        lambda *refs: attention_back_kernel(*refs, frames=frames, lead=quarters, pairs=pairs), steps,
        [
            once, pl.BlockSpec((quarter, width), turn(0, quarters, lambda i: (i, 0))),
            pl.BlockSpec((count, quarter), turn(0, quarters, lambda i: (0, i))),
        ] + [pair_b] * 5 + [table_once] * 3 + [once],
        [
            pl.BlockSpec((quarter, width), turn(0, quarters, lambda i: (i, 0))),
            pl.BlockSpec((3, count, LANE), turn(quarters, pairs, lambda i: (0, 0, i))),
            pl.BlockSpec((1, 3, LANE), turn(quarters, pairs, lambda i: (i, 0, 0))),
            pl.BlockSpec((1, width, width), turn(quarters + pairs, 3, lambda i: (i, 0, 0))),
        ],
        [
            like((width, width), bf16), like((3, count, width), bf16), like((pairs, 3, LANE), f32),
            like((3, width, width), bf16),
        ],
        (d_attn, full_out, attended, query, key, value, attended, aug, see, cosine, sine, act_one),
        [pltpu.VMEM((count, width), bf16), pltpu.VMEM((3, count, width), bf16), pltpu.VMEM((count, LANE), f32)],
        name="attb", moves=[last_b, sum_a, core, first, second], sizes=sizes, group=7,
    )
    wdown_high, wup_low, up_b = moved[0], moved[1], moved[7:10]
    wdown_grad = jnp.concatenate([wdown_low, wdown_high], axis=1)
    wout, wqkv = blocks(wout), blocks(wqkv, 1)

    bqkv = jnp.transpose(bqkv, (1, 0, 2)).reshape(1, -1)
    shares = [b.reshape(ndev, -1) for b in (bqkv, bout, bup, bdown)]
    packed = jnp.concatenate(shares, axis=1)
    bias_len = packed.shape[1]
    packed = jnp.pad(packed, ((0, 0), (0, 8 * LANE - bias_len))).reshape(-1, LANE)
    packed = blocks(packed)
    mod_block = Held((6 * frames, width), bf16)
    d_mod = Gather(sizes, mod_block, ())
    bias = Reduce(sizes, packed, ())
    qkv_out, out_out = Held((width // ndev, 3 * width), f32), Held((width // ndev, width), f32)
    marks = ([(0, "0"), (0, "1"), (1, "2"), (2, "3")], [(0, "0"), (0, "1"), (2, "2")], [(0, "0"), (1, "1")])
    q, k, v = [Reduce(sizes, wqkv, marks[i], i, (qkv_out, i * width)) for i in range(3)]
    halves = ((0, width // 2), (width // 2, width))
    oa = Reduce(sizes, wout, [(0, "0"), (2, "1")], halves[0], (out_out, 0))
    ob = Reduce(sizes, wout, [(0, "0")], halves[1], (out_out, width // 2))
    last_b = ReduceLast(sizes, up_b, [(0, "l"), (0, "a"), (3, "w")])

    def pack_modulation(ins, outs, scratch):
        one, two, gate = outs[1], ins[5], ins[6]
        parts = [one[:, 0, :], one[:, 1, :], two[:, 0, :], two[:, 1, :], two[:, 2, :], gate[...]]
        mod_block.ref = scratch[1]
        qkv_out.ref, out_out.ref = outs[2:]
        scratch[1][...] = jnp.concatenate(parts, axis=0).astype(bf16)

    def set_block(refs):
        input_back_kernel(*refs[:5], *refs[7:9], refs[11])

    token_grad, stat_one, wqkv_grad, wout_grad, *moved = run(
        lambda *refs: set_block(refs), 3,
        [stacked, by_cols(width, width), once, once, mod_once, held((frames, 3, width)), held((frames, width))],
        [once, held((frames, 2, width)), VMEM, VMEM],
        [acts, like((frames, 2, width), f32), like(qkv_out.shape, f32), like(out_out.shape, f32)],
        (d_projected, full_qkv, tokens, d_middle, modulation, stat_two, d_gate_two),
        [acc, pltpu.VMEM(mod_block.shape, bf16)], name="dact1",
        moves=[d_mod, q, k, v, oa, ob, last_b, bias], sizes=sizes, group=8,
        script=[
            (bias, "0"), pack_modulation, (d_mod, "s0"), (v, "2"), (k, "3"), (ob, "1"), (bias, "1"), (d_mod, "n0"), (oa, "2"),
            (v, "3"), (ob, "2"), (bias, "2"), (d_mod, "n1"), (oa, "3"), (ob, "3"), (d_mod, "n2"), (bias, "3"), (q, "4"),
            (k, "4"), (bias, "4"), (v, "4"), (d_mod, "w3"), (oa, "4"), (ob, "4"),
        ],
    )
    d_mod, wup_high, bias_sum = moved
    wup_grad = jnp.concatenate([wup_low, wup_high], axis=1)
    d_mod = jnp.transpose(d_mod.reshape(ndev, 6, frames, width), (0, 2, 1, 3))
    d_mod = d_mod.reshape(ndev * frames, -1)
    bias_sum = bias_sum.reshape(-1)[:bias_len]
    bias_grads, at = [], 0
    for share in shares:
        bias_grads.append(bias_sum[at : at + share.shape[1]])
        at += share.shape[1]
    hot = (all_levels[:, None] == jnp.arange(noise_table.shape[1], dtype=jnp.int32)[None, :]).astype(bf16)
    embedded = dot(hot, noise_table, NT)
    cond = jax.nn.silu(embedded).astype(bf16)
    wmod_grad = dot(cond, d_mod, TN)
    mine = b_mod.shape[0]
    bmod_grad = jnp.sum(lax.dynamic_slice(d_mod, (0, me * mine), (d_mod.shape[0], mine)).astype(f32), axis=0)
    gate = jax.nn.sigmoid(embedded)
    d_embed = dot(d_mod, w_mod, NT) * gate * (1.0 + embedded * (1.0 - gate))
    table_grad = lax.dot_general(
        d_embed, hot.astype(f32), TN, precision=lax.Precision.HIGHEST, preferred_element_type=f32
    )
    return (
        block_out, token_grad, wmod_grad, bmod_grad, wqkv_grad, bias_grads[0], wout_grad, bias_grads[1],
        wup_grad, bias_grads[2], wdown_grad, bias_grads[3], table_grad,
    )


def solution(mesh):
    rows, vec = P(AXES, None), P(AXES)
    return jax.shard_map(
        per_device,
        mesh=mesh,
        in_specs=(rows, rows, rows, vec, vec) + (rows, vec) * 5 + (rows,),
        out_specs=(rows, rows) + (rows, vec) * 5 + (rows,),
        check_vma=False,
    )
```
